32 devices in a mesh: dp: 8 (over z, y), tensor: 4 (over x, core).
Axes of the slice: x: 2, y: 2, z: 4, core: 2. Of those that a mesh axis runs over, the one named last changes fastest.
Arguments:
- inputs: bfloat16 [8, 4096, 768], P('dp', 'tensor'), may hold values from -6 to 6
- w_qkv: bfloat16 [3, 768, 768], P(None, None, 'tensor'), may hold values from -0.21875 to 0.21875
- qv_bias: float32 [2, 768], P(None, 'tensor'), may hold values from -3 to 3
- w_proj: bfloat16 [768, 768], P('tensor'), may hold values from -0.875 to 0.875
- proj_bias: float32 [768], replicated, may hold values from -3 to 3
- w_fc1: bfloat16 [768, 3072], P(None, 'tensor'), may hold values from -0.21875 to 0.21875
- fc1_bias: float32 [3072], P('tensor'), may hold values from -3 to 3
- w_fc2: bfloat16 [3072, 768], P('tensor'), may hold values from -0.109375 to 0.109375
- fc2_bias: float32 [768], replicated, may hold values from -3 to 3
- norm1_gain: float32 [768], replicated, may hold values from 0.25 to 1.75
- norm1_shift: float32 [768], replicated, may hold values from -2 to 2
- norm2_gain: float32 [768], replicated, may hold values from 0.25 to 1.75
- norm2_shift: float32 [768], replicated, may hold values from -2 to 2
- rel_h: bfloat16 [27, 64], replicated, may hold values from -0.59765625 to 0.59765625
- rel_w: bfloat16 [27, 64], replicated, may hold values from -0.59765625 to 0.59765625
- cotangent: bfloat16 [8, 4096, 768], P('dp', 'tensor'), may hold values from -9 to 9
Outputs:
- output: bfloat16 [8, 4096, 768], P('dp', 'tensor')
- input_grad: bfloat16 [8, 4096, 768], P('dp', 'tensor')
- grad_qkv: float32 [3, 768, 768], P(None, None, 'tensor')
- grad_qv_bias: float32 [2, 768], P(None, 'tensor')
- grad_proj: float32 [768, 768], P('tensor')
- grad_proj_bias: float32 [768], replicated
- grad_fc1: float32 [768, 3072], P(None, 'tensor')
- grad_fc1_bias: float32 [3072], P('tensor')
- grad_fc2: float32 [3072, 768], P('tensor')
- grad_fc2_bias: float32 [768], replicated
- grad_norms: float32 [4, 768], replicated
- grad_rel: float32 [2, 27, 64], replicated
- clipped_qk: bfloat16 [2, 768, 768], P(None, None, 'tensor')
- head_max: float32 [12], P('tensor')
The draws below stay inside these ranges and needn't reach their ends.
All inputs are finite; a program needn't handle non-finite values.
Results may differ from the reference program's by a relative error of at most 0.019.
Values may be sent and summed in bfloat16 or wider, within the bound.
A program may use at most 384 MiB of HBM per device.

```python
import jax
import jax.numpy as jnp
from jax import lax

D = 768
HEADS = 12
HD = 64
MLP = 3072
GRID = 64
WIN = 14
IMAGES = 8
TOK = 4096
PADG = 70
NWIN = 25
RELN = 27


def draw_cotangent(key, part):
    base = jnp.clip(jax.random.normal(key, (IMAGES, TOK, D), jnp.float32), -6.0, 6.0)
    ramp = 0.5 + jnp.arange(IMAGES, dtype=jnp.float32) / max(IMAGES - 1, 1)
    return (base * ramp[:, None, None]).astype(jnp.bfloat16)


def steps_of(rng, extent, pieces, low, high):
    level = 1.0
    for axis_at, parts in pieces:
        steps = jax.random.uniform(jax.random.fold_in(jax.random.fold_in(rng, 6), axis_at), (parts,), jnp.float32, low / len(pieces), high / len(pieces))
        level = level * jnp.repeat(jnp.exp(steps), extent[axis_at] // parts).reshape((-1,) + (1,) * (len(extent) - 1 - axis_at))
    return level


def normal_values(stream_key, extent, deviation, limit, shards=(), held_as=jnp.bfloat16):
    array = jax.random.normal(stream_key, extent, jnp.float32) * deviation
    if len(shards) > 0:
        array = steps_of(stream_key, extent, shards, -0.22, 0.18) * array
    return jnp.clip(array, min=-limit, max=limit).astype(held_as)


def setup_inputs(seed: int = 0) -> dict:
    key_of = jax.random.split(jax.random.key(seed), 17)
    return {
        "inputs": normal_values(key_of[0], (IMAGES, TOK, D), 1.0, 6.0, ((0, 8), (1, 4))),
        "w_qkv": normal_values(key_of[1], (3, D, D), D ** -0.5, 0.21875, ((2, 4),)),
        "qv_bias": normal_values(key_of[2], (2, D), 0.5, 3.0, ((1, 4),), jnp.float32),
        "w_proj": normal_values(key_of[3], (D, D), (D // 16) ** -0.5, 0.875, ((0, 4),)),
        "proj_bias": normal_values(key_of[4], (D,), 0.5, 3.0, (), jnp.float32),
        "w_fc1": normal_values(key_of[5], (D, MLP), D ** -0.5, 0.21875, ((1, 4),)),
        "fc1_bias": normal_values(key_of[6], (MLP,), 0.5, 3.0, ((0, 4),), jnp.float32),
        "w_fc2": normal_values(key_of[7], (MLP, D), MLP ** -0.5, 0.109375, ((0, 4),)),
        "fc2_bias": normal_values(key_of[8], (D,), 0.5, 3.0, (), jnp.float32),
        "norm1_gain": jnp.clip(1.0 + 0.15 * jax.random.normal(key_of[9], (D,), jnp.float32), 0.25, 1.75),
        "norm1_shift": normal_values(key_of[10], (D,), 0.3, 2.0, (), jnp.float32),
        "norm2_gain": jnp.clip(1.0 + 0.15 * jax.random.normal(key_of[11], (D,), jnp.float32), 0.25, 1.75),
        "norm2_shift": normal_values(key_of[12], (D,), 0.3, 2.0, (), jnp.float32),
        "rel_h": normal_values(key_of[13], (RELN, HD), 0.1, 0.59765625),
        "rel_w": normal_values(key_of[14], (RELN, HD), 0.1, 0.59765625),
        "cotangent": draw_cotangent(jax.random.fold_in(key_of[16], 71), 0),
    }


eps_norm = 1e-06
clip_limit = 3.0
precise = lax.Precision.HIGHEST

@jax.custom_vjp
def low(v):
    return lax.optimization_barrier(v.astype(jnp.bfloat16)).astype(jnp.float32)

@jax.custom_vjp
def low_back(v):
    return v

def low_keep(v):
    return (low(v), None)

def low_pass(kept, grad):
    return (grad,)

def back_keep(v):
    return (v, None)

def back_low(kept, grad):
    return (low(grad),)
low.defvjp(low_keep, low_pass)
low_back.defvjp(back_keep, back_low)

def both_low(values):
    return low(low_back(values))

def norm_rows(values, gain, shift):
    centre = values - lax.optimization_barrier(jnp.mean(values, axis=-1, keepdims=True))
    spread = lax.optimization_barrier(jnp.mean(centre * centre, axis=-1, keepdims=True))
    return centre * lax.rsqrt(spread + eps_norm) * gain + shift

def rel_table(table):
    offsets = jnp.arange(WIN, dtype=jnp.int32)[:, None] - jnp.arange(WIN, dtype=jnp.int32)[None, :] + (WIN - 1)
    return table[offsets]

def valid_windows():
    inside = jnp.arange(PADG, dtype=jnp.int32) < GRID
    inside = inside[:, None] & inside[None, :]
    count = PADG // WIN
    return inside.reshape(count, WIN, count, WIN).transpose(0, 2, 1, 3).reshape(NWIN, 1, WIN, WIN, 1, 1)

def block(inputs, w_qkv, qv_bias, w_proj, proj_bias, w_fc1, fc1_bias, w_fc2, fc2_bias, norm1_gain, norm1_shift, norm2_gain, norm2_shift, rel_h, rel_w):
    count = PADG // WIN
    first = low(norm_rows(inputs, norm1_gain, norm1_shift))
    padded = jnp.pad(first.reshape(GRID, GRID, D), ((0, PADG - GRID), (0, PADG - GRID), (0, 0))).reshape(PADG * PADG, D)
    query = both_low(jnp.dot(padded, w_qkv[0], precision=precise) + qv_bias[0])
    keys = both_low(jnp.dot(padded, w_qkv[1], precision=precise))
    value = both_low(jnp.dot(padded, w_qkv[2], precision=precise) + qv_bias[1])

    def windows(field):
        return field.reshape(count, WIN, count, WIN, HEADS, HD).transpose(0, 2, 4, 1, 3, 5).reshape(NWIN, HEADS, WIN, WIN, HD)
    q_win, k_win, v_win = (windows(query), windows(keys), windows(value))
    logits = jnp.einsum('nhxyc,nhabc->nhxyab', q_win, k_win, precision=precise) * 0.125
    rel_rows = jnp.einsum('nhxyc,xac->nhxya', q_win, rel_table(rel_h), precision=precise)
    rel_cols = jnp.einsum('nhxyc,ybc->nhxyb', q_win, rel_table(rel_w), precision=precise)
    scores = low_back(logits + rel_rows[..., :, None] + rel_cols[..., None, :])
    scores = scores.reshape(NWIN, HEADS, WIN * WIN, WIN * WIN)
    largest = lax.optimization_barrier(jnp.max(jnp.where(valid_windows(), logits, -1e+30), axis=(0, 2, 3, 4, 5)))
    probs = low(jax.nn.softmax(scores, axis=-1))
    mixed = both_low(jnp.einsum('nhlm,nhmc->nhlc', probs, v_win.reshape(NWIN, HEADS, WIN * WIN, HD), precision=precise))
    merged = mixed.reshape(count, count, HEADS, WIN, WIN, HD).transpose(0, 3, 1, 4, 2, 5).reshape(PADG, PADG, D)
    merged = merged[:GRID, :GRID].reshape(TOK, D)
    attn = low_back(jnp.dot(merged, w_proj, precision=precise) + proj_bias)
    middle = inputs + attn
    second = low(norm_rows(middle, norm2_gain, norm2_shift))
    hidden_pre = low_back(jnp.dot(second, w_fc1, precision=precise) + fc1_bias)
    hidden = low(jax.nn.gelu(hidden_pre, approximate=False))
    branch = low_back(jnp.dot(hidden, w_fc2, precision=precise) + fc2_bias)
    return (middle + branch, largest)

def reference(inputs, w_qkv, qv_bias, w_proj, proj_bias, w_fc1, fc1_bias, w_fc2, fc2_bias, norm1_gain, norm1_shift, norm2_gain, norm2_shift, rel_h, rel_w, cotangent):
    params = (w_qkv.astype(jnp.float32), qv_bias.astype(jnp.float32), w_proj.astype(jnp.float32), proj_bias.astype(jnp.float32), w_fc1.astype(jnp.float32), fc1_bias.astype(jnp.float32), w_fc2.astype(jnp.float32), fc2_bias.astype(jnp.float32), norm1_gain.astype(jnp.float32), norm1_shift.astype(jnp.float32), norm2_gain.astype(jnp.float32), norm2_shift.astype(jnp.float32), rel_h.astype(jnp.float32), rel_w.astype(jnp.float32))

    def one_image(totals, pair):
        image, grad_image = pair
        result, pull, largest = jax.vjp(block, image.astype(jnp.float32), *params, has_aux=True)
        grads = pull(grad_image.astype(jnp.float32))
        totals = jax.tree.map(lambda total, part: total + part, totals, tuple(grads[1:]))
        return (totals, (result.astype(jnp.bfloat16), grads[0].astype(jnp.bfloat16), largest))
    zeros = jax.tree.map(lambda param: jnp.zeros(param.shape, jnp.float32), params)
    totals, (output, input_grad, maxima) = lax.scan(one_image, zeros, (inputs, cotangent))
    head_max = lax.optimization_barrier(jnp.max(maxima, axis=0))
    factor = jnp.sqrt(clip_limit / jnp.maximum(head_max, clip_limit))
    columns = jnp.repeat(factor, HD)
    clipped_qk = (params[0][:2] * columns).astype(jnp.bfloat16)
    grad_norms = jnp.stack([totals[8], totals[9], totals[10], totals[11]])
    grad_rel = jnp.stack([totals[12], totals[13]])
    return (output, input_grad, totals[0], totals[1], totals[2], totals[3], totals[4], totals[5], totals[6], totals[7], grad_norms, grad_rel, clipped_qk, head_max)
```

```python
import functools

import jax
import jax.numpy as jnp
import numpy as np
from jax import lax
from jax.experimental import pallas as pl
from jax.experimental.pallas import tpu as pltpu
from jax.sharding import PartitionSpec as P

HD = 64
GRID = 64
WIN = 14
TILES = 5
SPAN = WIN * WIN
ROWS = 208
SLOTS = 7
SLAB = 6 * ROWS
LEFT = 6
RIGHT = 12
LANES = 128
EPS = 1e-6
CLIP = 3.0
VMEM = 60 * 1024 * 1024

single = jnp.float32
narrow = jnp.bfloat16

OWNED = (
    ((0, 0), (0, 1), (0, 2), (0, 3), (0, 4), (1, 0)),
    ((1, 1), (1, 2), (1, 3), (1, 4), (2, 0), (2, 1)),
    ((2, 2), (2, 3), (2, 4), (3, 0), (3, 1), (3, 2)),
    ((3, 3), (3, 4), (4, 0), (4, 1), (4, 2), (4, 3), (4, 4)),
)
FIELDS = 6


def owner_table(rows_held):
    table = np.zeros((len(OWNED), SLOTS, FIELDS), np.int32)
    for device, windows in enumerate(OWNED):
        offset = 0
        for slot, (i, j) in enumerate(windows):
            high = min(WIN, GRID - i * WIN)
            wide = min(WIN, GRID - j * WIN)
            first = i * WIN - device * rows_held + LEFT
            table[device, slot] = (first, j * WIN, high, wide, offset, 1)
            offset += ROWS if high == WIN else -(-high * WIN // 16) * 16
    return table.reshape(len(OWNED), SLOTS * FIELDS)


def lane_tables():
    row = np.arange(ROWS)
    x, y = row // WIN, row % WIN
    lane = np.arange(LANES) % 64
    part = lane // 32
    at = lane % 32
    amount = np.where(part[None, :] == 0, 13 - x[:, None], 13 - y[:, None])
    amount = np.where((row < SPAN)[:, None], amount, 0)
    bits = np.stack([(amount >> b) & 1 for b in range(4)]).astype(np.float32)
    lanes = np.zeros((8, LANES), np.float32)
    lanes[0] = at < WIN
    lanes[1] = (at >= 16) & (at < 16 + WIN)
    lanes[2] = lane == 31
    sides = np.zeros((16, LANES), np.float32)
    sides[0] = np.arange(LANES) < 64
    sides[1] = np.arange(LANES) >= 64
    place = np.where(part[None, :] == 0, x[:, None], y[:, None])
    hot = ((at % 16)[None, :] == place) & ((at % 16) < WIN)[None, :] & (row < SPAN)[:, None]
    keys = hot.astype(np.float32)
    keys[SPAN:, lane == 31] = -1e30
    return (
        jnp.asarray(bits),
        jnp.asarray(lanes),
        jnp.asarray(sides, narrow),
        jnp.asarray(keys, narrow),
    )


def dot(a, b):
    return jnp.dot(a, b, preferred_element_type=single)


def dot_nt(a, b):
    return lax.dot_general(a, b, (((1,), (1,)), ((), ())), preferred_element_type=single)


def dot_tn(a, b):
    return lax.dot_general(a, b, (((0,), (0,)), ((), ())), preferred_element_type=single)


def norm_parts(values):
    centre = values - jnp.mean(values, axis=-1, keepdims=True)
    inverse = lax.rsqrt(jnp.mean(centre * centre, axis=-1, keepdims=True) + EPS)
    return centre * inverse, inverse


def norm_back(grad, normal, inverse, gain):
    scaled = grad * gain
    first = jnp.mean(scaled, axis=-1, keepdims=True)
    second = jnp.mean(scaled * normal, axis=-1, keepdims=True)
    return inverse * (scaled - first - normal * second)


def slot_fields(tab):
    base = pl.program_id(0) * FIELDS
    return tuple(tab[base + i] for i in range(FIELDS))


def positions(axis, first_col, high, wide):
    shape = (ROWS, 1) if axis == 0 else (1, ROWS)
    row = lax.broadcasted_iota(jnp.int32, shape, axis)
    x = lax.shift_right_logical(row * 4682, 16)
    y = row - x * WIN
    valid = (x < high) & (y < wide)
    return jnp.where(valid, x * GRID + first_col + y, -1), valid


def gather_window(source, target):
    token = lax.broadcasted_iota(jnp.int32, (ROWS, WIN * GRID), 1)
    choose = jnp.where(token == target, 1.0, 0.0).astype(narrow)
    return dot(choose, source)


def shift_left(values, bits):
    for b in range(4):
        values = jnp.where(bits[b] > 0.5, pltpu.roll(values, LANES - (1 << b), 1), values)
    return values


def shift_right(values, bits):
    for b in range(4):
        values = jnp.where(bits[b] > 0.5, pltpu.roll(values, 1 << b, 1), values)
    return values


def forward_kernel(
    first, tab, ext, gain, shift, known, w, bias, wproj, wrel, bits, lanes, sides, keys, *outs
):
    if first:
        slab, n1_out, qkv, mixed, attn, peak = outs
    else:
        slab, qkv, mixed, attn, peak = outs
    row0, col0, high, wide, offset, live = slot_fields(tab)
    half = w.shape[2]

    @pl.when(pl.program_id(0) == 0)
    def _():
        slab[...] = jnp.zeros_like(slab)
        attn[...] = jnp.zeros_like(attn)
        peak[...] = jnp.zeros_like(peak)

    @pl.when(live == 1)
    def _():
        target, valid = positions(0, col0, high, wide)
        source = ext[pl.ds(pl.multiple_of(row0 * GRID, GRID), WIN * GRID), :]
        window = gather_window(source, target)
        place = pl.ds(pl.multiple_of(offset, 16), ROWS)
        slab[place, :] = window.astype(narrow)
        if first:
            normal, _ = norm_parts(window)
            n1 = jnp.where(valid, normal * gain[...] + shift[...], 0.0).astype(narrow)
            n1_out[0] = n1
        else:
            n1 = known[0]
        query = jnp.where(valid, dot(n1, w[0]) + bias[0:1], 0.0).astype(narrow)
        key8 = dot(n1, w[1]).astype(narrow) * jnp.asarray(0.125, narrow)
        value = (dot(n1, w[2]) + bias[1:2]).astype(narrow)
        qkv[0, 0] = query
        qkv[0, 1] = key8
        qkv[0, 2] = value
        low_lane = lax.broadcasted_iota(jnp.int32, (ROWS, LANES), 1) < 64
        for pair in range(half // LANES):
            cut = slice(pair * LANES, (pair + 1) * LANES)
            q, k8, v = query[:, cut], key8[:, cut], value[:, cut]
            rel = shift_left(dot(q, wrel[...]), bits)
            rest = rel - rel.astype(narrow).astype(single)
            rel = rel * lanes[0:1] + pltpu.roll(rest, 16, 1) * lanes[1:2] + lanes[2:3]
            rel = rel.astype(narrow)
            qkv[0, 3, :, cut] = rel
            pieces = []
            for head in range(2):
                mine, other = sides[head : head + 1], sides[1 - head : 2 - head]
                only = q * mine
                logits = dot_nt(only, k8)
                at = 2 * pair + head
                peak[at : at + 1, :] = jnp.maximum(
                    peak[at : at + 1, :], jnp.max(logits, axis=0, keepdims=True)
                )
                scores = dot_nt(only + rel * other, k8 * mine + keys[...] * other)
                top = jnp.max(scores, axis=1, keepdims=True)
                probs = jnp.exp(scores - top)
                total = jnp.sum(probs, axis=1, keepdims=True)
                pieces.append(dot(probs.astype(narrow), v) * (1.0 / total))
            mixed[0, :, cut] = jnp.where(low_lane, pieces[0], pieces[1]).astype(narrow)
        terms = dot(mixed[0], wproj[...])
        attn[place, :] = jnp.where(valid, terms, 0.0)


def whole(shape):
    zeros = (0,) * len(shape)
    return pl.BlockSpec(shape, lambda *_: zeros, pipeline_mode=pl.Buffered(1))


def held(shape):
    zeros = (0,) * len(shape)
    return pl.BlockSpec(shape, lambda *_: zeros)


def by_slot(shape):
    rest = (0,) * len(shape)
    return pl.BlockSpec((1,) + tuple(shape), lambda s, *_: (s,) + rest)


def forward_half(tab, ext, norm, known, w, bias, wproj, wrel, tables):
    first = known is None
    width = ext.shape[1]
    half = w.shape[2]
    bits, lanes, sides, keys = tables
    if first:
        known = jnp.zeros((SLOTS, 16, LANES), narrow)
    known_spec = by_slot(known.shape[1:])
    outs = [
        (jax.ShapeDtypeStruct((SLAB, width), narrow), held((SLAB, width))),
        (jax.ShapeDtypeStruct((SLOTS, ROWS, width), narrow), by_slot((ROWS, width))),
        (jax.ShapeDtypeStruct((SLOTS, 4, ROWS, half), narrow), by_slot((4, ROWS, half))),
        (jax.ShapeDtypeStruct((SLOTS, ROWS, half), narrow), by_slot((ROWS, half))),
        (jax.ShapeDtypeStruct((SLAB, width), single), held((SLAB, width))),
        (jax.ShapeDtypeStruct((8, ROWS), single), held((8, ROWS))),
    ]
    if not first:
        del outs[1]
    gain, shift = norm
    operands = (ext, gain, shift, known, w, bias, wproj, wrel, bits, lanes, sides, keys)
    in_specs = [whole(a.shape) for a in operands]
    in_specs[3] = known_spec
    return pl.pallas_call(
        functools.partial(forward_kernel, first),
        out_shape=[o[0] for o in outs],
        grid_spec=pltpu.PrefetchScalarGridSpec(
            num_scalar_prefetch=1,
            grid=(SLOTS,),
            in_specs=in_specs,
            out_specs=[o[1] for o in outs],
        ),
        compiler_params=pltpu.CompilerParams(vmem_limit_bytes=VMEM),
        cost_estimate=pl.CostEstimate(
            flops=13_000_000_000, bytes_accessed=30_000_000, transcendentals=4_000_000
        ),
        name="attention_forward",
    )(tab, *operands)


BLOCK = 256
CHUNK = 416


def gelu_parts(z):
    size = jnp.abs(z)
    bell = jnp.exp(-0.5 * z * z)
    t = 1.0 / (1.0 + 0.2316418882663604 * size)
    poly = 0.5 * 1.061405429 * t + (0.5 * -1.453152027)
    poly = poly * t + 0.5 * 1.421413741
    poly = poly * t + 0.5 * -0.284496736
    poly = poly * t + 0.5 * 0.254829592
    tail = poly * t * bell
    phi_total = jnp.where(z >= 0, 1.0 - tail, tail)
    return z * phi_total, phi_total + z * bell * 0.3989422804014327


def mlp_kernel(first, *refs):
    if first:
        (xs, attn1, attn2, gs, pbias, gain, shift, w1a, w1b, b1a, b1b, w2a, w2b) = refs[:13]
        (x1, n2, n2t, gt, branch, dn2, gw1a, gw1b, gw2a, gw2b, w1, w2, b1, hs, zs, gb) = refs[13:]
    else:
        (x1, n2, n2t, gs, gt, branch0, dn20, fbias, gain, w1a, w1b, b1a, b1b, w2a, w2b) = refs[:15]
        (out, dx1, da, sums, gw1a, gw1b, gw2a, gw2b, branch, dn2, w1, w2, b1, hs, zs, gb) = refs[15:]
    step = pl.program_id(0)
    count = pl.num_programs(0) // 2
    rows, width = gs.shape

    @pl.when(step == 0)
    def _():
        if first:

            @pl.loop(0, SLAB // ROWS)
            def _(c):
                sl = pl.ds(pl.multiple_of(c * ROWS, 16), ROWS)
                middle = xs[sl, :].astype(single) + (attn1[sl, :] + attn2[sl, :] + pbias[...])
                x1[sl, :] = middle
                normal, _ = norm_parts(middle)
                n2[sl, :] = (normal * gain[...] + shift[...]).astype(narrow)
                branch[sl, :] = jnp.zeros((ROWS, width), single)
                dn2[sl, :] = jnp.zeros((ROWS, width), single)

            for j in range(width // LANES):
                cut = slice(j * LANES, (j + 1) * LANES)
                n2t[cut, :] = n2[:, cut].T
                gt[cut, :] = gs[:, cut].T
        else:

            @pl.loop(0, SLAB // ROWS)
            def _(c):
                sl = pl.ds(pl.multiple_of(c * ROWS, 16), ROWS)
                branch[sl, :] = branch0[sl, :]
                dn2[sl, :] = dn20[sl, :]

    @pl.when(step < count)
    def _():
        w1[...] = w1a[...]
        w2[...] = w2a[...]
        b1[...] = b1a[...]

    @pl.when(step >= count)
    def _():
        w1[...] = w1b[...]
        w2[...] = w2b[...]
        b1[...] = b1b[...]

    gb[...] = jnp.zeros_like(gb)

    @pl.loop(0, SLAB // CHUNK)
    def _(c):
        sl = pl.ds(pl.multiple_of(c * CHUNK, 16), CHUNK)
        z = dot(n2[sl, :], w1[...]) + b1[0:1]
        dh = dot_nt(gs[sl, :], w2[...])
        act, slope = gelu_parts(z)
        h = act.astype(narrow)
        dz = (dh * slope).astype(narrow)
        hs[sl, :] = h
        zs[sl, :] = dz
        gb[0:1, :] += jnp.sum(dz.astype(single), axis=0, keepdims=True)
        branch[sl, :] += dot(h, w2[...])
        dn2[sl, :] += dot_nt(dz, w1[...])

    def store(gw1, gw2):
        @pl.loop(0, width // 256)
        def _(r):
            sl = pl.ds(pl.multiple_of(r * 256, 256), 256)
            gw1[sl, :] = dot(n2t[sl, :], zs[...]).astype(narrow)
            gw2[sl, :] = dot(gt[sl, :], hs[...]).astype(narrow)

        pad = gw1.shape[0] - width
        gw1[width:, :] = jnp.broadcast_to(gb[0:1, :], (pad, BLOCK)).astype(narrow)

    @pl.when(step < count)
    def _():
        store(gw1a, gw2a)

    @pl.when(step >= count)
    def _():
        store(gw1b, gw2b)

    if not first:

        @pl.when(step == 2 * count - 1)
        def _():
            sums[...] = jnp.zeros_like(sums)

            @pl.loop(0, SLAB // ROWS)
            def _(c):
                sl = pl.ds(pl.multiple_of(c * ROWS, 16), ROWS)
                middle = x1[sl, :]
                normal, inverse = norm_parts(middle)
                out[sl, :] = (middle + (branch[sl, :] + fbias[...])).astype(narrow)
                grad = dn2[sl, :]
                cot = gs[sl, :].astype(single)
                total = cot + norm_back(grad, normal, inverse, gain[...])
                dx1[sl, :] = total
                low = total.astype(narrow)
                da[sl, :] = low
                sums[0:1, :] += jnp.sum(grad * normal, axis=0, keepdims=True)
                sums[1:2, :] += jnp.sum(grad, axis=0, keepdims=True)
                sums[2:3, :] += jnp.sum(low.astype(single), axis=0, keepdims=True)
                sums[3:4, :] += jnp.sum(cot, axis=0, keepdims=True)


PADROWS = 16


def mlp_half(first, residents, w1a, w1b, b1a, b1b, w2a, w2b):
    width, local = w1a.shape
    count = local // BLOCK

    def early(shape, dim):
        def index(i):
            at = jnp.minimum(i, count - 1)
            return (0, at) if dim == 1 else (at, 0)

        return pl.BlockSpec(shape, index)

    def late(shape, dim):
        def index(i):
            at = jnp.maximum(i - count, 0)
            return (0, at) if dim == 1 else (at, 0)

        return pl.BlockSpec(shape, index)

    in_specs = [whole(a.shape) for a in residents] + [
        early((width, BLOCK), 1),
        late((width, BLOCK), 1),
        early((1, BLOCK), 1),
        late((1, BLOCK), 1),
        early((BLOCK, width), 0),
        late((BLOCK, width), 0),
    ]
    slab = (SLAB, width)
    flipped = (width, SLAB)
    shape = jax.ShapeDtypeStruct
    if first:
        outs = [
            (shape(slab, single), whole(slab)),
            (shape(slab, narrow), whole(slab)),
            (shape(flipped, narrow), whole(flipped)),
            (shape(flipped, narrow), whole(flipped)),
            (shape(slab, single), whole(slab)),
            (shape(slab, single), whole(slab)),
        ]
        scratch = []
    else:
        outs = [
            (shape(slab, narrow), whole(slab)),
            (shape(slab, single), whole(slab)),
            (shape(slab, narrow), whole(slab)),
            (shape((8, width), single), whole((8, width))),
        ]
        scratch = [pltpu.VMEM(slab, single), pltpu.VMEM(slab, single)]
    tall = width + PADROWS
    outs += [
        (shape((tall, local), narrow), early((tall, BLOCK), 1)),
        (shape((tall, local), narrow), late((tall, BLOCK), 1)),
        (shape((width, local), narrow), early((width, BLOCK), 1)),
        (shape((width, local), narrow), late((width, BLOCK), 1)),
    ]
    scratch += [
        pltpu.VMEM((width, BLOCK), narrow),
        pltpu.VMEM((BLOCK, width), narrow),
        pltpu.VMEM((1, BLOCK), single),
        pltpu.VMEM((SLAB, BLOCK), narrow),
        pltpu.VMEM((SLAB, BLOCK), narrow),
        pltpu.VMEM((8, BLOCK), single),
    ]
    return pl.pallas_call(
        functools.partial(mlp_kernel, first),
        out_shape=[o[0] for o in outs],
        grid=(2 * count,),
        in_specs=in_specs,
        out_specs=[o[1] for o in outs],
        scratch_shapes=scratch,
        compiler_params=pltpu.CompilerParams(vmem_limit_bytes=VMEM),
        cost_estimate=pl.CostEstimate(
            flops=18_000_000_000, bytes_accessed=40_000_000, transcendentals=4_000_000
        ),
        name="mlp",
    )(*residents, w1a, w1b, b1a[None], b1b[None], w2a, w2b)


def backward_kernel(first, *refs):
    if first:
        (tab, da, n1, qkv, mixed, w, wproj, wrel, bits, lanes, sides, keys) = refs[:12]
        (dn1, gw, gproj, grel, gw_acc, gproj_acc, bias_acc, dqkv) = refs[12:]
    else:
        (tab, da, n1, qkv, mixed, w, wproj, wrel, bits, lanes, sides, keys) = refs[:12]
        (prior, xs, dx1, gain) = refs[12:16]
        (back, sums, gw, gproj, grel, gw_acc, gproj_acc, bias_acc, dqkv) = refs[16:]
    _, col0, high, wide, offset, live = slot_fields(tab)
    half = w.shape[2]
    width = w.shape[1]

    @pl.when(pl.program_id(0) == 0)
    def _():
        gw_acc[...] = jnp.zeros_like(gw_acc)
        gproj_acc[...] = jnp.zeros_like(gproj_acc)
        bias_acc[...] = jnp.zeros_like(bias_acc)
        grel[...] = jnp.zeros_like(grel)
        if not first:
            back[...] = jnp.zeros_like(back)
            sums[...] = jnp.zeros_like(sums)

    @pl.when(live == 1)
    def _():
        _, valid = positions(0, col0, high, wide)
        place = pl.ds(pl.multiple_of(offset, 16), ROWS)
        da_win = jnp.where(valid, da[place, :].astype(single), 0.0).astype(narrow)
        gproj_acc[...] += dot_tn(mixed[0], da_win)
        dmix = dot_nt(da_win, wproj[...]).astype(narrow)
        low_lane = lax.broadcasted_iota(jnp.int32, (ROWS, LANES), 1) < 64
        for pair in range(half // LANES):
            cut = slice(pair * LANES, (pair + 1) * LANES)
            q, k8, v, rel = (qkv[0, j, :, cut] for j in range(4))
            do = dmix[:, cut]
            dqs, dks, dvs = [], [], []
            for head in range(2):
                mine, other = sides[head : head + 1], sides[1 - head : 2 - head]
                full_key = k8 * mine + keys[...] * other
                scores = dot_nt(full_key, q * mine + rel * other)
                top = jnp.max(scores, axis=0, keepdims=True)
                probs = jnp.exp(scores - top)
                probs = probs * (1.0 / jnp.sum(probs, axis=0, keepdims=True))
                dprobs = dot_nt(v, do * mine)
                mean = jnp.sum(probs * dprobs, axis=0, keepdims=True)
                dscores = (probs * (dprobs - mean)).astype(narrow)
                dvs.append(dot(probs.astype(narrow), do))
                dks.append(dot(dscores, q))
                dqs.append(dot_tn(dscores, full_key))
            dv = jnp.where(low_lane, dvs[0], dvs[1])
            dk = jnp.where(low_lane, dks[0], dks[1]) * 0.125
            dq = jnp.where(low_lane, dqs[0], dqs[1])
            drel = jnp.where(low_lane, dqs[1], dqs[0]) * lanes[0:1]
            drel = shift_right(drel, bits).astype(narrow)
            dq = dq + dot_nt(drel, wrel[...])
            grel[...] += dot_tn(drel, q)
            dqkv[0, :, cut] = dq.astype(narrow)
            dqkv[1, :, cut] = dk.astype(narrow)
            dqkv[2, :, cut] = dv.astype(narrow)
        n1t = n1[0].T
        total = None
        for j in range(3):
            part = dqkv[j]
            gw_acc[j] += dot(n1t, part)
            bias_acc[j : j + 1, :] += jnp.sum(part.astype(single), axis=0, keepdims=True)
            back_part = dot_nt(part, w[j])
            total = back_part if total is None else total + back_part
        if first:
            dn1[0] = total
        else:
            grad = jnp.where(valid, total + prior[0], 0.0)
            normal, inverse = norm_parts(xs[place, :].astype(single))
            sums[0:1, :] += jnp.sum(grad * normal, axis=0, keepdims=True)
            sums[1:2, :] += jnp.sum(grad, axis=0, keepdims=True)
            result = dx1[place, :] + norm_back(grad, normal, inverse, gain[...])
            back[place, :] = jnp.where(valid, result, 0.0).astype(narrow)

    @pl.when(pl.program_id(0) == SLOTS - 1)
    def _():
        gproj[...] = gproj_acc[...].astype(narrow)
        pad = gw.shape[1] - width
        for j in range(3):
            gw[j, :width, :] = gw_acc[j].astype(narrow)
            gw[j, width:, :] = jnp.broadcast_to(bias_acc[j : j + 1, :], (pad, half)).astype(narrow)


def backward_half(tab, da, n1, qkv, mixed, w, wproj, wrel, tables, final):
    first = final is None
    width = da.shape[1]
    half = w.shape[2]
    shape = jax.ShapeDtypeStruct
    operands = [da, n1, qkv, mixed, w, wproj, wrel, *tables]
    in_specs = [whole(a.shape) for a in operands]
    for at in (1, 2, 3):
        in_specs[at] = by_slot(operands[at].shape[1:])
    tall = width + PADROWS
    if first:
        outs = [(shape((SLOTS, ROWS, width), single), by_slot((ROWS, width)))]
    else:
        prior, xs, dx1, gain = final
        operands += [prior, xs, dx1, gain]
        in_specs += [by_slot((ROWS, width)), whole(xs.shape), whole(dx1.shape), whole(gain.shape)]
        outs = [
            (shape((SLAB, width), narrow), whole((SLAB, width))),
            (shape((8, width), single), whole((8, width))),
        ]
    outs += [
        (shape((3, tall, half), narrow), whole((3, tall, half))),
        (shape((half, width), narrow), whole((half, width))),
        (shape((LANES, LANES), single), whole((LANES, LANES))),
    ]
    return pl.pallas_call(
        functools.partial(backward_kernel, first),
        out_shape=[o[0] for o in outs],
        grid_spec=pltpu.PrefetchScalarGridSpec(
            num_scalar_prefetch=1,
            grid=(SLOTS,),
            in_specs=in_specs,
            out_specs=[o[1] for o in outs],
            scratch_shapes=[
                pltpu.VMEM((3, width, half), single),
                pltpu.VMEM((half, width), single),
                pltpu.VMEM((8, half), single),
                pltpu.VMEM((3, ROWS, half), narrow),
            ],
        ),
        compiler_params=pltpu.CompilerParams(vmem_limit_bytes=VMEM),
        cost_estimate=pl.CostEstimate(
            flops=26_000_000_000, bytes_accessed=40_000_000, transcendentals=4_000_000
        ),
        name="attention_backward",
    )(tab, *operands)


def place_kernel(tab, slab, ext):
    row0, col0, high, wide, offset, live = slot_fields(tab)

    @pl.when(pl.program_id(0) == 0)
    def _():
        ext[...] = jnp.zeros_like(ext)

    @pl.when(live == 1)
    def _():
        target, _ = positions(1, col0, high, wide)
        token = lax.broadcasted_iota(jnp.int32, (WIN * GRID, ROWS), 0)
        choose = jnp.where(token == target, 1.0, 0.0).astype(narrow)
        window = slab[pl.ds(pl.multiple_of(offset, 16), ROWS), :]
        where_to = pl.ds(pl.multiple_of(row0 * GRID, GRID), WIN * GRID)
        ext[where_to, :] += dot(choose, window).astype(narrow)


def place_windows(tab, slab, tokens):
    width = slab.shape[1]
    return pl.pallas_call(
        place_kernel,
        out_shape=jax.ShapeDtypeStruct((tokens, width), narrow),
        grid_spec=pltpu.PrefetchScalarGridSpec(
            num_scalar_prefetch=1,
            grid=(SLOTS,),
            in_specs=[whole(slab.shape)],
            out_specs=whole((tokens, width)),
        ),
        compiler_params=pltpu.CompilerParams(vmem_limit_bytes=VMEM),
        cost_estimate=pl.CostEstimate(
            flops=2_000_000_000, bytes_accessed=6_000_000, transcendentals=0
        ),
        name="place_windows",
    )(tab, slab)


CORE_SWAP = ((0, 1), (1, 0), (2, 3), (3, 2))
CHIP_SWAP = ((0, 2), (2, 0), (1, 3), (3, 1))
UP = ((0, 1), (1, 2), (2, 3))
DOWN = ((1, 0), (2, 1), (3, 2))


def swap(value, pairs):
    return jax.tree.map(lambda a: lax.ppermute(a, "tensor", pairs), value)


def add_low(a, b):
    return jax.tree.map(lambda u, v: (u.astype(single) + v.astype(single)).astype(narrow), a, b)


def spread(tokens, rows):
    grid = tokens.reshape(rows, GRID, tokens.shape[-1])
    above = lax.ppermute(grid[rows - LEFT :], "tensor", UP)
    below = lax.ppermute(grid[:RIGHT], "tensor", DOWN)
    whole_grid = jnp.concatenate([above, grid, below], axis=0)
    return whole_grid.reshape(-1, tokens.shape[-1])


def collect(ext, rows):
    width = ext.shape[-1]
    grid = ext.reshape(rows + LEFT + RIGHT, GRID, width)
    from_below = lax.ppermute(grid[:LEFT], "tensor", DOWN)
    from_above = lax.ppermute(grid[LEFT + rows :], "tensor", UP)
    mine = grid[LEFT : LEFT + rows]
    mine = mine + jnp.pad(from_below, ((rows - LEFT, 0), (0, 0), (0, 0)))
    mine = mine + jnp.pad(from_above, ((0, rows - RIGHT), (0, 0), (0, 0)))
    return mine.reshape(1, rows * GRID, width)


def shards(
    inputs,
    w_qkv,
    qv_bias,
    w_proj,
    proj_bias,
    w_fc1,
    fc1_bias,
    w_fc2,
    fc2_bias,
    norm1_gain,
    norm1_shift,
    norm2_gain,
    norm2_shift,
    rel_h,
    rel_w,
    cotangent,
):
    width = inputs.shape[2]
    rows = inputs.shape[1] // GRID
    local = w_qkv.shape[2]
    heads = local // HD
    place = lax.axis_index("tensor")
    tab = jnp.asarray(owner_table(rows))[place]
    tables = lane_tables()

    block = jnp.zeros((2, 32, HD), narrow)
    block = block.at[0, : 2 * WIN - 1].set(rel_h[::-1]).at[1, : 2 * WIN - 1].set(rel_w[::-1])
    block = block.reshape(HD, HD).T
    wrel = jnp.zeros((LANES, LANES), narrow).at[:HD, HD:].set(block).at[HD:, :HD].set(block)

    x_ext = spread(inputs[0], rows)
    g_ext = spread(cotangent[0], rows)

    mine = (w_qkv, qv_bias, w_proj, w_fc1, fc1_bias, w_fc2)
    beside = swap(mine, CORE_SWAP)
    across = swap(mine, CHIP_SWAP)
    corner = swap(across, CORE_SWAP)

    def joined(a, b):
        return (
            jnp.concatenate([a[0], b[0]], axis=2),
            jnp.concatenate([a[1], b[1]], axis=1),
            jnp.concatenate([a[2], b[2]], axis=0),
        )

    near_w, near_bias, near_proj = joined(mine, beside)
    far_w, far_bias, far_proj = joined(across, corner)
    norm1 = (norm1_gain[None], norm1_shift[None])

    xs, n1, near_qkv, near_mixed, near_attn, near_peak = forward_half(
        tab, x_ext, norm1, None, near_w, near_bias, near_proj, wrel, tables
    )
    gs, far_qkv, far_mixed, far_attn, far_peak = forward_half(
        tab, g_ext, norm1, n1, far_w, far_bias, far_proj, wrel, tables
    )

    x1, n2, n2t, gt, branch, dn2, *near_fc = mlp_half(
        True,
        (xs, near_attn, far_attn, gs, proj_bias[None], norm2_gain[None], norm2_shift[None]),
        mine[3],
        beside[3],
        mine[4],
        beside[4],
        mine[5],
        beside[5],
    )
    out, dx1, da, sums2, *far_fc = mlp_half(
        False,
        (x1, n2, n2t, gs, gt, branch, dn2, fc2_bias[None], norm2_gain[None]),
        across[3],
        corner[3],
        across[4],
        corner[4],
        across[5],
        corner[5],
    )

    dn1, far_gw, far_gproj, far_rel = backward_half(
        tab, da, n1, far_qkv, far_mixed, far_w, far_proj, wrel, tables, None
    )
    back, sums1, near_gw, near_gproj, near_rel = backward_half(
        tab,
        da,
        n1,
        near_qkv,
        near_mixed,
        near_w,
        near_proj,
        wrel,
        tables,
        (dn1, xs, dx1, norm1_gain[None]),
    )

    output = collect(place_windows(tab, out, x_ext.shape[0]), rows)
    input_grad = collect(place_windows(tab, back, x_ext.shape[0]), rows)

    def both(fc, gw, gproj):
        keep = (fc[0], fc[2], gw[:, :, :local], gproj[:local])
        send = (fc[1], fc[3], gw[:, :, local:], gproj[local:])
        return add_low(keep, swap(send, CORE_SWAP))

    far_total = both(far_fc, far_gw, far_gproj)
    near_total = both(near_fc, near_gw, near_gproj)
    totals = add_low(near_total, swap(far_total, CHIP_SWAP))
    totals = lax.psum(totals, "dp")
    gw1, gw2, gw, gproj = jax.tree.map(lambda a: a.astype(single), totals)

    blocks = near_rel + far_rel
    blocks = blocks[HD:, :HD] + blocks[:HD, HD:]
    grad_rel = jnp.stack([blocks[: 2 * WIN - 1][::-1], blocks[32 : 32 + 2 * WIN - 1][::-1]])
    sums, grad_rel = lax.psum((jnp.concatenate([sums1[:2], sums2[:4]]), grad_rel), ("dp", "tensor"))

    def peaks(peak):
        top = jnp.max(peak, axis=1)[: 2 * heads]
        return jnp.maximum(top[:heads], lax.ppermute(top[heads:], "tensor", CORE_SWAP))

    head_max = jnp.maximum(
        peaks(near_peak), lax.ppermute(peaks(far_peak), "tensor", CHIP_SWAP)
    )
    head_max = lax.pmax(head_max, "dp")
    factor = jnp.sqrt(CLIP / jnp.maximum(head_max, CLIP))
    clipped_qk = (w_qkv[:2].astype(single) * jnp.repeat(factor, HD)).astype(narrow)

    return (
        output,
        input_grad,
        gw[:, :width],
        jnp.stack([gw[0, width], gw[2, width]]),
        gproj,
        sums[4],
        gw1[:width],
        gw1[width],
        gw2.T,
        sums[5],
        sums[:4],
        grad_rel,
        clipped_qk,
        head_max,
    )


def solution(mesh):
    return jax.shard_map(
        shards,
        mesh=mesh,
        in_specs=(
            P("dp", "tensor", None),
            P(None, None, "tensor"),
            P(None, "tensor"),
            P("tensor", None),
            P(),
            P(None, "tensor"),
            P("tensor"),
            P("tensor", None),
            P(),
            P(),
            P(),
            P(),
            P(),
            P(),
            P(),
            P("dp", "tensor", None),
        ),
        out_specs=(
            P("dp", "tensor", None),
            P("dp", "tensor", None),
            P(None, None, "tensor"),
            P(None, "tensor"),
            P("tensor", None),
            P(),
            P(None, "tensor"),
            P("tensor"),
            P("tensor", None),
            P(),
            P(),
            P(),
            P(None, None, "tensor"),
            P("tensor"),
        ),
        check_vma=False,
    )
```

```python
import functools

import jax
import jax.numpy as jnp
import numpy as np
from jax import lax
from jax.experimental import pallas as pl
from jax.experimental.pallas import tpu as pltpu
from jax.sharding import PartitionSpec as P

HD = 64
GRID = 64
WIN = 14
TILES = 5
SPAN = WIN * WIN
ROWS = 208
SLOTS = 7
SLAB = 6 * ROWS
SPLIT = 4
SHORT = 112
LEFT = 6
RIGHT = 12
LANES = 128
EPS = 1e-6
CLIP = 3.0
VMEM = 60 * 1024 * 1024

single = jnp.float32
narrow = jnp.bfloat16

def lane_tables():
    row = np.arange(ROWS)
    x, y = row // WIN, row % WIN
    lane = np.arange(LANES) % 64
    part = lane // 32
    at = lane % 32
    amount = np.where(part[None, :] == 0, 13 - x[:, None], 13 - y[:, None])
    amount = np.where((row < SPAN)[:, None], amount, 0)
    bits = np.stack([(amount >> b) & 1 for b in range(4)]).astype(np.float32)
    lanes = np.zeros((8, LANES), np.float32)
    lanes[0] = at < WIN
    lanes[1] = (at >= 16) & (at < 16 + WIN)
    lanes[2] = lane == 31
    sides = np.zeros((16, LANES), np.float32)
    sides[0] = np.arange(LANES) < 64
    sides[1] = np.arange(LANES) >= 64
    place = np.where(part[None, :] == 0, x[:, None], y[:, None])
    hot = ((at % 16)[None, :] == place) & ((at % 16) < WIN)[None, :] & (row < SPAN)[:, None]
    keys = hot.astype(np.float32)
    keys[SPAN:, lane == 31] = -1e30
    return (
        jnp.asarray(bits),
        jnp.asarray(lanes),
        jnp.asarray(sides, narrow),
        jnp.asarray(keys, narrow),
    )


def dot(a, b):
    return jnp.dot(a, b, preferred_element_type=single)


def dot_nt(a, b):
    return lax.dot_general(a, b, (((1,), (1,)), ((), ())), preferred_element_type=single)


def dot_tn(a, b):
    return lax.dot_general(a, b, (((0,), (0,)), ((), ())), preferred_element_type=single)


def norm_parts(values):
    centre = values - jnp.mean(values, axis=-1, keepdims=True)
    inverse = lax.rsqrt(jnp.mean(centre * centre, axis=-1, keepdims=True) + EPS)
    return centre * inverse, inverse


def norm_back(grad, normal, inverse, gain):
    scaled = grad * gain
    first = jnp.mean(scaled, axis=-1, keepdims=True)
    second = jnp.mean(scaled * normal, axis=-1, keepdims=True)
    return inverse * (scaled - first - normal * second)


def slot_fields(rows_held):
    device, slot = lax.axis_index("tensor"), pl.program_id(0)
    return window_fields(rows_held, device, slot)


def window_fields(rows_held, device, slot):
    window = device * (SLOTS - 1) + slot
    i, j = window // TILES, window % TILES
    last = device // (SPLIT - 1)
    live = slot < SLOTS - 1 + last
    row0 = i * WIN - device * rows_held + LEFT
    high = jnp.minimum(WIN, GRID - i * WIN)
    wide = jnp.minimum(WIN, GRID - j * WIN)
    tall = jnp.where(last == 1, SLOTS - TILES, SLOTS)
    offset = ROWS * jnp.minimum(slot, tall) + SHORT * jnp.maximum(slot - tall, 0)
    return row0, j * WIN, high, wide, offset, live


def positions(axis, first_col, high, wide):
    shape = (ROWS, 1) if axis == 0 else (1, ROWS)
    row = lax.broadcasted_iota(jnp.int32, shape, axis)
    x = lax.shift_right_logical(row * 4682, 16)
    y = row - x * WIN
    valid = (x < high) & (y < wide)
    return jnp.where(valid, x * GRID + first_col + y, -1), valid


def gather_window(source, target):
    token = lax.broadcasted_iota(jnp.int32, (ROWS, WIN * GRID), 1)
    choose = jnp.where(token == target, 1.0, 0.0).astype(narrow)
    return dot(choose, source)


def shift_left(values, bits):
    for b in range(4):
        values = jnp.where(bits[b] > 0.5, pltpu.roll(values, LANES - (1 << b), 1), values)
    return values


def shift_right(values, bits):
    for b in range(4):
        values = jnp.where(bits[b] > 0.5, pltpu.roll(values, 1 << b, 1), values)
    return values


def partners(device):
    beside = device + 1 - 2 * (device % 2)
    across = (device + 2) % SPLIT
    corner = (beside + 2) % SPLIT
    return beside, across, corner


def greet(places):
    barrier = pltpu.get_barrier_semaphore()
    for place in places:
        pl.semaphore_signal(barrier, inc=1, device_id=place, device_id_type=pl.DeviceIdType.MESH)
    pl.semaphore_wait(barrier, len(places))


class Sender:
    def __init__(self, sends, recvs, locals_):
        self.sends, self.recvs, self.locals = sends, recvs, locals_

    def remote(self, at, source, target, place):
        return pltpu.make_async_remote_copy(
            src_ref=source,
            dst_ref=target,
            send_sem=self.sends.at[at],
            recv_sem=self.recvs.at[at],
            device_id=place,
            device_id_type=pl.DeviceIdType.MESH,
        )

    def local(self, at, source, target):
        return pltpu.make_async_copy(source, target, self.locals.at[at])


def attend(n1, valid, weights, qbias, vbias, wrel, bits, lanes, sides, keys, qkv, mixed, peak):
    half = weights.shape[1]
    query = jnp.where(valid, dot_nt(n1, weights[0]) + qbias, 0.0).astype(narrow)
    key8 = dot_nt(n1, weights[1]).astype(narrow) * jnp.asarray(0.125, narrow)
    value = (dot_nt(n1, weights[2]) + vbias).astype(narrow)
    qkv[0, 0] = query
    qkv[0, 1] = key8
    qkv[0, 2] = value
    low_lane = lax.broadcasted_iota(jnp.int32, (ROWS, LANES), 1) < 64
    for pair in range(half // LANES):
        cut = slice(pair * LANES, (pair + 1) * LANES)
        q, k8, v = query[:, cut], key8[:, cut], value[:, cut]
        rel = shift_left(dot(q, wrel[...]), bits)
        rest = rel - rel.astype(narrow).astype(single)
        rel = rel * lanes[0:1] + pltpu.roll(rest, 16, 1) * lanes[1:2] + lanes[2:3]
        rel = rel.astype(narrow)
        qkv[0, 3, :, cut] = rel
        pieces = []
        for head in range(2):
            mine, other = sides[head : head + 1], sides[1 - head : 2 - head]
            only = q * mine
            logits = dot_nt(only, k8)
            at = 2 * pair + head
            peak[at : at + 1, :] = jnp.maximum(
                peak[at : at + 1, :], jnp.max(logits, axis=0, keepdims=True)
            )
            scores = dot_nt(only + rel * other, k8 * mine + keys[...] * other)
            top = jnp.max(scores, axis=1, keepdims=True)
            probs = jnp.exp(scores - top)
            total = jnp.sum(probs, axis=1, keepdims=True)
            pieces.append(dot(probs.astype(narrow), v) * (1.0 / total))
        mixed[0, :, cut] = jnp.where(low_lane, pieces[0], pieces[1]).astype(narrow)
    return dot(mixed[0], weights[3])


def halo_copies(send, base, grid, ext, device, rows):
    top, bottom = LEFT * GRID, RIGHT * GRID
    held_rows = rows * GRID
    down = send.remote(
        base,
        grid.at[pl.ds(held_rows - top, top), :],
        ext.at[pl.ds(0, top), :],
        {"tensor": (device + 1) % SPLIT},
    )
    up = send.remote(
        base + 1,
        grid.at[pl.ds(0, bottom), :],
        ext.at[pl.ds(top + held_rows, bottom), :],
        {"tensor": (device + SPLIT - 1) % SPLIT},
    )
    return down, up


def when_all(*conditions):
    def run(action):
        flag = conditions[0]
        for more in conditions[1:]:
            flag = jnp.logical_and(flag, more)
        pl.when(flag)(action)

    return run


def near_kernel(
    x, pack, fc1, fc2, small, gain, shift, wrel, bits, lanes, sides, keys,
    slab, n1_out, qkv, mixed, attn, peak, weights_out, across_out, beside1, beside2, small_out,
    ext, weights, smalls, sends, recvs, locals_,
):
    step = pl.program_id(0)
    device = lax.axis_index("tensor")
    tokens, width = x.shape
    rows = tokens // GRID
    part = pack.shape[0] // 4
    beside, across, corner = partners(device)
    send = Sender(sends, recvs, locals_)
    down, up = halo_copies(send, 0, x, ext, device, rows)
    packs = [
        send.remote(
            2 + j,
            pack.at[pl.ds(j * part, part), :],
            weights.at[j, pl.ds(part, part), :],
            {"tensor": beside},
        )
        for j in range(4)
    ]
    notes = [
        send.remote(6 + k, small, smalls.at[k + 1], {"tensor": place})
        for k, place in enumerate((beside, across, corner))
    ]
    far = send.remote(9, pack, across_out, {"tensor": across})
    fcs = [
        send.remote(10, fc1, beside1, {"tensor": beside}),
        send.remote(11, fc2, beside2, {"tensor": beside}),
    ]
    mine = [
        send.local(j, pack.at[pl.ds(j * part, part), :], weights.at[j, pl.ds(0, part), :])
        for j in range(4)
    ]
    mine.append(send.local(4, x, ext.at[pl.ds(LEFT * GRID, tokens), :]))
    mine.append(send.local(5, small, smalls.at[0]))
    kept = [send.local(6, weights, weights_out), send.local(7, smalls, small_out)]
    row0, col0, high, wide, offset, live = slot_fields(rows)

    @pl.when(step == 0)
    def _():
        slab[...] = jnp.zeros_like(slab)
        attn[...] = jnp.zeros_like(attn)
        peak[...] = jnp.zeros_like(peak)
        ext[pl.ds(0, LEFT * GRID), :] = jnp.zeros((LEFT * GRID, width), narrow)
        ext[pl.ds(LEFT * GRID + tokens, RIGHT * GRID), :] = jnp.zeros((RIGHT * GRID, width), narrow)
        greet([{"tensor": place} for place in (beside, across, corner)])
        pl.when(device < SPLIT - 1)(down.start)
        pl.when(device > 0)(up.start)
        for copy in packs + notes + mine:
            copy.start()
        far.start()
        for copy in fcs:
            copy.start()
        for copy in mine:
            copy.wait()
        for copy in packs + notes:
            copy.wait()
        for copy in kept:
            copy.start()
        pl.when(device > 0)(down.wait_recv)

    when_all(step == 3, device < SPLIT - 1)(up.wait_recv)

    @pl.when(live)
    def _():
        target, valid = positions(0, col0, high, wide)
        source = ext[pl.ds(pl.multiple_of(row0 * GRID, GRID), WIN * GRID), :]
        window = gather_window(source, target)
        place = pl.ds(pl.multiple_of(offset, 16), ROWS)
        slab[place, :] = window.astype(narrow)
        normal, _ = norm_parts(window)
        n1 = jnp.where(valid, normal * gain[...] + shift[...], 0.0).astype(narrow)
        n1_out[0] = n1
        half = 2 * part
        qbias = smalls[0, 1:2, :half] + smalls[1, 2:3, :half]
        vbias = smalls[0, 3:4, :half] + smalls[1, 4:5, :half]
        terms = attend(
            n1, valid, weights, qbias, vbias, wrel, bits, lanes, sides, keys, qkv, mixed, peak
        )
        attn[place, :] = jnp.where(valid, terms, 0.0)

    @pl.when(step == SLOTS - 1)
    def _():
        pl.when(device < SPLIT - 1)(down.wait_send)
        pl.when(device > 0)(up.wait_send)
        for copy in kept + fcs:
            copy.wait()
        far.wait()


def far_kernel(
    g, pack, fc1, fc2, smalls, n1_in, wrel, bits, lanes, sides, keys,
    slab, qkv, mixed, attn, peak, weights_out, across1, across2,
    ext, weights, sends, recvs, locals_,
):
    step = pl.program_id(0)
    device, image = lax.axis_index("tensor"), lax.axis_index("dp")
    tokens, width = g.shape
    rows = tokens // GRID
    part = pack.shape[0] // 4
    beside, across, _ = partners(device)
    side = image % 2
    mate = image + 1 - 2 * side
    send = Sender(sends, recvs, locals_)
    down, up = halo_copies(send, 0, g, ext, device, rows)
    packs = [
        send.remote(
            2 + j,
            pack.at[pl.ds(j * part, part), :],
            weights.at[j, pl.ds(part, part), :],
            {"tensor": beside},
        )
        for j in range(4)
    ]
    firsts, seconds = [], []
    for k, (source, target) in enumerate(((fc1, across1), (fc2, across2))):
        quarter = source.shape[0] // 4
        for piece in range(2):
            cut = pl.ds(pl.multiple_of((side * 2 + piece) * quarter, 16), quarter)
            at = 6 + 2 * (2 * k + piece)
            firsts.append(send.remote(at, source.at[cut, :], target.at[cut, :], {"tensor": across}))
            seconds.append(
                send.remote(at + 1, target.at[cut, :], target.at[cut, :], {"dp": mate})
            )
    mine = [
        send.local(j, pack.at[pl.ds(j * part, part), :], weights.at[j, pl.ds(0, part), :])
        for j in range(4)
    ]
    whole_grid = send.local(4, g, ext.at[pl.ds(LEFT * GRID, tokens), :])
    kept = send.local(5, weights, weights_out)

    @pl.when(step == 0)
    def _():
        slab[...] = jnp.zeros_like(slab)
        attn[...] = jnp.zeros_like(attn)
        peak[...] = jnp.zeros_like(peak)
        ext[pl.ds(0, LEFT * GRID), :] = jnp.zeros((LEFT * GRID, width), narrow)
        ext[pl.ds(LEFT * GRID + tokens, RIGHT * GRID), :] = jnp.zeros((RIGHT * GRID, width), narrow)
        greet(
            [
                {"tensor": beside},
                {"tensor": across},
                {"tensor": (beside + 2) % SPLIT},
                {"dp": mate},
            ]
        )
        for copy in packs + mine + firsts:
            copy.start()
        pl.when(device < SPLIT - 1)(down.start)
        pl.when(device > 0)(up.start)
        whole_grid.start()
        for copy in packs + mine:
            copy.wait()
        kept.start()

    for piece, at in enumerate((2, 3, 5, 6)):

        @pl.when(step == at)
        def _():
            firsts[piece].wait_recv()
            seconds[piece].start()

    _, col0, high, wide, offset, live = slot_fields(rows)

    @pl.when(live)
    def _():
        _, valid = positions(0, col0, high, wide)
        place = pl.ds(pl.multiple_of(offset, 16), ROWS)
        half = 2 * part
        qbias = smalls[2, 1:2, :half] + smalls[3, 2:3, :half]
        vbias = smalls[2, 3:4, :half] + smalls[3, 4:5, :half]
        terms = attend(
            n1_in[0], valid, weights, qbias, vbias, wrel, bits, lanes, sides, keys, qkv, mixed, peak
        )
        attn[place, :] = jnp.where(valid, terms, 0.0)

    @pl.when(step == SLOTS - 1)
    def _():
        whole_grid.wait()
        pl.when(device < SPLIT - 1)(down.wait_send)
        pl.when(device > 0)(down.wait_recv)
        pl.when(device > 0)(up.wait_send)
        pl.when(device < SPLIT - 1)(up.wait_recv)

        @pl.loop(0, SLOTS)
        def _(slot):
            row0, col0, high, wide, offset, live = window_fields(rows, device, slot)

            @pl.when(live)
            def _():
                target, _ = positions(0, col0, high, wide)
                source = ext[pl.ds(pl.multiple_of(row0 * GRID, GRID), WIN * GRID), :]
                slab[pl.ds(pl.multiple_of(offset, 16), ROWS), :] = gather_window(
                    source, target
                ).astype(narrow)

        kept.wait()
        for copy in firsts:
            copy.wait_send()
        for copy in seconds:
            copy.wait()


def whole(shape):
    zeros = (0,) * len(shape)
    return pl.BlockSpec(shape, lambda *_: zeros, pipeline_mode=pl.Buffered(1))


def by_slot(shape):
    rest = (0,) * len(shape)
    return pl.BlockSpec((1,) + tuple(shape), lambda s, *_: (s,) + rest)


ANY = pl.BlockSpec(memory_space=pl.ANY)


def of(shape, dtype=narrow):
    return jax.ShapeDtypeStruct(shape, dtype)


FORWARD_COST = pl.CostEstimate(
    flops=13_000_000_000, bytes_accessed=30_000_000, transcendentals=4_000_000
)


def near_forward(x, pack, fc1, fc2, small, norm, wrel, tables):
    tokens, width = x.shape
    half = pack.shape[0] // 2
    slab = (SLAB, width)
    outs = [
        (of(slab), whole(slab)),
        (of((SLOTS, ROWS, width)), by_slot((ROWS, width))),
        (of((SLOTS, 4, ROWS, half)), by_slot((4, ROWS, half))),
        (of((SLOTS, ROWS, half)), by_slot((ROWS, half))),
        (of(slab, single), whole(slab)),
        (of((8, ROWS), single), whole((8, ROWS))),
        (of((4, half, width)), ANY),
        (of(pack.shape), ANY),
        (of(fc1.shape), ANY),
        (of(fc2.shape), ANY),
        (of((SPLIT,) + small.shape, single), ANY),
    ]
    operands = (x, pack, fc1, fc2, small, *norm, wrel, *tables)
    return pl.pallas_call(
        near_kernel,
        out_shape=[o[0] for o in outs],
        grid=(SLOTS,),
        in_specs=[ANY] * 5 + [whole(a.shape) for a in operands[5:]],
        out_specs=[o[1] for o in outs],
        scratch_shapes=[
            pltpu.VMEM((tokens + (LEFT + RIGHT) * GRID, width), narrow),
            pltpu.VMEM((4, half, width), narrow),
            pltpu.VMEM((SPLIT,) + small.shape, single),
            pltpu.SemaphoreType.DMA((12,)),
            pltpu.SemaphoreType.DMA((12,)),
            pltpu.SemaphoreType.DMA((8,)),
        ],
        compiler_params=pltpu.CompilerParams(
            vmem_limit_bytes=VMEM, collective_id=0, has_side_effects=True
        ),
        cost_estimate=FORWARD_COST,
        name="near_forward",
    )(*operands)


def far_forward(g, pack, fc1, fc2, smalls, n1, wrel, tables):
    tokens, width = g.shape
    half = pack.shape[0] // 2
    slab = (SLAB, width)
    outs = [
        (of(slab), whole(slab)),
        (of((SLOTS, 4, ROWS, half)), by_slot((4, ROWS, half))),
        (of((SLOTS, ROWS, half)), by_slot((ROWS, half))),
        (of(slab, single), whole(slab)),
        (of((8, ROWS), single), whole((8, ROWS))),
        (of((4, half, width)), ANY),
        (of(fc1.shape), ANY),
        (of(fc2.shape), ANY),
    ]
    operands = (g, pack, fc1, fc2, smalls, n1, wrel, *tables)
    in_specs = [ANY] * 4 + [whole(a.shape) for a in operands[4:]]
    in_specs[5] = by_slot((ROWS, width))
    return pl.pallas_call(
        far_kernel,
        out_shape=[o[0] for o in outs],
        grid=(SLOTS,),
        in_specs=in_specs,
        out_specs=[o[1] for o in outs],
        scratch_shapes=[
            pltpu.VMEM((tokens + (LEFT + RIGHT) * GRID, width), narrow),
            pltpu.VMEM((4, half, width), narrow),
            pltpu.SemaphoreType.DMA((14,)),
            pltpu.SemaphoreType.DMA((14,)),
            pltpu.SemaphoreType.DMA((6,)),
        ],
        compiler_params=pltpu.CompilerParams(
            vmem_limit_bytes=VMEM, collective_id=1, has_side_effects=True
        ),
        cost_estimate=FORWARD_COST,
        name="far_forward",
    )(*operands)


BLOCK = 256
CHUNK = 416


def gelu_parts(z):
    size = jnp.abs(z)
    bell = jnp.exp(-0.5 * z * z)
    t = 1.0 / (1.0 + 0.2316418882663604 * size)
    poly = 0.5 * 1.061405429 * t + (0.5 * -1.453152027)
    poly = poly * t + 0.5 * 1.421413741
    poly = poly * t + 0.5 * -0.284496736
    poly = poly * t + 0.5 * 0.254829592
    tail = poly * t * bell
    phi_total = jnp.where(z >= 0, 1.0 - tail, tail)
    return z * phi_total, phi_total + z * bell * 0.3989422804014327


def mlp_kernel(first, *refs):
    if first:
        (xs, attn1, attn2, gs, pbias, gain, shift, smalls, src1, src2, w1a, w2a) = refs[:12]
        (x1, n2, n2t, gt, branch, dn2, gw1a, gw1b, gw2a, gw2b, gb) = refs[12:23]
        (corner1, corner2, sends, recvs, w1, w2, b1, hs, zs) = refs[23:]
        kinds = (2, 3)
    else:
        (x1, n2, n2t, gs, gt, branch0, dn20, fbias, gain, smalls, w1a, w1b, w2a, w2b) = refs[:14]
        (out, dx1, da, sums, gw1a, gw1b, gw2a, gw2b, gb) = refs[14:23]
        (branch, dn2, w1, w2, b1, hs, zs) = refs[23:]
        kinds = (0, 1)
    step = pl.program_id(0)
    count = pl.num_programs(0) // 2
    rows, width = gs.shape
    if first:
        beside, _, _ = partners(lax.axis_index("tensor"))
        send = Sender(sends, recvs, None)
        corners = [
            send.remote(0, src1, corner1, {"tensor": beside}),
            send.remote(1, src2, corner2, {"tensor": beside}),
        ]

    @pl.when(step == 0)
    def _():
        gb[...] = jnp.zeros_like(gb)
        if first:
            greet([{"tensor": beside}])
            for copy in corners:
                copy.start()

            @pl.loop(0, SLAB // ROWS)
            def _(c):
                sl = pl.ds(pl.multiple_of(c * ROWS, 16), ROWS)
                middle = xs[sl, :].astype(single) + (attn1[sl, :] + attn2[sl, :] + pbias[...])
                x1[sl, :] = middle
                normal, _ = norm_parts(middle)
                n2[sl, :] = (normal * gain[...] + shift[...]).astype(narrow)
                branch[sl, :] = jnp.zeros((ROWS, width), single)
                dn2[sl, :] = jnp.zeros((ROWS, width), single)

            for j in range(width // LANES):
                cut = slice(j * LANES, (j + 1) * LANES)
                n2t[cut, :] = n2[:, cut].T
                gt[cut, :] = gs[:, cut].T
        else:

            @pl.loop(0, SLAB // ROWS)
            def _(c):
                sl = pl.ds(pl.multiple_of(c * ROWS, 16), ROWS)
                branch[sl, :] = branch0[sl, :]
                dn2[sl, :] = dn20[sl, :]

    if first:

        @pl.when(step == count)
        def _():
            for copy in corners:
                copy.wait()

    @pl.when(step < count)
    def _():
        w1[...] = w1a[...]
        w2[...] = w2a[...]
        b1[...] = smalls[kinds[0], 0:1, pl.ds(pl.multiple_of(step * BLOCK, BLOCK), BLOCK)]

    @pl.when(step >= count)
    def _():
        cut = pl.ds(pl.multiple_of((step - count) * BLOCK, BLOCK), BLOCK)
        if first:
            w1[...] = corner1[:, cut]
            w2[...] = corner2[cut, :]
        else:
            w1[...] = w1b[...]
            w2[...] = w2b[...]
        b1[...] = smalls[kinds[1], 0:1, cut]

    bias_row = step // count
    bias_cut = pl.ds(pl.multiple_of((step % count) * BLOCK, BLOCK), BLOCK)

    @pl.loop(0, SLAB // CHUNK)
    def _(c):
        sl = pl.ds(pl.multiple_of(c * CHUNK, 16), CHUNK)
        z = dot(n2[sl, :], w1[...]) + b1[0:1]
        dh = dot_nt(gs[sl, :], w2[...])
        act, slope = gelu_parts(z)
        h = act.astype(narrow)
        dz = (dh * slope).astype(narrow)
        hs[sl, :] = h
        zs[sl, :] = dz
        gb[bias_row, 0:1, bias_cut] += jnp.sum(dz.astype(single), axis=0, keepdims=True)
        branch[sl, :] += dot(h, w2[...])
        dn2[sl, :] += dot_nt(dz, w1[...])

    def store(gw1, gw2):
        @pl.loop(0, width // 256)
        def _(r):
            sl = pl.ds(pl.multiple_of(r * 256, 256), 256)
            gw1[sl, :] = dot(n2t[sl, :], zs[...]).astype(narrow)
            gw2[sl, :] = dot(gt[sl, :], hs[...]).astype(narrow)

    @pl.when(step < count)
    def _():
        store(gw1a, gw2a)

    @pl.when(step >= count)
    def _():
        store(gw1b, gw2b)

    if not first:

        @pl.when(step == 2 * count - 1)
        def _():
            sums[...] = jnp.zeros_like(sums)

            @pl.loop(0, SLAB // ROWS)
            def _(c):
                sl = pl.ds(pl.multiple_of(c * ROWS, 16), ROWS)
                middle = x1[sl, :]
                normal, inverse = norm_parts(middle)
                out[sl, :] = (middle + (branch[sl, :] + fbias[...])).astype(narrow)
                grad = dn2[sl, :]
                cot = gs[sl, :].astype(single)
                total = cot + norm_back(grad, normal, inverse, gain[...])
                dx1[sl, :] = total
                low = total.astype(narrow)
                da[sl, :] = low
                sums[0:1, :] += jnp.sum(grad * normal, axis=0, keepdims=True)
                sums[1:2, :] += jnp.sum(grad, axis=0, keepdims=True)
                sums[2:3, :] += jnp.sum(low.astype(single), axis=0, keepdims=True)
                sums[3:4, :] += jnp.sum(cot, axis=0, keepdims=True)


def mlp_half(first, residents, w1a, w1b, w2a, w2b):
    width, local = w1a.shape
    count = local // BLOCK

    def early(shape, dim):
        def index(i):
            at = jnp.minimum(i, count - 1)
            return (0, at) if dim == 1 else (at, 0)

        return pl.BlockSpec(shape, index)

    def late(shape, dim):
        def index(i):
            at = jnp.maximum(i - count, 0)
            return (0, at) if dim == 1 else (at, 0)

        return pl.BlockSpec(shape, index)

    slab = (SLAB, width)
    flipped = (width, SLAB)
    in_specs = [whole(a.shape) for a in residents]
    if first:
        operands = (*residents, w1a, w2a, w1a, w2a)
        in_specs += [ANY, ANY, early((width, BLOCK), 1), early((BLOCK, width), 0)]
        outs = [
            (of(slab, single), whole(slab)),
            (of(slab), whole(slab)),
            (of(flipped), whole(flipped)),
            (of(flipped), whole(flipped)),
            (of(slab, single), whole(slab)),
            (of(slab, single), whole(slab)),
        ]
        scratch = [
            pltpu.VMEM((width, local), narrow),
            pltpu.VMEM((local, width), narrow),
            pltpu.SemaphoreType.DMA((2,)),
            pltpu.SemaphoreType.DMA((2,)),
        ]
        params = pltpu.CompilerParams(
            vmem_limit_bytes=VMEM, collective_id=2, has_side_effects=True
        )
    else:
        operands = (*residents, w1a, w1b, w2a, w2b)
        in_specs += [
            early((width, BLOCK), 1),
            late((width, BLOCK), 1),
            early((BLOCK, width), 0),
            late((BLOCK, width), 0),
        ]
        outs = [
            (of(slab), whole(slab)),
            (of(slab, single), whole(slab)),
            (of(slab), whole(slab)),
            (of((8, width), single), whole((8, width))),
        ]
        scratch = [pltpu.VMEM(slab, single), pltpu.VMEM(slab, single)]
        params = pltpu.CompilerParams(vmem_limit_bytes=VMEM)
    outs += [
        (of((width, local)), early((width, BLOCK), 1)),
        (of((width, local)), late((width, BLOCK), 1)),
        (of((width, local)), early((width, BLOCK), 1)),
        (of((width, local)), late((width, BLOCK), 1)),
        (of((2, 8, local), single), whole((2, 8, local))),
    ]
    scratch += [
        pltpu.VMEM((width, BLOCK), narrow),
        pltpu.VMEM((BLOCK, width), narrow),
        pltpu.VMEM((1, BLOCK), single),
        pltpu.VMEM((SLAB, BLOCK), narrow),
        pltpu.VMEM((SLAB, BLOCK), narrow),
    ]
    return pl.pallas_call(
        functools.partial(mlp_kernel, first),
        out_shape=[o[0] for o in outs],
        grid=(2 * count,),
        in_specs=in_specs,
        out_specs=[o[1] for o in outs],
        scratch_shapes=scratch,
        compiler_params=params,
        cost_estimate=pl.CostEstimate(
            flops=18_000_000_000, bytes_accessed=40_000_000, transcendentals=4_000_000
        ),
        name="mlp",
    )(*operands)


def backward_kernel(first, rows_held, *refs):
    (da, n1, qkv, mixed, weights, wrel, bits, lanes, sides, keys) = refs[:10]
    if first:
        (dn1, keep, give, bias, grel, acc, dqkv) = refs[10:]
    else:
        (prior, xs, dx1, gain) = refs[10:14]
        (back, sums, keep, give, bias, grel, acc, dqkv) = refs[14:]
    _, col0, high, wide, offset, live = slot_fields(rows_held)
    half, width = weights.shape[1:]

    @pl.when(pl.program_id(0) == 0)
    def _():
        acc[...] = jnp.zeros_like(acc)
        bias[...] = jnp.zeros_like(bias)
        grel[...] = jnp.zeros_like(grel)
        if not first:
            back[...] = jnp.zeros_like(back)
            sums[...] = jnp.zeros_like(sums)

    @pl.when(live)
    def _():
        _, valid = positions(0, col0, high, wide)
        place = pl.ds(pl.multiple_of(offset, 16), ROWS)
        da_win = jnp.where(valid, da[place, :].astype(single), 0.0).astype(narrow)
        acc[3] += dot_tn(mixed[0], da_win)
        dmix = dot_nt(da_win, weights[3]).astype(narrow)
        low_lane = lax.broadcasted_iota(jnp.int32, (ROWS, LANES), 1) < 64
        for pair in range(half // LANES):
            cut = slice(pair * LANES, (pair + 1) * LANES)
            q, k8, v, rel = (qkv[0, j, :, cut] for j in range(4))
            do = dmix[:, cut]
            dqs, dks, dvs = [], [], []
            for head in range(2):
                mine, other = sides[head : head + 1], sides[1 - head : 2 - head]
                full_key = k8 * mine + keys[...] * other
                scores = dot_nt(full_key, q * mine + rel * other)
                top = jnp.max(scores, axis=0, keepdims=True)
                probs = jnp.exp(scores - top)
                probs = probs * (1.0 / jnp.sum(probs, axis=0, keepdims=True))
                dprobs = dot_nt(v, do * mine)
                mean = jnp.sum(probs * dprobs, axis=0, keepdims=True)
                dscores = (probs * (dprobs - mean)).astype(narrow)
                dvs.append(dot(probs.astype(narrow), do))
                dks.append(dot(dscores, q))
                dqs.append(dot_tn(dscores, full_key))
            dv = jnp.where(low_lane, dvs[0], dvs[1])
            dk = jnp.where(low_lane, dks[0], dks[1]) * 0.125
            dq = jnp.where(low_lane, dqs[0], dqs[1])
            drel = jnp.where(low_lane, dqs[1], dqs[0]) * lanes[0:1]
            drel = shift_right(drel, bits).astype(narrow)
            dq = dq + dot_nt(drel, wrel[...])
            grel[...] += dot_tn(drel, q)
            dqkv[0, :, cut] = dq.astype(narrow)
            dqkv[1, :, cut] = dk.astype(narrow)
            dqkv[2, :, cut] = dv.astype(narrow)
        total = None
        for j in range(3):
            piece = dqkv[j]
            acc[j] += dot_tn(piece, n1[0])
            bias[j : j + 1, :] += jnp.sum(piece.astype(single), axis=0, keepdims=True)
            back_part = dot(piece, weights[j])
            total = back_part if total is None else total + back_part
        if first:
            dn1[0] = total
        else:
            grad = jnp.where(valid, total + prior[0], 0.0)
            normal, inverse = norm_parts(xs[place, :].astype(single))
            sums[0:1, :] += jnp.sum(grad * normal, axis=0, keepdims=True)
            sums[1:2, :] += jnp.sum(grad, axis=0, keepdims=True)
            result = dx1[place, :] + norm_back(grad, normal, inverse, gain[...])
            back[place, :] = jnp.where(valid, result, 0.0).astype(narrow)

    @pl.when(pl.program_id(0) == SLOTS - 1)
    def _():
        part = half // 2
        for j in range(4):
            keep[j * part : (j + 1) * part, :] = acc[j, :part, :].astype(narrow)
            give[j * part : (j + 1) * part, :] = acc[j, part:, :].astype(narrow)


def backward_half(rows_held, da, n1, qkv, mixed, weights, wrel, tables, final):
    first = final is None
    half, width = weights.shape[1:]
    operands = [da, n1, qkv, mixed, weights, wrel, *tables]
    in_specs = [whole(a.shape) for a in operands]
    for at in (1, 2, 3):
        in_specs[at] = by_slot(operands[at].shape[1:])
    if first:
        outs = [(of((SLOTS, ROWS, width), single), by_slot((ROWS, width)))]
    else:
        prior, xs, dx1, gain = final
        operands += [prior, xs, dx1, gain]
        in_specs += [by_slot((ROWS, width)), whole(xs.shape), whole(dx1.shape), whole(gain.shape)]
        outs = [
            (of((SLAB, width)), whole((SLAB, width))),
            (of((8, width), single), whole((8, width))),
        ]
    outs += [
        (of((2 * half, width)), whole((2 * half, width))),
        (of((2 * half, width)), whole((2 * half, width))),
        (of((8, half), single), whole((8, half))),
        (of((LANES, LANES), single), whole((LANES, LANES))),
    ]
    return pl.pallas_call(
        functools.partial(backward_kernel, first, rows_held),
        out_shape=[o[0] for o in outs],
        grid=(SLOTS,),
        in_specs=in_specs,
        out_specs=[o[1] for o in outs],
        scratch_shapes=[
            pltpu.VMEM((4, half, width), single),
            pltpu.VMEM((3, ROWS, half), narrow),
        ],
        compiler_params=pltpu.CompilerParams(vmem_limit_bytes=VMEM),
        cost_estimate=pl.CostEstimate(
            flops=26_000_000_000, bytes_accessed=40_000_000, transcendentals=4_000_000
        ),
        name="attention_backward",
    )(*operands)


def place_kernel(rows_held, slab, ext):
    row0, col0, high, wide, offset, live = slot_fields(rows_held)

    @pl.when(pl.program_id(0) == 0)
    def _():
        ext[...] = jnp.zeros_like(ext)

    @pl.when(live)
    def _():
        target, _ = positions(1, col0, high, wide)
        token = lax.broadcasted_iota(jnp.int32, (WIN * GRID, ROWS), 0)
        choose = jnp.where(token == target, 1.0, 0.0).astype(narrow)
        window = slab[pl.ds(pl.multiple_of(offset, 16), ROWS), :]
        where_to = pl.ds(pl.multiple_of(row0 * GRID, GRID), WIN * GRID)
        ext[where_to, :] += dot(choose, window).astype(narrow)


def place_windows(rows_held, slab):
    width = slab.shape[1]
    tokens = (rows_held + LEFT + RIGHT) * GRID
    return pl.pallas_call(
        functools.partial(place_kernel, rows_held),
        out_shape=of((tokens, width)),
        grid=(SLOTS,),
        in_specs=[whole(slab.shape)],
        out_specs=whole((tokens, width)),
        compiler_params=pltpu.CompilerParams(vmem_limit_bytes=VMEM),
        cost_estimate=pl.CostEstimate(
            flops=2_000_000_000, bytes_accessed=6_000_000, transcendentals=0
        ),
        name="place_windows",
    )(slab)


CORE_SWAP = ((0, 1), (1, 0), (2, 3), (3, 2))
CHIP_SWAP = ((0, 2), (2, 0), (1, 3), (3, 1))
UP = ((0, 1), (1, 2), (2, 3))
DOWN = ((1, 0), (2, 1), (3, 2))


def swap(value, pairs):
    return jax.tree.map(lambda a: lax.ppermute(a, "tensor", pairs), value)


def add_low(a, b):
    return jax.tree.map(lambda u, v: (u.astype(single) + v.astype(single)).astype(narrow), a, b)


def collect(ext, rows):
    width = ext.shape[-1]
    grid = ext.reshape(rows + LEFT + RIGHT, GRID, width)
    from_below = lax.ppermute(grid[:LEFT], "tensor", DOWN)
    from_above = lax.ppermute(grid[LEFT + rows :], "tensor", UP)
    mine = grid[LEFT : LEFT + rows]
    mine = mine + jnp.pad(from_below, ((rows - LEFT, 0), (0, 0), (0, 0)))
    mine = mine + jnp.pad(from_above, ((0, rows - RIGHT), (0, 0), (0, 0)))
    return mine.reshape(1, rows * GRID, width)


def shards(
    inputs,
    w_qkv,
    qv_bias,
    w_proj,
    proj_bias,
    w_fc1,
    fc1_bias,
    w_fc2,
    fc2_bias,
    norm1_gain,
    norm1_shift,
    norm2_gain,
    norm2_shift,
    rel_h,
    rel_w,
    cotangent,
):
    width = inputs.shape[2]
    rows = inputs.shape[1] // GRID
    local = w_qkv.shape[2]
    heads = local // HD
    device = lax.axis_index("tensor")
    tables = lane_tables()

    block = jnp.zeros((2, 32, HD), narrow)
    block = block.at[0, : 2 * WIN - 1].set(rel_h[::-1]).at[1, : 2 * WIN - 1].set(rel_w[::-1])
    block = block.reshape(HD, HD).T
    wrel = jnp.zeros((LANES, LANES), narrow).at[:HD, HD:].set(block).at[HD:, :HD].set(block)

    pack = jnp.concatenate([w_qkv.transpose(0, 2, 1).reshape(3 * local, width), w_proj])
    small = jnp.zeros((8, fc1_bias.shape[0]), single).at[0].set(fc1_bias)
    for j in range(2):
        small = small.at[1 + 2 * j, :local].set(qv_bias[j])
        small = small.at[2 + 2 * j, local : 2 * local].set(qv_bias[j])
    norm1 = (norm1_gain[None], norm1_shift[None])

    (
        xs, n1, near_qkv, near_mixed, near_attn, near_peak,
        near_w, across, beside1, beside2, smalls,
    ) = near_forward(inputs[0], pack, w_fc1, w_fc2, small, norm1, wrel, tables)
    gs, far_qkv, far_mixed, far_attn, far_peak, far_w, across1, across2 = far_forward(
        cotangent[0], across, w_fc1, w_fc2, smalls, n1, wrel, tables
    )

    x1, n2, n2t, gt, branch, dn2, *far_fc = mlp_half(
        True,
        (xs, near_attn, far_attn, gs, proj_bias[None], norm2_gain[None], norm2_shift[None], smalls),
        across1,
        None,
        across2,
        None,
    )
    out, dx1, da, sums2, *near_fc = mlp_half(
        False,
        (x1, n2, n2t, gs, gt, branch, dn2, fc2_bias[None], norm2_gain[None], smalls),
        w_fc1,
        beside1,
        w_fc2,
        beside2,
    )

    dn1, far_keep, far_give, far_bias, far_rel = backward_half(
        rows, da, n1, far_qkv, far_mixed, far_w, wrel, tables, None
    )
    back, sums1, near_keep, near_give, near_bias, near_rel = backward_half(
        rows, da, n1, near_qkv, near_mixed, near_w, wrel, tables, (dn1, xs, dx1, norm1_gain[None])
    )

    output = collect(place_windows(rows, out), rows)
    input_grad = collect(place_windows(rows, back), rows)

    far_total = add_low(
        (far_fc[0], far_fc[2], far_keep), swap((far_fc[1], far_fc[3], far_give), CORE_SWAP)
    )
    near_total = add_low(
        (near_fc[0], near_fc[2], near_keep), swap((near_fc[1], near_fc[3], near_give), CORE_SWAP)
    )
    totals = add_low(near_total, swap(far_total, CHIP_SWAP))
    totals = lax.psum(totals, "dp")
    gw1, gw2, gpack = jax.tree.map(lambda a: a.astype(single), totals)

    blocks = near_rel + far_rel
    blocks = blocks[HD:, :HD] + blocks[:HD, HD:]
    grad_rel = jnp.stack([blocks[: 2 * WIN - 1][::-1], blocks[32 : 32 + 2 * WIN - 1][::-1]])
    fc_bias = jnp.concatenate([near_fc[4][:, 0], far_fc[4][:, 0]])
    qv = jnp.concatenate(
        [b[jnp.array([0, 2])].reshape(2, 2, local).transpose(1, 0, 2) for b in (near_bias, far_bias)]
    )
    biases = jnp.concatenate([fc_bias, qv.reshape(SPLIT, 2 * local)], axis=1)
    biases = biases[jnp.arange(SPLIT) ^ device]
    sums, grad_rel, biases = lax.psum(
        (jnp.concatenate([sums1[:2], sums2[:4]]), grad_rel, biases), ("dp", "tensor")
    )
    biases = biases[device]

    def peaks(peak):
        top = jnp.max(peak, axis=1)[: 2 * heads]
        return jnp.maximum(top[:heads], lax.ppermute(top[heads:], "tensor", CORE_SWAP))

    head_max = jnp.maximum(
        peaks(near_peak), lax.ppermute(peaks(far_peak), "tensor", CHIP_SWAP)
    )
    head_max = lax.pmax(head_max, "dp")
    factor = jnp.sqrt(CLIP / jnp.maximum(head_max, CLIP))
    clipped_qk = (w_qkv[:2].astype(single) * jnp.repeat(factor, HD)).astype(narrow)

    return (
        output,
        input_grad,
        gpack[: 3 * local].reshape(3, local, width).transpose(0, 2, 1),
        biases[fc1_bias.shape[0] :].reshape(2, local),
        gpack[3 * local :],
        sums[4],
        gw1,
        biases[: fc1_bias.shape[0]],
        gw2.T,
        sums[5],
        sums[:4],
        grad_rel,
        clipped_qk,
        head_max,
    )


def solution(mesh):
    return jax.shard_map(
        shards,
        mesh=mesh,
        in_specs=(
            P("dp", "tensor", None),
            P(None, None, "tensor"),
            P(None, "tensor"),
            P("tensor", None),
            P(),
            P(None, "tensor"),
            P("tensor"),
            P("tensor", None),
            P(),
            P(),
            P(),
            P(),
            P(),
            P(),
            P(),
            P("dp", "tensor", None),
        ),
        out_specs=(
            P("dp", "tensor", None),
            P("dp", "tensor", None),
            P(None, None, "tensor"),
            P(None, "tensor"),
            P("tensor", None),
            P(),
            P(None, "tensor"),
            P("tensor"),
            P("tensor", None),
            P(),
            P(),
            P(),
            P(None, None, "tensor"),
            P("tensor"),
        ),
        check_vma=False,
    )
```

```python
import functools

import jax
import jax.numpy as jnp
import numpy as np
from jax import lax
from jax.experimental import pallas as pl
from jax.experimental.pallas import tpu as pltpu
from jax.sharding import PartitionSpec as P

HD = 64
GRID = 64
WIN = 14
TILES = 5
SPAN = WIN * WIN
ROWS = 208
SLOTS = 7
SLAB = 6 * ROWS
SPLIT = 4
SHORT = 112
LEFT = 6
RIGHT = 12
LANES = 128
EPS = 1e-6
CLIP = 3.0
VMEM = 60 * 1024 * 1024

single = jnp.float32
narrow = jnp.bfloat16

def lane_tables():
    row = np.arange(ROWS)
    x, y = row // WIN, row % WIN
    lane = np.arange(LANES) % 64
    part = lane // 32
    at = lane % 32
    amount = np.where(part[None, :] == 0, 13 - x[:, None], 13 - y[:, None])
    amount = np.where((row < SPAN)[:, None], amount, 0)
    bits = np.stack([(amount >> b) & 1 for b in range(4)]).astype(np.float32)
    lanes = np.zeros((8, LANES), np.float32)
    lanes[0] = at < WIN
    lanes[1] = (at >= 16) & (at < 16 + WIN)
    lanes[2] = lane == 31
    sides = np.zeros((16, LANES), np.float32)
    sides[0] = np.arange(LANES) < 64
    sides[1] = np.arange(LANES) >= 64
    place = np.where(part[None, :] == 0, x[:, None], y[:, None])
    hot = ((at % 16)[None, :] == place) & ((at % 16) < WIN)[None, :] & (row < SPAN)[:, None]
    keys = hot.astype(np.float32)
    keys[SPAN:, lane == 31] = -1e30
    return (
        jnp.asarray(bits),
        jnp.asarray(lanes),
        jnp.asarray(sides, narrow),
        jnp.asarray(keys, narrow),
    )


def dot(a, b):
    return jnp.dot(a, b, preferred_element_type=single)


def dot_nt(a, b):
    return lax.dot_general(a, b, (((1,), (1,)), ((), ())), preferred_element_type=single)


def dot_tn(a, b):
    return lax.dot_general(a, b, (((0,), (0,)), ((), ())), preferred_element_type=single)


def norm_parts(values):
    centre = values - jnp.mean(values, axis=-1, keepdims=True)
    inverse = lax.rsqrt(jnp.mean(centre * centre, axis=-1, keepdims=True) + EPS)
    return centre * inverse, inverse


def norm_back(grad, normal, inverse, gain):
    scaled = grad * gain
    first = jnp.mean(scaled, axis=-1, keepdims=True)
    second = jnp.mean(scaled * normal, axis=-1, keepdims=True)
    return inverse * (scaled - first - normal * second)


def slot_fields(rows_held):
    device, slot = lax.axis_index("tensor"), pl.program_id(0)
    return window_fields(rows_held, device, slot)


def window_fields(rows_held, device, slot):
    window = device * (SLOTS - 1) + slot
    i, j = window // TILES, window % TILES
    last = device // (SPLIT - 1)
    live = slot < SLOTS - 1 + last
    row0 = i * WIN - device * rows_held + LEFT
    high = jnp.minimum(WIN, GRID - i * WIN)
    wide = jnp.minimum(WIN, GRID - j * WIN)
    tall = jnp.where(last == 1, SLOTS - TILES, SLOTS)
    offset = ROWS * jnp.minimum(slot, tall) + SHORT * jnp.maximum(slot - tall, 0)
    return row0, j * WIN, high, wide, offset, live


def positions(axis, first_col, high, wide):
    shape = (ROWS, 1) if axis == 0 else (1, ROWS)
    row = lax.broadcasted_iota(jnp.int32, shape, axis)
    x = lax.shift_right_logical(row * 4682, 16)
    y = row - x * WIN
    valid = (x < high) & (y < wide)
    return jnp.where(valid, x * GRID + first_col + y, -1), valid


def gather_window(source, target):
    token = lax.broadcasted_iota(jnp.int32, (ROWS, WIN * GRID), 1)
    choose = jnp.where(token == target, 1.0, 0.0).astype(narrow)
    return dot(choose, source)


def shift_left(values, bits):
    for b in range(4):
        values = jnp.where(bits[b] > 0.5, pltpu.roll(values, LANES - (1 << b), 1), values)
    return values


def shift_right(values, bits):
    for b in range(4):
        values = jnp.where(bits[b] > 0.5, pltpu.roll(values, 1 << b, 1), values)
    return values


def partners(device):
    beside = device + 1 - 2 * (device % 2)
    across = (device + 2) % SPLIT
    corner = (beside + 2) % SPLIT
    return beside, across, corner


def greet(places):
    barrier = pltpu.get_barrier_semaphore()
    for place in places:
        pl.semaphore_signal(barrier, inc=1, device_id=place, device_id_type=pl.DeviceIdType.MESH)
    pl.semaphore_wait(barrier, len(places))


class Sender:
    def __init__(self, sends, recvs, locals_):
        self.sends, self.recvs, self.locals = sends, recvs, locals_

    def remote(self, at, source, target, place):
        return pltpu.make_async_remote_copy(
            src_ref=source,
            dst_ref=target,
            send_sem=self.sends.at[at],
            recv_sem=self.recvs.at[at],
            device_id=place,
            device_id_type=pl.DeviceIdType.MESH,
        )

    def local(self, at, source, target):
        return pltpu.make_async_copy(source, target, self.locals.at[at])


def mate_of(image, bit):
    unit = 1 << bit
    return image + unit * (1 - 2 * ((image // unit) % 2))


def rows_at(start, count):
    return pl.ds(pl.multiple_of(start, 16), count)


def add_rows(target, target_at, sources, count):
    chunk = 48 if count % 48 == 0 else 16

    @pl.loop(0, count // chunk)
    def _(c):
        total = None
        for ref, at in sources:
            value = ref[rows_at(at + c * chunk, chunk), :].astype(single)
            total = value if total is None else total + value
        target[rows_at(target_at + c * chunk, chunk), :] = total.astype(target.dtype)


HALVINGS = 3


class Reducer:
    def __init__(self, send, base, image, images, rows):
        bits = images.bit_length() - 1
        assert images == 1 << bits and bits >= HALVINGS
        self.send, self.base, self.image = send, base, image
        self.extra_bits = range(HALVINGS, bits)
        self.stages = [[] for _ in range(HALVINGS)]
        self.final = []
        landing = 0
        for start, order in ((0, (0, 1, 2)), (rows // 2, (1, 0, 2))):
            length = rows // 2
            for stage, bit in enumerate(order):
                length //= 2
                mine = (image // (1 << bit)) % 2
                keep = start + mine * length
                give = start + (1 - mine) * length
                self.stages[stage].append((mate_of(image, bit), keep, give, length, landing))
                landing += length
                start = keep
            self.final.append((start, length))
        self.extra_landing = []
        for _ in self.extra_bits:
            for _, length in self.final:
                self.extra_landing.append(landing)
                landing += length
        self.landing_rows = landing
        self.copies = 2 * HALVINGS + len(self.extra_landing)
        self.mates = [{"dp": mate_of(image, bit)} for bit in range(bits)]

    def out(self, stage, held, landing):
        copies = []
        for part, (mate, _, give, length, at) in enumerate(self.stages[stage]):
            copies.append(
                self.send.remote(
                    self.base + 2 * stage + part,
                    held.at[rows_at(give, length), :],
                    landing.at[pl.ds(at, length), :],
                    {"dp": mate},
                )
            )
        return copies

    def start(self, stage, held, landing):
        for copy in self.out(stage, held, landing):
            copy.start()

    def finish(self, stage, held, landing):
        for copy in self.out(stage, held, landing):
            copy.wait()
        for _, keep, _, length, at in self.stages[stage]:
            add_rows(held, keep, [(held, keep), (landing, at)], length)

    def extras(self, held, landing):
        for k, bit in enumerate(self.extra_bits):
            copies = []
            for part, (start, length) in enumerate(self.final):
                at = 2 * k + part
                copies.append(
                    self.send.remote(
                        self.base + 2 * HALVINGS + at,
                        held.at[rows_at(start, length), :],
                        landing.at[pl.ds(self.extra_landing[at], length), :],
                        {"dp": mate_of(self.image, bit)},
                    )
                )
            for copy in copies:
                copy.start()
            for copy in copies:
                copy.wait()
            for part, (start, length) in enumerate(self.final):
                at = self.extra_landing[2 * k + part]
                add_rows(held, start, [(held, start), (landing, at)], length)

    def back(self, base, stage, held):
        copies = []
        for part, (mate, keep, _, length, _) in enumerate(self.stages[stage]):
            cut = rows_at(keep, length)
            copies.append(
                self.send.remote(base + 2 * stage + part, held.at[cut, :], held.at[cut, :], {"dp": mate})
            )
        return copies


def attend(n1, valid, weights, qbias, vbias, wrel, bits, lanes, sides, keys, qkv, mixed, peak):
    half = weights.shape[1]
    query = jnp.where(valid, dot_nt(n1, weights[0]) + qbias, 0.0).astype(narrow)
    key8 = dot_nt(n1, weights[1]).astype(narrow) * jnp.asarray(0.125, narrow)
    value = (dot_nt(n1, weights[2]) + vbias).astype(narrow)
    qkv[0, 0] = query
    qkv[0, 1] = key8
    qkv[0, 2] = value
    low_lane = lax.broadcasted_iota(jnp.int32, (ROWS, LANES), 1) < 64
    for pair in range(half // LANES):
        cut = slice(pair * LANES, (pair + 1) * LANES)
        q, k8, v = query[:, cut], key8[:, cut], value[:, cut]
        rel = shift_left(dot(q, wrel[...]), bits)
        rest = rel - rel.astype(narrow).astype(single)
        rel = rel * lanes[0:1] + pltpu.roll(rest, 16, 1) * lanes[1:2] + lanes[2:3]
        rel = rel.astype(narrow)
        qkv[0, 3, :, cut] = rel
        pieces = []
        for head in range(2):
            mine, other = sides[head : head + 1], sides[1 - head : 2 - head]
            only = q * mine
            logits = dot_nt(only, k8)
            at = 2 * pair + head
            peak[at : at + 1, :] = jnp.maximum(
                peak[at : at + 1, :], jnp.max(logits, axis=0, keepdims=True)
            )
            scores = dot_nt(only + rel * other, k8 * mine + keys[...] * other)
            top = jnp.max(scores, axis=1, keepdims=True)
            probs = jnp.exp(scores - top)
            total = jnp.sum(probs, axis=1, keepdims=True)
            pieces.append(dot(probs.astype(narrow), v) * (1.0 / total))
        mixed[0, :, cut] = jnp.where(low_lane, pieces[0], pieces[1]).astype(narrow)
    return dot(mixed[0], weights[3])


def halo_copies(send, base, grid, ext, device, rows):
    top, bottom = LEFT * GRID, RIGHT * GRID
    held_rows = rows * GRID
    down = send.remote(
        base,
        grid.at[pl.ds(held_rows - top, top), :],
        ext.at[pl.ds(0, top), :],
        {"tensor": (device + 1) % SPLIT},
    )
    up = send.remote(
        base + 1,
        grid.at[pl.ds(0, bottom), :],
        ext.at[pl.ds(top + held_rows, bottom), :],
        {"tensor": (device + SPLIT - 1) % SPLIT},
    )
    return down, up


def when_all(*conditions):
    def run(action):
        flag = conditions[0]
        for more in conditions[1:]:
            flag = jnp.logical_and(flag, more)
        pl.when(flag)(action)

    return run


def near_kernel(
    x, pack, fc1, fc2, small, gain, shift, wrel, bits, lanes, sides, keys,
    slab, n1_out, qkv, mixed, attn, peak, weights_out, across_out, beside1, beside2, small_out,
    ext, weights, smalls, sends, recvs, locals_,
):
    step = pl.program_id(0)
    device = lax.axis_index("tensor")
    tokens, width = x.shape
    rows = tokens // GRID
    part = pack.shape[0] // 4
    beside, across, corner = partners(device)
    send = Sender(sends, recvs, locals_)
    down, up = halo_copies(send, 0, x, ext, device, rows)
    packs = [
        send.remote(
            2 + j,
            pack.at[pl.ds(j * part, part), :],
            weights.at[j, pl.ds(part, part), :],
            {"tensor": beside},
        )
        for j in range(4)
    ]
    notes = [
        send.remote(6 + k, small, smalls.at[k + 1], {"tensor": place})
        for k, place in enumerate((beside, across, corner))
    ]
    far = send.remote(9, pack, across_out, {"tensor": across})
    fcs = [
        send.remote(10, fc1, beside1, {"tensor": beside}),
        send.remote(11, fc2, beside2, {"tensor": beside}),
    ]
    mine = [
        send.local(j, pack.at[pl.ds(j * part, part), :], weights.at[j, pl.ds(0, part), :])
        for j in range(4)
    ]
    mine.append(send.local(4, x, ext.at[pl.ds(LEFT * GRID, tokens), :]))
    mine.append(send.local(5, small, smalls.at[0]))
    kept = [send.local(6, weights, weights_out), send.local(7, smalls, small_out)]
    row0, col0, high, wide, offset, live = slot_fields(rows)

    @pl.when(step == 0)
    def _():
        slab[...] = jnp.zeros_like(slab)
        attn[...] = jnp.zeros_like(attn)
        peak[...] = jnp.zeros_like(peak)
        ext[pl.ds(0, LEFT * GRID), :] = jnp.zeros((LEFT * GRID, width), narrow)
        ext[pl.ds(LEFT * GRID + tokens, RIGHT * GRID), :] = jnp.zeros((RIGHT * GRID, width), narrow)
        greet([{"tensor": place} for place in (beside, across, corner)])
        pl.when(device < SPLIT - 1)(down.start)
        pl.when(device > 0)(up.start)
        for copy in packs + notes + mine:
            copy.start()
        far.start()
        for copy in fcs:
            copy.start()
        for copy in mine:
            copy.wait()
        for copy in packs + notes:
            copy.wait()
        for copy in kept:
            copy.start()
        pl.when(device > 0)(down.wait_recv)

    when_all(step == 3, device < SPLIT - 1)(up.wait_recv)

    @pl.when(live)
    def _():
        target, valid = positions(0, col0, high, wide)
        source = ext[pl.ds(pl.multiple_of(row0 * GRID, GRID), WIN * GRID), :]
        window = gather_window(source, target)
        place = pl.ds(pl.multiple_of(offset, 16), ROWS)
        slab[place, :] = window.astype(narrow)
        normal, _ = norm_parts(window)
        n1 = jnp.where(valid, normal * gain[...] + shift[...], 0.0).astype(narrow)
        n1_out[0] = n1
        half = 2 * part
        qbias = smalls[0, 1:2, :half] + smalls[1, 2:3, :half]
        vbias = smalls[0, 3:4, :half] + smalls[1, 4:5, :half]
        terms = attend(
            n1, valid, weights, qbias, vbias, wrel, bits, lanes, sides, keys, qkv, mixed, peak
        )
        attn[place, :] = jnp.where(valid, terms, 0.0)

    @pl.when(step == SLOTS - 1)
    def _():
        pl.when(device < SPLIT - 1)(down.wait_send)
        pl.when(device > 0)(up.wait_send)
        for copy in kept + fcs:
            copy.wait()
        far.wait()


def far_kernel(
    g, pack, fc1, fc2, smalls, n1_in, wrel, bits, lanes, sides, keys,
    slab, qkv, mixed, attn, peak, weights_out, across1, across2,
    ext, weights, sends, recvs, locals_,
):
    step = pl.program_id(0)
    device, image = lax.axis_index("tensor"), lax.axis_index("dp")
    tokens, width = g.shape
    rows = tokens // GRID
    part = pack.shape[0] // 4
    beside, across, _ = partners(device)
    side = image % 2
    mate = image + 1 - 2 * side
    send = Sender(sends, recvs, locals_)
    down, up = halo_copies(send, 0, g, ext, device, rows)
    packs = [
        send.remote(
            2 + j,
            pack.at[pl.ds(j * part, part), :],
            weights.at[j, pl.ds(part, part), :],
            {"tensor": beside},
        )
        for j in range(4)
    ]
    firsts, seconds = [], []
    for k, (source, target) in enumerate(((fc1, across1), (fc2, across2))):
        quarter = source.shape[0] // 4
        for piece in range(2):
            cut = pl.ds(pl.multiple_of((side * 2 + piece) * quarter, 16), quarter)
            at = 6 + 2 * (2 * k + piece)
            firsts.append(send.remote(at, source.at[cut, :], target.at[cut, :], {"tensor": across}))
            seconds.append(
                send.remote(at + 1, target.at[cut, :], target.at[cut, :], {"dp": mate})
            )
    mine = [
        send.local(j, pack.at[pl.ds(j * part, part), :], weights.at[j, pl.ds(0, part), :])
        for j in range(4)
    ]
    whole_grid = send.local(4, g, ext.at[pl.ds(LEFT * GRID, tokens), :])
    kept = send.local(5, weights, weights_out)

    @pl.when(step == 0)
    def _():
        slab[...] = jnp.zeros_like(slab)
        attn[...] = jnp.zeros_like(attn)
        peak[...] = jnp.zeros_like(peak)
        ext[pl.ds(0, LEFT * GRID), :] = jnp.zeros((LEFT * GRID, width), narrow)
        ext[pl.ds(LEFT * GRID + tokens, RIGHT * GRID), :] = jnp.zeros((RIGHT * GRID, width), narrow)
        greet(
            [
                {"tensor": beside},
                {"tensor": across},
                {"tensor": (beside + 2) % SPLIT},
                {"dp": mate},
            ]
        )
        for copy in packs + mine + firsts:
            copy.start()
        pl.when(device < SPLIT - 1)(down.start)
        pl.when(device > 0)(up.start)
        whole_grid.start()
        for copy in packs + mine:
            copy.wait()
        kept.start()

    for piece, at in enumerate((2, 3, 5, 6)):

        @pl.when(step == at)
        def _():
            firsts[piece].wait_recv()
            seconds[piece].start()

    _, col0, high, wide, offset, live = slot_fields(rows)

    @pl.when(live)
    def _():
        _, valid = positions(0, col0, high, wide)
        place = pl.ds(pl.multiple_of(offset, 16), ROWS)
        half = 2 * part
        qbias = smalls[2, 1:2, :half] + smalls[3, 2:3, :half]
        vbias = smalls[2, 3:4, :half] + smalls[3, 4:5, :half]
        terms = attend(
            n1_in[0], valid, weights, qbias, vbias, wrel, bits, lanes, sides, keys, qkv, mixed, peak
        )
        attn[place, :] = jnp.where(valid, terms, 0.0)

    @pl.when(step == SLOTS - 1)
    def _():
        whole_grid.wait()
        pl.when(device < SPLIT - 1)(down.wait_send)
        pl.when(device > 0)(down.wait_recv)
        pl.when(device > 0)(up.wait_send)
        pl.when(device < SPLIT - 1)(up.wait_recv)

        @pl.loop(0, SLOTS)
        def _(slot):
            row0, col0, high, wide, offset, live = window_fields(rows, device, slot)

            @pl.when(live)
            def _():
                target, _ = positions(0, col0, high, wide)
                source = ext[pl.ds(pl.multiple_of(row0 * GRID, GRID), WIN * GRID), :]
                slab[pl.ds(pl.multiple_of(offset, 16), ROWS), :] = gather_window(
                    source, target
                ).astype(narrow)

        kept.wait()
        for copy in firsts:
            copy.wait_send()
        for copy in seconds:
            copy.wait()


def whole(shape):
    zeros = (0,) * len(shape)
    return pl.BlockSpec(shape, lambda *_: zeros, pipeline_mode=pl.Buffered(1))


def by_slot(shape):
    rest = (0,) * len(shape)
    return pl.BlockSpec((1,) + tuple(shape), lambda s, *_: (s,) + rest)


ANY = pl.BlockSpec(memory_space=pl.ANY)


def of(shape, dtype=narrow):
    return jax.ShapeDtypeStruct(shape, dtype)


FORWARD_COST = pl.CostEstimate(
    flops=13_000_000_000, bytes_accessed=30_000_000, transcendentals=4_000_000
)


def near_forward(x, pack, fc1, fc2, small, norm, wrel, tables):
    tokens, width = x.shape
    half = pack.shape[0] // 2
    slab = (SLAB, width)
    outs = [
        (of(slab), whole(slab)),
        (of((SLOTS, ROWS, width)), by_slot((ROWS, width))),
        (of((SLOTS, 4, ROWS, half)), by_slot((4, ROWS, half))),
        (of((SLOTS, ROWS, half)), by_slot((ROWS, half))),
        (of(slab, single), whole(slab)),
        (of((8, ROWS), single), whole((8, ROWS))),
        (of((4, half, width)), ANY),
        (of(pack.shape), ANY),
        (of(fc1.shape), ANY),
        (of(fc2.shape), ANY),
        (of((SPLIT,) + small.shape, single), ANY),
    ]
    operands = (x, pack, fc1, fc2, small, *norm, wrel, *tables)
    return pl.pallas_call(
        near_kernel,
        out_shape=[o[0] for o in outs],
        grid=(SLOTS,),
        in_specs=[ANY] * 5 + [whole(a.shape) for a in operands[5:]],
        out_specs=[o[1] for o in outs],
        scratch_shapes=[
            pltpu.VMEM((tokens + (LEFT + RIGHT) * GRID, width), narrow),
            pltpu.VMEM((4, half, width), narrow),
            pltpu.VMEM((SPLIT,) + small.shape, single),
            pltpu.SemaphoreType.DMA((12,)),
            pltpu.SemaphoreType.DMA((12,)),
            pltpu.SemaphoreType.DMA((8,)),
        ],
        compiler_params=pltpu.CompilerParams(
            vmem_limit_bytes=VMEM, collective_id=0, has_side_effects=True
        ),
        cost_estimate=FORWARD_COST,
        name="near_forward",
    )(*operands)


def far_forward(g, pack, fc1, fc2, smalls, n1, wrel, tables):
    tokens, width = g.shape
    half = pack.shape[0] // 2
    slab = (SLAB, width)
    outs = [
        (of(slab), whole(slab)),
        (of((SLOTS, 4, ROWS, half)), by_slot((4, ROWS, half))),
        (of((SLOTS, ROWS, half)), by_slot((ROWS, half))),
        (of(slab, single), whole(slab)),
        (of((8, ROWS), single), whole((8, ROWS))),
        (of((4, half, width)), ANY),
        (of(fc1.shape), ANY),
        (of(fc2.shape), ANY),
    ]
    operands = (g, pack, fc1, fc2, smalls, n1, wrel, *tables)
    in_specs = [ANY] * 4 + [whole(a.shape) for a in operands[4:]]
    in_specs[5] = by_slot((ROWS, width))
    return pl.pallas_call(
        far_kernel,
        out_shape=[o[0] for o in outs],
        grid=(SLOTS,),
        in_specs=in_specs,
        out_specs=[o[1] for o in outs],
        scratch_shapes=[
            pltpu.VMEM((tokens + (LEFT + RIGHT) * GRID, width), narrow),
            pltpu.VMEM((4, half, width), narrow),
            pltpu.SemaphoreType.DMA((14,)),
            pltpu.SemaphoreType.DMA((14,)),
            pltpu.SemaphoreType.DMA((6,)),
        ],
        compiler_params=pltpu.CompilerParams(
            vmem_limit_bytes=VMEM, collective_id=1, has_side_effects=True
        ),
        cost_estimate=FORWARD_COST,
        name="far_forward",
    )(*operands)


BLOCK = 256
CHUNK = 416


def gelu_parts(z):
    size = jnp.abs(z)
    bell = jnp.exp(-0.5 * z * z)
    t = 1.0 / (1.0 + 0.2316418882663604 * size)
    poly = 0.5 * 1.061405429 * t + (0.5 * -1.453152027)
    poly = poly * t + 0.5 * 1.421413741
    poly = poly * t + 0.5 * -0.284496736
    poly = poly * t + 0.5 * 0.254829592
    tail = poly * t * bell
    phi_total = jnp.where(z >= 0, 1.0 - tail, tail)
    return z * phi_total, phi_total + z * bell * 0.3989422804014327


def mlp_kernel(first, *refs):
    if first:
        (xs, attn1, attn2, gs, pbias, gain, shift, smalls, src1, src2, w1a, w2a) = refs[:12]
        (x1, n2, n2t, gt, branch, dn2, gw1a, gw1b, gw2a, gw2b, gb) = refs[12:23]
        (corner1, corner2, sends, recvs, w1, w2, b1, hs, zs) = refs[23:]
        kinds = (2, 3)
    else:
        (x1, n2, n2t, gs, gt, branch0, dn20, fbias, gain, smalls, keep1, keep2) = refs[:12]
        (give1, give2, w1a, w1b, w2a, w2b) = refs[12:18]
        (out, dx1, da, sums, far1, far2, gw1a, gw1b, gw2a, gw2b, gb) = refs[18:29]
        (branch, dn2, got1, got2, sends, recvs, w1, w2, b1, hs, zs) = refs[29:]
        kinds = (0, 1)
    step = pl.program_id(0)
    count = pl.num_programs(0) // 2
    rows, width = gs.shape
    beside, across, _ = partners(lax.axis_index("tensor"))
    send = Sender(sends, recvs, None)
    if not first:
        swaps = [
            send.remote(0, give1, got1, {"tensor": beside}),
            send.remote(1, give2, got2, {"tensor": beside}),
        ]
        crossings = [
            send.remote(2, got1, far1, {"tensor": across}),
            send.remote(3, got2, far2, {"tensor": across}),
        ]
    if first:
        corners = [
            send.remote(0, src1, corner1, {"tensor": beside}),
            send.remote(1, src2, corner2, {"tensor": beside}),
        ]

    @pl.when(step == 0)
    def _():
        gb[...] = jnp.zeros_like(gb)
        if first:
            greet([{"tensor": beside}])
            for copy in corners:
                copy.start()

            @pl.loop(0, SLAB // ROWS)
            def _(c):
                sl = pl.ds(pl.multiple_of(c * ROWS, 16), ROWS)
                middle = xs[sl, :].astype(single) + (attn1[sl, :] + attn2[sl, :] + pbias[...])
                x1[sl, :] = middle
                normal, _ = norm_parts(middle)
                n2[sl, :] = (normal * gain[...] + shift[...]).astype(narrow)
                branch[sl, :] = jnp.zeros((ROWS, width), single)
                dn2[sl, :] = jnp.zeros((ROWS, width), single)

            for j in range(width // LANES):
                cut = slice(j * LANES, (j + 1) * LANES)
                n2t[cut, :] = n2[:, cut].T
                gt[cut, :] = gs[:, cut].T
        else:
            greet([{"tensor": beside}, {"tensor": across}])
            for copy in swaps:
                copy.start()

            @pl.loop(0, SLAB // ROWS)
            def _(c):
                sl = pl.ds(pl.multiple_of(c * ROWS, 16), ROWS)
                branch[sl, :] = branch0[sl, :]
                dn2[sl, :] = dn20[sl, :]

    if first:

        @pl.when(step == count)
        def _():
            for copy in corners:
                copy.wait()

    @pl.when(step < count)
    def _():
        w1[...] = w1a[...]
        w2[...] = w2a[...]
        b1[...] = smalls[kinds[0], 0:1, pl.ds(pl.multiple_of(step * BLOCK, BLOCK), BLOCK)]

    @pl.when(step >= count)
    def _():
        cut = pl.ds(pl.multiple_of((step - count) * BLOCK, BLOCK), BLOCK)
        if first:
            w1[...] = corner1[:, cut]
            w2[...] = corner2[cut, :]
        else:
            w1[...] = w1b[...]
            w2[...] = w2b[...]
        b1[...] = smalls[kinds[1], 0:1, cut]

    bias_row = step // count
    bias_cut = pl.ds(pl.multiple_of((step % count) * BLOCK, BLOCK), BLOCK)

    @pl.loop(0, SLAB // CHUNK)
    def _(c):
        sl = pl.ds(pl.multiple_of(c * CHUNK, 16), CHUNK)
        z = dot(n2[sl, :], w1[...]) + b1[0:1]
        dh = dot_nt(gs[sl, :], w2[...])
        act, slope = gelu_parts(z)
        h = act.astype(narrow)
        dz = (dh * slope).astype(narrow)
        hs[sl, :] = h
        zs[sl, :] = dz
        gb[bias_row, 0:1, bias_cut] += jnp.sum(dz.astype(single), axis=0, keepdims=True)
        branch[sl, :] += dot(h, w2[...])
        dn2[sl, :] += dot_nt(dz, w1[...])

    if not first:

        @pl.when(step == 0)
        def _():
            for copy, got, keep, crossing in zip(
                swaps, (got1, got2), (keep1, keep2), crossings, strict=True
            ):
                copy.wait()
                add_rows(got, 0, [(got, 0), (keep, 0)], got.shape[0])
                crossing.start()

    def store(gw1, gw2):
        @pl.loop(0, width // 256)
        def _(r):
            sl = pl.ds(pl.multiple_of(r * 256, 256), 256)
            gw1[sl, :] = dot(n2t[sl, :], zs[...]).astype(narrow)
            gw2[sl, :] = dot(gt[sl, :], hs[...]).astype(narrow)

    @pl.when(step < count)
    def _():
        store(gw1a, gw2a)

    @pl.when(step >= count)
    def _():
        store(gw1b, gw2b)

    if not first:

        @pl.when(step == 2 * count - 1)
        def _():
            for copy in crossings:
                copy.wait()
            sums[...] = jnp.zeros_like(sums)

            @pl.loop(0, SLAB // ROWS)
            def _(c):
                sl = pl.ds(pl.multiple_of(c * ROWS, 16), ROWS)
                middle = x1[sl, :]
                normal, inverse = norm_parts(middle)
                out[sl, :] = (middle + (branch[sl, :] + fbias[...])).astype(narrow)
                grad = dn2[sl, :]
                cot = gs[sl, :].astype(single)
                total = cot + norm_back(grad, normal, inverse, gain[...])
                dx1[sl, :] = total
                low = total.astype(narrow)
                da[sl, :] = low
                sums[0:1, :] += jnp.sum(grad * normal, axis=0, keepdims=True)
                sums[1:2, :] += jnp.sum(grad, axis=0, keepdims=True)
                sums[2:3, :] += jnp.sum(low.astype(single), axis=0, keepdims=True)
                sums[3:4, :] += jnp.sum(cot, axis=0, keepdims=True)


def mlp_half(first, residents, gives, w1a, w1b, w2a, w2b):
    width, local = w1a.shape
    count = local // BLOCK

    def early(shape, dim):
        def index(i):
            at = jnp.minimum(i, count - 1)
            return (0, at) if dim == 1 else (at, 0)

        return pl.BlockSpec(shape, index)

    def late(shape, dim):
        def index(i):
            at = jnp.maximum(i - count, 0)
            return (0, at) if dim == 1 else (at, 0)

        return pl.BlockSpec(shape, index)

    slab = (SLAB, width)
    flipped = (width, SLAB)
    in_specs = [whole(a.shape) for a in residents]
    if first:
        operands = (*residents, w1a, w2a, w1a, w2a)
        in_specs += [ANY, ANY, early((width, BLOCK), 1), early((BLOCK, width), 0)]
        outs = [
            (of(slab, single), whole(slab)),
            (of(slab), whole(slab)),
            (of(flipped), whole(flipped)),
            (of(flipped), whole(flipped)),
            (of(slab, single), whole(slab)),
            (of(slab, single), whole(slab)),
        ]
        scratch = [
            pltpu.VMEM((width, local), narrow),
            pltpu.VMEM((local, width), narrow),
            pltpu.SemaphoreType.DMA((2,)),
            pltpu.SemaphoreType.DMA((2,)),
        ]
        params = pltpu.CompilerParams(
            vmem_limit_bytes=VMEM, collective_id=2, has_side_effects=True
        )
    else:
        operands = (*residents, *gives, w1a, w1b, w2a, w2b)
        in_specs += [
            ANY,
            ANY,
            early((width, BLOCK), 1),
            late((width, BLOCK), 1),
            early((BLOCK, width), 0),
            late((BLOCK, width), 0),
        ]
        outs = [
            (of(slab), whole(slab)),
            (of(slab, single), whole(slab)),
            (of(slab), whole(slab)),
            (of((8, width), single), whole((8, width))),
            (of((width, local)), ANY),
            (of((width, local)), ANY),
        ]
        scratch = [
            pltpu.VMEM(slab, single),
            pltpu.VMEM(slab, single),
            pltpu.VMEM((width, local), narrow),
            pltpu.VMEM((width, local), narrow),
            pltpu.SemaphoreType.DMA((4,)),
            pltpu.SemaphoreType.DMA((4,)),
        ]
        params = pltpu.CompilerParams(
            vmem_limit_bytes=VMEM, collective_id=3, has_side_effects=True
        )
    outs += [
        (of((width, local)), early((width, BLOCK), 1)),
        (of((width, local)), late((width, BLOCK), 1)),
        (of((width, local)), early((width, BLOCK), 1)),
        (of((width, local)), late((width, BLOCK), 1)),
        (of((2, 8, local), single), whole((2, 8, local))),
    ]
    scratch += [
        pltpu.VMEM((width, BLOCK), narrow),
        pltpu.VMEM((BLOCK, width), narrow),
        pltpu.VMEM((1, BLOCK), single),
        pltpu.VMEM((SLAB, BLOCK), narrow),
        pltpu.VMEM((SLAB, BLOCK), narrow),
    ]
    return pl.pallas_call(
        functools.partial(mlp_kernel, first),
        out_shape=[o[0] for o in outs],
        grid=(2 * count,),
        in_specs=in_specs,
        out_specs=[o[1] for o in outs],
        scratch_shapes=scratch,
        compiler_params=params,
        cost_estimate=pl.CostEstimate(
            flops=18_000_000_000, bytes_accessed=40_000_000, transcendentals=4_000_000
        ),
        name="mlp",
    )(*operands)


def backward_kernel(first, rows_held, images, *refs):
    (da, n1, qkv, mixed, weights, wrel, bits, lanes, sides, keys) = refs[:10]
    if first:
        (keep1, keep2, far1, far2, give1, give2) = refs[10:16]
        (dn1, keep, give, bias, grel, reduced, acc, dqkv) = refs[16:24]
        (got, total_fc, landing, sends, recvs) = refs[24:]
        fc_rows = 2 * keep1.shape[0]
    else:
        (prior, xs, dx1, gain, keep_far, give_far, reduced) = refs[10:17]
        (back, sums, keep, give, bias, grel, cross, summed, acc, dqkv) = refs[17:27]
        (got, sends, recvs, locals_) = refs[27:]
        fc_rows = summed.shape[0]
    step = pl.program_id(0)
    image = lax.axis_index("dp")
    beside, across, _ = partners(lax.axis_index("tensor"))
    send = Sender(sends, recvs, None if first else locals_)
    reducer = Reducer(send, 2, image, images, fc_rows)
    if first:
        swaps = [
            send.remote(k, g, got.at[pl.ds(k * fc_rows // 2, fc_rows // 2), :], {"tensor": beside})
            for k, g in enumerate((give1, give2))
        ]

        @pl.when(step == 0)
        def _():
            greet([{"tensor": beside}] + reducer.mates)
            for copy in swaps:
                copy.start()

        @pl.when(step == 1)
        def _():
            part = fc_rows // 2
            for k, (mine, crossed) in enumerate(((keep1, far1), (keep2, far2))):
                swaps[k].wait()
                add_rows(
                    total_fc, k * part, [(mine, 0), (got, k * part), (crossed, 0)], part
                )
            reducer.start(0, total_fc, landing)

        for stage, at in ((0, 4), (1, 5)):

            @pl.when(step == at)
            def _():
                reducer.finish(stage, total_fc, landing)
                reducer.start(stage + 1, total_fc, landing)

    else:
        swap_far = send.remote(0, give_far, got, {"tensor": beside})
        crossing = send.remote(1, got, cross, {"tensor": across})

        @pl.when(step == 0)
        def _():
            greet([{"tensor": beside}, {"tensor": across}] + reducer.mates)
            swap_far.start()
            seeds = [
                send.local(k, reduced.at[k], summed.at[rows_at(start, length), :])
                for k, (start, length) in enumerate(reducer.final)
            ]
            for copy in seeds:
                copy.start()
            for copy in seeds:
                copy.wait()
            for copy in reducer.back(2, 2, summed):
                copy.start()

        @pl.when(step == 1)
        def _():
            swap_far.wait()
            add_rows(got, 0, [(got, 0), (keep_far, 0)], got.shape[0])
            crossing.start()

        for stage, at in ((1, 3), (0, 5)):

            @pl.when(step == at)
            def _():
                for copy in reducer.back(2, stage + 1, summed):
                    copy.wait()
                for copy in reducer.back(2, stage, summed):
                    copy.start()

    _, col0, high, wide, offset, live = slot_fields(rows_held)
    half, width = weights.shape[1:]

    @pl.when(pl.program_id(0) == 0)
    def _():
        acc[...] = jnp.zeros_like(acc)
        bias[...] = jnp.zeros_like(bias)
        grel[...] = jnp.zeros_like(grel)
        if not first:
            back[...] = jnp.zeros_like(back)
            sums[...] = jnp.zeros_like(sums)

    @pl.when(live)
    def _():
        _, valid = positions(0, col0, high, wide)
        place = pl.ds(pl.multiple_of(offset, 16), ROWS)
        da_win = jnp.where(valid, da[place, :].astype(single), 0.0).astype(narrow)
        acc[3] += dot_tn(mixed[0], da_win)
        dmix = dot_nt(da_win, weights[3]).astype(narrow)
        low_lane = lax.broadcasted_iota(jnp.int32, (ROWS, LANES), 1) < 64
        for pair in range(half // LANES):
            cut = slice(pair * LANES, (pair + 1) * LANES)
            q, k8, v, rel = (qkv[0, j, :, cut] for j in range(4))
            do = dmix[:, cut]
            dqs, dks, dvs = [], [], []
            for head in range(2):
                mine, other = sides[head : head + 1], sides[1 - head : 2 - head]
                full_key = k8 * mine + keys[...] * other
                scores = dot_nt(full_key, q * mine + rel * other)
                top = jnp.max(scores, axis=0, keepdims=True)
                probs = jnp.exp(scores - top)
                probs = probs * (1.0 / jnp.sum(probs, axis=0, keepdims=True))
                dprobs = dot_nt(v, do * mine)
                mean = jnp.sum(probs * dprobs, axis=0, keepdims=True)
                dscores = (probs * (dprobs - mean)).astype(narrow)
                dvs.append(dot(probs.astype(narrow), do))
                dks.append(dot(dscores, q))
                dqs.append(dot_tn(dscores, full_key))
            dv = jnp.where(low_lane, dvs[0], dvs[1])
            dk = jnp.where(low_lane, dks[0], dks[1]) * 0.125
            dq = jnp.where(low_lane, dqs[0], dqs[1])
            drel = jnp.where(low_lane, dqs[1], dqs[0]) * lanes[0:1]
            drel = shift_right(drel, bits).astype(narrow)
            dq = dq + dot_nt(drel, wrel[...])
            grel[...] += dot_tn(drel, q)
            dqkv[0, :, cut] = dq.astype(narrow)
            dqkv[1, :, cut] = dk.astype(narrow)
            dqkv[2, :, cut] = dv.astype(narrow)
        total = None
        for j in range(3):
            piece = dqkv[j]
            acc[j] += dot_tn(piece, n1[0])
            bias[j : j + 1, :] += jnp.sum(piece.astype(single), axis=0, keepdims=True)
            back_part = dot(piece, weights[j])
            total = back_part if total is None else total + back_part
        if first:
            dn1[0] = total
        else:
            grad = jnp.where(valid, total + prior[0], 0.0)
            normal, inverse = norm_parts(xs[place, :].astype(single))
            sums[0:1, :] += jnp.sum(grad * normal, axis=0, keepdims=True)
            sums[1:2, :] += jnp.sum(grad, axis=0, keepdims=True)
            result = dx1[place, :] + norm_back(grad, normal, inverse, gain[...])
            back[place, :] = jnp.where(valid, result, 0.0).astype(narrow)

    @pl.when(pl.program_id(0) == SLOTS - 1)
    def _():
        part = half // 2
        for j in range(4):
            keep[j * part : (j + 1) * part, :] = acc[j, :part, :].astype(narrow)
            give[j * part : (j + 1) * part, :] = acc[j, part:, :].astype(narrow)
        if first:
            reducer.finish(2, total_fc, landing)
            reducer.extras(total_fc, landing)
            for k, (start, length) in enumerate(reducer.final):
                reduced[k] = total_fc[rows_at(start, length), :]
        else:
            for copy in reducer.back(2, 0, summed):
                copy.wait()
            crossing.wait()


def backward_half(first, rows_held, images, da, n1, qkv, mixed, weights, wrel, tables, final):
    half, width = weights.shape[1:]
    operands = [da, n1, qkv, mixed, weights, wrel, *tables]
    in_specs = [whole(a.shape) for a in operands]
    for at in (1, 2, 3):
        in_specs[at] = by_slot(operands[at].shape[1:])
    extra_bits = images.bit_length() - 1 - HALVINGS
    operands += final
    if first:
        fc_rows = 2 * final[0].shape[0]
        last = fc_rows >> (HALVINGS + 1)
        in_specs += [whole(a.shape) for a in final[:4]] + [ANY, ANY]
        outs = [(of((SLOTS, ROWS, width), single), by_slot((ROWS, width)))]
        more = [(of((2, last, width)), whole((2, last, width)))]
        landing = fc_rows - 2 * last + 2 * last * extra_bits
        copies = 2 + 2 * HALVINGS + 2 * extra_bits
        scratch = [
            pltpu.VMEM((fc_rows, width), narrow),
            pltpu.VMEM((fc_rows, width), narrow),
            pltpu.VMEM((landing, width), narrow),
            pltpu.SemaphoreType.DMA((copies,)),
            pltpu.SemaphoreType.DMA((copies,)),
        ]
    else:
        prior, xs, dx1, gain, keep_far, give_far, reduced = final
        fc_rows = reduced.shape[1] << (HALVINGS + 1)
        in_specs += [by_slot((ROWS, width)), whole(xs.shape), whole(dx1.shape), whole(gain.shape)]
        in_specs += [whole(keep_far.shape), ANY, ANY]
        outs = [
            (of((SLAB, width)), whole((SLAB, width))),
            (of((8, width), single), whole((8, width))),
        ]
        more = [(of(keep_far.shape), ANY), (of((fc_rows, width)), ANY)]
        scratch = [
            pltpu.VMEM(keep_far.shape, narrow),
            pltpu.SemaphoreType.DMA((2 + 2 * HALVINGS,)),
            pltpu.SemaphoreType.DMA((2 + 2 * HALVINGS,)),
            pltpu.SemaphoreType.DMA((2,)),
        ]
    outs += [
        (of((2 * half, width)), whole((2 * half, width))),
        (of((2 * half, width)), whole((2 * half, width))),
        (of((8, half), single), whole((8, half))),
        (of((LANES, LANES), single), whole((LANES, LANES))),
    ] + more
    return pl.pallas_call(
        functools.partial(backward_kernel, first, rows_held, images),
        out_shape=[o[0] for o in outs],
        grid=(SLOTS,),
        in_specs=in_specs,
        out_specs=[o[1] for o in outs],
        scratch_shapes=[
            pltpu.VMEM((4, half, width), single),
            pltpu.VMEM((3, ROWS, half), narrow),
            *scratch,
        ],
        compiler_params=pltpu.CompilerParams(
            vmem_limit_bytes=VMEM, collective_id=4 if first else 5, has_side_effects=True
        ),
        cost_estimate=pl.CostEstimate(
            flops=26_000_000_000, bytes_accessed=40_000_000, transcendentals=4_000_000
        ),
        name="attention_backward",
    )(*operands)


def place_windows(rows_held, device, slab, ext):
    @pl.loop(0, ext.shape[0] // GRID)
    def _(r):
        ext[rows_at(r * GRID, GRID), :] = jnp.zeros((GRID, ext.shape[1]), narrow)

    @pl.loop(0, SLOTS)
    def _(slot):
        row0, col0, high, wide, offset, live = window_fields(rows_held, device, slot)

        @pl.when(live)
        def _():
            target, _ = positions(1, col0, high, wide)
            token = lax.broadcasted_iota(jnp.int32, (WIN * GRID, ROWS), 0)
            choose = jnp.where(token == target, 1.0, 0.0).astype(narrow)
            window = slab[rows_at(offset, ROWS), :]
            where_to = pl.ds(pl.multiple_of(row0 * GRID, GRID), WIN * GRID)
            ext[where_to, :] += dot(choose, window).astype(narrow)


def tail_kernel(
    rows_held, images,
    out, back, keep, crossed, sums1, sums2, bias0, bias1, rel0, rel1, fb0, fb1, peak0, peak1, give,
    output, input_grad, packed, totals, tops,
    ext0, ext1, below0, below1, above0, above1, got, landing, held, sum_land, top_land, sends, recvs,
):
    device, image = lax.axis_index("tensor"), lax.axis_index("dp")
    width = out.shape[1]
    beside, across, corner = partners(device)
    send = Sender(sends, recvs, None)
    reducer = Reducer(send, 1, image, images, held.shape[0])
    back_base = 1 + reducer.copies
    halo_base = back_base + 2 * HALVINGS
    small_base = halo_base + 4
    tokens = rows_held * GRID
    top, bottom = LEFT * GRID, RIGHT * GRID
    held_by = (device, beside, across, corner)
    ring = [{"tensor": beside}, {"tensor": across}] + reducer.mates

    greet([{"tensor": place} for place in (beside, across, corner)] + reducer.mates)
    swap = send.remote(0, give, got, {"tensor": beside})
    swap.start()

    totals[...] = jnp.zeros_like(totals)
    tops[...] = jnp.zeros_like(tops)
    totals[0:2, :] = sums1[0:2, :]
    totals[2:6, :] = sums2[0:4, :]
    rel = rel0[...] + rel1[...]
    rel = rel[HD:] + pltpu.roll(rel[:HD], HD, 1)
    for g in range(HD // 8):
        at = 8 * (1 + g // 6)
        totals[at : at + 8, (g % 6) * LANES : (g % 6 + 1) * LANES] = rel[8 * g : 8 * g + 8]
    half = bias0.shape[1]
    for k, (fb, bias, peak) in enumerate(
        ((fb0, bias0, peak0), (fb0, bias0, peak0), (fb1, bias1, peak1), (fb1, bias1, peak1))
    ):
        odd = k % 2
        totals[pl.ds(24 + held_by[k], 1), :] = fb[odd, 0:1, :]
        for j, row in enumerate((0, 2)):
            value = bias[row : row + 1, :]
            if odd:
                value = pltpu.roll(value, half // 2, 1)
            totals[pl.ds(28 + held_by[k], 1), j * half : (j + 1) * half] = value
        best = jnp.broadcast_to(jnp.max(peak[...], axis=1, keepdims=True), (8, LANES))
        if odd:
            best = pltpu.roll(best, 8 - half // LANES, 0)
        tops[pl.ds(pl.multiple_of(held_by[k] * 8, 8), 8), :] = best

    def small_copies(k):
        return [
            send.remote(small_base + 2 * k, totals, sum_land.at[k], ring[k]),
            send.remote(small_base + 2 * k + 1, tops, top_land.at[k], ring[k]),
        ]

    def small_start(k):
        for copy in small_copies(k):
            copy.start()

    def small_finish(k):
        for copy in small_copies(k):
            copy.wait()
        totals[...] += sum_land[k]
        tops[...] = jnp.maximum(tops[...], top_land[k])

    def halo(base, ext, below, above):
        up = send.remote(
            base, ext.at[pl.ds(0, top), :], below, {"tensor": (device + SPLIT - 1) % SPLIT}
        )
        down = send.remote(
            base + 1, ext.at[pl.ds(top + tokens, bottom), :], above, {"tensor": (device + 1) % SPLIT}
        )
        return up, down

    def halo_start(copies):
        up, down = copies
        pl.when(device > 0)(up.start)
        pl.when(device < SPLIT - 1)(down.start)

    def halo_finish(copies, ext, below, above, result):
        up, down = copies
        pl.when(device > 0)(up.wait_send)
        pl.when(device < SPLIT - 1)(down.wait_send)
        add_rows(result, 0, [(ext, top)], tokens)

        @pl.when(device < SPLIT - 1)
        def _():
            up.wait_recv()
            at = tokens - top
            add_rows(result, at, [(result, at), (below, 0)], top)

        @pl.when(device > 0)
        def _():
            down.wait_recv()
            add_rows(result, 0, [(result, 0), (above, 0)], bottom)

    small_start(0)
    place_windows(rows_held, device, back, ext1)
    halos1 = halo(halo_base, ext1, below1, above1)
    halo_start(halos1)
    swap.wait()
    add_rows(held, 0, [(keep, 0), (got, 0), (crossed, 0)], held.shape[0])
    reducer.start(0, held, landing)
    small_finish(0)
    small_start(1)
    place_windows(rows_held, device, out, ext0)
    halos0 = halo(halo_base + 2, ext0, below0, above0)
    halo_start(halos0)
    small_finish(1)
    small_start(2)
    reducer.finish(0, held, landing)
    reducer.start(1, held, landing)
    small_finish(2)
    small_start(3)
    reducer.finish(1, held, landing)
    reducer.start(2, held, landing)
    small_finish(3)
    small_start(4)
    reducer.finish(2, held, landing)
    reducer.extras(held, landing)
    for start, length in reducer.final:
        packed[rows_at(start, length), :] = held[rows_at(start, length), :]
    stages = [reducer.back(back_base, stage, packed) for stage in range(HALVINGS)]
    for copy in stages[2]:
        copy.start()
    for k in range(4, len(ring)):
        small_finish(k)
        if k + 1 < len(ring):
            small_start(k + 1)
    for copy in stages[2]:
        copy.wait()
    for copy in stages[1]:
        copy.start()
    halo_finish(halos1, ext1, below1, above1, input_grad)
    for copy in stages[1]:
        copy.wait()
    for copy in stages[0]:
        copy.start()
    halo_finish(halos0, ext0, below0, above0, output)
    for copy in stages[0]:
        copy.wait()


def tail(rows_held, images, *operands):
    width = operands[0].shape[1]
    packed = operands[2].shape
    tokens = rows_held * GRID
    bits = images.bit_length() - 1
    extra = bits - HALVINGS
    last = packed[0] >> (HALVINGS + 1)
    copies = 1 + 4 * HALVINGS + 2 * extra + 4 + 2 * (2 + bits)
    ext = ((rows_held + LEFT + RIGHT) * GRID, width)
    outs = [
        of((tokens, width)), of((tokens, width)), of(packed),
        of((32, width), single), of((32, LANES), single),
    ]
    return pl.pallas_call(
        functools.partial(tail_kernel, rows_held, images),
        out_shape=outs,
        in_specs=[pl.BlockSpec(memory_space=pltpu.VMEM)] * (len(operands) - 1) + [ANY],
        out_specs=[pl.BlockSpec(memory_space=pltpu.VMEM)] * len(outs),
        scratch_shapes=[
            pltpu.VMEM(ext, narrow),
            pltpu.VMEM(ext, narrow),
            pltpu.VMEM((LEFT * GRID, width), narrow),
            pltpu.VMEM((LEFT * GRID, width), narrow),
            pltpu.VMEM((RIGHT * GRID, width), narrow),
            pltpu.VMEM((RIGHT * GRID, width), narrow),
            pltpu.VMEM(packed, narrow),
            pltpu.VMEM((packed[0] - 2 * last + 2 * last * extra, width), narrow),
            pltpu.VMEM(packed, narrow),
            pltpu.VMEM((2 + bits, 32, width), single),
            pltpu.VMEM((2 + bits, 32, LANES), single),
            pltpu.SemaphoreType.DMA((copies,)),
            pltpu.SemaphoreType.DMA((copies,)),
        ],
        compiler_params=pltpu.CompilerParams(
            vmem_limit_bytes=VMEM, collective_id=6, has_side_effects=True
        ),
        cost_estimate=pl.CostEstimate(
            flops=4_000_000_000, bytes_accessed=20_000_000, transcendentals=0
        ),
        name="tail",
    )(*operands)


def shards(
    inputs,
    w_qkv,
    qv_bias,
    w_proj,
    proj_bias,
    w_fc1,
    fc1_bias,
    w_fc2,
    fc2_bias,
    norm1_gain,
    norm1_shift,
    norm2_gain,
    norm2_shift,
    rel_h,
    rel_w,
    cotangent,
):
    width = inputs.shape[2]
    rows = inputs.shape[1] // GRID
    local = w_qkv.shape[2]
    heads = local // HD
    device = lax.axis_index("tensor")
    tables = lane_tables()

    block = jnp.zeros((2, 32, HD), narrow)
    block = block.at[0, : 2 * WIN - 1].set(rel_h[::-1]).at[1, : 2 * WIN - 1].set(rel_w[::-1])
    block = block.reshape(HD, HD).T
    wrel = jnp.zeros((LANES, LANES), narrow).at[:HD, HD:].set(block).at[HD:, :HD].set(block)

    pack = jnp.concatenate([w_qkv.transpose(0, 2, 1).reshape(3 * local, width), w_proj])
    small = jnp.zeros((8, fc1_bias.shape[0]), single).at[0].set(fc1_bias)
    for j in range(2):
        small = small.at[1 + 2 * j, :local].set(qv_bias[j])
        small = small.at[2 + 2 * j, local : 2 * local].set(qv_bias[j])
    norm1 = (norm1_gain[None], norm1_shift[None])

    (
        xs, n1, near_qkv, near_mixed, near_attn, near_peak,
        near_w, across, beside1, beside2, smalls,
    ) = near_forward(inputs[0], pack, w_fc1, w_fc2, small, norm1, wrel, tables)
    gs, far_qkv, far_mixed, far_attn, far_peak, far_w, across1, across2 = far_forward(
        cotangent[0], across, w_fc1, w_fc2, smalls, n1, wrel, tables
    )

    x1, n2, n2t, gt, branch, dn2, *far_fc = mlp_half(
        True,
        (xs, near_attn, far_attn, gs, proj_bias[None], norm2_gain[None], norm2_shift[None], smalls),
        None,
        across1,
        None,
        across2,
        None,
    )
    out, dx1, da, sums2, far1, far2, *near_fc = mlp_half(
        False,
        (
            x1, n2, n2t, gs, gt, branch, dn2, fc2_bias[None], norm2_gain[None], smalls,
            far_fc[0], far_fc[2],
        ),
        (far_fc[1], far_fc[3]),
        w_fc1,
        beside1,
        w_fc2,
        beside2,
    )

    images = lax.axis_size("dp")
    dn1, far_keep, far_give, far_bias, far_rel, reduced = backward_half(
        True, rows, images, da, n1, far_qkv, far_mixed, far_w, wrel, tables,
        [near_fc[0], near_fc[2], far1, far2, near_fc[1], near_fc[3]],
    )
    back, sums1, near_keep, near_give, near_bias, near_rel, crossed, summed = backward_half(
        False, rows, images, da, n1, near_qkv, near_mixed, near_w, wrel, tables,
        [dn1, xs, dx1, norm1_gain[None], far_keep, far_give, reduced],
    )
    output, input_grad, gpack, totals, tops = tail(
        rows, images, out, back, near_keep, crossed, sums1, sums2, near_bias, far_bias,
        near_rel, far_rel, near_fc[4], far_fc[4], near_peak, far_peak, near_give,
    )

    hidden = fc1_bias.shape[0]
    summed = summed.astype(single)
    gpack = gpack.astype(single)
    blocks = totals[8:24].reshape(2, 8, 6, LANES).transpose(0, 2, 1, 3).reshape(-1, LANES)[:HD, :HD]
    grad_rel = jnp.stack([blocks[: 2 * WIN - 1][::-1], blocks[32 : 32 + 2 * WIN - 1][::-1]])
    qv = lax.dynamic_slice_in_dim(totals, 28 + device, 1)[0].reshape(2, 2 * local)[:, :local]
    head_max = lax.dynamic_slice(tops, (8 * device, 0), (heads, 1))[:, 0]
    factor = jnp.sqrt(CLIP / jnp.maximum(head_max, CLIP))
    clipped_qk = (w_qkv[:2].astype(single) * jnp.repeat(factor, HD)).astype(narrow)

    return (
        output[None],
        input_grad[None],
        gpack[: 3 * local].reshape(3, local, width).transpose(0, 2, 1),
        qv,
        gpack[3 * local :],
        totals[4],
        summed[:hidden],
        lax.dynamic_slice_in_dim(totals, 24 + device, 1)[0],
        summed[hidden:].T,
        totals[5],
        totals[:4],
        grad_rel,
        clipped_qk,
        head_max,
    )


def solution(mesh):
    return jax.shard_map(
        shards,
        mesh=mesh,
        in_specs=(
            P("dp", "tensor", None),
            P(None, None, "tensor"),
            P(None, "tensor"),
            P("tensor", None),
            P(),
            P(None, "tensor"),
            P("tensor"),
            P("tensor", None),
            P(),
            P(),
            P(),
            P(),
            P(),
            P(),
            P(),
            P("dp", "tensor", None),
        ),
        out_specs=(
            P("dp", "tensor", None),
            P("dp", "tensor", None),
            P(None, None, "tensor"),
            P(None, "tensor"),
            P("tensor", None),
            P(),
            P(None, "tensor"),
            P("tensor"),
            P("tensor", None),
            P(),
            P(),
            P(),
            P(None, None, "tensor"),
            P("tensor"),
        ),
        check_vma=False,
    )
```

```python
import functools

import jax
import jax.numpy as jnp
import numpy as np
from jax import lax
from jax.experimental import pallas as pl
from jax.experimental.pallas import tpu as pltpu
from jax.sharding import PartitionSpec as P

HD = 64
GRID = 64
WIN = 14
TILES = 5
SPAN = WIN * WIN
ROWS = 208
SLOTS = 7
SLAB = 6 * ROWS
SPLIT = 4
SHORT = 112
LEFT = 6
RIGHT = 12
LANES = 128
EPS = 1e-6
CLIP = 3.0
VMEM = 60 * 1024 * 1024

single = jnp.float32
narrow = jnp.bfloat16

def lane_tables():
    row = np.arange(ROWS)
    x, y = row // WIN, row % WIN
    lane = np.arange(LANES) % 64
    part = lane // 32
    at = lane % 32
    amount = np.where(part[None, :] == 0, 13 - x[:, None], 13 - y[:, None])
    amount = np.where((row < SPAN)[:, None], amount, 0)
    bits = np.stack([(amount >> b) & 1 for b in range(4)]).astype(np.float32)
    lanes = np.zeros((8, LANES), np.float32)
    lanes[0] = at < WIN
    lanes[1] = (at >= 16) & (at < 16 + WIN)
    lanes[2] = lane == 31
    sides = np.zeros((16, LANES), np.float32)
    sides[0] = np.arange(LANES) < 64
    sides[1] = np.arange(LANES) >= 64
    place = np.where(part[None, :] == 0, x[:, None], y[:, None])
    hot = ((at % 16)[None, :] == place) & ((at % 16) < WIN)[None, :] & (row < SPAN)[:, None]
    keys = hot.astype(np.float32)
    keys[SPAN:, lane == 31] = -1e30
    return (
        jnp.asarray(bits),
        jnp.asarray(lanes),
        jnp.asarray(sides, narrow),
        jnp.asarray(keys, narrow),
    )


def dot(a, b):
    return jnp.dot(a, b, preferred_element_type=single)


def dot_nt(a, b):
    return lax.dot_general(a, b, (((1,), (1,)), ((), ())), preferred_element_type=single)


def dot_tn(a, b):
    return lax.dot_general(a, b, (((0,), (0,)), ((), ())), preferred_element_type=single)


def norm_parts(values):
    centre = values - jnp.mean(values, axis=-1, keepdims=True)
    inverse = lax.rsqrt(jnp.mean(centre * centre, axis=-1, keepdims=True) + EPS)
    return centre * inverse, inverse


def norm_back(grad, normal, inverse, gain):
    scaled = grad * gain
    first = jnp.mean(scaled, axis=-1, keepdims=True)
    second = jnp.mean(scaled * normal, axis=-1, keepdims=True)
    return inverse * (scaled - first - normal * second)


def slot_fields(rows_held):
    return window_fields(rows_held, lax.axis_index("tensor"), pl.program_id(0) % SLOTS)


def window_fields(rows_held, device, slot):
    window = device * (SLOTS - 1) + slot
    i, j = window // TILES, window % TILES
    last = device // (SPLIT - 1)
    live = slot < SLOTS - 1 + last
    row0 = i * WIN - device * rows_held + LEFT
    high = jnp.minimum(WIN, GRID - i * WIN)
    wide = jnp.minimum(WIN, GRID - j * WIN)
    tall = jnp.where(last == 1, SLOTS - TILES, SLOTS)
    offset = ROWS * jnp.minimum(slot, tall) + SHORT * jnp.maximum(slot - tall, 0)
    return row0, j * WIN, high, wide, offset, live


def positions(axis, first_col, high, wide):
    shape = (ROWS, 1) if axis == 0 else (1, ROWS)
    row = lax.broadcasted_iota(jnp.int32, shape, axis)
    x = lax.shift_right_logical(row * 4682, 16)
    y = row - x * WIN
    valid = (x < high) & (y < wide)
    return jnp.where(valid, x * GRID + first_col + y, -1), valid


def gather_window(source, target):
    token = lax.broadcasted_iota(jnp.int32, (ROWS, WIN * GRID), 1)
    choose = jnp.where(token == target, 1.0, 0.0).astype(narrow)
    return dot(choose, source)


def shift_left(values, bits):
    for b in range(4):
        values = jnp.where(bits[b] > 0.5, pltpu.roll(values, LANES - (1 << b), 1), values)
    return values


def shift_right(values, bits):
    for b in range(4):
        values = jnp.where(bits[b] > 0.5, pltpu.roll(values, 1 << b, 1), values)
    return values


def partners(device):
    beside = device + 1 - 2 * (device % 2)
    across = (device + 2) % SPLIT
    corner = (beside + 2) % SPLIT
    return beside, across, corner


def greet(places):
    barrier = pltpu.get_barrier_semaphore()
    for place in places:
        pl.semaphore_signal(barrier, inc=1, device_id=place, device_id_type=pl.DeviceIdType.MESH)
    pl.semaphore_wait(barrier, len(places))


class Sender:
    def __init__(self, sends, recvs, locals_):
        self.sends, self.recvs, self.locals = sends, recvs, locals_

    def remote(self, at, source, target, place):
        return pltpu.make_async_remote_copy(
            src_ref=source,
            dst_ref=target,
            send_sem=self.sends.at[at],
            recv_sem=self.recvs.at[at],
            device_id=place,
            device_id_type=pl.DeviceIdType.MESH,
        )

    def local(self, at, source, target):
        return pltpu.make_async_copy(source, target, self.locals.at[at])


def mate_of(image, bit):
    unit = 1 << bit
    return image + unit * (1 - 2 * ((image // unit) % 2))


def rows_at(start, count):
    return pl.ds(pl.multiple_of(start, 16), count)


def add_rows(target, target_at, sources, count):
    chunk = 48 if count % 48 == 0 else 16

    @pl.loop(0, count // chunk)
    def _(c):
        total = None
        for ref, at in sources:
            value = ref[rows_at(at + c * chunk, chunk), :].astype(single)
            total = value if total is None else total + value
        target[rows_at(target_at + c * chunk, chunk), :] = total.astype(target.dtype)


HALVINGS = 3


class Halver:
    def __init__(self, send, base, image, images, start, rows, order):
        bits = images.bit_length() - 1
        assert images == 1 << bits and bits >= HALVINGS
        self.send, self.base, self.image = send, base, image
        self.extra_bits = range(HALVINGS, bits)
        self.stages = []
        landing, length = 0, rows
        for bit in order:
            length //= 2
            mine = (image // (1 << bit)) % 2
            keep, give = start + mine * length, start + (1 - mine) * length
            self.stages.append((mate_of(image, bit), keep, give, length, landing))
            landing += length
            start = keep
        self.final = (start, length)
        self.landing = landing

    @staticmethod
    def copies(images):
        return 2 * HALVINGS + images.bit_length() - 1 - HALVINGS

    @staticmethod
    def landing_rows(images, rows):
        last = rows >> HALVINGS
        return rows - last + last * (images.bit_length() - 1 - HALVINGS)

    def out(self, stage, held, landing):
        mate, _, give, length, at = self.stages[stage]
        return self.send.remote(
            self.base + stage,
            held.at[rows_at(give, length), :],
            landing.at[pl.ds(at, length), :],
            {"dp": mate},
        )

    def start(self, stage, held, landing):
        self.out(stage, held, landing).start()

    def finish(self, stage, held, landing):
        self.out(stage, held, landing).wait()
        _, keep, _, length, at = self.stages[stage]
        add_rows(held, keep, [(held, keep), (landing, at)], length)

    def extras(self, held, landing):
        start, length = self.final
        for k, bit in enumerate(self.extra_bits):
            at = self.landing + k * length
            copy = self.send.remote(
                self.base + HALVINGS + k,
                held.at[rows_at(start, length), :],
                landing.at[pl.ds(at, length), :],
                {"dp": mate_of(self.image, bit)},
            )
            copy.start()
            copy.wait()
            add_rows(held, start, [(held, start), (landing, at)], length)

    def back(self, stage, held):
        mate, keep, _, length, _ = self.stages[stage]
        cut = rows_at(keep, length)
        at = self.base + HALVINGS + len(self.extra_bits) + stage
        return self.send.remote(at, held.at[cut, :], held.at[cut, :], {"dp": mate})


def dp_mates(image, images):
    return [{"dp": mate_of(image, bit)} for bit in range(images.bit_length() - 1)]


def attend(n1, valid, weights, qbias, vbias, wrel, bits, lanes, sides, keys, qkv, mixed, peak):
    half = weights.shape[1]
    query = jnp.where(valid, dot_nt(n1, weights[0]) + qbias, 0.0).astype(narrow)
    key8 = dot_nt(n1, weights[1]).astype(narrow) * jnp.asarray(0.125, narrow)
    value = (dot_nt(n1, weights[2]) + vbias).astype(narrow)
    qkv[0, 0] = query
    qkv[0, 1] = key8
    qkv[0, 2] = value
    low_lane = lax.broadcasted_iota(jnp.int32, (ROWS, LANES), 1) < 64
    for pair in range(half // LANES):
        cut = slice(pair * LANES, (pair + 1) * LANES)
        q, k8, v = query[:, cut], key8[:, cut], value[:, cut]
        rel = shift_left(dot(q, wrel[...]), bits)
        rest = rel - rel.astype(narrow).astype(single)
        rel = rel * lanes[0:1] + pltpu.roll(rest, 16, 1) * lanes[1:2] + lanes[2:3]
        rel = rel.astype(narrow)
        qkv[0, 3, :, cut] = rel
        pieces = []
        for head in range(2):
            mine, other = sides[head : head + 1], sides[1 - head : 2 - head]
            only = q * mine
            logits = dot_nt(only, k8)
            at = 2 * pair + head
            peak[at : at + 1, :] = jnp.maximum(
                peak[at : at + 1, :], jnp.max(logits, axis=0, keepdims=True)
            )
            scores = dot_nt(only + rel * other, k8 * mine + keys[...] * other)
            top = jnp.max(scores, axis=1, keepdims=True)
            probs = jnp.exp(scores - top)
            total = jnp.sum(probs, axis=1, keepdims=True)
            pieces.append(dot(probs.astype(narrow), v) * (1.0 / total))
        mixed[0, :, cut] = jnp.where(low_lane, pieces[0], pieces[1]).astype(narrow)
    return dot(mixed[0], weights[3])


def halo_copies(send, base, grid, ext, device, rows):
    top, bottom = LEFT * GRID, RIGHT * GRID
    held_rows = rows * GRID
    down = send.remote(
        base,
        grid.at[pl.ds(held_rows - top, top), :],
        ext.at[pl.ds(0, top), :],
        {"tensor": (device + 1) % SPLIT},
    )
    up = send.remote(
        base + 1,
        grid.at[pl.ds(0, bottom), :],
        ext.at[pl.ds(top + held_rows, bottom), :],
        {"tensor": (device + SPLIT - 1) % SPLIT},
    )
    return down, up


def when_all(*conditions):
    def run(action):
        flag = conditions[0]
        for more in conditions[1:]:
            flag = jnp.logical_and(flag, more)
        pl.when(flag)(action)

    return run


def forward_kernel(
    x, g, pack, fc1, fc2, small, gain, shift, wrel, bits, lanes, sides, keys,
    xs, gs, n1_all, qkv, mixed, attn, peak, weights_out, across1, across2, beside1, beside2, small_out,
    xext, gext, weights, smalls, sends, recvs, locals_,
):
    step = pl.program_id(0)
    far, slot = step // SLOTS, step % SLOTS
    device, image = lax.axis_index("tensor"), lax.axis_index("dp")
    tokens, width = x.shape
    rows = tokens // GRID
    part = pack.shape[1]
    half = 2 * part
    beside, across, corner = partners(device)
    side = image % 2
    mate = {"dp": mate_of(image, 0)}
    send = Sender(sends, recvs, locals_)
    first, last = device > 0, device < SPLIT - 1

    def cut(array, halves, index):
        size = array.shape[0] // halves
        return array.at[rows_at(index * size, size), :]

    x_down, x_up = halo_copies(send, 0, x, xext, device, rows)
    g_down, g_up = halo_copies(send, 2, g, gext, device, rows)
    own_pack = send.remote(4, pack, weights.at[0, :, pl.ds(part, part), :], {"tensor": beside})
    notes = [
        send.remote(5 + k, small, smalls.at[k + 1], {"tensor": place})
        for k, place in enumerate((beside, across, corner))
    ]
    taken = pl.ds(pl.multiple_of(side * (part // 2), 16), part // 2)
    awaited = pl.ds(pl.multiple_of((1 - side) * (part // 2), 16), part // 2)
    pack_x = send.remote(8, pack.at[:, taken, :], weights.at[1, :, taken, :], {"tensor": across})
    pack_y = send.remote(9, weights.at[1, :, taken, :], weights.at[1, :, taken, :], mate)

    def beside_rows(which):
        half_rows = part // 2
        start = jnp.where(which == 0, side, 1 - side) * half_rows + part
        return pl.ds(pl.multiple_of(start, 16), half_rows)

    corner_x = send.remote(
        10, weights.at[1, :, taken, :], weights.at[1, :, beside_rows(0), :], {"tensor": beside}
    )
    corner_y = send.remote(
        11, weights.at[1, :, awaited, :], weights.at[1, :, beside_rows(1), :], {"tensor": beside}
    )
    fc_beside = [
        send.remote(12, fc1, beside1, {"tensor": beside}),
        send.remote(13, fc2, beside2, {"tensor": beside}),
    ]
    fc_x = [
        send.remote(14 + k, cut(source, 2, side), cut(target, 2, side), {"tensor": across})
        for k, (source, target) in enumerate(((fc1, across1), (fc2, across2)))
    ]
    fc_y = [
        send.remote(16 + k, cut(target, 2, side), cut(target, 2, side), mate)
        for k, target in enumerate((across1, across2))
    ]
    own = [
        send.local(0, pack, weights.at[0, :, pl.ds(0, part), :]),
        send.local(1, x, xext.at[pl.ds(LEFT * GRID, tokens), :]),
        send.local(2, small, smalls.at[0]),
    ]
    g_own = send.local(3, g, gext.at[pl.ds(LEFT * GRID, tokens), :])
    kept = [send.local(4, weights, weights_out), send.local(5, smalls, small_out)]

    @pl.when(step == 0)
    def _():
        for ref in (xs, gs, attn, peak):
            ref[...] = jnp.zeros_like(ref)
        for ref in (xext, gext):
            ref[pl.ds(0, LEFT * GRID), :] = jnp.zeros((LEFT * GRID, width), narrow)
            ref[pl.ds(LEFT * GRID + tokens, RIGHT * GRID), :] = jnp.zeros(
                (RIGHT * GRID, width), narrow
            )
        greet([{"tensor": place} for place in (beside, across, corner)] + [mate])
        own_pack.start()
        for copy in notes + own:
            copy.start()
        pl.when(last)(x_down.start)
        pl.when(first)(x_up.start)
        pack_x.start()
        for copy in own + notes + [own_pack]:
            copy.wait()
        pl.when(first)(x_down.wait_recv)

    @pl.when(step == 1)
    def _():
        for copy in fc_beside + [g_own]:
            copy.start()

    when_all(step == 3, last)(x_up.wait_recv)

    @pl.when(step == 4)
    def _():
        pack_x.wait_recv()
        pack_y.start()
        corner_x.start()
        fc_x[0].start()
        pl.when(last)(g_down.start)
        pl.when(first)(g_up.start)

    @pl.when(step == SLOTS)
    def _():
        pack_y.wait_recv()
        corner_y.start()
        fc_x[1].start()
        corner_x.wait_recv()
        corner_y.wait_recv()
        for copy in kept:
            copy.start()

    for k, at in ((0, 9), (1, 11)):

        @pl.when(step == at)
        def _():
            fc_x[k].wait_recv()
            fc_y[k].start()

    row0, col0, high, wide, offset, live = slot_fields(rows)

    @pl.when(live & (far == 0))
    def _():
        target, valid = positions(0, col0, high, wide)
        source = xext[pl.ds(pl.multiple_of(row0 * GRID, GRID), WIN * GRID), :]
        window = gather_window(source, target)
        xs[rows_at(offset, ROWS), :] = window.astype(narrow)
        normal, _ = norm_parts(window)
        n1_all[slot] = jnp.where(valid, normal * gain[...] + shift[...], 0.0).astype(narrow)

    @pl.when(live)
    def _():
        _, valid = positions(0, col0, high, wide)
        place = rows_at(offset, ROWS)
        qbias = smalls[2 * far, 1:2, :half] + smalls[2 * far + 1, 2:3, :half]
        vbias = smalls[2 * far, 3:4, :half] + smalls[2 * far + 1, 4:5, :half]
        terms = attend(
            n1_all[slot], valid, weights.at[far], qbias, vbias, wrel, bits, lanes, sides, keys,
            qkv, mixed, peak.at[far],
        )
        attn[place, :] += jnp.where(valid, terms, 0.0)

    @pl.when(step == 2 * SLOTS - 1)
    def _():
        g_own.wait()
        for down, up in ((x_down, x_up), (g_down, g_up)):
            pl.when(last)(down.wait_send)
            pl.when(first)(up.wait_send)
        pl.when(first)(g_down.wait_recv)
        pl.when(last)(g_up.wait_recv)

        @pl.loop(0, SLOTS)
        def _(slot):
            row0, col0, high, wide, offset, live = window_fields(rows, device, slot)

            @pl.when(live)
            def _():
                target, _ = positions(0, col0, high, wide)
                source = gext[pl.ds(pl.multiple_of(row0 * GRID, GRID), WIN * GRID), :]
                gs[rows_at(offset, ROWS), :] = gather_window(source, target).astype(narrow)

        for copy in (pack_x, pack_y, corner_x, corner_y, *fc_x):
            copy.wait_send()
        for copy in kept + fc_beside + fc_y:
            copy.wait()


def whole(shape):
    zeros = (0,) * len(shape)
    return pl.BlockSpec(shape, lambda *_: zeros, pipeline_mode=pl.Buffered(1))


def by_slot(shape):
    rest = (0,) * len(shape)
    return pl.BlockSpec((1,) + tuple(shape), lambda s, *_: (s,) + rest)


ANY = pl.BlockSpec(memory_space=pl.ANY)


def of(shape, dtype=narrow):
    return jax.ShapeDtypeStruct(shape, dtype)


def forward(x, g, pack, fc1, fc2, small, norm, wrel, tables):
    tokens, width = x.shape
    half = 2 * pack.shape[1]
    slab = (SLAB, width)
    outs = [
        (of(slab), whole(slab)),
        (of(slab), whole(slab)),
        (of((SLOTS, ROWS, width)), whole((SLOTS, ROWS, width))),
        (of((2 * SLOTS, 4, ROWS, half)), by_slot((4, ROWS, half))),
        (of((2 * SLOTS, ROWS, half)), by_slot((ROWS, half))),
        (of(slab, single), whole(slab)),
        (of((2, 8, ROWS), single), whole((2, 8, ROWS))),
        (of((2, 4, half, width)), ANY),
        (of(fc1.shape), ANY),
        (of(fc2.shape), ANY),
        (of(fc1.shape), ANY),
        (of(fc2.shape), ANY),
        (of((SPLIT,) + small.shape, single), ANY),
    ]
    operands = (x, g, pack, fc1, fc2, small, *norm, wrel, *tables)
    ext = (tokens + (LEFT + RIGHT) * GRID, width)
    return pl.pallas_call(
        forward_kernel,
        out_shape=[o[0] for o in outs],
        grid=(2 * SLOTS,),
        in_specs=[ANY] * 6 + [whole(a.shape) for a in operands[6:]],
        out_specs=[o[1] for o in outs],
        scratch_shapes=[
            pltpu.VMEM(ext, narrow),
            pltpu.VMEM(ext, narrow),
            pltpu.VMEM((2, 4, half, width), narrow),
            pltpu.VMEM((SPLIT,) + small.shape, single),
            pltpu.SemaphoreType.DMA((18,)),
            pltpu.SemaphoreType.DMA((18,)),
            pltpu.SemaphoreType.DMA((6,)),
        ],
        compiler_params=pltpu.CompilerParams(
            vmem_limit_bytes=VMEM, collective_id=0, has_side_effects=True
        ),
        cost_estimate=pl.CostEstimate(
            flops=26_000_000_000, bytes_accessed=60_000_000, transcendentals=8_000_000
        ),
        name="attention_forward",
    )(*operands)


BLOCK = 256
CHUNK = 416


def gelu_parts(z):
    size = jnp.abs(z)
    bell = jnp.exp(-0.5 * z * z)
    t = 1.0 / (1.0 + 0.2316418882663604 * size)
    poly = 0.5 * 1.061405429 * t + (0.5 * -1.453152027)
    poly = poly * t + 0.5 * 1.421413741
    poly = poly * t + 0.5 * -0.284496736
    poly = poly * t + 0.5 * 0.254829592
    tail = poly * t * bell
    phi_total = jnp.where(z >= 0, 1.0 - tail, tail)
    return z * phi_total, phi_total + z * bell * 0.3989422804014327


def mlp_kernel(
    xs, attn, gs, pbias, gain, shift, fbias, smalls, src1, src2,
    w1_across, w1_beside, w1_own, w2_across, w2_beside, w2_own,
    out, dx1, da, sums, near1, near2, far1, far2, rest, gb,
    n2, n2t, gt, branch, dn2, corner1, corner2, keep1, keep2, give1, give2, got1, got2, near_got1,
    near_got2, w1, w2, b1, hs, zs, sends, recvs,
):
    step = pl.program_id(0)
    count = pl.num_programs(0) // SPLIT
    group, index = step // count, step % count
    width = gs.shape[1]
    cut = pl.ds(pl.multiple_of(index * BLOCK, BLOCK), BLOCK)
    holder = jnp.where(group == 0, 2, jnp.where(group == 1, 3, jnp.where(group == 2, 1, 0)))
    beside, across, _ = partners(lax.axis_index("tensor"))
    send = Sender(sends, recvs, None)
    corners = [
        send.remote(0, src1, corner1, {"tensor": beside}),
        send.remote(1, src2, corner2, {"tensor": beside}),
    ]
    swaps = [
        send.remote(2, give1, got1, {"tensor": beside}),
        send.remote(3, give2, got2, {"tensor": beside}),
    ]
    upper = got2.shape[0] // 2
    crossings = [
        send.remote(4, got1, far1, {"tensor": across}),
        send.remote(5, got2.at[pl.ds(0, upper), :], far2, {"tensor": across}),
    ]
    near_swaps = [
        send.remote(6, corner1, near_got1, {"tensor": beside}),
        send.remote(7, corner2, near_got2, {"tensor": beside}),
    ]

    @pl.when(step == 0)
    def _():
        gb[...] = jnp.zeros_like(gb)
        greet([{"tensor": beside}, {"tensor": across}])
        for copy in corners:
            copy.start()

        @pl.loop(0, SLAB // ROWS)
        def _(c):
            sl = rows_at(c * ROWS, ROWS)
            middle = xs[sl, :].astype(single) + (attn[sl, :] + pbias[...])
            dx1[sl, :] = middle
            normal, _ = norm_parts(middle)
            n2[sl, :] = (normal * gain[...] + shift[...]).astype(narrow)
            branch[sl, :] = jnp.zeros((ROWS, width), single)
            dn2[sl, :] = jnp.zeros((ROWS, width), single)

        for j in range(width // LANES):
            lanes = slice(j * LANES, (j + 1) * LANES)
            n2t[lanes, :] = n2[:, lanes].T
            gt[lanes, :] = gs[:, lanes].T

    @pl.when(step == count)
    def _():
        for copy in corners:
            copy.wait()

    @pl.when(step == 2 * count)
    def _():
        for copy in swaps:
            copy.start()

    for k, (first, second) in enumerate(
        ((w1_across, w2_across), (None, None), (w1_beside, w2_beside), (w1_own, w2_own))
    ):

        @pl.when(group == k)
        def _():
            if first is None:
                w1[...] = corner1[:, cut]
                w2[...] = corner2[cut, :]
            else:
                w1[...] = first[...]
                w2[...] = second[...]

    b1[...] = smalls[holder, 0:1, cut]

    @pl.loop(0, SLAB // CHUNK)
    def _(c):
        sl = rows_at(c * CHUNK, CHUNK)
        z = dot(n2[sl, :], w1[...]) + b1[0:1]
        dh = dot_nt(gs[sl, :], w2[...])
        act, slope = gelu_parts(z)
        h = act.astype(narrow)
        dz = (dh * slope).astype(narrow)
        hs[sl, :] = h
        zs[sl, :] = dz
        gb[holder, 0:1, cut] += jnp.sum(dz.astype(single), axis=0, keepdims=True)
        branch[sl, :] += dot(h, w2[...])
        dn2[sl, :] += dot_nt(dz, w1[...])

    @pl.when(step == 2 * count)
    def _():
        for copy, got, keep, crossing in zip(
            swaps, (got1, got2), (keep1, keep2), crossings, strict=True
        ):
            copy.wait()
            add_rows(got, 0, [(got, 0), (keep, 0)], got.shape[0])
            crossing.start()
        rest[...] = got2[pl.ds(upper, upper), :]

    for k, (first, second) in enumerate(
        ((keep1, keep2), (give1, give2), (corner1, corner2), (near1, near2))
    ):

        @pl.when(group == k)
        def _():
            @pl.loop(0, width // 256)
            def _(r):
                sl = rows_at(r * 256, 256)
                first[sl, cut] = dot(n2t[sl, :], zs[...]).astype(narrow)
                second[sl, cut] = dot(gt[sl, :], hs[...]).astype(narrow)

    @pl.when(step == 3 * count - 1)
    def _():
        for copy in near_swaps:
            copy.start()

    @pl.when(step == 4 * count - 1)
    def _():
        for copy, near, got in zip(
            near_swaps, (near1, near2), (near_got1, near_got2), strict=True
        ):
            copy.wait()
            add_rows(near, 0, [(near, 0), (got, 0)], near.shape[0])
        sums[...] = jnp.zeros_like(sums)

        @pl.loop(0, SLAB // ROWS)
        def _(c):
            sl = rows_at(c * ROWS, ROWS)
            middle = dx1[sl, :]
            normal, inverse = norm_parts(middle)
            out[sl, :] = (middle + (branch[sl, :] + fbias[...])).astype(narrow)
            grad = dn2[sl, :]
            cot = gs[sl, :].astype(single)
            total = cot + norm_back(grad, normal, inverse, gain[...])
            dx1[sl, :] = total
            low = total.astype(narrow)
            da[sl, :] = low
            sums[0:1, :] += jnp.sum(grad * normal, axis=0, keepdims=True)
            sums[1:2, :] += jnp.sum(grad, axis=0, keepdims=True)
            sums[2:3, :] += jnp.sum(low.astype(single), axis=0, keepdims=True)
            sums[3:4, :] += jnp.sum(cot, axis=0, keepdims=True)

        for copy in crossings:
            copy.wait()


def mlp(residents, across, beside, own):
    width, local = own[0].shape
    count = local // BLOCK

    def block(shape, group, dim):
        def index(i):
            at = jnp.clip(i - group * count, 0, count - 1)
            return (0, at) if dim == 1 else (at, 0)

        return pl.BlockSpec(shape, index)

    slab = (SLAB, width)
    square = (width, local)
    in_specs = [whole(a.shape) for a in residents] + [ANY, ANY]
    in_specs += [block((width, BLOCK), group, 1) for group in (0, 2, 3)]
    in_specs += [block((BLOCK, width), group, 0) for group in (0, 2, 3)]
    outs = [
        (of(slab), whole(slab)),
        (of(slab, single), whole(slab)),
        (of(slab), whole(slab)),
        (of((8, width), single), whole((8, width))),
        (of(square), whole(square)),
        (of(square), whole(square)),
        (of(square), ANY),
        (of((width // 2, local)), ANY),
        (of((width // 2, local)), whole((width // 2, local))),
        (of((SPLIT, 8, local), single), whole((SPLIT, 8, local))),
    ]
    flipped = pltpu.VMEM((width, SLAB), narrow)
    return pl.pallas_call(
        mlp_kernel,
        out_shape=[o[0] for o in outs],
        grid=(SPLIT * count,),
        in_specs=in_specs,
        out_specs=[o[1] for o in outs],
        scratch_shapes=[
            pltpu.VMEM(slab, narrow),
            flipped,
            flipped,
            pltpu.VMEM(slab, single),
            pltpu.VMEM(slab, single),
            *[pltpu.VMEM(square, narrow)] * 10,
            pltpu.VMEM((width, BLOCK), narrow),
            pltpu.VMEM((BLOCK, width), narrow),
            pltpu.VMEM((1, BLOCK), single),
            pltpu.VMEM((SLAB, BLOCK), narrow),
            pltpu.VMEM((SLAB, BLOCK), narrow),
            pltpu.SemaphoreType.DMA((8,)),
            pltpu.SemaphoreType.DMA((8,)),
        ],
        compiler_params=pltpu.CompilerParams(
            vmem_limit_bytes=VMEM, collective_id=1, has_side_effects=True
        ),
        cost_estimate=pl.CostEstimate(
            flops=36_000_000_000, bytes_accessed=60_000_000, transcendentals=8_000_000
        ),
        name="mlp",
    )(*residents, *across, across[0], beside[0], own[0], across[1], beside[1], own[1])


def backward_kernel(
    rows_held, images,
    da, n1, qkv, mixed, weights, wrel, bits, lanes, sides, keys, xs, dx1, gain, near1, near2, far1, far2, rest,
    back, sums, keep, give, bias, grel, crossed, summed1, summed2,
    acc, dqkv, dmix, dn1, keep_far, give_far, got_far, held1, held2, land1, land2, rest_got,
    sends, recvs, locals_,
):
    step = pl.program_id(0)
    slot, far = step % SLOTS, 1 - step // SLOTS
    image = lax.axis_index("dp")
    beside, across, _ = partners(lax.axis_index("tensor"))
    send = Sender(sends, recvs, locals_)
    half, width = weights.shape[2:]
    per = Halver.copies(images)
    sum1 = Halver(send, 3, image, images, 0, held1.shape[0], (0, 1, 2))
    sum2 = Halver(send, 3 + per, image, images, 0, held2.shape[0], (0, 1, 2))
    rest_cross = send.remote(0, rest, rest_got, {"tensor": across})
    far_swap = send.remote(1, give_far, got_far, {"tensor": beside})
    far_cross = send.remote(2, got_far, crossed, {"tensor": across})
    upper = held2.shape[0] - rest_got.shape[0]

    def seed(k, halver, held, summed):
        start, length = halver.final
        copy = send.local(k, held.at[rows_at(start, length), :], summed.at[rows_at(start, length), :])
        copy.start()
        copy.wait()

    def begin():
        greet([{"tensor": beside}, {"tensor": across}] + dp_mates(image, images))
        rest_cross.start()
        add_rows(held1, 0, [(near1, 0), (far1, 0)], held1.shape[0])
        sum1.start(0, held1, land1)

    def second():
        add_rows(held2, 0, [(near2, 0), (far2, 0)], upper)
        rest_cross.wait()
        add_rows(held2, upper, [(near2, upper), (rest_got, 0)], rest_got.shape[0])

    def third():
        sum1.finish(0, held1, land1)
        sum1.start(1, held1, land1)
        sum2.start(0, held2, land2)

    def fourth():
        sum1.finish(1, held1, land1)
        sum1.start(2, held1, land1)

    def fifth():
        sum2.finish(0, held2, land2)
        sum2.start(1, held2, land2)
        sum1.finish(2, held1, land1)
        sum1.extras(held1, land1)
        seed(0, sum1, held1, summed1)
        sum1.back(2, summed1).start()

    def sixth():
        far_swap.start()
        sum2.finish(1, held2, land2)
        sum2.start(2, held2, land2)
        sum1.back(2, summed1).wait()
        sum1.back(1, summed1).start()

    def seventh():
        far_swap.wait()
        add_rows(got_far, 0, [(got_far, 0), (keep_far, 0)], got_far.shape[0])
        far_cross.start()

    def eighth():
        sum2.finish(2, held2, land2)
        sum2.extras(held2, land2)
        seed(1, sum2, held2, summed2)
        sum2.back(2, summed2).start()
        sum1.back(1, summed1).wait()
        sum1.back(0, summed1).start()

    def ninth():
        sum2.back(2, summed2).wait()
        sum2.back(1, summed2).start()

    def tenth():
        sum2.back(1, summed2).wait()
        sum1.back(0, summed1).wait()
        sum2.back(0, summed2).start()

    events = {
        (0, 0): begin,
        (2, 2): second,
        (3, 1): third,
        (4, 2): fourth,
        (5, 3): fifth,
        (7, 0): sixth,
        (8, 0): seventh,
        (8, 2): eighth,
        (10, 0): ninth,
        (11, 1): tenth,
    }

    def fire(section):
        for (at, place), event in events.items():
            if place == section:
                pl.when(step == at)(event)

    _, col0, high, wide, offset, live = slot_fields(rows_held)
    place = rows_at(offset, ROWS)

    @pl.when(slot == 0)
    def _():
        acc[...] = jnp.zeros_like(acc)

    @pl.when(step == 0)
    def _():
        for ref in (bias, grel, back, sums):
            ref[...] = jnp.zeros_like(ref)

    fire(0)

    @pl.when(live)
    def _():
        _, valid = positions(0, col0, high, wide)
        da_win = jnp.where(valid, da[place, :].astype(single), 0.0).astype(narrow)
        acc[3] += dot_tn(mixed[0], da_win)
        dmix[...] = dot_nt(da_win, weights[far, 3]).astype(narrow)

    def one_pair(pair):
        low_lane = lax.broadcasted_iota(jnp.int32, (ROWS, LANES), 1) < 64
        cut = slice(pair * LANES, (pair + 1) * LANES)
        q, k8, v, rel = (qkv[0, j, :, cut] for j in range(4))
        do = dmix[:, cut]
        dqs, dks, dvs = [], [], []
        for head in range(2):
            mine, other = sides[head : head + 1], sides[1 - head : 2 - head]
            full_key = k8 * mine + keys[...] * other
            scores = dot_nt(full_key, q * mine + rel * other)
            top = jnp.max(scores, axis=0, keepdims=True)
            probs = jnp.exp(scores - top)
            probs = probs * (1.0 / jnp.sum(probs, axis=0, keepdims=True))
            dprobs = dot_nt(v, do * mine)
            mean = jnp.sum(probs * dprobs, axis=0, keepdims=True)
            dscores = (probs * (dprobs - mean)).astype(narrow)
            dvs.append(dot(probs.astype(narrow), do))
            dks.append(dot(dscores, q))
            dqs.append(dot_tn(dscores, full_key))
        dv = jnp.where(low_lane, dvs[0], dvs[1])
        dk = jnp.where(low_lane, dks[0], dks[1]) * 0.125
        dq = jnp.where(low_lane, dqs[0], dqs[1])
        drel = jnp.where(low_lane, dqs[1], dqs[0]) * lanes[0:1]
        drel = shift_right(drel, bits).astype(narrow)
        dq = dq + dot_nt(drel, wrel[...])
        grel[...] += dot_tn(drel, q)
        dqkv[0, :, cut] = dq.astype(narrow)
        dqkv[1, :, cut] = dk.astype(narrow)
        dqkv[2, :, cut] = dv.astype(narrow)

    for pair in range(half // LANES):
        fire(pair + 1)
        pl.when(live)(functools.partial(one_pair, pair))

    @pl.when(live)
    def _():
        total = None
        for j in range(3):
            piece = dqkv[j]
            acc[j] += dot_tn(piece, n1[0])
            bias[far, j : j + 1, :] += jnp.sum(piece.astype(single), axis=0, keepdims=True)
            back_part = dot(piece, weights[far, j])
            total = back_part if total is None else total + back_part

        @pl.when(far == 1)
        def _():
            dn1[slot] = total

        @pl.when(far == 0)
        def _():
            _, valid = positions(0, col0, high, wide)
            grad = jnp.where(valid, total + dn1[slot], 0.0)
            normal, inverse = norm_parts(xs[place, :].astype(single))
            sums[0:1, :] += jnp.sum(grad * normal, axis=0, keepdims=True)
            sums[1:2, :] += jnp.sum(grad, axis=0, keepdims=True)
            result = dx1[place, :] + norm_back(grad, normal, inverse, gain[...])
            back[place, :] = jnp.where(valid, result, 0.0).astype(narrow)

    def flush(keep, give):
        part = half // 2
        for j in range(4):
            keep[j * part : (j + 1) * part, :] = acc[j, :part, :].astype(narrow)
            give[j * part : (j + 1) * part, :] = acc[j, part:, :].astype(narrow)

    @pl.when(step == SLOTS - 1)
    def _():
        flush(keep_far, give_far)

    @pl.when(step == 2 * SLOTS - 1)
    def _():
        flush(keep, give)
        sum2.back(0, summed2).wait()
        far_cross.wait()


def backward(rows_held, images, da, n1, qkv, mixed, weights, wrel, tables, residents, rest):
    half, width = weights.shape[2:]
    operands = [da, n1, qkv, mixed, weights, wrel, *tables, *residents, rest]
    in_specs = [whole(a.shape) for a in operands]
    in_specs[1] = pl.BlockSpec((1, ROWS, width), lambda i: (i % SLOTS, 0, 0))

    def halved(i):
        return (1 - i // SLOTS) * SLOTS + i % SLOTS

    in_specs[2] = pl.BlockSpec((1, 4, ROWS, half), lambda i: (halved(i), 0, 0, 0))
    in_specs[3] = pl.BlockSpec((1, ROWS, half), lambda i: (halved(i), 0, 0))
    in_specs[-1] = ANY
    packed = (2 * half, width)
    square = residents[3].shape
    outs = [
        (of((SLAB, width)), whole((SLAB, width))),
        (of((8, width), single), whole((8, width))),
        (of(packed), whole(packed)),
        (of(packed), whole(packed)),
        (of((2, 8, half), single), whole((2, 8, half))),
        (of((LANES, LANES), single), whole((LANES, LANES))),
        (of(packed), ANY),
        (of(square), ANY),
        (of(square), ANY),
    ]
    landing = (Halver.landing_rows(images, square[0]), width)
    copies = 3 + 2 * Halver.copies(images)
    return pl.pallas_call(
        functools.partial(backward_kernel, rows_held, images),
        out_shape=[o[0] for o in outs],
        grid=(2 * SLOTS,),
        in_specs=in_specs,
        out_specs=[o[1] for o in outs],
        scratch_shapes=[
            pltpu.VMEM((4, half, width), single),
            pltpu.VMEM((3, ROWS, half), narrow),
            pltpu.VMEM((ROWS, half), narrow),
            pltpu.VMEM((SLOTS, ROWS, width), single),
            *[pltpu.VMEM(packed, narrow)] * 3,
            *[pltpu.VMEM(square, narrow)] * 2,
            *[pltpu.VMEM(landing, narrow)] * 2,
            pltpu.VMEM(rest.shape, narrow),
            pltpu.SemaphoreType.DMA((copies,)),
            pltpu.SemaphoreType.DMA((copies,)),
            pltpu.SemaphoreType.DMA((2,)),
        ],
        compiler_params=pltpu.CompilerParams(
            vmem_limit_bytes=VMEM, collective_id=2, has_side_effects=True
        ),
        cost_estimate=pl.CostEstimate(
            flops=52_000_000_000, bytes_accessed=80_000_000, transcendentals=8_000_000
        ),
        name="attention_backward",
    )(*operands)


def clear_rows(ext):
    @pl.loop(0, ext.shape[0] // GRID)
    def _(r):
        ext[rows_at(r * GRID, GRID), :] = jnp.zeros((GRID, ext.shape[1]), narrow)


def place_windows(rows_held, device, slab, ext, first, last):
    @pl.loop(first, last)
    def _(slot):
        row0, col0, high, wide, offset, live = window_fields(rows_held, device, slot)

        @pl.when(live)
        def _():
            target, _ = positions(1, col0, high, wide)
            token = lax.broadcasted_iota(jnp.int32, (WIN * GRID, ROWS), 0)
            choose = jnp.where(token == target, 1.0, 0.0).astype(narrow)
            window = slab[rows_at(offset, ROWS), :]
            where_to = pl.ds(pl.multiple_of(row0 * GRID, GRID), WIN * GRID)
            ext[where_to, :] += dot(choose, window).astype(narrow)


def tail_kernel(
    rows_held, images,
    out, back, keep, crossed, sums1, sums2, bias, rel_sum, fc_bias, peak, give,
    output, input_grad, packed, totals, tops,
    ext0, ext1, below0, below1, above0, above1, got, landing, held, sum_land, top_land, sends, recvs,
):
    device, image = lax.axis_index("tensor"), lax.axis_index("dp")
    beside, across, corner = partners(device)
    send = Sender(sends, recvs, None)
    per = Halver.copies(images)
    middle = held.shape[0] // 2
    landing_rows = Halver.landing_rows(images, middle)
    landings = [landing.at[pl.ds(k * landing_rows, landing_rows), :] for k in range(2)]
    halvers = [
        Halver(send, 1 + k * per, image, images, k * middle, middle, order)
        for k, order in enumerate(((0, 1, 2), (1, 0, 2)))
    ]
    halo_base = 1 + 2 * per
    small_base = halo_base + 4
    tokens = rows_held * GRID
    top, bottom = LEFT * GRID, RIGHT * GRID
    held_by = (device, beside, across, corner)
    mates = dp_mates(image, images)
    ring = [{"tensor": beside}, {"tensor": across}] + mates

    def reduce_start(stage):
        for halver, land in zip(halvers, landings, strict=True):
            halver.start(stage, held, land)

    def reduce_finish(stage):
        for halver, land in zip(halvers, landings, strict=True):
            halver.finish(stage, held, land)

    def hand_start(stage):
        for halver in halvers:
            halver.back(stage, packed).start()

    def hand_finish(stage):
        for halver in halvers:
            halver.back(stage, packed).wait()

    greet([{"tensor": place} for place in (beside, across, corner)] + mates)
    swap = send.remote(0, give, got, {"tensor": beside})
    swap.start()

    totals[...] = jnp.zeros_like(totals)
    tops[...] = jnp.zeros_like(tops)
    totals[0:2, :] = sums1[0:2, :]
    totals[2:6, :] = sums2[0:4, :]
    rel = rel_sum[...]
    rel = rel[HD:] + pltpu.roll(rel[:HD], HD, 1)
    for g in range(HD // 8):
        at = 8 * (1 + g // 6)
        totals[at : at + 8, (g % 6) * LANES : (g % 6 + 1) * LANES] = rel[8 * g : 8 * g + 8]
    half = bias.shape[2]
    for k in range(SPLIT):
        far, odd = k // 2, k % 2
        totals[pl.ds(24 + held_by[k], 1), :] = fc_bias[k, 0:1, :]
        for j, row in enumerate((0, 2)):
            value = bias[far, row : row + 1, :]
            if odd:
                value = pltpu.roll(value, half // 2, 1)
            totals[pl.ds(28 + held_by[k], 1), j * half : (j + 1) * half] = value
        best = jnp.broadcast_to(jnp.max(peak[far], axis=1, keepdims=True), (8, LANES))
        if odd:
            best = pltpu.roll(best, 8 - half // LANES, 0)
        tops[pl.ds(pl.multiple_of(held_by[k] * 8, 8), 8), :] = best

    def small_copies(k):
        return [
            send.remote(small_base + 2 * k, totals, sum_land.at[k], ring[k]),
            send.remote(small_base + 2 * k + 1, tops, top_land.at[k], ring[k]),
        ]

    def small_start(k):
        for copy in small_copies(k):
            copy.start()

    def small_finish(k):
        for copy in small_copies(k):
            copy.wait()
        totals[...] += sum_land[k]
        tops[...] = jnp.maximum(tops[...], top_land[k])

    def halo(base, ext, below, above):
        up = send.remote(
            base, ext.at[pl.ds(0, top), :], below, {"tensor": (device + SPLIT - 1) % SPLIT}
        )
        down = send.remote(
            base + 1, ext.at[pl.ds(top + tokens, bottom), :], above, {"tensor": (device + 1) % SPLIT}
        )
        return up, down

    def halo_start(copies):
        up, down = copies
        pl.when(device > 0)(up.start)
        pl.when(device < SPLIT - 1)(down.start)

    def halo_finish(copies, ext, below, above, result):
        up, down = copies
        pl.when(device > 0)(up.wait_send)
        pl.when(device < SPLIT - 1)(down.wait_send)
        add_rows(result, 0, [(ext, top)], tokens)

        @pl.when(device < SPLIT - 1)
        def _():
            up.wait_recv()
            at = tokens - top
            add_rows(result, at, [(result, at), (below, 0)], top)

        @pl.when(device > 0)
        def _():
            down.wait_recv()
            add_rows(result, 0, [(result, 0), (above, 0)], bottom)

    small_start(0)
    clear_rows(ext0)
    clear_rows(ext1)
    swap.wait()
    add_rows(held, 0, [(keep, 0), (got, 0), (crossed, 0)], held.shape[0])
    reduce_start(0)
    small_finish(0)
    small_start(1)
    place_windows(rows_held, device, back, ext1, 0, SLOTS)
    halos1 = halo(halo_base, ext1, below1, above1)
    halo_start(halos1)
    small_finish(1)
    small_start(2)
    reduce_finish(0)
    reduce_start(1)
    place_windows(rows_held, device, out, ext0, 0, 3)
    small_finish(2)
    small_start(3)
    reduce_finish(1)
    reduce_start(2)
    place_windows(rows_held, device, out, ext0, 3, SLOTS)
    halos0 = halo(halo_base + 2, ext0, below0, above0)
    halo_start(halos0)
    small_finish(3)
    small_start(4)
    reduce_finish(2)
    for halver, land in zip(halvers, landings, strict=True):
        halver.extras(held, land)
        start, length = halver.final
        packed[rows_at(start, length), :] = held[rows_at(start, length), :]
    hand_start(2)
    for k in range(4, len(ring)):
        small_finish(k)
        if k + 1 < len(ring):
            small_start(k + 1)
    halo_finish(halos1, ext1, below1, above1, input_grad)
    hand_finish(2)
    hand_start(1)
    hand_finish(1)
    hand_start(0)
    halo_finish(halos0, ext0, below0, above0, output)
    hand_finish(0)


def tail(rows_held, images, *operands):
    width = operands[0].shape[1]
    packed = operands[2].shape
    tokens = rows_held * GRID
    bits = images.bit_length() - 1
    landing = 2 * Halver.landing_rows(images, packed[0] // 2)
    copies = 1 + 2 * Halver.copies(images) + 4 + 2 * (2 + bits)
    ext = ((rows_held + LEFT + RIGHT) * GRID, width)
    outs = [
        of((tokens, width)), of((tokens, width)), of(packed),
        of((32, width), single), of((32, LANES), single),
    ]
    return pl.pallas_call(
        functools.partial(tail_kernel, rows_held, images),
        out_shape=outs,
        in_specs=[pl.BlockSpec(memory_space=pltpu.VMEM)] * (len(operands) - 1) + [ANY],
        out_specs=[pl.BlockSpec(memory_space=pltpu.VMEM)] * len(outs),
        scratch_shapes=[
            pltpu.VMEM(ext, narrow),
            pltpu.VMEM(ext, narrow),
            pltpu.VMEM((LEFT * GRID, width), narrow),
            pltpu.VMEM((LEFT * GRID, width), narrow),
            pltpu.VMEM((RIGHT * GRID, width), narrow),
            pltpu.VMEM((RIGHT * GRID, width), narrow),
            pltpu.VMEM(packed, narrow),
            pltpu.VMEM((landing, width), narrow),
            pltpu.VMEM(packed, narrow),
            pltpu.VMEM((2 + bits, 32, width), single),
            pltpu.VMEM((2 + bits, 32, LANES), single),
            pltpu.SemaphoreType.DMA((copies,)),
            pltpu.SemaphoreType.DMA((copies,)),
        ],
        compiler_params=pltpu.CompilerParams(
            vmem_limit_bytes=VMEM, collective_id=3, has_side_effects=True
        ),
        cost_estimate=pl.CostEstimate(
            flops=4_000_000_000, bytes_accessed=20_000_000, transcendentals=0
        ),
        name="tail",
    )(*operands)


def shards(
    inputs,
    w_qkv,
    qv_bias,
    w_proj,
    proj_bias,
    w_fc1,
    fc1_bias,
    w_fc2,
    fc2_bias,
    norm1_gain,
    norm1_shift,
    norm2_gain,
    norm2_shift,
    rel_h,
    rel_w,
    cotangent,
):
    width = inputs.shape[2]
    rows = inputs.shape[1] // GRID
    local = w_qkv.shape[2]
    heads = local // HD
    device = lax.axis_index("tensor")
    tables = lane_tables()

    block = jnp.zeros((2, 32, HD), narrow)
    block = block.at[0, : 2 * WIN - 1].set(rel_h[::-1]).at[1, : 2 * WIN - 1].set(rel_w[::-1])
    block = block.reshape(HD, HD).T
    wrel = jnp.zeros((LANES, LANES), narrow).at[:HD, HD:].set(block).at[HD:, :HD].set(block)

    pack = jnp.concatenate([w_qkv.transpose(0, 2, 1), w_proj[None]])
    small = jnp.zeros((8, fc1_bias.shape[0]), single).at[0].set(fc1_bias)
    for j in range(2):
        small = small.at[1 + 2 * j, :local].set(qv_bias[j])
        small = small.at[2 + 2 * j, local : 2 * local].set(qv_bias[j])
    norm1 = (norm1_gain[None], norm1_shift[None])

    (
        xs, gs, n1, qkv, mixed, attn, peak,
        weights, across1, across2, beside1, beside2, smalls,
    ) = forward(inputs[0], cotangent[0], pack, w_fc1, w_fc2, small, norm1, wrel, tables)
    out, dx1, da, sums2, near1, near2, far1, far2, rest, fc_bias = mlp(
        (
            xs, attn, gs, proj_bias[None], norm2_gain[None], norm2_shift[None], fc2_bias[None],
            smalls,
        ),
        (across1, across2),
        (beside1, beside2),
        (w_fc1, w_fc2),
    )
    images = lax.axis_size("dp")
    back, sums1, keep, give, bias, rel_sum, crossed, summed1, summed2 = backward(
        rows, images, da, n1, qkv, mixed, weights, wrel, tables,
        [xs, dx1, norm1_gain[None], near1, near2, far1, far2], rest,
    )
    output, input_grad, gpack, totals, tops = tail(
        rows, images, out, back, keep, crossed, sums1, sums2, bias, rel_sum, fc_bias, peak, give
    )

    gpack = gpack.astype(single)
    blocks = totals[8:24].reshape(2, 8, 6, LANES).transpose(0, 2, 1, 3).reshape(-1, LANES)[:HD, :HD]
    grad_rel = jnp.stack([blocks[: 2 * WIN - 1][::-1], blocks[32 : 32 + 2 * WIN - 1][::-1]])
    qv = lax.dynamic_slice_in_dim(totals, 28 + device, 1)[0].reshape(2, 2 * local)[:, :local]
    head_max = lax.dynamic_slice(tops, (8 * device, 0), (heads, 1))[:, 0]
    factor = jnp.sqrt(CLIP / jnp.maximum(head_max, CLIP))
    clipped_qk = (w_qkv[:2].astype(single) * jnp.repeat(factor, HD)).astype(narrow)

    return (
        output[None],
        input_grad[None],
        gpack[: 3 * local].reshape(3, local, width).transpose(0, 2, 1),
        qv,
        gpack[3 * local :],
        totals[4],
        summed1.astype(single),
        lax.dynamic_slice_in_dim(totals, 24 + device, 1)[0],
        summed2.T.astype(single),
        totals[5],
        totals[:4],
        grad_rel,
        clipped_qk,
        head_max,
    )


def solution(mesh):
    return jax.shard_map(
        shards,
        mesh=mesh,
        in_specs=(
            P("dp", "tensor", None),
            P(None, None, "tensor"),
            P(None, "tensor"),
            P("tensor", None),
            P(),
            P(None, "tensor"),
            P("tensor"),
            P("tensor", None),
            P(),
            P(),
            P(),
            P(),
            P(),
            P(),
            P(),
            P("dp", "tensor", None),
        ),
        out_specs=(
            P("dp", "tensor", None),
            P("dp", "tensor", None),
            P(None, None, "tensor"),
            P(None, "tensor"),
            P("tensor", None),
            P(),
            P(None, "tensor"),
            P("tensor"),
            P("tensor", None),
            P(),
            P(),
            P(),
            P(None, None, "tensor"),
            P("tensor"),
        ),
        check_vma=False,
    )
```

```python
import functools

import jax
import jax.numpy as jnp
import numpy as np
from jax import lax
from jax.experimental import pallas as pl
from jax.experimental.pallas import tpu as pltpu
from jax.sharding import PartitionSpec as P

HD = 64
GRID = 64
WIN = 14
TILES = 5
SPAN = WIN * WIN
ROWS = 208
SLOTS = 7
EDGE = GRID % WIN
SHORT = EDGE * WIN
SLAB = (SLOTS - 2) * ROWS + SHORT
STRIP = SLAB // 6
SPLIT = 4
LEFT = 6
RIGHT = 12
LANES = 128
EPS = 1e-6
CLIP = 3.0
VMEM = 60 * 1024 * 1024

single = jnp.float32
narrow = jnp.bfloat16

def lane_tables():
    row = np.arange(ROWS)
    late = np.maximum(row - SHORT, 0)
    outer = WIN - EDGE
    orders = (
        (row // WIN, row % WIN),
        (
            np.where(row < SHORT, row // EDGE, late // outer),
            np.where(row < SHORT, row % EDGE, EDGE + late % outer),
        ),
    )
    lane = np.arange(LANES) % 64
    part = lane // 32
    at = lane % 32
    bits, keys = [], []
    for x, y in orders:
        amount = np.where(part[None, :] == 0, x[:, None], y[:, None])
        amount = np.where((row < SPAN)[:, None], amount, 0)
        bits.append(np.stack([(amount >> b) & 1 for b in range(4)]).astype(np.float32))
        place = WIN - 1 - np.where(part[None, :] == 0, x[:, None], y[:, None])
        hot = ((at % 16)[None, :] == place) & ((at % 16) < WIN)[None, :] & (row < SPAN)[:, None]
        hot = hot.astype(np.float32)
        hot[SPAN:, lane == 31] = -1e30
        keys.append(hot)
    lanes = np.zeros((8, LANES), np.float32)
    lanes[0] = at < WIN
    lanes[1] = (at >= 16) & (at < 16 + WIN)
    lanes[2] = lane == 31
    sides = np.zeros((16, LANES), np.float32)
    sides[0] = np.arange(LANES) < 64
    sides[1] = np.arange(LANES) >= 64
    return (
        jnp.asarray(np.stack(bits)),
        jnp.asarray(lanes),
        jnp.asarray(sides, narrow),
        jnp.asarray(np.stack(keys), narrow),
    )


def dot(a, b):
    return jnp.dot(a, b, preferred_element_type=single)


def dot_nt(a, b):
    return lax.dot_general(a, b, (((1,), (1,)), ((), ())), preferred_element_type=single)


def dot_tn(a, b):
    return lax.dot_general(a, b, (((0,), (0,)), ((), ())), preferred_element_type=single)


def norm_parts(values):
    centre = values - jnp.mean(values, axis=-1, keepdims=True)
    inverse = lax.rsqrt(jnp.mean(centre * centre, axis=-1, keepdims=True) + EPS)
    return centre * inverse, inverse


def norm_back(grad, normal, inverse, gain):
    scaled = grad * gain
    first = jnp.mean(scaled, axis=-1, keepdims=True)
    second = jnp.mean(scaled * normal, axis=-1, keepdims=True)
    return inverse * (scaled - first - normal * second)


def slot_fields(rows_held):
    return window_fields(rows_held, lax.axis_index("tensor"), pl.program_id(0) % SLOTS)


def window_fields(rows_held, device, slot):
    first = device * (SLOTS - 1)
    window = first + slot
    i, j = window // TILES, window % TILES
    last = device // (SPLIT - 1)
    live = slot < SLOTS - 1 + last
    row0 = i * WIN - device * rows_held + LEFT
    high = jnp.minimum(WIN, GRID - i * WIN)
    wide = jnp.minimum(WIN, GRID - j * WIN)

    def short_before(n):
        return jnp.minimum(n // TILES, TILES - 1) + jnp.maximum(n - TILES * (TILES - 1), 0)

    offset = ROWS * slot - (ROWS - SHORT) * (short_before(window) - short_before(first))
    return row0, j * WIN, j // (TILES - 1), high * wide, offset, live


def positions(axis, count, first_col, kind, inside):
    shape = (count, 1) if axis == 0 else (1, count)
    row = lax.broadcasted_iota(jnp.int32, shape, axis)
    x = lax.shift_right_logical(row * 4682, 16)
    plain = x * GRID + (row - x * WIN)
    x = lax.shift_right_logical(row, EDGE.bit_length() - 1)
    edge = x * GRID + (row - x * EDGE)
    token = jnp.where(kind == 1, edge, plain) + first_col
    return jnp.where(row < inside, token, -1), row < inside


def gather_window(source, target):
    token = lax.broadcasted_iota(jnp.int32, (target.shape[0], WIN * GRID), 1)
    choose = jnp.where(token == target, 1.0, 0.0).astype(narrow)
    return dot(choose, source)


def shift_left(values, bits):
    for b in range(4):
        taken = bits[b, : values.shape[0]] > 0.5
        values = jnp.where(taken, pltpu.roll(values, LANES - (1 << b), 1), values)
    return values


def shift_right(values, bits):
    for b in range(4):
        taken = bits[b, : values.shape[0]] > 0.5
        values = jnp.where(taken, pltpu.roll(values, 1 << b, 1), values)
    return values


def partners(device):
    beside = device + 1 - 2 * (device % 2)
    across = (device + 2) % SPLIT
    corner = (beside + 2) % SPLIT
    return beside, across, corner


def greet(places):
    barrier = pltpu.get_barrier_semaphore()
    for place in places:
        pl.semaphore_signal(barrier, inc=1, device_id=place, device_id_type=pl.DeviceIdType.MESH)
    pl.semaphore_wait(barrier, len(places))


class Sender:
    def __init__(self, sends, recvs, locals_):
        self.sends, self.recvs, self.locals = sends, recvs, locals_

    def remote(self, at, source, target, place):
        return pltpu.make_async_remote_copy(
            src_ref=source,
            dst_ref=target,
            send_sem=self.sends.at[at],
            recv_sem=self.recvs.at[at],
            device_id=place,
            device_id_type=pl.DeviceIdType.MESH,
        )

    def local(self, at, source, target):
        return pltpu.make_async_copy(source, target, self.locals.at[at])


def mate_of(image, bit):
    unit = 1 << bit
    return image + unit * (1 - 2 * ((image // unit) % 2))


def rows_at(start, count):
    return pl.ds(pl.multiple_of(start, 16), count)


def add_rows(target, target_at, sources, count):
    chunk = next(c for c in (96, 48, 16) if count % c == 0)

    @pl.loop(0, count // chunk)
    def _(c):
        total = None
        for ref, at in sources:
            value = ref[rows_at(at + c * chunk, chunk), :]
            total = value if total is None else total + value
        target[rows_at(target_at + c * chunk, chunk), :] = total


HALVINGS = 3


class Halver:
    def __init__(self, send, base, image, images, start, rows, order):
        bits = images.bit_length() - 1
        assert images == 1 << bits and bits >= HALVINGS
        self.send, self.base, self.image = send, base, image
        self.extra_bits = range(HALVINGS, bits)
        self.stages = []
        landing, length = 0, rows
        for bit in order:
            length //= 2
            mine = (image // (1 << bit)) % 2
            keep, give = start + mine * length, start + (1 - mine) * length
            self.stages.append((mate_of(image, bit), keep, give, length, landing))
            landing += length
            start = keep
        self.final = (start, length)
        self.landing = landing

    @staticmethod
    def copies(images):
        return 2 * HALVINGS + images.bit_length() - 1 - HALVINGS

    @staticmethod
    def landing_rows(images, rows):
        last = rows >> HALVINGS
        return rows - last + last * (images.bit_length() - 1 - HALVINGS)

    def out(self, stage, held, landing):
        mate, _, give, length, at = self.stages[stage]
        return self.send.remote(
            self.base + stage,
            held.at[rows_at(give, length), :],
            landing.at[pl.ds(at, length), :],
            {"dp": mate},
        )

    def start(self, stage, held, landing):
        self.out(stage, held, landing).start()

    def finish(self, stage, held, landing):
        self.out(stage, held, landing).wait()
        _, keep, _, length, at = self.stages[stage]
        add_rows(held, keep, [(held, keep), (landing, at)], length)

    def extras(self, held, landing):
        start, length = self.final
        for k, bit in enumerate(self.extra_bits):
            at = self.landing + k * length
            copy = self.send.remote(
                self.base + HALVINGS + k,
                held.at[rows_at(start, length), :],
                landing.at[pl.ds(at, length), :],
                {"dp": mate_of(self.image, bit)},
            )
            copy.start()
            copy.wait()
            add_rows(held, start, [(held, start), (landing, at)], length)

    def back(self, stage, held):
        mate, keep, _, length, _ = self.stages[stage]
        cut = rows_at(keep, length)
        at = self.base + HALVINGS + len(self.extra_bits) + stage
        return self.send.remote(at, held.at[cut, :], held.at[cut, :], {"dp": mate})


def dp_mates(image, images):
    return [{"dp": mate_of(image, bit)} for bit in range(images.bit_length() - 1)]


def attend(n1, valid, weights, qbias, vbias, wrel, bits, lanes, sides, keys, qkv, mixed, peak):
    half = weights.shape[1]
    count = n1.shape[0]
    query = jnp.where(valid, dot_nt(n1, weights[0]) + qbias, 0.0).astype(narrow)
    key8 = dot_nt(n1, weights[1]).astype(narrow) * jnp.asarray(0.125, narrow)
    value = (dot_nt(n1, weights[2]) + vbias).astype(narrow)
    qkv[0, 0, :count] = query
    qkv[0, 1, :count] = key8
    qkv[0, 2, :count] = value
    if count < ROWS:
        left = ROWS - count
        qkv[0, 1, count:] = jnp.zeros((left, half), narrow)
        qkv[0, 2, count:] = jnp.broadcast_to(vbias, (left, half)).astype(narrow)
    low_lane = lax.broadcasted_iota(jnp.int32, (count, LANES), 1) < 64
    for pair in range(half // LANES):
        cut = slice(pair * LANES, (pair + 1) * LANES)
        q = query[:, cut]
        k8, v = qkv[0, 1, :, cut], qkv[0, 2, :, cut]
        rel = shift_left(dot_nt(q, wrel[...]), bits)
        rest = rel - rel.astype(narrow).astype(single)
        rel = rel * lanes[0:1] + pltpu.roll(rest, 16, 1) * lanes[1:2] + lanes[2:3]
        rel = rel.astype(narrow)
        qkv[0, 3, :count, cut] = rel
        pieces = []
        for head in range(2):
            mine, other = sides[head : head + 1], sides[1 - head : 2 - head]
            only = q * mine
            logits = dot_nt(only, k8)
            at = 2 * pair + head
            peak[at : at + 1, :] = jnp.maximum(
                peak[at : at + 1, :], jnp.max(logits, axis=0, keepdims=True)
            )
            scores = dot_nt(only + rel * other, k8 * mine + keys[...] * other)
            top = jnp.max(scores, axis=1, keepdims=True)
            probs = jnp.exp(scores - top)
            total = jnp.sum(probs, axis=1, keepdims=True)
            pieces.append(dot(probs.astype(narrow), v) * (1.0 / total))
        mixed[0, :count, cut] = jnp.where(low_lane, pieces[0], pieces[1]).astype(narrow)
    return dot(mixed[0, :count], weights[3])


class Halo:
    def __init__(self, send, base, grid, ext, device, rows):
        below, above = {"tensor": (device + 1) % SPLIT}, {"tensor": (device + SPLIT - 1) % SPLIT}
        self.has_below, self.has_above = device < SPLIT - 1, device > 0
        self.cross_below, self.cross_above = device == 1, device == 2

        def copy(at, first, count, first_col, cols, target_row, place):
            window = (pl.ds(first, count), pl.ds(first_col, cols), slice(None))
            return send.remote(
                at, grid.at[window], ext.at[(pl.ds(target_row, count), *window[1:])], place
            )

        few, many = 4, 10
        self.down = copy(base, rows - LEFT, LEFT, 0, GRID, 0, below)
        self.down_cross = copy(base, rows - few, few, 16, GRID - 16, LEFT - few, below)
        self.up = copy(base + 1, 0, RIGHT, 0, GRID, LEFT + rows, above)
        self.up_cross = copy(base + 1, 0, many, 0, 32, LEFT + rows, above)

    def _each(self, down_here, up_here, act):
        for here, crossing, plain, crossed in (
            (*down_here, self.down, self.down_cross),
            (*up_here, self.up, self.up_cross),
        ):

            @pl.when(here & jnp.logical_not(crossing))
            def _():
                act(plain)

            @pl.when(crossing)
            def _():
                act(crossed)

    def _senders(self, act):
        self._each((self.has_below, self.cross_below), (self.has_above, self.cross_above), act)

    def start(self):
        self._senders(lambda copy: copy.start())

    def wait_send(self):
        self._senders(lambda copy: copy.wait_send())

    def wait_from_above(self):
        pl.when(self.has_above & jnp.logical_not(self.cross_above))(self.down.wait_recv)
        pl.when(self.cross_above)(self.down_cross.wait_recv)

    def wait_from_below(self):
        pl.when(self.has_below & jnp.logical_not(self.cross_below))(self.up.wait_recv)
        pl.when(self.cross_below)(self.up_cross.wait_recv)


class Quartet:
    def __init__(self, send, base, image, pieces, across):
        side, deep = image % 2, (image // 2) % 2
        beside, behind = {"dp": mate_of(image, 0)}, {"dp": mate_of(image, 1)}
        mine = 2 * deep + side
        from_beside, from_behind = 2 * deep + 1 - side, 2 * (1 - deep) + side
        self.first, self.second, self.third = [], [], []
        for k, (source, target, view) in enumerate(pieces):
            at = base + 5 * k

            def copy(number, origin, quarter, part, place):
                return send.remote(at + number, view(origin, quarter, part), view(target, quarter, part), place)

            self.first.append(copy(0, source, mine, None, across))
            self.second.append(copy(1, target, mine, None, beside))
            self.second.append(copy(2, target, mine, None, behind))
            if view(target, from_behind, 0) is not None:
                self.third.append(copy(3, target, from_behind, 0, beside))
            self.third.append(copy(4, target, from_beside, 1, behind))


def quarter_rows(array, quarter, part):
    size = array.shape[0] // 4
    start = quarter * size
    if part is not None:
        size //= 2
        start += part * size
    return array.at[rows_at(start, size), :]


def start_all(copies):
    for copy in copies:
        copy.start()


def receive_all(copies):
    for copy in copies:
        copy.wait_recv()


def forward_kernel(
    x, g, wqkv, wproj, fc1, fc2, notes_in, params, wrel, bits, lanes, sides, keys,
    xs, gs, n1_all, qkv, mixed, attn, peak, weights_out, across1, across2, beside1, beside2, small_out,
    xext, gext, weights, smalls, sends, recvs, locals_,
):
    step = pl.program_id(0)
    far, slot = step // SLOTS, step % SLOTS
    device, image = lax.axis_index("tensor"), lax.axis_index("dp")
    rows, _, width = x.shape
    part = wproj.shape[0]
    half = 2 * part
    beside, across, corner = partners(device)
    send = Sender(sends, recvs, locals_)
    x_halo = Halo(send, 0, x, xext, device, rows)
    g_halo = Halo(send, 2, g, gext, device, rows)
    small = notes_in.at[pl.ds(0, 8), :]

    own_pack = [
        send.remote(4, wqkv, weights.at[0, 0:3, pl.ds(part, part), :], {"tensor": beside}),
        send.remote(5, wproj, weights.at[0, 3, pl.ds(part, part), :], {"tensor": beside}),
    ]
    notes = [
        send.remote(6 + k, small, smalls.at[k + 1], {"tensor": place})
        for k, place in enumerate((beside, across, corner))
    ]
    fc_beside = [
        send.remote(9, fc1, beside1, {"tensor": beside}),
        send.remote(10, fc2, beside2, {"tensor": beside}),
    ]
    corner_pack = send.remote(
        11, weights.at[1, :, pl.ds(0, part), :], weights.at[1, :, pl.ds(part, part), :], {"tensor": beside}
    )

    def of_qkv(array, quarter, half_of):
        size = part // 4
        cut = rows_at(quarter * size, size)
        if array is wqkv:
            return array.at[:, cut, :]
        if half_of is None:
            return array.at[1, 0:3, cut, :]
        return array.at[1, 0:2, cut, :] if half_of == 0 else array.at[1, 2:3, cut, :]

    def of_proj(array, quarter, half_of):
        size = part // 4
        cut = rows_at(quarter * size, size)
        if array is wproj:
            return array.at[cut, :]
        return None if half_of == 0 else array.at[1, 3, cut, :]

    pack_far = Quartet(
        send, 12, image, ((wqkv, weights, of_qkv), (wproj, weights, of_proj)), {"tensor": across}
    )
    fc_far = Quartet(
        send, 22, image, ((fc1, across1, quarter_rows), (fc2, across2, quarter_rows)), {"tensor": across}
    )
    own = [
        send.local(0, wqkv, weights.at[0, 0:3, pl.ds(0, part), :]),
        send.local(1, wproj, weights.at[0, 3, pl.ds(0, part), :]),
        send.local(2, x, xext.at[pl.ds(LEFT, rows)]),
        send.local(3, small, smalls.at[0]),
    ]
    g_own = send.local(4, g, gext.at[pl.ds(LEFT, rows)])
    kept = [send.local(5, weights, weights_out), send.local(6, smalls, small_out)]

    @pl.when(step == 0)
    def _():
        for ref in (xext, gext):
            ref[pl.ds(0, LEFT)] = jnp.zeros((LEFT, GRID, width), narrow)
            ref[pl.ds(LEFT + rows, RIGHT)] = jnp.zeros((RIGHT, GRID, width), narrow)
        greet(
            [{"tensor": place} for place in (beside, across, corner)]
            + [{"dp": mate_of(image, bit)} for bit in range(2)]
        )
        start_all(own_pack + notes + own)
        x_halo.start()
        start_all(pack_far.first)
        for ref in (xs, gs, attn, peak):
            ref[...] = jnp.zeros_like(ref)
        for copy in own + notes + own_pack:
            copy.wait()
        x_halo.wait_from_above()

    @pl.when(step == 1)
    def _():
        start_all(fc_beside + [g_own])

    @pl.when(step == 2)
    def _():
        receive_all(pack_far.first)
        start_all(pack_far.second)
        start_all(fc_far.first)

    @pl.when(step == 3)
    def _():
        x_halo.wait_from_below()

    @pl.when(step == 4)
    def _():
        receive_all(pack_far.second)
        start_all(pack_far.third)

    @pl.when(step == 5)
    def _():
        receive_all(fc_far.first)
        start_all(fc_far.second)
        g_halo.start()

    @pl.when(step == 6)
    def _():
        receive_all(pack_far.third)
        corner_pack.start()

    @pl.when(step == SLOTS)
    def _():
        corner_pack.wait_recv()
        start_all(kept)

    @pl.when(step == SLOTS + 2)
    def _():
        receive_all(fc_far.second)
        start_all(fc_far.third)

    row0, col0, kind, inside, offset, live = slot_fields(rows)
    whole_window = inside == SPAN
    tables = (wrel, bits.at[kind], lanes, sides, keys.at[kind])

    def work(count):
        place = rows_at(offset, count)

        @pl.when(far == 0)
        def _():
            target, valid = positions(0, count, col0, kind, inside)
            source = xext[pl.ds(row0, WIN)].reshape(WIN * GRID, width)
            window = gather_window(source, target)
            xs[place, :] = window.astype(narrow)
            normal, _ = norm_parts(window)
            n1 = jnp.where(valid, normal * params[8:9] + params[9:10], 0.0).astype(narrow)
            n1_all[slot, :count] = n1

        _, valid = positions(0, count, col0, kind, inside)
        qbias = smalls[2 * far, 1:2, :half] + smalls[2 * far + 1, 2:3, :half]
        vbias = smalls[2 * far, 3:4, :half] + smalls[2 * far + 1, 4:5, :half]
        terms = attend(
            n1_all[slot, :count], valid, weights.at[far], qbias, vbias, *tables,
            qkv, mixed, peak.at[far],
        )
        attn[place, :] += jnp.where(valid, terms, 0.0)

    pl.when(live & whole_window)(functools.partial(work, ROWS))
    pl.when(live & jnp.logical_not(whole_window))(functools.partial(work, SHORT))

    @pl.when(step == 2 * SLOTS - 1)
    def _():
        g_own.wait()
        g_halo.wait_from_above()
        g_halo.wait_from_below()

        @pl.loop(0, SLOTS)
        def _(slot):
            row0, col0, kind, inside, offset, live = window_fields(rows, device, slot)

            @pl.when(live)
            def _():
                target, _ = positions(0, ROWS, col0, kind, inside)
                source = gext[pl.ds(row0, WIN)].reshape(WIN * GRID, width)
                gs[rows_at(offset, ROWS), :] = gather_window(source, target).astype(narrow)

        for halo in (x_halo, g_halo):
            halo.wait_send()
        for group in (pack_far, fc_far):
            for copy in group.first + group.second:
                copy.wait_send()
        for copy in pack_far.third + [corner_pack]:
            copy.wait_send()
        for copy in kept + fc_beside + fc_far.third:
            copy.wait()


def whole(shape):
    zeros = (0,) * len(shape)
    return pl.BlockSpec(shape, lambda *_: zeros, pipeline_mode=pl.Buffered(1))


def by_slot(shape):
    rest = (0,) * len(shape)
    return pl.BlockSpec((1,) + tuple(shape), lambda s, *_: (s,) + rest)


ANY = pl.BlockSpec(memory_space=pl.ANY)


def of(shape, dtype=narrow):
    return jax.ShapeDtypeStruct(shape, dtype)


def forward(x, g, wqkv, wproj, fc1, fc2, params, wrel, tables):
    rows, _, width = x.shape
    half = 2 * wproj.shape[0]
    slab = (SLAB, width)
    outs = [
        (of(slab), whole(slab)),
        (of(slab), whole(slab)),
        (of((SLOTS, ROWS, width)), whole((SLOTS, ROWS, width))),
        (of((2 * SLOTS, 4, ROWS, half)), by_slot((4, ROWS, half))),
        (of((2 * SLOTS, ROWS, half)), by_slot((ROWS, half))),
        (of(slab, single), whole(slab)),
        (of((2, 8, ROWS), single), whole((2, 8, ROWS))),
        (of((2, 4, half, width)), ANY),
        (of(fc1.shape), ANY),
        (of(fc2.shape), ANY),
        (of(fc1.shape), ANY),
        (of(fc2.shape), ANY),
        (of((SPLIT, 8, width), single), ANY),
    ]
    operands = (x, g, wqkv, wproj, fc1, fc2, params, params, wrel, *tables)
    ext = (rows + LEFT + RIGHT, GRID, width)
    return pl.pallas_call(
        forward_kernel,
        out_shape=[o[0] for o in outs],
        grid=(2 * SLOTS,),
        in_specs=[ANY] * 7 + [whole(a.shape) for a in operands[7:]],
        out_specs=[o[1] for o in outs],
        scratch_shapes=[
            pltpu.VMEM(ext, narrow),
            pltpu.VMEM(ext, narrow),
            pltpu.VMEM((2, 4, half, width), narrow),
            pltpu.VMEM((SPLIT, 8, width), single),
            pltpu.SemaphoreType.DMA((32,)),
            pltpu.SemaphoreType.DMA((32,)),
            pltpu.SemaphoreType.DMA((7,)),
        ],
        compiler_params=pltpu.CompilerParams(
            vmem_limit_bytes=VMEM, collective_id=0, has_side_effects=True
        ),
        cost_estimate=pl.CostEstimate(
            flops=26_000_000_000, bytes_accessed=60_000_000, transcendentals=8_000_000
        ),
        name="attention_forward",
    )(*operands)


BLOCK = 256
CHUNK = SLAB // 3


def gelu_parts(z):
    size = jnp.abs(z)
    bell = jnp.exp(-0.5 * z * z)
    t = 1.0 / (1.0 + 0.2316418882663604 * size)
    poly = 0.5 * 1.061405429 * t + (0.5 * -1.453152027)
    poly = poly * t + 0.5 * 1.421413741
    poly = poly * t + 0.5 * -0.284496736
    poly = poly * t + 0.5 * 0.254829592
    tail = poly * t * bell
    phi_total = jnp.where(z >= 0, 1.0 - tail, tail)
    return z * phi_total, phi_total + z * bell * 0.3989422804014327


def mlp_kernel(
    xs, attn, gs, params, smalls, src1, src2,
    w1_across, w1_beside, w1_own, w2_across, w2_beside, w2_own,
    out, dx1, da, sums, near1, near2, far1, rest, gb,
    n2, n2t, gt, branch, dn2, corner1, corner2, keep1, keep2, give1, give2, got1, got2, near_got1,
    near_got2, landing, w1, w2, b1, hs, zs, sends, recvs,
):
    step = pl.program_id(0)
    count = pl.num_programs(0) // SPLIT
    group, index = step // count, step % count
    width = gs.shape[1]
    cut = pl.ds(pl.multiple_of(index * BLOCK, BLOCK), BLOCK)
    holder = jnp.where(group == 0, 2, jnp.where(group == 1, 3, jnp.where(group == 2, 1, 0)))
    beside, across, _ = partners(lax.axis_index("tensor"))
    send = Sender(sends, recvs, None)
    corners = [
        send.remote(0, src1, corner1, {"tensor": beside}),
        send.remote(1, src2, corner2, {"tensor": beside}),
    ]
    swaps = [
        send.remote(2, give1, got1, {"tensor": beside}),
        send.remote(3, give2, got2, {"tensor": beside}),
    ]
    crossing = send.remote(4, got1, far1, {"tensor": across})
    image = lax.axis_index("dp")
    mate = {"dp": mate_of(image, 0)}
    upper = got2.shape[0] // 2
    mine = (image % 2) * upper
    halving = send.remote(7, got2.at[rows_at(upper - mine, upper), :], landing, mate)
    near_swaps = [
        send.remote(5, corner1, near_got1, {"tensor": beside}),
        send.remote(6, corner2, near_got2, {"tensor": beside}),
    ]

    @pl.when(step == 0)
    def _():
        gb[...] = jnp.zeros_like(gb)
        greet([{"tensor": beside}, {"tensor": across}, mate])
        for copy in corners:
            copy.start()

        @pl.loop(0, SLAB // STRIP)
        def _(c):
            sl = rows_at(c * STRIP, STRIP)
            middle = xs[sl, :].astype(single) + (attn[sl, :] + params[10:11])
            dx1[sl, :] = middle
            normal, _ = norm_parts(middle)
            n2[sl, :] = (normal * params[11:12] + params[12:13]).astype(narrow)
            branch[sl, :] = jnp.zeros((STRIP, width), single)
            dn2[sl, :] = jnp.zeros((STRIP, width), single)

        for j in range(width // LANES):
            lanes = slice(j * LANES, (j + 1) * LANES)
            n2t[lanes, :] = n2[:, lanes].T
            gt[lanes, :] = gs[:, lanes].T

    @pl.when(step == count)
    def _():
        for copy in corners:
            copy.wait()

    @pl.when(step == 2 * count)
    def _():
        for copy in swaps:
            copy.start()

    for k, (first, second) in enumerate(
        ((w1_across, w2_across), (None, None), (w1_beside, w2_beside), (w1_own, w2_own))
    ):

        @pl.when(group == k)
        def _():
            if first is None:
                w1[...] = corner1[:, cut]
                w2[...] = corner2[cut, :]
            else:
                w1[...] = first[...]
                w2[...] = second[...]

    b1[...] = smalls[holder, 0:1, cut]

    @pl.loop(0, SLAB // CHUNK)
    def _(c):
        sl = rows_at(c * CHUNK, CHUNK)
        z = dot(n2[sl, :], w1[...]) + b1[0:1]
        dh = dot_nt(gs[sl, :], w2[...])
        act, slope = gelu_parts(z)
        h = act.astype(narrow)
        dz = (dh * slope).astype(narrow)
        hs[sl, :] = h
        zs[sl, :] = dz
        gb[holder, 0:1, cut] += jnp.sum(dz.astype(single), axis=0, keepdims=True)
        branch[sl, :] += dot(h, w2[...])
        dn2[sl, :] += dot_nt(dz, w1[...])

    @pl.when(step == 2 * count)
    def _():
        swaps[0].wait()
        add_rows(got1, 0, [(got1, 0), (keep1, 0)], got1.shape[0])
        crossing.start()
        swaps[1].wait()
        add_rows(got2, 0, [(got2, 0), (keep2, 0)], got2.shape[0])
        halving.start()

    for k, (first, second) in enumerate(
        ((keep1, keep2), (give1, give2), (corner1, corner2), (near1, near2))
    ):

        @pl.when(group == k)
        def _():
            @pl.loop(0, width // 256)
            def _(r):
                sl = rows_at(r * 256, 256)
                first[sl, cut] = dot(n2t[sl, :], zs[...]).astype(narrow)
                second[sl, cut] = dot(gt[sl, :], hs[...]).astype(narrow)

    @pl.when(step == 3 * count - 1)
    def _():
        for copy in near_swaps:
            copy.start()

    @pl.when(step == 3 * count)
    def _():
        halving.wait()
        add_rows(rest, 0, [(got2, mine), (landing, 0)], upper)

    @pl.when(step == 4 * count - 1)
    def _():
        for copy, near, got in zip(
            near_swaps, (near1, near2), (near_got1, near_got2), strict=True
        ):
            copy.wait()
            add_rows(near, 0, [(near, 0), (got, 0)], near.shape[0])
        sums[...] = jnp.zeros_like(sums)

        @pl.loop(0, SLAB // STRIP)
        def _(c):
            sl = rows_at(c * STRIP, STRIP)
            middle = dx1[sl, :]
            normal, inverse = norm_parts(middle)
            out[sl, :] = (middle + (branch[sl, :] + params[13:14])).astype(narrow)
            grad = dn2[sl, :]
            cot = gs[sl, :].astype(single)
            total = cot + norm_back(grad, normal, inverse, params[11:12])
            dx1[sl, :] = total
            low = total.astype(narrow)
            da[sl, :] = low
            sums[0:1, :] += jnp.sum(grad * normal, axis=0, keepdims=True)
            sums[1:2, :] += jnp.sum(grad, axis=0, keepdims=True)
            sums[2:3, :] += jnp.sum(low.astype(single), axis=0, keepdims=True)
            sums[3:4, :] += jnp.sum(cot, axis=0, keepdims=True)

        crossing.wait()


def mlp(residents, across, beside, own):
    width, local = own[0].shape
    count = local // BLOCK

    def block(shape, group, dim):
        def index(i):
            at = jnp.clip(i - group * count, 0, count - 1)
            return (0, at) if dim == 1 else (at, 0)

        return pl.BlockSpec(shape, index)

    slab = (SLAB, width)
    square = (width, local)
    in_specs = [whole(a.shape) for a in residents] + [ANY, ANY]
    in_specs += [block((width, BLOCK), group, 1) for group in (0, 2, 3)]
    in_specs += [block((BLOCK, width), group, 0) for group in (0, 2, 3)]
    outs = [
        (of(slab), whole(slab)),
        (of(slab, single), whole(slab)),
        (of(slab), whole(slab)),
        (of((8, width), single), whole((8, width))),
        (of(square), whole(square)),
        (of(square), whole(square)),
        (of(square), ANY),
        (of((local // 2, width)), whole((local // 2, width))),
        (of((SPLIT, 8, local), single), whole((SPLIT, 8, local))),
    ]
    flipped = pltpu.VMEM((width, SLAB), narrow)
    return pl.pallas_call(
        mlp_kernel,
        out_shape=[o[0] for o in outs],
        grid=(SPLIT * count,),
        in_specs=in_specs,
        out_specs=[o[1] for o in outs],
        scratch_shapes=[
            pltpu.VMEM(slab, narrow),
            flipped,
            flipped,
            pltpu.VMEM(slab, single),
            pltpu.VMEM(slab, single),
            *[pltpu.VMEM(square, narrow)] * 10,
            pltpu.VMEM((width // 2, local), narrow),
            pltpu.VMEM((width, BLOCK), narrow),
            pltpu.VMEM((BLOCK, width), narrow),
            pltpu.VMEM((1, BLOCK), single),
            pltpu.VMEM((SLAB, BLOCK), narrow),
            pltpu.VMEM((SLAB, BLOCK), narrow),
            pltpu.SemaphoreType.DMA((8,)),
            pltpu.SemaphoreType.DMA((8,)),
        ],
        compiler_params=pltpu.CompilerParams(
            vmem_limit_bytes=VMEM, collective_id=1, has_side_effects=True
        ),
        cost_estimate=pl.CostEstimate(
            flops=36_000_000_000, bytes_accessed=60_000_000, transcendentals=8_000_000
        ),
        name="mlp",
    )(*residents, *across, across[0], beside[0], own[0], across[1], beside[1], own[1])


def backward_kernel(
    rows_held, images,
    da, n1, qkv, mixed, weights, wrel, bits, lanes, sides, keys, xs, dx1, params, near1, near2, far1, rest,
    back, sums, keep, give, bias, grel, crossed, summed1, summed2,
    acc, dqkv, dmix, dn1, keep_far, give_far, got_far, held1, held2, land1, land2, rest_got,
    sends, recvs, locals_,
):
    step = pl.program_id(0)
    slot, far = step % SLOTS, 1 - step // SLOTS
    image = lax.axis_index("dp")
    beside, across, _ = partners(lax.axis_index("tensor"))
    send = Sender(sends, recvs, locals_)
    half, width = weights.shape[2:]
    per = Halver.copies(images)
    sum1 = Halver(send, 3, image, images, 0, held1.shape[0], (1, 0, 2))
    sum2 = Halver(send, 3 + per, image, images, 0, held2.shape[0], (0, 1, 2))
    rest_cross = send.remote(0, rest, rest_got, {"tensor": across})
    far_swap = send.remote(1, give_far, got_far, {"tensor": beside})
    far_cross = send.remote(2, got_far, crossed, {"tensor": across})

    halvers = ((sum1, held1, land1), (sum2, held2, land2))
    summed = (summed1, summed2)

    def seed(k, halver, held, summed):
        start, length = halver.final
        copy = send.local(k, held.at[rows_at(start, length), :], summed.at[rows_at(start, length), :])
        copy.start()
        copy.wait()

    def begin():
        greet([{"tensor": beside}, {"tensor": across}] + dp_mates(image, images))
        rest_cross.start()
        sum2.start(0, near2, land2)
        add_rows(held1, 0, [(near1, 0), (far1, 0)], held1.shape[0])
        sum1.start(0, held1, land1)

    def second():
        sum1.finish(0, held1, land1)
        sum1.start(1, held1, land1)
        sum2.out(0, near2, land2).wait()
        rest_cross.wait()
        _, kept, _, length, at = sum2.stages[0]
        add_rows(held2, kept, [(near2, kept), (land2, at), (rest_got, 0)], length)
        sum2.start(1, held2, land2)

    def third():
        for halver, held, land in halvers:
            halver.finish(1, held, land)
            halver.start(2, held, land)

    def fourth():
        for n, (halver, held, land) in enumerate(halvers):
            halver.finish(2, held, land)
            halver.extras(held, land)
            seed(n, halver, held, summed[n])
            halver.back(2, summed[n]).start()

    def hand(stage):
        for (halver, _, _), total in zip(halvers, summed, strict=True):
            halver.back(stage + 1, total).wait()
            halver.back(stage, total).start()

    def swap_far():
        far_swap.start()

    def cross_far():
        far_swap.wait()
        add_rows(got_far, 0, [(got_far, 0), (keep_far, 0)], got_far.shape[0])
        far_cross.start()

    events = {
        (0, 0): begin,
        (3, 0): second,
        (4, 2): third,
        (7, 0): swap_far,
        (7, 1): fourth,
        (8, 0): cross_far,
        (9, 2): functools.partial(hand, 1),
        (11, 0): functools.partial(hand, 0),
    }

    def fire(section):
        for (at, place), event in events.items():
            if place == section:
                pl.when(step == at)(event)

    _, col0, kind, inside, offset, live = slot_fields(rows_held)
    whole_window = inside == SPAN

    def on_window(action):
        for count, holds in ((ROWS, whole_window), (SHORT, jnp.logical_not(whole_window))):
            pl.when(live & holds)(functools.partial(action, count))

    @pl.when(slot == 0)
    def _():
        acc[...] = jnp.zeros_like(acc)

    @pl.when(step == 0)
    def _():
        for ref in (bias, grel, back, sums):
            ref[...] = jnp.zeros_like(ref)

    fire(0)

    def before_pairs(count):
        da_win = da[rows_at(offset, count), :]
        acc[3] += dot_tn(mixed[0, :count], da_win)
        dmix[:count] = dot_nt(da_win, weights[far, 3]).astype(narrow)

    on_window(before_pairs)

    def one_pair(pair, count):
        cut = slice(pair * LANES, (pair + 1) * LANES)
        q, k8, v, rel = (qkv[0, j, :n, cut] for j, n in enumerate((count, ROWS, ROWS, count)))
        do = dmix[:count, cut]
        dqs, dks, dvs = [], [], []
        for head in range(2):
            mine, other = sides[head : head + 1], sides[1 - head : 2 - head]
            full_key = k8 * mine + keys[kind] * other
            scores = dot_nt(full_key, q * mine + rel * other)
            top = jnp.max(scores, axis=0, keepdims=True)
            probs = jnp.exp(scores - top)
            probs = probs * (1.0 / jnp.sum(probs, axis=0, keepdims=True))
            dprobs = dot_nt(v, do * mine)
            mean = jnp.sum(probs * dprobs, axis=0, keepdims=True)
            dscores = (probs * (dprobs - mean)).astype(narrow)
            dvs.append(dot(probs.astype(narrow), do))
            dks.append(dot(dscores, q))
            dqs.append(dot_tn(dscores, full_key))
        low_lane = lax.broadcasted_iota(jnp.int32, (ROWS, LANES), 1) < 64
        dv = jnp.where(low_lane, dvs[0], dvs[1])
        dk = jnp.where(low_lane, dks[0], dks[1]) * 0.125
        low_lane = lax.broadcasted_iota(jnp.int32, (count, LANES), 1) < 64
        dq = jnp.where(low_lane, dqs[0], dqs[1])
        drel = jnp.where(low_lane, dqs[1], dqs[0]) * lanes[0:1]
        drel = shift_right(drel, bits.at[kind]).astype(narrow)
        dq = dq + dot(drel, wrel[...])
        grel[...] += dot_tn(drel, q)
        dqkv[0, :count, cut] = dq.astype(narrow)
        dqkv[1, :, cut] = dk.astype(narrow)
        dqkv[2, :, cut] = dv.astype(narrow)

    for pair in range(half // LANES):
        fire(pair + 1)
        on_window(functools.partial(one_pair, pair))

    def after_pairs(count):
        total = None
        for j in range(3):
            piece = dqkv[j, :count]
            acc[j] += dot_tn(piece, n1[0, :count])
            every = piece if j == 0 else dqkv[j]
            bias[far, j : j + 1, :] += jnp.sum(every.astype(single), axis=0, keepdims=True)
            back_part = dot(piece, weights[far, j])
            total = back_part if total is None else total + back_part

        @pl.when(far == 1)
        def _():
            dn1[slot, :count] = total

        @pl.when(far == 0)
        def _():
            _, valid = positions(0, count, col0, kind, inside)
            place = rows_at(offset, count)
            grad = jnp.where(valid, total + dn1[slot, :count], 0.0)
            normal, inverse = norm_parts(xs[place, :].astype(single))
            sums[0:1, :] += jnp.sum(grad * normal, axis=0, keepdims=True)
            sums[1:2, :] += jnp.sum(grad, axis=0, keepdims=True)
            result = dx1[place, :] + norm_back(grad, normal, inverse, params[8:9])
            back[place, :] = jnp.where(valid, result, 0.0).astype(narrow)

    on_window(after_pairs)

    def flush(keep, give):
        part = half // 2
        for j in range(4):
            keep[j * part : (j + 1) * part, :] = acc[j, :part, :].astype(narrow)
            give[j * part : (j + 1) * part, :] = acc[j, part:, :].astype(narrow)

    @pl.when(step == SLOTS - 1)
    def _():
        flush(keep_far, give_far)

    @pl.when(step == 2 * SLOTS - 1)
    def _():
        flush(keep, give)
        for (halver, _, _), total in zip(halvers, summed, strict=True):
            halver.back(0, total).wait()
        far_cross.wait()


def backward(rows_held, images, da, n1, qkv, mixed, weights, wrel, tables, residents, rest):
    half, width = weights.shape[2:]
    operands = [da, n1, qkv, mixed, weights, wrel, *tables, *residents, rest]
    in_specs = [whole(a.shape) for a in operands]
    in_specs[1] = pl.BlockSpec((1, ROWS, width), lambda i: (i % SLOTS, 0, 0))

    def halved(i):
        return (1 - i // SLOTS) * SLOTS + i % SLOTS

    in_specs[2] = pl.BlockSpec((1, 4, ROWS, half), lambda i: (halved(i), 0, 0, 0))
    in_specs[3] = pl.BlockSpec((1, ROWS, half), lambda i: (halved(i), 0, 0))
    in_specs[-1] = ANY
    packed = (2 * half, width)
    square = residents[3].shape
    outs = [
        (of((SLAB, width)), whole((SLAB, width))),
        (of((8, width), single), whole((8, width))),
        (of(packed), whole(packed)),
        (of(packed), whole(packed)),
        (of((2, 8, half), single), whole((2, 8, half))),
        (of((LANES, LANES), single), whole((LANES, LANES))),
        (of(packed), ANY),
        (of(square), ANY),
        (of(square), ANY),
    ]
    landing = (Halver.landing_rows(images, square[0]), width)
    copies = 3 + 2 * Halver.copies(images)
    return pl.pallas_call(
        functools.partial(backward_kernel, rows_held, images),
        out_shape=[o[0] for o in outs],
        grid=(2 * SLOTS,),
        in_specs=in_specs,
        out_specs=[o[1] for o in outs],
        scratch_shapes=[
            pltpu.VMEM((4, half, width), single),
            pltpu.VMEM((3, ROWS, half), narrow),
            pltpu.VMEM((ROWS, half), narrow),
            pltpu.VMEM((SLOTS, ROWS, width), single),
            *[pltpu.VMEM(packed, narrow)] * 3,
            *[pltpu.VMEM(square, narrow)] * 2,
            *[pltpu.VMEM(landing, narrow)] * 2,
            pltpu.VMEM(rest.shape, narrow),
            pltpu.SemaphoreType.DMA((copies,)),
            pltpu.SemaphoreType.DMA((copies,)),
            pltpu.SemaphoreType.DMA((2,)),
        ],
        compiler_params=pltpu.CompilerParams(
            vmem_limit_bytes=VMEM, collective_id=2, has_side_effects=True
        ),
        cost_estimate=pl.CostEstimate(
            flops=52_000_000_000, bytes_accessed=80_000_000, transcendentals=8_000_000
        ),
        name="attention_backward",
    )(*operands)


def clear_rows(ext):
    @pl.loop(0, ext.shape[0] // GRID)
    def _(r):
        ext[rows_at(r * GRID, GRID), :] = jnp.zeros((GRID, ext.shape[1]), narrow)


def place_windows(rows_held, device, slab, ext, first, last):
    @pl.loop(first, last)
    def _(slot):
        row0, col0, kind, inside, offset, live = window_fields(rows_held, device, slot)

        @pl.when(live)
        def _():
            target, _ = positions(1, ROWS, col0, kind, inside)
            token = lax.broadcasted_iota(jnp.int32, (WIN * GRID, ROWS), 0)
            choose = jnp.where(token == target, 1.0, 0.0).astype(narrow)
            window = slab[rows_at(offset, ROWS), :]
            where_to = pl.ds(pl.multiple_of(row0 * GRID, GRID), WIN * GRID)
            ext[where_to, :] += dot(choose, window).astype(narrow)


def tail_kernel(
    rows_held, images,
    out, back, keep, crossed, sums1, sums2, bias, rel_sum, fc_bias, peak, give,
    output, input_grad, packed, totals, tops,
    ext0, ext1, below0, below1, above0, above1, got, landing, held, sum_land, top_land, sends, recvs,
):
    device, image = lax.axis_index("tensor"), lax.axis_index("dp")
    beside, across, corner = partners(device)
    send = Sender(sends, recvs, None)
    per = Halver.copies(images)
    middle = held.shape[0] // 2
    landing_rows = Halver.landing_rows(images, middle)
    landings = [landing.at[pl.ds(k * landing_rows, landing_rows), :] for k in range(2)]
    halvers = [
        Halver(send, 1 + k * per, image, images, k * middle, middle, order)
        for k, order in enumerate(((0, 1, 2), (1, 0, 2)))
    ]
    halo_base = 1 + 2 * per
    small_base = halo_base + 4
    tokens = rows_held * GRID
    top, bottom = LEFT * GRID, RIGHT * GRID
    held_by = (device, beside, across, corner)
    mates = dp_mates(image, images)
    ring = [{"tensor": beside}, {"tensor": across}] + mates

    def reduce_start(stage):
        for halver, land in zip(halvers, landings, strict=True):
            halver.start(stage, held, land)

    def reduce_finish(stage):
        for halver, land in zip(halvers, landings, strict=True):
            halver.finish(stage, held, land)

    def hand_start(stage):
        for halver in halvers:
            halver.back(stage, packed).start()

    def hand_finish(stage):
        for halver in halvers:
            halver.back(stage, packed).wait()

    greet([{"tensor": place} for place in (beside, across, corner)] + mates)
    swap = send.remote(0, give, got, {"tensor": beside})
    swap.start()

    totals[...] = jnp.zeros_like(totals)
    tops[...] = jnp.zeros_like(tops)
    totals[0:2, :] = sums1[0:2, :]
    totals[2:6, :] = sums2[0:4, :]
    rel = rel_sum[...]
    rel = rel[HD:] + pltpu.roll(rel[:HD], HD, 1)
    for g in range(HD // 8):
        at = 8 * (1 + g // 6)
        totals[at : at + 8, (g % 6) * LANES : (g % 6 + 1) * LANES] = rel[8 * g : 8 * g + 8]
    half = bias.shape[2]
    for k in range(SPLIT):
        far, odd = k // 2, k % 2
        totals[pl.ds(24 + held_by[k], 1), :] = fc_bias[k, 0:1, :]
        for j, row in enumerate((0, 2)):
            value = bias[far, row : row + 1, :]
            if odd:
                value = pltpu.roll(value, half // 2, 1)
            totals[pl.ds(28 + held_by[k], 1), j * half : (j + 1) * half] = value
        best = jnp.broadcast_to(jnp.max(peak[far], axis=1, keepdims=True), (8, LANES))
        if odd:
            best = pltpu.roll(best, 8 - half // LANES, 0)
        tops[pl.ds(pl.multiple_of(held_by[k] * 8, 8), 8), :] = best

    def small_copies(k):
        return [
            send.remote(small_base + 2 * k, totals, sum_land.at[k], ring[k]),
            send.remote(small_base + 2 * k + 1, tops, top_land.at[k], ring[k]),
        ]

    def small_start(k):
        for copy in small_copies(k):
            copy.start()

    def small_finish(k):
        for copy in small_copies(k):
            copy.wait()
        totals[...] += sum_land[k]
        tops[...] = jnp.maximum(tops[...], top_land[k])

    def halo(base, ext, below, above):
        up = send.remote(
            base, ext.at[pl.ds(0, top), :], below, {"tensor": (device + SPLIT - 1) % SPLIT}
        )
        down = send.remote(
            base + 1, ext.at[pl.ds(top + tokens, bottom), :], above, {"tensor": (device + 1) % SPLIT}
        )
        return up, down

    def halo_start(copies):
        up, down = copies
        pl.when(device > 0)(up.start)
        pl.when(device < SPLIT - 1)(down.start)

    def halo_finish(copies, ext, below, above, result):
        up, down = copies
        pl.when(device > 0)(up.wait_send)
        pl.when(device < SPLIT - 1)(down.wait_send)
        add_rows(result, 0, [(ext, top)], tokens)

        @pl.when(device < SPLIT - 1)
        def _():
            up.wait_recv()
            at = tokens - top
            add_rows(result, at, [(result, at), (below, 0)], top)

        @pl.when(device > 0)
        def _():
            down.wait_recv()
            add_rows(result, 0, [(result, 0), (above, 0)], bottom)

    small_start(0)
    clear_rows(ext0)
    clear_rows(ext1)
    swap.wait()
    add_rows(held, 0, [(keep, 0), (got, 0), (crossed, 0)], held.shape[0])
    reduce_start(0)
    small_finish(0)
    small_start(1)
    place_windows(rows_held, device, back, ext1, 0, SLOTS)
    halos1 = halo(halo_base, ext1, below1, above1)
    halo_start(halos1)
    small_finish(1)
    small_start(2)
    reduce_finish(0)
    reduce_start(1)
    place_windows(rows_held, device, out, ext0, 0, 3)
    small_finish(2)
    small_start(3)
    reduce_finish(1)
    reduce_start(2)
    place_windows(rows_held, device, out, ext0, 3, SLOTS)
    halos0 = halo(halo_base + 2, ext0, below0, above0)
    halo_start(halos0)
    small_finish(3)
    small_start(4)
    reduce_finish(2)
    for halver, land in zip(halvers, landings, strict=True):
        halver.extras(held, land)
        start, length = halver.final
        packed[rows_at(start, length), :] = held[rows_at(start, length), :]
    hand_start(2)
    for k in range(4, len(ring)):
        small_finish(k)
        if k + 1 < len(ring):
            small_start(k + 1)
    halo_finish(halos1, ext1, below1, above1, input_grad)
    hand_finish(2)
    hand_start(1)
    hand_finish(1)
    hand_start(0)
    halo_finish(halos0, ext0, below0, above0, output)
    hand_finish(0)


def tail(rows_held, images, *operands):
    width = operands[0].shape[1]
    packed = operands[2].shape
    tokens = rows_held * GRID
    bits = images.bit_length() - 1
    landing = 2 * Halver.landing_rows(images, packed[0] // 2)
    copies = 1 + 2 * Halver.copies(images) + 4 + 2 * (2 + bits)
    ext = ((rows_held + LEFT + RIGHT) * GRID, width)
    outs = [
        of((tokens, width)), of((tokens, width)), of(packed),
        of((32, width), single), of((32, LANES), single),
    ]
    return pl.pallas_call(
        functools.partial(tail_kernel, rows_held, images),
        out_shape=outs,
        in_specs=[pl.BlockSpec(memory_space=pltpu.VMEM)] * (len(operands) - 1) + [ANY],
        out_specs=[pl.BlockSpec(memory_space=pltpu.VMEM)] * len(outs),
        scratch_shapes=[
            pltpu.VMEM(ext, narrow),
            pltpu.VMEM(ext, narrow),
            pltpu.VMEM((LEFT * GRID, width), narrow),
            pltpu.VMEM((LEFT * GRID, width), narrow),
            pltpu.VMEM((RIGHT * GRID, width), narrow),
            pltpu.VMEM((RIGHT * GRID, width), narrow),
            pltpu.VMEM(packed, narrow),
            pltpu.VMEM((landing, width), narrow),
            pltpu.VMEM(packed, narrow),
            pltpu.VMEM((2 + bits, 32, width), single),
            pltpu.VMEM((2 + bits, 32, LANES), single),
            pltpu.SemaphoreType.DMA((copies,)),
            pltpu.SemaphoreType.DMA((copies,)),
        ],
        compiler_params=pltpu.CompilerParams(
            vmem_limit_bytes=VMEM, collective_id=3, has_side_effects=True
        ),
        cost_estimate=pl.CostEstimate(
            flops=4_000_000_000, bytes_accessed=20_000_000, transcendentals=0
        ),
        name="tail",
    )(*operands)


def shards(
    inputs,
    w_qkv,
    qv_bias,
    w_proj,
    proj_bias,
    w_fc1,
    fc1_bias,
    w_fc2,
    fc2_bias,
    norm1_gain,
    norm1_shift,
    norm2_gain,
    norm2_shift,
    rel_h,
    rel_w,
    cotangent,
):
    width = inputs.shape[2]
    rows = inputs.shape[1] // GRID
    local = w_qkv.shape[2]
    heads = local // HD
    device = lax.axis_index("tensor")
    tables = lane_tables()

    span = 2 * WIN - 1
    wrel = sum(
        jnp.pad(table, ((at, LANES - span - at), (side, HD - side)))
        for table, at, side in (
            (rel_h, HD, 0), (rel_w, HD + 32, 0), (rel_h, 0, HD), (rel_w, 32, HD),
        )
    )

    entries = (
        (fc1_bias, 0, 0), (qv_bias[0], 1, 0), (qv_bias[0], 2, local), (qv_bias[1], 3, 0),
        (qv_bias[1], 4, local), (norm1_gain, 8, 0), (norm1_shift, 9, 0), (proj_bias, 10, 0),
        (norm2_gain, 11, 0), (norm2_shift, 12, 0), (fc2_bias, 13, 0),
    )
    params = 0.0
    for values, row, at in entries:
        before = row * width + at
        params = params + jnp.pad(values, (before, 16 * width - before - values.shape[0]))
    params = params.reshape(16, width)
    wqkv = w_qkv.transpose(0, 2, 1)

    (
        xs, gs, n1, qkv, mixed, attn, peak,
        weights, across1, across2, beside1, beside2, smalls,
    ) = forward(
        *(a.reshape(rows, GRID, width) for a in (inputs, cotangent)), wqkv, w_proj, w_fc1, w_fc2, params,
        wrel, tables
    )
    out, dx1, da, sums2, near1, near2, far1, rest, fc_bias = mlp(
        (
            xs, attn, gs, params, smalls,
        ),
        (across1, across2),
        (beside1, beside2),
        (w_fc1, w_fc2),
    )
    images = lax.axis_size("dp")
    back, sums1, keep, give, bias, rel_sum, crossed, summed1, summed2 = backward(
        rows, images, da, n1, qkv, mixed, weights, wrel, tables,
        [xs, dx1, params, near1, near2, far1], rest,
    )
    output, input_grad, gpack, totals, tops = tail(
        rows, images, out, back, keep, crossed, sums1, sums2, bias, rel_sum, fc_bias, peak, give
    )

    gpack = gpack.astype(single)
    blocks = totals[8:24].reshape(2, 8, 6, LANES).transpose(0, 2, 1, 3).reshape(-1, LANES)[:HD, :HD]
    grad_rel = jnp.stack([blocks[: 2 * WIN - 1], blocks[32 : 32 + 2 * WIN - 1]])
    qv = lax.dynamic_slice_in_dim(totals, 28 + device, 1)[0].reshape(2, 2 * local)[:, :local]
    head_max = lax.dynamic_slice(tops, (8 * device, 0), (heads, 1))[:, 0]
    factor = jnp.sqrt(CLIP / jnp.maximum(head_max, CLIP))
    clipped_qk = (w_qkv[:2].astype(single) * jnp.repeat(factor, HD)).astype(narrow)

    return (
        output[None],
        input_grad[None],
        gpack[: 3 * local].reshape(3, local, width).transpose(0, 2, 1),
        qv,
        gpack[3 * local :],
        totals[4],
        summed1.astype(single),
        lax.dynamic_slice_in_dim(totals, 24 + device, 1)[0],
        summed2.T.astype(single),
        totals[5],
        totals[:4],
        grad_rel,
        clipped_qk,
        head_max,
    )


def solution(mesh):
    return jax.shard_map(
        shards,
        mesh=mesh,
        in_specs=(
            P("dp", "tensor", None),
            P(None, None, "tensor"),
            P(None, "tensor"),
            P("tensor", None),
            P(),
            P(None, "tensor"),
            P("tensor"),
            P("tensor", None),
            P(),
            P(),
            P(),
            P(),
            P(),
            P(),
            P(),
            P("dp", "tensor", None),
        ),
        out_specs=(
            P("dp", "tensor", None),
            P("dp", "tensor", None),
            P(None, None, "tensor"),
            P(None, "tensor"),
            P("tensor", None),
            P(),
            P(None, "tensor"),
            P("tensor"),
            P("tensor", None),
            P(),
            P(),
            P(),
            P(None, None, "tensor"),
            P("tensor"),
        ),
        check_vma=False,
    )
```

```python
import functools

import jax
import jax.numpy as jnp
import numpy as np
from jax import lax
from jax.experimental import pallas as pl
from jax.experimental.pallas import tpu as pltpu
from jax.sharding import PartitionSpec as P

HD = 64
GRID = 64
WIN = 14
TILES = 5
SPAN = WIN * WIN
ROWS = 208
SLOTS = 7
EDGE = GRID % WIN
SHORT = EDGE * WIN
SLAB = (SLOTS - 2) * ROWS + SHORT
STRIP = SLAB // 6
SPLIT = 4
LEFT = 6
RIGHT = 12
LANES = 128
EPS = 1e-6
CLIP = 3.0
VMEM = 60 * 1024 * 1024

single = jnp.float32
narrow = jnp.bfloat16

def lane_tables():
    row = np.arange(ROWS)
    late = np.maximum(row - SHORT, 0)
    outer = WIN - EDGE
    orders = (
        (row // WIN, row % WIN),
        (
            np.where(row < SHORT, row // EDGE, late // outer),
            np.where(row < SHORT, row % EDGE, EDGE + late % outer),
        ),
    )
    lane = np.arange(LANES) % 64
    part = lane // 32
    at = lane % 32
    bits, keys = [], []
    for x, y in orders:
        amount = np.where(part[None, :] == 0, x[:, None], y[:, None])
        amount = np.where((row < SPAN)[:, None], amount, 0)
        bits.append(np.stack([(amount >> b) & 1 for b in range(4)]).astype(np.float32))
        place = WIN - 1 - np.where(part[None, :] == 0, x[:, None], y[:, None])
        hot = ((at % 16)[None, :] == place) & ((at % 16) < WIN)[None, :] & (row < SPAN)[:, None]
        hot = hot.astype(np.float32)
        hot[SPAN:, lane == 31] = -1e30
        keys.append(hot)
    lanes = np.zeros((8, LANES), np.float32)
    lanes[0] = at < WIN
    lanes[1] = (at >= 16) & (at < 16 + WIN)
    lanes[2] = lane == 31
    sides = np.zeros((16, LANES), np.float32)
    sides[0] = np.arange(LANES) < 64
    sides[1] = np.arange(LANES) >= 64
    return (
        jnp.asarray(np.stack(bits)),
        jnp.asarray(lanes),
        jnp.asarray(sides, narrow),
        jnp.asarray(np.stack(keys), narrow),
    )


def dot(a, b):
    return jnp.dot(a, b, preferred_element_type=single)


def dot_nt(a, b):
    return lax.dot_general(a, b, (((1,), (1,)), ((), ())), preferred_element_type=single)


def dot_tn(a, b):
    return lax.dot_general(a, b, (((0,), (0,)), ((), ())), preferred_element_type=single)


def norm_parts(values):
    centre = values - jnp.mean(values, axis=-1, keepdims=True)
    inverse = lax.rsqrt(jnp.mean(centre * centre, axis=-1, keepdims=True) + EPS)
    return centre * inverse, inverse


def norm_back(grad, normal, inverse, gain):
    scaled = grad * gain
    first = jnp.mean(scaled, axis=-1, keepdims=True)
    second = jnp.mean(scaled * normal, axis=-1, keepdims=True)
    return inverse * (scaled - first - normal * second)


def slot_fields(rows_held):
    return window_fields(rows_held, lax.axis_index("tensor"), pl.program_id(0) % SLOTS)


def window_fields(rows_held, device, slot):
    first = device * (SLOTS - 1)
    window = first + slot
    i, j = window // TILES, window % TILES
    last = device // (SPLIT - 1)
    live = slot < SLOTS - 1 + last
    row0 = i * WIN - device * rows_held + LEFT
    high = jnp.minimum(WIN, GRID - i * WIN)
    wide = jnp.minimum(WIN, GRID - j * WIN)

    def short_before(n):
        return jnp.minimum(n // TILES, TILES - 1) + jnp.maximum(n - TILES * (TILES - 1), 0)

    offset = ROWS * slot - (ROWS - SHORT) * (short_before(window) - short_before(first))
    return row0, j * WIN, j // (TILES - 1), high * wide, offset, live


def positions(axis, count, first_col, kind, inside):
    shape = (count, 1) if axis == 0 else (1, count)
    row = lax.broadcasted_iota(jnp.int32, shape, axis)
    x = lax.shift_right_logical(row * 4682, 16)
    plain = x * GRID + (row - x * WIN)
    x = lax.shift_right_logical(row, EDGE.bit_length() - 1)
    edge = x * GRID + (row - x * EDGE)
    token = jnp.where(kind == 1, edge, plain) + first_col
    return jnp.where(row < inside, token, -1), row < inside


def gather_window(source, target):
    token = lax.broadcasted_iota(jnp.int32, (target.shape[0], WIN * GRID), 1)
    choose = jnp.where(token == target, 1.0, 0.0).astype(narrow)
    return dot(choose, source)


def shift_left(values, bits):
    for b in range(4):
        taken = bits[b, : values.shape[0]] > 0.5
        values = jnp.where(taken, pltpu.roll(values, LANES - (1 << b), 1), values)
    return values


def shift_right(values, bits):
    for b in range(4):
        taken = bits[b, : values.shape[0]] > 0.5
        values = jnp.where(taken, pltpu.roll(values, 1 << b, 1), values)
    return values


def partners(device):
    beside = device + 1 - 2 * (device % 2)
    across = (device + 2) % SPLIT
    corner = (beside + 2) % SPLIT
    return beside, across, corner


def greet(places):
    barrier = pltpu.get_barrier_semaphore()
    for place in places:
        pl.semaphore_signal(barrier, inc=1, device_id=place, device_id_type=pl.DeviceIdType.MESH)
    pl.semaphore_wait(barrier, len(places))


class Sender:
    def __init__(self, sends, recvs, locals_):
        self.sends, self.recvs, self.locals = sends, recvs, locals_

    def remote(self, at, source, target, place):
        return pltpu.make_async_remote_copy(
            src_ref=source,
            dst_ref=target,
            send_sem=self.sends.at[at],
            recv_sem=self.recvs.at[at],
            device_id=place,
            device_id_type=pl.DeviceIdType.MESH,
        )

    def local(self, at, source, target):
        return pltpu.make_async_copy(source, target, self.locals.at[at])


def mate_of(image, bit):
    unit = 1 << bit
    return image + unit * (1 - 2 * ((image // unit) % 2))


def rows_at(start, count):
    return pl.ds(pl.multiple_of(start, 16), count)


def add_rows(target, target_at, sources, count):
    chunk = next(c for c in (96, 48, 16) if count % c == 0)

    @pl.loop(0, count // chunk)
    def _(c):
        total = None
        for ref, at in sources:
            value = ref[rows_at(at + c * chunk, chunk), :]
            total = value if total is None else total + value
        target[rows_at(target_at + c * chunk, chunk), :] = total


HALVINGS = 3


class Halver:
    def __init__(self, send, base, image, images, start, rows, order):
        bits = images.bit_length() - 1
        assert images == 1 << bits and bits >= HALVINGS
        self.send, self.base, self.image = send, base, image
        self.extra_bits = range(HALVINGS, bits)
        self.stages = []
        landing, length = 0, rows
        for bit in order:
            length //= 2
            mine = (image // (1 << bit)) % 2
            keep, give = start + mine * length, start + (1 - mine) * length
            self.stages.append((mate_of(image, bit), keep, give, length, landing))
            landing += length
            start = keep
        self.final = (start, length)
        self.landing = landing

    @staticmethod
    def copies(images):
        return 2 * HALVINGS + images.bit_length() - 1 - HALVINGS

    @staticmethod
    def landing_rows(images, rows):
        last = rows >> HALVINGS
        return rows - last + last * (images.bit_length() - 1 - HALVINGS)

    def out(self, stage, held, landing):
        mate, _, give, length, at = self.stages[stage]
        return self.send.remote(
            self.base + stage,
            held.at[rows_at(give, length), :],
            landing.at[pl.ds(at, length), :],
            {"dp": mate},
        )

    def start(self, stage, held, landing):
        self.out(stage, held, landing).start()

    def finish(self, stage, held, landing):
        self.out(stage, held, landing).wait()
        _, keep, _, length, at = self.stages[stage]
        add_rows(held, keep, [(held, keep), (landing, at)], length)

    def extras(self, held, landing):
        start, length = self.final
        for k, bit in enumerate(self.extra_bits):
            at = self.landing + k * length
            copy = self.send.remote(
                self.base + HALVINGS + k,
                held.at[rows_at(start, length), :],
                landing.at[pl.ds(at, length), :],
                {"dp": mate_of(self.image, bit)},
            )
            copy.start()
            copy.wait()
            add_rows(held, start, [(held, start), (landing, at)], length)

    def back(self, stage, held):
        mate, keep, _, length, _ = self.stages[stage]
        cut = rows_at(keep, length)
        at = self.base + HALVINGS + len(self.extra_bits) + stage
        return self.send.remote(at, held.at[cut, :], held.at[cut, :], {"dp": mate})


def dp_mates(image, images):
    return [{"dp": mate_of(image, bit)} for bit in range(images.bit_length() - 1)]


def attend(n1, valid, weights, qbias, vbias, wrel, bits, lanes, sides, keys, qkv, mixed, peak):
    half = weights.shape[1]
    count = n1.shape[0]
    query = jnp.where(valid, dot_nt(n1, weights[0]) + qbias, 0.0).astype(narrow)
    key8 = dot_nt(n1, weights[1]).astype(narrow) * jnp.asarray(0.125, narrow)
    value = (dot_nt(n1, weights[2]) + vbias).astype(narrow)
    qkv[0, 0, :count] = query
    qkv[0, 1, :count] = key8
    qkv[0, 2, :count] = value
    if count < ROWS:
        left = ROWS - count
        qkv[0, 1, count:] = jnp.zeros((left, half), narrow)
        qkv[0, 2, count:] = jnp.broadcast_to(vbias, (left, half)).astype(narrow)
    low_lane = lax.broadcasted_iota(jnp.int32, (count, LANES), 1) < 64
    for pair in range(half // LANES):
        cut = slice(pair * LANES, (pair + 1) * LANES)
        q = query[:, cut]
        k8, v = qkv[0, 1, :, cut], qkv[0, 2, :, cut]
        rel = shift_left(dot_nt(q, wrel[...]), bits)
        rest = rel - rel.astype(narrow).astype(single)
        rel = rel * lanes[0:1] + pltpu.roll(rest, 16, 1) * lanes[1:2] + lanes[2:3]
        rel = rel.astype(narrow)
        qkv[0, 3, :count, cut] = rel
        pieces = []
        for head in range(2):
            mine, other = sides[head : head + 1], sides[1 - head : 2 - head]
            only = q * mine
            logits = dot_nt(only, k8)
            at = 2 * pair + head
            peak[at : at + 1, :] = jnp.maximum(
                peak[at : at + 1, :], jnp.max(logits, axis=0, keepdims=True)
            )
            scores = dot_nt(only + rel * other, k8 * mine + keys[...] * other)
            top = jnp.max(scores, axis=1, keepdims=True)
            probs = jnp.exp(scores - top)
            total = jnp.sum(probs, axis=1, keepdims=True)
            pieces.append(dot(probs.astype(narrow), v) * (1.0 / total))
        mixed[0, :count, cut] = jnp.where(low_lane, pieces[0], pieces[1]).astype(narrow)
    return dot(mixed[0, :count], weights[3])


class Halo:
    def __init__(self, send, base, grid, ext, device, rows):
        below, above = {"tensor": (device + 1) % SPLIT}, {"tensor": (device + SPLIT - 1) % SPLIT}
        self.has_below, self.has_above = device < SPLIT - 1, device > 0
        self.cross_below, self.cross_above = device == 1, device == 2

        def copy(at, first, count, first_col, cols, target_row, place):
            window = (pl.ds(first, count), pl.ds(first_col, cols), slice(None))
            return send.remote(
                at, grid.at[window], ext.at[(pl.ds(target_row, count), *window[1:])], place
            )

        few, many = 4, 10
        self.down = copy(base, rows - LEFT, LEFT, 0, GRID, 0, below)
        self.down_cross = copy(base, rows - few, few, 16, GRID - 16, LEFT - few, below)
        self.up = copy(base + 1, 0, RIGHT, 0, GRID, LEFT + rows, above)
        self.up_cross = copy(base + 1, 0, many, 0, 32, LEFT + rows, above)

    def _each(self, down_here, up_here, act):
        for here, crossing, plain, crossed in (
            (*down_here, self.down, self.down_cross),
            (*up_here, self.up, self.up_cross),
        ):

            @pl.when(here & jnp.logical_not(crossing))
            def _():
                act(plain)

            @pl.when(crossing)
            def _():
                act(crossed)

    def _senders(self, act):
        self._each((self.has_below, self.cross_below), (self.has_above, self.cross_above), act)

    def start(self):
        self._senders(lambda copy: copy.start())

    def wait_send(self):
        self._senders(lambda copy: copy.wait_send())

    def wait_from_above(self):
        pl.when(self.has_above & jnp.logical_not(self.cross_above))(self.down.wait_recv)
        pl.when(self.cross_above)(self.down_cross.wait_recv)

    def wait_from_below(self):
        pl.when(self.has_below & jnp.logical_not(self.cross_below))(self.up.wait_recv)
        pl.when(self.cross_below)(self.up_cross.wait_recv)


class Quartet:
    def __init__(self, send, base, image, pieces, across):
        side, deep = image % 2, (image // 2) % 2
        beside, behind = {"dp": mate_of(image, 0)}, {"dp": mate_of(image, 1)}
        mine = 2 * deep + side
        from_beside, from_behind = 2 * deep + 1 - side, 2 * (1 - deep) + side
        self.first, self.second, self.third = [], [], []
        for k, (source, target, view) in enumerate(pieces):
            at = base + 5 * k

            def copy(number, origin, quarter, part, place):
                return send.remote(at + number, view(origin, quarter, part), view(target, quarter, part), place)

            self.first.append(copy(0, source, mine, None, across))
            self.second.append(copy(1, target, mine, None, beside))
            self.second.append(copy(2, target, mine, None, behind))
            if view(target, from_behind, 0) is not None:
                self.third.append(copy(3, target, from_behind, 0, beside))
            self.third.append(copy(4, target, from_beside, 1, behind))


def quarter_rows(array, quarter, part):
    size = array.shape[0] // 4
    start = quarter * size
    if part is not None:
        size //= 2
        start += part * size
    return array.at[rows_at(start, size), :]


def start_all(copies):
    for copy in copies:
        copy.start()


def receive_all(copies):
    for copy in copies:
        copy.wait_recv()


def forward_kernel(
    x, g, wqkv, wproj, fc1, fc2, notes_in, params, wrel, bits, lanes, sides, keys,
    xs, gs, n1_all, qkv, mixed, attn, peak, weights_out, across1, across2, beside1, beside2, small_out,
    xext, gext, weights, smalls, sends, recvs, locals_,
):
    step = pl.program_id(0)
    far, slot = step // SLOTS, step % SLOTS
    device, image = lax.axis_index("tensor"), lax.axis_index("dp")
    rows, _, width = x.shape
    part = wproj.shape[0]
    half = 2 * part
    beside, across, corner = partners(device)
    send = Sender(sends, recvs, locals_)
    x_halo = Halo(send, 0, x, xext, device, rows)
    g_halo = Halo(send, 2, g, gext, device, rows)
    small = notes_in.at[pl.ds(0, 8), :]

    own_pack = [
        send.remote(4, wqkv, weights.at[0, 0:3, pl.ds(part, part), :], {"tensor": beside}),
        send.remote(5, wproj, weights.at[0, 3, pl.ds(part, part), :], {"tensor": beside}),
    ]
    notes = [
        send.remote(6 + k, small, smalls.at[k + 1], {"tensor": place})
        for k, place in enumerate((beside, across, corner))
    ]
    fc_beside = [
        send.remote(9, fc1, beside1, {"tensor": beside}),
        send.remote(10, fc2, beside2, {"tensor": beside}),
    ]
    corner_pack = send.remote(
        11, weights.at[1, :, pl.ds(0, part), :], weights.at[1, :, pl.ds(part, part), :], {"tensor": beside}
    )

    def of_qkv(array, quarter, half_of):
        size = part // 4
        cut = rows_at(quarter * size, size)
        if array is wqkv:
            return array.at[:, cut, :]
        if half_of is None:
            return array.at[1, 0:3, cut, :]
        return array.at[1, 0:2, cut, :] if half_of == 0 else array.at[1, 2:3, cut, :]

    def of_proj(array, quarter, half_of):
        size = part // 4
        cut = rows_at(quarter * size, size)
        if array is wproj:
            return array.at[cut, :]
        return None if half_of == 0 else array.at[1, 3, cut, :]

    pack_far = Quartet(
        send, 12, image, ((wqkv, weights, of_qkv), (wproj, weights, of_proj)), {"tensor": across}
    )
    fc_far = Quartet(
        send, 22, image, ((fc1, across1, quarter_rows), (fc2, across2, quarter_rows)), {"tensor": across}
    )
    own = [
        send.local(0, wqkv, weights.at[0, 0:3, pl.ds(0, part), :]),
        send.local(1, wproj, weights.at[0, 3, pl.ds(0, part), :]),
        send.local(2, x, xext.at[pl.ds(LEFT, rows)]),
        send.local(3, small, smalls.at[0]),
    ]
    g_own = send.local(4, g, gext.at[pl.ds(LEFT, rows)])
    kept = [send.local(5, weights, weights_out), send.local(6, smalls, small_out)]

    @pl.when(step == 0)
    def _():
        for ref in (xext, gext):
            ref[pl.ds(0, LEFT)] = jnp.zeros((LEFT, GRID, width), narrow)
            ref[pl.ds(LEFT + rows, RIGHT)] = jnp.zeros((RIGHT, GRID, width), narrow)
        greet(
            [{"tensor": place} for place in (beside, across, corner)]
            + [{"dp": mate_of(image, bit)} for bit in range(2)]
        )
        start_all(own_pack + notes + own)
        x_halo.start()
        start_all(pack_far.first)
        for ref in (xs, gs, attn, peak):
            ref[...] = jnp.zeros_like(ref)
        for copy in own + notes + own_pack:
            copy.wait()
        x_halo.wait_from_above()

    @pl.when(step == 1)
    def _():
        start_all(fc_beside + [g_own])

    @pl.when(step == 2)
    def _():
        receive_all(pack_far.first)
        start_all(pack_far.second)
        start_all(fc_far.first)

    @pl.when(step == 3)
    def _():
        x_halo.wait_from_below()

    @pl.when(step == 4)
    def _():
        receive_all(pack_far.second)
        start_all(pack_far.third)

    @pl.when(step == 5)
    def _():
        receive_all(fc_far.first)
        start_all(fc_far.second)
        g_halo.start()

    @pl.when(step == 6)
    def _():
        receive_all(pack_far.third)
        corner_pack.start()

    @pl.when(step == SLOTS)
    def _():
        corner_pack.wait_recv()
        start_all(kept)

    @pl.when(step == SLOTS + 2)
    def _():
        receive_all(fc_far.second)
        start_all(fc_far.third)

    row0, col0, kind, inside, offset, live = slot_fields(rows)
    whole_window = inside == SPAN
    tables = (wrel, bits.at[kind], lanes, sides, keys.at[kind])

    def work(count):
        place = rows_at(offset, count)

        @pl.when(far == 0)
        def _():
            target, valid = positions(0, count, col0, kind, inside)
            source = xext[pl.ds(row0, WIN)].reshape(WIN * GRID, width)
            window = gather_window(source, target)
            xs[place, :] = window.astype(narrow)
            normal, _ = norm_parts(window)
            n1 = jnp.where(valid, normal * params[8:9] + params[9:10], 0.0).astype(narrow)
            n1_all[slot, :count] = n1

        _, valid = positions(0, count, col0, kind, inside)
        qbias = smalls[2 * far, 1:2, :half] + smalls[2 * far + 1, 2:3, :half]
        vbias = smalls[2 * far, 3:4, :half] + smalls[2 * far + 1, 4:5, :half]
        terms = attend(
            n1_all[slot, :count], valid, weights.at[far], qbias, vbias, *tables,
            qkv, mixed, peak.at[far],
        )
        attn[place, :] += jnp.where(valid, terms, 0.0)

    pl.when(live & whole_window)(functools.partial(work, ROWS))
    pl.when(live & jnp.logical_not(whole_window))(functools.partial(work, SHORT))

    @pl.when(step == 2 * SLOTS - 1)
    def _():
        g_own.wait()
        g_halo.wait_from_above()
        g_halo.wait_from_below()

        @pl.loop(0, SLOTS)
        def _(slot):
            row0, col0, kind, inside, offset, live = window_fields(rows, device, slot)

            @pl.when(live)
            def _():
                target, _ = positions(0, ROWS, col0, kind, inside)
                source = gext[pl.ds(row0, WIN)].reshape(WIN * GRID, width)
                gs[rows_at(offset, ROWS), :] = gather_window(source, target).astype(narrow)

        for halo in (x_halo, g_halo):
            halo.wait_send()
        for group in (pack_far, fc_far):
            for copy in group.first + group.second:
                copy.wait_send()
        for copy in pack_far.third + [corner_pack]:
            copy.wait_send()
        for copy in kept + fc_beside + fc_far.third:
            copy.wait()


def whole(shape):
    zeros = (0,) * len(shape)
    return pl.BlockSpec(shape, lambda *_: zeros, pipeline_mode=pl.Buffered(1))


def by_slot(shape):
    rest = (0,) * len(shape)
    return pl.BlockSpec((1,) + tuple(shape), lambda s, *_: (s,) + rest)


ANY = pl.BlockSpec(memory_space=pl.ANY)


def of(shape, dtype=narrow):
    return jax.ShapeDtypeStruct(shape, dtype)


def forward(x, g, wqkv, wproj, fc1, fc2, params, wrel, tables):
    rows, _, width = x.shape
    half = 2 * wproj.shape[0]
    slab = (SLAB, width)
    outs = [
        (of(slab), whole(slab)),
        (of(slab), whole(slab)),
        (of((SLOTS, ROWS, width)), whole((SLOTS, ROWS, width))),
        (of((2 * SLOTS, 4, ROWS, half)), by_slot((4, ROWS, half))),
        (of((2 * SLOTS, ROWS, half)), by_slot((ROWS, half))),
        (of(slab, single), whole(slab)),
        (of((2, 8, ROWS), single), whole((2, 8, ROWS))),
        (of((2, 4, half, width)), ANY),
        (of(fc1.shape), ANY),
        (of(fc2.shape), ANY),
        (of(fc1.shape), ANY),
        (of(fc2.shape), ANY),
        (of((SPLIT, 8, width), single), ANY),
    ]
    operands = (x, g, wqkv, wproj, fc1, fc2, params, params, wrel, *tables)
    ext = (rows + LEFT + RIGHT, GRID, width)
    return pl.pallas_call(
        forward_kernel,
        out_shape=[o[0] for o in outs],
        grid=(2 * SLOTS,),
        in_specs=[ANY] * 7 + [whole(a.shape) for a in operands[7:]],
        out_specs=[o[1] for o in outs],
        scratch_shapes=[
            pltpu.VMEM(ext, narrow),
            pltpu.VMEM(ext, narrow),
            pltpu.VMEM((2, 4, half, width), narrow),
            pltpu.VMEM((SPLIT, 8, width), single),
            pltpu.SemaphoreType.DMA((32,)),
            pltpu.SemaphoreType.DMA((32,)),
            pltpu.SemaphoreType.DMA((7,)),
        ],
        compiler_params=pltpu.CompilerParams(
            vmem_limit_bytes=VMEM, collective_id=0, has_side_effects=True
        ),
        cost_estimate=pl.CostEstimate(
            flops=26_000_000_000, bytes_accessed=60_000_000, transcendentals=8_000_000
        ),
        name="attention_forward",
    )(*operands)


CHUNK = SLAB // 3


def gelu_parts(z):
    size = jnp.abs(z)
    bell = jnp.exp(-0.5 * z * z)
    t = 1.0 / (1.0 + 0.2316418882663604 * size)
    poly = 0.5 * 1.061405429 * t + (0.5 * -1.453152027)
    poly = poly * t + 0.5 * 1.421413741
    poly = poly * t + 0.5 * -0.284496736
    poly = poly * t + 0.5 * 0.254829592
    tail = poly * t * bell
    phi_total = jnp.where(z >= 0, 1.0 - tail, tail)
    return z * phi_total, phi_total + z * bell * 0.3989422804014327


def mlp_kernel(
    xs, attn, gs, params, smalls, across1, across2, beside1, beside2, own1, own2,
    out, dx1, da, sums, near1, near2, far1, rest, gb,
    n2, n2t, gt, branch, dn2, w1, w2, grad1, grad2, got1, got2, near_got1, near_got2, landing,
    hs, zs, sends, recvs, locals_,
):
    step = pl.program_id(0)
    room = step % 2
    width = gs.shape[1]
    holder = jnp.where(step == 0, 2, jnp.where(step == 1, 3, jnp.where(step == 2, 1, 0)))
    beside, across, _ = partners(lax.axis_index("tensor"))
    send = Sender(sends, recvs, locals_)
    corners = [
        send.remote(0, across1, w1.at[1], {"tensor": beside}),
        send.remote(1, across2, w2.at[1], {"tensor": beside}),
    ]
    loads = [
        [send.local(2 * k, first, w1.at[at]), send.local(2 * k + 1, second, w2.at[at])]
        for k, (first, second, at) in enumerate(
            ((across1, across2, 0), (beside1, beside2, 0), (own1, own2, 1))
        )
    ]
    swaps = [
        send.remote(2, grad1.at[1], got1, {"tensor": beside}),
        send.remote(3, grad2.at[1], got2, {"tensor": beside}),
    ]
    crossing = send.remote(4, got1, far1, {"tensor": across})
    image = lax.axis_index("dp")
    mate = {"dp": mate_of(image, 0)}
    upper = got2.shape[0] // 2
    mine = (image % 2) * upper
    halving = send.remote(5, got2.at[rows_at(upper - mine, upper), :], landing, mate)
    near_swaps = [
        send.remote(6, grad1.at[2], near_got1, {"tensor": beside}),
        send.remote(7, grad2.at[2], near_got2, {"tensor": beside}),
    ]

    @pl.when(step == 0)
    def _():
        gb[...] = jnp.zeros_like(gb)
        start_all(loads[0])
        greet([{"tensor": beside}, {"tensor": across}, mate])
        start_all(corners)

        @pl.loop(0, SLAB // STRIP)
        def _(c):
            sl = rows_at(c * STRIP, STRIP)
            middle = xs[sl, :].astype(single) + (attn[sl, :] + params[10:11])
            dx1[sl, :] = middle
            normal, _ = norm_parts(middle)
            n2[sl, :] = (normal * params[11:12] + params[12:13]).astype(narrow)
            branch[sl, :] = jnp.zeros((STRIP, width), single)
            dn2[sl, :] = jnp.zeros((STRIP, width), single)

        for j in range(width // LANES):
            lanes = slice(j * LANES, (j + 1) * LANES)
            n2t[lanes, :] = n2[:, lanes].T
            gt[lanes, :] = gs[:, lanes].T
        for copy in loads[0]:
            copy.wait()

    @pl.when(step == 1)
    def _():
        start_all(loads[1])
        for copy in corners:
            copy.wait()

    @pl.when(step == 2)
    def _():
        start_all(swaps)
        start_all(loads[2])
        for copy in loads[1]:
            copy.wait()

    @pl.when(step == 3)
    def _():
        start_all(near_swaps)
        for copy in loads[2]:
            copy.wait()

    @pl.loop(0, SLAB // CHUNK)
    def _(c):
        @pl.when((step == 2) & (c == 1))
        def _():
            swaps[0].wait()
            add_rows(got1, 0, [(got1, 0), (grad1.at[0], 0)], got1.shape[0])
            crossing.start()
            swaps[1].wait()
            add_rows(got2, 0, [(got2, 0), (grad2.at[0], 0)], got2.shape[0])
            halving.start()

        sl = rows_at(c * CHUNK, CHUNK)
        z = dot(n2[sl, :], w1[room]) + smalls[holder, 0:1, :]
        dh = dot_nt(gs[sl, :], w2[room])
        act, slope = gelu_parts(z)
        h = act.astype(narrow)
        dz = (dh * slope).astype(narrow)
        hs[sl, :] = h
        zs[sl, :] = dz
        gb[holder, 0:1, :] += jnp.sum(dz.astype(single), axis=0, keepdims=True)
        branch[sl, :] += dot(h, w2[room])
        dn2[sl, :] += dot_nt(dz, w1[room])

    @pl.loop(0, 2)
    def _(r):
        sl = rows_at(r * (width // 2), width // 2)
        grad1[step, sl, :] = dot(n2t[sl, :], zs[...]).astype(narrow)
        grad2[step, sl, :] = dot(gt[sl, :], hs[...]).astype(narrow)

    @pl.when(step == 3)
    def _():
        halving.wait()
        add_rows(rest, 0, [(got2, mine), (landing, 0)], upper)
        for copy, near, grad, got in zip(
            near_swaps, (near1, near2), (grad1, grad2), (near_got1, near_got2), strict=True
        ):
            copy.wait()
            add_rows(near, 0, [(grad.at[3], 0), (got, 0)], near.shape[0])
        sums[...] = jnp.zeros_like(sums)

        @pl.loop(0, SLAB // STRIP)
        def _(c):
            sl = rows_at(c * STRIP, STRIP)
            middle = dx1[sl, :]
            normal, inverse = norm_parts(middle)
            out[sl, :] = (middle + (branch[sl, :] + params[13:14])).astype(narrow)
            grad = dn2[sl, :]
            cot = gs[sl, :].astype(single)
            total = cot + norm_back(grad, normal, inverse, params[11:12])
            dx1[sl, :] = total
            low = total.astype(narrow)
            da[sl, :] = low
            sums[0:1, :] += jnp.sum(grad * normal, axis=0, keepdims=True)
            sums[1:2, :] += jnp.sum(grad, axis=0, keepdims=True)
            sums[2:3, :] += jnp.sum(low.astype(single), axis=0, keepdims=True)
            sums[3:4, :] += jnp.sum(cot, axis=0, keepdims=True)

        crossing.wait()


def mlp(residents, across, beside, own):
    width, local = own[0].shape
    slab = (SLAB, width)
    square = (width, local)
    outs = [
        (of(slab), whole(slab)),
        (of(slab, single), whole(slab)),
        (of(slab), whole(slab)),
        (of((8, width), single), whole((8, width))),
        (of(square), whole(square)),
        (of(square), whole(square)),
        (of(square), ANY),
        (of((local // 2, width)), whole((local // 2, width))),
        (of((SPLIT, 8, local), single), whole((SPLIT, 8, local))),
    ]
    return pl.pallas_call(
        mlp_kernel,
        out_shape=[o[0] for o in outs],
        grid=(SPLIT,),
        in_specs=[whole(a.shape) for a in residents] + [ANY] * 6,
        out_specs=[o[1] for o in outs],
        scratch_shapes=[
            pltpu.VMEM(slab, narrow),
            *[pltpu.VMEM((width, SLAB), narrow)] * 2,
            *[pltpu.VMEM(slab, single)] * 2,
            *[pltpu.VMEM((2, *square), narrow)] * 2,
            *[pltpu.VMEM((SPLIT, *square), narrow)] * 2,
            *[pltpu.VMEM(square, narrow)] * 4,
            pltpu.VMEM((width // 2, local), narrow),
            *[pltpu.VMEM((SLAB, local), narrow)] * 2,
            pltpu.SemaphoreType.DMA((8,)),
            pltpu.SemaphoreType.DMA((8,)),
            pltpu.SemaphoreType.DMA((6,)),
        ],
        compiler_params=pltpu.CompilerParams(
            vmem_limit_bytes=VMEM, collective_id=1, has_side_effects=True
        ),
        cost_estimate=pl.CostEstimate(
            flops=36_000_000_000, bytes_accessed=60_000_000, transcendentals=8_000_000
        ),
        name="mlp",
    )(*residents, *across, *beside, *own)


def backward_kernel(
    rows_held, images,
    da, n1, qkv, mixed, weights, wrel, bits, lanes, sides, keys, xs, dx1, params, near1, near2, far1, rest,
    back, sums, keep, give, bias, grel, crossed, summed1, summed2,
    acc, dqkv, dmix, dn1, keep_far, give_far, got_far, held1, held2, land1, land2, rest_got,
    sends, recvs, locals_,
):
    step = pl.program_id(0)
    slot, far = step % SLOTS, 1 - step // SLOTS
    image = lax.axis_index("dp")
    beside, across, _ = partners(lax.axis_index("tensor"))
    send = Sender(sends, recvs, locals_)
    half, width = weights.shape[2:]
    per = Halver.copies(images)
    sum1 = Halver(send, 3, image, images, 0, held1.shape[0], (1, 0, 2))
    sum2 = Halver(send, 3 + per, image, images, 0, held2.shape[0], (0, 1, 2))
    rest_cross = send.remote(0, rest, rest_got, {"tensor": across})
    far_swap = send.remote(1, give_far, got_far, {"tensor": beside})
    far_cross = send.remote(2, got_far, crossed, {"tensor": across})

    halvers = ((sum1, held1, land1), (sum2, held2, land2))
    summed = (summed1, summed2)

    def seed(k, halver, held, summed):
        start, length = halver.final
        copy = send.local(k, held.at[rows_at(start, length), :], summed.at[rows_at(start, length), :])
        copy.start()
        copy.wait()

    def begin():
        greet([{"tensor": beside}, {"tensor": across}] + dp_mates(image, images))
        rest_cross.start()
        sum2.start(0, near2, land2)
        add_rows(held1, 0, [(near1, 0), (far1, 0)], held1.shape[0])
        sum1.start(0, held1, land1)

    def second():
        sum1.finish(0, held1, land1)
        sum1.start(1, held1, land1)
        sum2.out(0, near2, land2).wait()
        rest_cross.wait()
        _, kept, _, length, at = sum2.stages[0]
        add_rows(held2, kept, [(near2, kept), (land2, at), (rest_got, 0)], length)
        sum2.start(1, held2, land2)

    def third():
        for halver, held, land in halvers:
            halver.finish(1, held, land)
            halver.start(2, held, land)

    def fourth():
        for n, (halver, held, land) in enumerate(halvers):
            halver.finish(2, held, land)
            halver.extras(held, land)
            seed(n, halver, held, summed[n])
            halver.back(2, summed[n]).start()

    def hand(stage):
        for (halver, _, _), total in zip(halvers, summed, strict=True):
            halver.back(stage + 1, total).wait()
            halver.back(stage, total).start()

    def swap_far():
        far_swap.start()

    def cross_far():
        far_swap.wait()
        add_rows(got_far, 0, [(got_far, 0), (keep_far, 0)], got_far.shape[0])
        far_cross.start()

    events = {
        (0, 0): begin,
        (3, 0): second,
        (4, 2): third,
        (7, 0): swap_far,
        (7, 1): fourth,
        (8, 0): cross_far,
        (9, 2): functools.partial(hand, 1),
        (11, 0): functools.partial(hand, 0),
    }

    def fire(section):
        for (at, place), event in events.items():
            if place == section:
                pl.when(step == at)(event)

    _, col0, kind, inside, offset, live = slot_fields(rows_held)
    whole_window = inside == SPAN

    def on_window(action):
        for count, holds in ((ROWS, whole_window), (SHORT, jnp.logical_not(whole_window))):
            pl.when(live & holds)(functools.partial(action, count))

    @pl.when(slot == 0)
    def _():
        acc[...] = jnp.zeros_like(acc)

    @pl.when(step == 0)
    def _():
        for ref in (bias, grel, back, sums):
            ref[...] = jnp.zeros_like(ref)

    fire(0)

    def before_pairs(count):
        da_win = da[rows_at(offset, count), :]
        acc[3] += dot_tn(mixed[0, :count], da_win)
        dmix[:count] = dot_nt(da_win, weights[far, 3]).astype(narrow)

    on_window(before_pairs)

    def one_pair(pair, count):
        cut = slice(pair * LANES, (pair + 1) * LANES)
        q, k8, v, rel = (qkv[0, j, :n, cut] for j, n in enumerate((count, ROWS, ROWS, count)))
        do = dmix[:count, cut]
        dqs, dks, dvs = [], [], []
        for head in range(2):
            mine, other = sides[head : head + 1], sides[1 - head : 2 - head]
            full_key = k8 * mine + keys[kind] * other
            scores = dot_nt(full_key, q * mine + rel * other)
            top = jnp.max(scores, axis=0, keepdims=True)
            probs = jnp.exp(scores - top)
            probs = probs * (1.0 / jnp.sum(probs, axis=0, keepdims=True))
            dprobs = dot_nt(v, do * mine)
            mean = jnp.sum(probs * dprobs, axis=0, keepdims=True)
            dscores = (probs * (dprobs - mean)).astype(narrow)
            dvs.append(dot(probs.astype(narrow), do))
            dks.append(dot(dscores, q))
            dqs.append(dot_tn(dscores, full_key))
        low_lane = lax.broadcasted_iota(jnp.int32, (ROWS, LANES), 1) < 64
        dv = jnp.where(low_lane, dvs[0], dvs[1])
        dk = jnp.where(low_lane, dks[0], dks[1]) * 0.125
        low_lane = lax.broadcasted_iota(jnp.int32, (count, LANES), 1) < 64
        dq = jnp.where(low_lane, dqs[0], dqs[1])
        drel = jnp.where(low_lane, dqs[1], dqs[0]) * lanes[0:1]
        drel = shift_right(drel, bits.at[kind]).astype(narrow)
        dq = dq + dot(drel, wrel[...])
        grel[...] += dot_tn(drel, q)
        dqkv[0, :count, cut] = dq.astype(narrow)
        dqkv[1, :, cut] = dk.astype(narrow)
        dqkv[2, :, cut] = dv.astype(narrow)

    for pair in range(half // LANES):
        fire(pair + 1)
        on_window(functools.partial(one_pair, pair))

    def after_pairs(count):
        total = None
        for j in range(3):
            piece = dqkv[j, :count]
            acc[j] += dot_tn(piece, n1[0, :count])
            every = piece if j == 0 else dqkv[j]
            bias[far, j : j + 1, :] += jnp.sum(every.astype(single), axis=0, keepdims=True)
            back_part = dot(piece, weights[far, j])
            total = back_part if total is None else total + back_part

        @pl.when(far == 1)
        def _():
            dn1[slot, :count] = total

        @pl.when(far == 0)
        def _():
            _, valid = positions(0, count, col0, kind, inside)
            place = rows_at(offset, count)
            grad = jnp.where(valid, total + dn1[slot, :count], 0.0)
            normal, inverse = norm_parts(xs[place, :].astype(single))
            sums[0:1, :] += jnp.sum(grad * normal, axis=0, keepdims=True)
            sums[1:2, :] += jnp.sum(grad, axis=0, keepdims=True)
            result = dx1[place, :] + norm_back(grad, normal, inverse, params[8:9])
            back[place, :] = jnp.where(valid, result, 0.0).astype(narrow)

    on_window(after_pairs)

    def flush(keep, give):
        part = half // 2
        for j in range(4):
            keep[j * part : (j + 1) * part, :] = acc[j, :part, :].astype(narrow)
            give[j * part : (j + 1) * part, :] = acc[j, part:, :].astype(narrow)

    @pl.when(step == SLOTS - 1)
    def _():
        flush(keep_far, give_far)

    @pl.when(step == 2 * SLOTS - 1)
    def _():
        flush(keep, give)
        for (halver, _, _), total in zip(halvers, summed, strict=True):
            halver.back(0, total).wait()
        far_cross.wait()


def backward(rows_held, images, da, n1, qkv, mixed, weights, wrel, tables, residents, rest):
    half, width = weights.shape[2:]
    operands = [da, n1, qkv, mixed, weights, wrel, *tables, *residents, rest]
    in_specs = [whole(a.shape) for a in operands]
    in_specs[1] = pl.BlockSpec((1, ROWS, width), lambda i: (i % SLOTS, 0, 0))

    def halved(i):
        return (1 - i // SLOTS) * SLOTS + i % SLOTS

    in_specs[2] = pl.BlockSpec((1, 4, ROWS, half), lambda i: (halved(i), 0, 0, 0))
    in_specs[3] = pl.BlockSpec((1, ROWS, half), lambda i: (halved(i), 0, 0))
    in_specs[-1] = ANY
    packed = (2 * half, width)
    square = residents[3].shape
    outs = [
        (of((SLAB, width)), whole((SLAB, width))),
        (of((8, width), single), whole((8, width))),
        (of(packed), whole(packed)),
        (of(packed), whole(packed)),
        (of((2, 8, half), single), whole((2, 8, half))),
        (of((LANES, LANES), single), whole((LANES, LANES))),
        (of(packed), ANY),
        (of(square), ANY),
        (of(square), ANY),
    ]
    landing = (Halver.landing_rows(images, square[0]), width)
    copies = 3 + 2 * Halver.copies(images)
    return pl.pallas_call(
        functools.partial(backward_kernel, rows_held, images),
        out_shape=[o[0] for o in outs],
        grid=(2 * SLOTS,),
        in_specs=in_specs,
        out_specs=[o[1] for o in outs],
        scratch_shapes=[
            pltpu.VMEM((4, half, width), single),
            pltpu.VMEM((3, ROWS, half), narrow),
            pltpu.VMEM((ROWS, half), narrow),
            pltpu.VMEM((SLOTS, ROWS, width), single),
            *[pltpu.VMEM(packed, narrow)] * 3,
            *[pltpu.VMEM(square, narrow)] * 2,
            *[pltpu.VMEM(landing, narrow)] * 2,
            pltpu.VMEM(rest.shape, narrow),
            pltpu.SemaphoreType.DMA((copies,)),
            pltpu.SemaphoreType.DMA((copies,)),
            pltpu.SemaphoreType.DMA((2,)),
        ],
        compiler_params=pltpu.CompilerParams(
            vmem_limit_bytes=VMEM, collective_id=2, has_side_effects=True
        ),
        cost_estimate=pl.CostEstimate(
            flops=52_000_000_000, bytes_accessed=80_000_000, transcendentals=8_000_000
        ),
        name="attention_backward",
    )(*operands)


def clear_rows(ext):
    @pl.loop(0, ext.shape[0] // GRID)
    def _(r):
        ext[rows_at(r * GRID, GRID), :] = jnp.zeros((GRID, ext.shape[1]), narrow)


def place_windows(rows_held, device, slab, ext, first, last):
    @pl.loop(first, last)
    def _(slot):
        row0, col0, kind, inside, offset, live = window_fields(rows_held, device, slot)

        @pl.when(live)
        def _():
            target, _ = positions(1, ROWS, col0, kind, inside)
            token = lax.broadcasted_iota(jnp.int32, (WIN * GRID, ROWS), 0)
            choose = jnp.where(token == target, 1.0, 0.0).astype(narrow)
            window = slab[rows_at(offset, ROWS), :]
            where_to = pl.ds(pl.multiple_of(row0 * GRID, GRID), WIN * GRID)
            ext[where_to, :] += dot(choose, window).astype(narrow)


def tail_kernel(
    rows_held, images,
    out, back, keep, crossed, sums1, sums2, bias, rel_sum, fc_bias, peak, give,
    output, input_grad, packed, totals, tops,
    ext0, ext1, below0, below1, above0, above1, got, landing, held, sum_land, top_land, sends, recvs,
):
    device, image = lax.axis_index("tensor"), lax.axis_index("dp")
    beside, across, corner = partners(device)
    send = Sender(sends, recvs, None)
    per = Halver.copies(images)
    middle = held.shape[0] // 2
    landing_rows = Halver.landing_rows(images, middle)
    landings = [landing.at[pl.ds(k * landing_rows, landing_rows), :] for k in range(2)]
    halvers = [
        Halver(send, 1 + k * per, image, images, k * middle, middle, order)
        for k, order in enumerate(((0, 1, 2), (1, 0, 2)))
    ]
    halo_base = 1 + 2 * per
    small_base = halo_base + 4
    tokens = rows_held * GRID
    top, bottom = LEFT * GRID, RIGHT * GRID
    held_by = (device, beside, across, corner)
    mates = dp_mates(image, images)
    ring = [{"tensor": beside}, {"tensor": across}] + mates

    def reduce_start(stage):
        for halver, land in zip(halvers, landings, strict=True):
            halver.start(stage, held, land)

    def reduce_finish(stage):
        for halver, land in zip(halvers, landings, strict=True):
            halver.finish(stage, held, land)

    def hand_start(stage):
        for halver in halvers:
            halver.back(stage, packed).start()

    def hand_finish(stage):
        for halver in halvers:
            halver.back(stage, packed).wait()

    greet([{"tensor": place} for place in (beside, across, corner)] + mates)
    swap = send.remote(0, give, got, {"tensor": beside})
    swap.start()

    totals[...] = jnp.zeros_like(totals)
    tops[...] = jnp.zeros_like(tops)
    totals[0:2, :] = sums1[0:2, :]
    totals[2:6, :] = sums2[0:4, :]
    rel = rel_sum[...]
    rel = rel[HD:] + pltpu.roll(rel[:HD], HD, 1)
    for g in range(HD // 8):
        at = 8 * (1 + g // 6)
        totals[at : at + 8, (g % 6) * LANES : (g % 6 + 1) * LANES] = rel[8 * g : 8 * g + 8]
    half = bias.shape[2]
    for k in range(SPLIT):
        far, odd = k // 2, k % 2
        totals[pl.ds(24 + held_by[k], 1), :] = fc_bias[k, 0:1, :]
        for j, row in enumerate((0, 2)):
            value = bias[far, row : row + 1, :]
            if odd:
                value = pltpu.roll(value, half // 2, 1)
            totals[pl.ds(28 + held_by[k], 1), j * half : (j + 1) * half] = value
        best = jnp.broadcast_to(jnp.max(peak[far], axis=1, keepdims=True), (8, LANES))
        if odd:
            best = pltpu.roll(best, 8 - half // LANES, 0)
        tops[pl.ds(pl.multiple_of(held_by[k] * 8, 8), 8), :] = best

    def small_copies(k):
        return [
            send.remote(small_base + 2 * k, totals, sum_land.at[k], ring[k]),
            send.remote(small_base + 2 * k + 1, tops, top_land.at[k], ring[k]),
        ]

    def small_start(k):
        for copy in small_copies(k):
            copy.start()

    def small_finish(k):
        for copy in small_copies(k):
            copy.wait()
        totals[...] += sum_land[k]
        tops[...] = jnp.maximum(tops[...], top_land[k])

    def halo(base, ext, below, above):
        up = send.remote(
            base, ext.at[pl.ds(0, top), :], below, {"tensor": (device + SPLIT - 1) % SPLIT}
        )
        down = send.remote(
            base + 1, ext.at[pl.ds(top + tokens, bottom), :], above, {"tensor": (device + 1) % SPLIT}
        )
        return up, down

    def halo_start(copies):
        up, down = copies
        pl.when(device > 0)(up.start)
        pl.when(device < SPLIT - 1)(down.start)

    def halo_finish(copies, ext, below, above, result):
        up, down = copies
        pl.when(device > 0)(up.wait_send)
        pl.when(device < SPLIT - 1)(down.wait_send)
        add_rows(result, 0, [(ext, top)], tokens)

        @pl.when(device < SPLIT - 1)
        def _():
            up.wait_recv()
            at = tokens - top
            add_rows(result, at, [(result, at), (below, 0)], top)

        @pl.when(device > 0)
        def _():
            down.wait_recv()
            add_rows(result, 0, [(result, 0), (above, 0)], bottom)

    small_start(0)
    clear_rows(ext0)
    clear_rows(ext1)
    swap.wait()
    add_rows(held, 0, [(keep, 0), (got, 0), (crossed, 0)], held.shape[0])
    reduce_start(0)
    small_finish(0)
    small_start(1)
    place_windows(rows_held, device, back, ext1, 0, SLOTS)
    halos1 = halo(halo_base, ext1, below1, above1)
    halo_start(halos1)
    small_finish(1)
    small_start(2)
    reduce_finish(0)
    reduce_start(1)
    place_windows(rows_held, device, out, ext0, 0, 3)
    small_finish(2)
    small_start(3)
    reduce_finish(1)
    reduce_start(2)
    place_windows(rows_held, device, out, ext0, 3, SLOTS)
    halos0 = halo(halo_base + 2, ext0, below0, above0)
    halo_start(halos0)
    small_finish(3)
    small_start(4)
    reduce_finish(2)
    for halver, land in zip(halvers, landings, strict=True):
        halver.extras(held, land)
        start, length = halver.final
        packed[rows_at(start, length), :] = held[rows_at(start, length), :]
    hand_start(2)
    for k in range(4, len(ring)):
        small_finish(k)
        if k + 1 < len(ring):
            small_start(k + 1)
    halo_finish(halos1, ext1, below1, above1, input_grad)
    hand_finish(2)
    hand_start(1)
    hand_finish(1)
    hand_start(0)
    halo_finish(halos0, ext0, below0, above0, output)
    hand_finish(0)


def tail(rows_held, images, *operands):
    width = operands[0].shape[1]
    packed = operands[2].shape
    tokens = rows_held * GRID
    bits = images.bit_length() - 1
    landing = 2 * Halver.landing_rows(images, packed[0] // 2)
    copies = 1 + 2 * Halver.copies(images) + 4 + 2 * (2 + bits)
    ext = ((rows_held + LEFT + RIGHT) * GRID, width)
    outs = [
        of((tokens, width)), of((tokens, width)), of(packed),
        of((32, width), single), of((32, LANES), single),
    ]
    return pl.pallas_call(
        functools.partial(tail_kernel, rows_held, images),
        out_shape=outs,
        in_specs=[pl.BlockSpec(memory_space=pltpu.VMEM)] * (len(operands) - 1) + [ANY],
        out_specs=[pl.BlockSpec(memory_space=pltpu.VMEM)] * len(outs),
        scratch_shapes=[
            pltpu.VMEM(ext, narrow),
            pltpu.VMEM(ext, narrow),
            pltpu.VMEM((LEFT * GRID, width), narrow),
            pltpu.VMEM((LEFT * GRID, width), narrow),
            pltpu.VMEM((RIGHT * GRID, width), narrow),
            pltpu.VMEM((RIGHT * GRID, width), narrow),
            pltpu.VMEM(packed, narrow),
            pltpu.VMEM((landing, width), narrow),
            pltpu.VMEM(packed, narrow),
            pltpu.VMEM((2 + bits, 32, width), single),
            pltpu.VMEM((2 + bits, 32, LANES), single),
            pltpu.SemaphoreType.DMA((copies,)),
            pltpu.SemaphoreType.DMA((copies,)),
        ],
        compiler_params=pltpu.CompilerParams(
            vmem_limit_bytes=VMEM, collective_id=3, has_side_effects=True
        ),
        cost_estimate=pl.CostEstimate(
            flops=4_000_000_000, bytes_accessed=20_000_000, transcendentals=0
        ),
        name="tail",
    )(*operands)


def shards(
    inputs,
    w_qkv,
    qv_bias,
    w_proj,
    proj_bias,
    w_fc1,
    fc1_bias,
    w_fc2,
    fc2_bias,
    norm1_gain,
    norm1_shift,
    norm2_gain,
    norm2_shift,
    rel_h,
    rel_w,
    cotangent,
):
    width = inputs.shape[2]
    rows = inputs.shape[1] // GRID
    local = w_qkv.shape[2]
    heads = local // HD
    device = lax.axis_index("tensor")
    tables = lane_tables()

    span = 2 * WIN - 1
    wrel = sum(
        jnp.pad(table, ((at, LANES - span - at), (side, HD - side)))
        for table, at, side in (
            (rel_h, HD, 0), (rel_w, HD + 32, 0), (rel_h, 0, HD), (rel_w, 32, HD),
        )
    )

    entries = (
        (fc1_bias, 0, 0), (qv_bias[0], 1, 0), (qv_bias[0], 2, local), (qv_bias[1], 3, 0),
        (qv_bias[1], 4, local), (norm1_gain, 8, 0), (norm1_shift, 9, 0), (proj_bias, 10, 0),
        (norm2_gain, 11, 0), (norm2_shift, 12, 0), (fc2_bias, 13, 0),
    )
    params = 0.0
    for values, row, at in entries:
        before = row * width + at
        params = params + jnp.pad(values, (before, 16 * width - before - values.shape[0]))
    params = params.reshape(16, width)
    wqkv = w_qkv.transpose(0, 2, 1)

    (
        xs, gs, n1, qkv, mixed, attn, peak,
        weights, across1, across2, beside1, beside2, smalls,
    ) = forward(
        *(a.reshape(rows, GRID, width) for a in (inputs, cotangent)), wqkv, w_proj, w_fc1, w_fc2, params,
        wrel, tables
    )
    out, dx1, da, sums2, near1, near2, far1, rest, fc_bias = mlp(
        (
            xs, attn, gs, params, smalls,
        ),
        (across1, across2),
        (beside1, beside2),
        (w_fc1, w_fc2),
    )
    images = lax.axis_size("dp")
    back, sums1, keep, give, bias, rel_sum, crossed, summed1, summed2 = backward(
        rows, images, da, n1, qkv, mixed, weights, wrel, tables,
        [xs, dx1, params, near1, near2, far1], rest,
    )
    output, input_grad, gpack, totals, tops = tail(
        rows, images, out, back, keep, crossed, sums1, sums2, bias, rel_sum, fc_bias, peak, give
    )

    gpack = gpack.astype(single)
    blocks = totals[8:24].reshape(2, 8, 6, LANES).transpose(0, 2, 1, 3).reshape(-1, LANES)[:HD, :HD]
    grad_rel = jnp.stack([blocks[: 2 * WIN - 1], blocks[32 : 32 + 2 * WIN - 1]])
    qv = lax.dynamic_slice_in_dim(totals, 28 + device, 1)[0].reshape(2, 2 * local)[:, :local]
    head_max = lax.dynamic_slice(tops, (8 * device, 0), (heads, 1))[:, 0]
    factor = jnp.sqrt(CLIP / jnp.maximum(head_max, CLIP))
    clipped_qk = (w_qkv[:2].astype(single) * jnp.repeat(factor, HD)).astype(narrow)

    return (
        output[None],
        input_grad[None],
        gpack[: 3 * local].reshape(3, local, width).transpose(0, 2, 1),
        qv,
        gpack[3 * local :],
        totals[4],
        summed1.astype(single),
        lax.dynamic_slice_in_dim(totals, 24 + device, 1)[0],
        summed2.T.astype(single),
        totals[5],
        totals[:4],
        grad_rel,
        clipped_qk,
        head_max,
    )


def solution(mesh):
    return jax.shard_map(
        shards,
        mesh=mesh,
        in_specs=(
            P("dp", "tensor", None),
            P(None, None, "tensor"),
            P(None, "tensor"),
            P("tensor", None),
            P(),
            P(None, "tensor"),
            P("tensor"),
            P("tensor", None),
            P(),
            P(),
            P(),
            P(),
            P(),
            P(),
            P(),
            P("dp", "tensor", None),
        ),
        out_specs=(
            P("dp", "tensor", None),
            P("dp", "tensor", None),
            P(None, None, "tensor"),
            P(None, "tensor"),
            P("tensor", None),
            P(),
            P(None, "tensor"),
            P("tensor"),
            P("tensor", None),
            P(),
            P(),
            P(),
            P(None, None, "tensor"),
            P("tensor"),
        ),
        check_vma=False,
    )
```

```python
import functools

import jax
import jax.numpy as jnp
import numpy as np
from jax import lax
from jax.experimental import pallas as pl
from jax.experimental.pallas import tpu as pltpu
from jax.sharding import PartitionSpec as P

HD = 64
GRID = 64
WIN = 14
TILES = 5
SPAN = WIN * WIN
ROWS = 208
SLOTS = 7
EDGE = GRID % WIN
SHORT = EDGE * WIN
SLAB = (SLOTS - 2) * ROWS + SHORT
STRIP = SLAB // 6
SPLIT = 4
LEFT = 6
RIGHT = 12
LANES = 128
EPS = 1e-6
CLIP = 3.0
VMEM = 60 * 1024 * 1024

single = jnp.float32
narrow = jnp.bfloat16

def lane_tables():
    row = np.arange(ROWS)
    late = np.maximum(row - SHORT, 0)
    outer = WIN - EDGE
    orders = (
        (row // WIN, row % WIN),
        (
            np.where(row < SHORT, row // EDGE, late // outer),
            np.where(row < SHORT, row % EDGE, EDGE + late % outer),
        ),
    )
    lane = np.arange(LANES) % 64
    part = lane // 32
    at = lane % 32
    bits, keys = [], []
    for x, y in orders:
        amount = np.where(part[None, :] == 0, x[:, None], y[:, None])
        amount = np.where((row < SPAN)[:, None], amount, 0)
        bits.append(np.stack([(amount >> b) & 1 for b in range(4)]).astype(np.float32))
        place = WIN - 1 - np.where(part[None, :] == 0, x[:, None], y[:, None])
        hot = ((at % 16)[None, :] == place) & ((at % 16) < WIN)[None, :] & (row < SPAN)[:, None]
        hot = hot.astype(np.float32)
        hot[SPAN:, lane == 31] = -1e30
        keys.append(hot)
    lanes = np.zeros((8, LANES), np.float32)
    lanes[0] = at < WIN
    lanes[1] = (at >= 16) & (at < 16 + WIN)
    lanes[2] = lane == 31
    sides = np.zeros((16, LANES), np.float32)
    sides[0] = np.arange(LANES) < 64
    sides[1] = np.arange(LANES) >= 64
    return (
        jnp.asarray(np.stack(bits)),
        jnp.asarray(lanes),
        jnp.asarray(sides, narrow),
        jnp.asarray(np.stack(keys), narrow),
    )


def dot(a, b):
    return jnp.dot(a, b, preferred_element_type=single)


def dot_nt(a, b):
    return lax.dot_general(a, b, (((1,), (1,)), ((), ())), preferred_element_type=single)


def dot_tn(a, b):
    return lax.dot_general(a, b, (((0,), (0,)), ((), ())), preferred_element_type=single)


def norm_parts(values):
    centre = values - jnp.mean(values, axis=-1, keepdims=True)
    inverse = lax.rsqrt(jnp.mean(centre * centre, axis=-1, keepdims=True) + EPS)
    return centre * inverse, inverse


def norm_back(grad, normal, inverse, gain):
    scaled = grad * gain
    first = jnp.mean(scaled, axis=-1, keepdims=True)
    second = jnp.mean(scaled * normal, axis=-1, keepdims=True)
    return inverse * (scaled - first - normal * second)


def slot_fields(rows_held):
    return window_fields(rows_held, lax.axis_index("tensor"), pl.program_id(0) % SLOTS)


def window_fields(rows_held, device, slot):
    first = device * (SLOTS - 1)
    window = first + slot
    i, j = window // TILES, window % TILES
    last = device // (SPLIT - 1)
    live = slot < SLOTS - 1 + last
    row0 = i * WIN - device * rows_held + LEFT
    high = jnp.minimum(WIN, GRID - i * WIN)
    wide = jnp.minimum(WIN, GRID - j * WIN)

    def short_before(n):
        return jnp.minimum(n // TILES, TILES - 1) + jnp.maximum(n - TILES * (TILES - 1), 0)

    offset = ROWS * slot - (ROWS - SHORT) * (short_before(window) - short_before(first))
    return row0, j * WIN, j // (TILES - 1), high * wide, offset, live


def positions(axis, count, first_col, kind, inside):
    shape = (count, 1) if axis == 0 else (1, count)
    row = lax.broadcasted_iota(jnp.int32, shape, axis)
    x = lax.shift_right_logical(row * 4682, 16)
    plain = x * GRID + (row - x * WIN)
    x = lax.shift_right_logical(row, EDGE.bit_length() - 1)
    edge = x * GRID + (row - x * EDGE)
    token = jnp.where(kind == 1, edge, plain) + first_col
    return jnp.where(row < inside, token, -1), row < inside


def gather_window(source, target):
    token = lax.broadcasted_iota(jnp.int32, (target.shape[0], WIN * GRID), 1)
    choose = jnp.where(token == target, 1.0, 0.0).astype(narrow)
    return dot(choose, source)


def shift_left(values, bits):
    for b in range(4):
        taken = bits[b, : values.shape[0]] > 0.5
        values = jnp.where(taken, pltpu.roll(values, LANES - (1 << b), 1), values)
    return values


def shift_right(values, bits):
    for b in range(4):
        taken = bits[b, : values.shape[0]] > 0.5
        values = jnp.where(taken, pltpu.roll(values, 1 << b, 1), values)
    return values


def partners(device):
    beside = device + 1 - 2 * (device % 2)
    across = (device + 2) % SPLIT
    corner = (beside + 2) % SPLIT
    return beside, across, corner


def greet(places):
    barrier = pltpu.get_barrier_semaphore()
    for place in places:
        pl.semaphore_signal(barrier, inc=1, device_id=place, device_id_type=pl.DeviceIdType.MESH)
    pl.semaphore_wait(barrier, len(places))


class Sender:
    def __init__(self, sends, recvs, locals_):
        self.sends, self.recvs, self.locals = sends, recvs, locals_

    def remote(self, at, source, target, place):
        return pltpu.make_async_remote_copy(
            src_ref=source,
            dst_ref=target,
            send_sem=self.sends.at[at],
            recv_sem=self.recvs.at[at],
            device_id=place,
            device_id_type=pl.DeviceIdType.MESH,
        )

    def local(self, at, source, target):
        return pltpu.make_async_copy(source, target, self.locals.at[at])


def mate_of(image, bit):
    unit = 1 << bit
    return image + unit * (1 - 2 * ((image // unit) % 2))


def rows_at(start, count):
    return pl.ds(pl.multiple_of(start, 16), count)


def add_rows(target, target_at, sources, count):
    chunk = next(c for c in (96, 48, 16) if count % c == 0)

    @pl.loop(0, count // chunk)
    def _(c):
        total = None
        for ref, at in sources:
            value = ref[rows_at(at + c * chunk, chunk), :]
            total = value if total is None else total + value
        target[rows_at(target_at + c * chunk, chunk), :] = total


HALVINGS = 3


class Halver:
    def __init__(self, send, base, image, images, start, rows, order):
        bits = images.bit_length() - 1
        assert images == 1 << bits and bits >= HALVINGS
        self.send, self.base, self.image = send, base, image
        self.extra_bits = range(HALVINGS, bits)
        self.stages = []
        landing, length = 0, rows
        for bit in order:
            length //= 2
            mine = (image // (1 << bit)) % 2
            keep, give = start + mine * length, start + (1 - mine) * length
            self.stages.append((mate_of(image, bit), keep, give, length, landing))
            landing += length
            start = keep
        self.final = (start, length)
        self.landing = landing

    @staticmethod
    def copies(images):
        return 2 * HALVINGS + images.bit_length() - 1 - HALVINGS

    @staticmethod
    def landing_rows(images, rows):
        last = rows >> HALVINGS
        return rows - last + last * (images.bit_length() - 1 - HALVINGS)

    def out(self, stage, held, landing):
        mate, _, give, length, at = self.stages[stage]
        return self.send.remote(
            self.base + stage,
            held.at[rows_at(give, length), :],
            landing.at[pl.ds(at, length), :],
            {"dp": mate},
        )

    def start(self, stage, held, landing):
        self.out(stage, held, landing).start()

    def finish(self, stage, held, landing):
        self.out(stage, held, landing).wait()
        _, keep, _, length, at = self.stages[stage]
        add_rows(held, keep, [(held, keep), (landing, at)], length)

    def extras(self, held, landing):
        start, length = self.final
        for k, bit in enumerate(self.extra_bits):
            at = self.landing + k * length
            copy = self.send.remote(
                self.base + HALVINGS + k,
                held.at[rows_at(start, length), :],
                landing.at[pl.ds(at, length), :],
                {"dp": mate_of(self.image, bit)},
            )
            copy.start()
            copy.wait()
            add_rows(held, start, [(held, start), (landing, at)], length)

    def back(self, stage, held):
        mate, keep, _, length, _ = self.stages[stage]
        cut = rows_at(keep, length)
        at = self.base + HALVINGS + len(self.extra_bits) + stage
        return self.send.remote(at, held.at[cut, :], held.at[cut, :], {"dp": mate})


def dp_mates(image, images):
    return [{"dp": mate_of(image, bit)} for bit in range(images.bit_length() - 1)]


def project(n1, weights, qbias, vbias, projected, place):
    projected[0, place, :] = (dot_nt(n1, weights[0]) + qbias).astype(narrow)
    projected[1, place, :] = dot_nt(n1, weights[1]).astype(narrow) * jnp.asarray(0.125, narrow)
    projected[2, place, :] = (dot_nt(n1, weights[2]) + vbias).astype(narrow)


def attend(count, place, valid, projected, vbias, wrel, bits, lanes, sides, keys, qkv, mixed, peak):
    half = projected.shape[2]
    qkv[0, 0, :count] = jnp.where(valid, projected[0, place, :].astype(single), 0.0).astype(narrow)
    qkv[0, 1, :count] = projected[1, place, :]
    qkv[0, 2, :count] = projected[2, place, :]
    if count < ROWS:
        left = ROWS - count
        qkv[0, 1, count:] = jnp.zeros((left, half), narrow)
        qkv[0, 2, count:] = jnp.broadcast_to(vbias, (left, half)).astype(narrow)
    low_lane = lax.broadcasted_iota(jnp.int32, (count, LANES), 1) < 64
    for pair in range(half // LANES):
        cut = slice(pair * LANES, (pair + 1) * LANES)
        q, k8, v = qkv[0, 0, :count, cut], qkv[0, 1, :, cut], qkv[0, 2, :, cut]
        rel = shift_left(dot_nt(q, wrel[...]), bits)
        rest = rel - rel.astype(narrow).astype(single)
        rel = rel * lanes[0:1] + pltpu.roll(rest, 16, 1) * lanes[1:2] + lanes[2:3]
        rel = rel.astype(narrow)
        qkv[0, 3, :count, cut] = rel
        pieces = []
        for head in range(2):
            mine, other = sides[head : head + 1], sides[1 - head : 2 - head]
            only = q * mine
            logits = dot_nt(only, k8)
            at = 2 * pair + head
            peak[at : at + 1, :] = jnp.maximum(
                peak[at : at + 1, :], jnp.max(logits, axis=0, keepdims=True)
            )
            scores = dot_nt(only + rel * other, k8 * mine + keys[...] * other)
            top = jnp.max(scores, axis=1, keepdims=True)
            probs = jnp.exp(scores - top)
            total = jnp.sum(probs, axis=1, keepdims=True)
            pieces.append(dot(probs.astype(narrow), v) * (1.0 / total))
        mixed[place, cut] = jnp.where(low_lane, pieces[0], pieces[1]).astype(narrow)


class Halo:
    def __init__(self, send, base, grid, ext, device, rows):
        below, above = {"tensor": (device + 1) % SPLIT}, {"tensor": (device + SPLIT - 1) % SPLIT}
        self.has_below, self.has_above = device < SPLIT - 1, device > 0
        self.cross_below, self.cross_above = device == 1, device == 2

        def copy(at, first, count, first_col, cols, target_row, place):
            window = (pl.ds(first, count), pl.ds(first_col, cols), slice(None))
            return send.remote(
                at, grid.at[window], ext.at[(pl.ds(target_row, count), *window[1:])], place
            )

        few, many = 4, 10
        self.down = copy(base, rows - LEFT, LEFT, 0, GRID, 0, below)
        self.down_cross = copy(base, rows - few, few, 16, GRID - 16, LEFT - few, below)
        self.up = copy(base + 1, 0, RIGHT, 0, GRID, LEFT + rows, above)
        self.up_cross = copy(base + 1, 0, many, 0, 32, LEFT + rows, above)

    def _each(self, down_here, up_here, act):
        for here, crossing, plain, crossed in (
            (*down_here, self.down, self.down_cross),
            (*up_here, self.up, self.up_cross),
        ):

            @pl.when(here & jnp.logical_not(crossing))
            def _():
                act(plain)

            @pl.when(crossing)
            def _():
                act(crossed)

    def _senders(self, act):
        self._each((self.has_below, self.cross_below), (self.has_above, self.cross_above), act)

    def start(self):
        self._senders(lambda copy: copy.start())

    def wait_send(self):
        self._senders(lambda copy: copy.wait_send())

    def wait_from_above(self):
        pl.when(self.has_above & jnp.logical_not(self.cross_above))(self.down.wait_recv)
        pl.when(self.cross_above)(self.down_cross.wait_recv)

    def wait_from_below(self):
        pl.when(self.has_below & jnp.logical_not(self.cross_below))(self.up.wait_recv)
        pl.when(self.cross_below)(self.up_cross.wait_recv)


class Quartet:
    def __init__(self, send, base, image, pieces, across):
        side, deep = image % 2, (image // 2) % 2
        beside, behind = {"dp": mate_of(image, 0)}, {"dp": mate_of(image, 1)}
        mine = 2 * deep + side
        from_beside, from_behind = 2 * deep + 1 - side, 2 * (1 - deep) + side
        self.first, self.second, self.third = [], [], []
        for k, (source, target, view) in enumerate(pieces):
            at = base + 5 * k

            def copy(number, origin, quarter, part, place):
                return send.remote(at + number, view(origin, quarter, part), view(target, quarter, part), place)

            self.first.append(copy(0, source, mine, None, across))
            self.second.append(copy(1, target, mine, None, beside))
            self.second.append(copy(2, target, mine, None, behind))
            if view(target, from_behind, 0) is not None:
                self.third.append(copy(3, target, from_behind, 0, beside))
            self.third.append(copy(4, target, from_beside, 1, behind))


def quarter_rows(array, quarter, part):
    size = array.shape[0] // 4
    start = quarter * size
    if part is not None:
        size //= 2
        start += part * size
    return array.at[rows_at(start, size), :]


def start_all(copies):
    for copy in copies:
        copy.start()


def receive_all(copies):
    for copy in copies:
        copy.wait_recv()


def forward_kernel(
    x, g, wqkv, wproj, fc1, fc2, notes_in, params, wrel, bits, lanes, sides, keys,
    xs, gs, n1_all, qkv, mixed, attn, peak, weights_out, across1, across2, beside1, beside2, small_out,
    xext, gext, weights, smalls, projected, sends, recvs, locals_,
):
    step = pl.program_id(0)
    far, slot = step // SLOTS, step % SLOTS
    device, image = lax.axis_index("tensor"), lax.axis_index("dp")
    rows, _, width = x.shape
    part = wproj.shape[0]
    half = 2 * part
    beside, across, corner = partners(device)
    send = Sender(sends, recvs, locals_)
    x_halo = Halo(send, 0, x, xext, device, rows)
    g_halo = Halo(send, 2, g, gext, device, rows)
    small = notes_in.at[pl.ds(0, 8), :]

    own_pack = [
        send.remote(4, wqkv, weights.at[0, 0:3, pl.ds(part, part), :], {"tensor": beside}),
        send.remote(5, wproj, weights.at[0, 3, pl.ds(part, part), :], {"tensor": beside}),
    ]
    notes = [
        send.remote(6 + k, small, smalls.at[k + 1], {"tensor": place})
        for k, place in enumerate((beside, across, corner))
    ]
    fc_beside = [
        send.remote(9, fc1, beside1, {"tensor": beside}),
        send.remote(10, fc2, beside2, {"tensor": beside}),
    ]
    corner_pack = send.remote(
        11, weights.at[1, :, pl.ds(0, part), :], weights.at[1, :, pl.ds(part, part), :], {"tensor": beside}
    )

    def of_qkv(array, quarter, half_of):
        size = part // 4
        cut = rows_at(quarter * size, size)
        if array is wqkv:
            return array.at[:, cut, :]
        if half_of is None:
            return array.at[1, 0:3, cut, :]
        return array.at[1, 0:2, cut, :] if half_of == 0 else array.at[1, 2:3, cut, :]

    def of_proj(array, quarter, half_of):
        size = part // 4
        cut = rows_at(quarter * size, size)
        if array is wproj:
            return array.at[cut, :]
        return None if half_of == 0 else array.at[1, 3, cut, :]

    pack_far = Quartet(
        send, 12, image, ((wqkv, weights, of_qkv), (wproj, weights, of_proj)), {"tensor": across}
    )
    fc_far = Quartet(
        send, 22, image, ((fc1, across1, quarter_rows), (fc2, across2, quarter_rows)), {"tensor": across}
    )
    own = [
        send.local(0, wqkv, weights.at[0, 0:3, pl.ds(0, part), :]),
        send.local(1, wproj, weights.at[0, 3, pl.ds(0, part), :]),
        send.local(2, x, xext.at[pl.ds(LEFT, rows)]),
        send.local(3, small, smalls.at[0]),
    ]
    g_own = send.local(4, g, gext.at[pl.ds(LEFT, rows)])
    kept = [send.local(5, weights, weights_out), send.local(6, smalls, small_out)]

    @pl.when(step == 0)
    def _():
        for ref in (xext, gext):
            ref[pl.ds(0, LEFT)] = jnp.zeros((LEFT, GRID, width), narrow)
            ref[pl.ds(LEFT + rows, RIGHT)] = jnp.zeros((RIGHT, GRID, width), narrow)
        greet(
            [{"tensor": place} for place in (beside, across, corner)]
            + [{"dp": mate_of(image, bit)} for bit in range(2)]
        )
        start_all(own_pack + notes + own)
        x_halo.start()
        start_all(pack_far.first)
        for ref in (xs, gs, n1_all, mixed, peak):
            ref[...] = jnp.zeros_like(ref)
        for copy in own + notes + own_pack:
            copy.wait()
        x_halo.wait_from_above()

    @pl.when(step == 1)
    def _():
        start_all(fc_beside + [g_own])

    @pl.when(step == 2)
    def _():
        receive_all(pack_far.first)
        start_all(pack_far.second)
        start_all(fc_far.first)

    @pl.when(step == 3)
    def _():
        x_halo.wait_from_below()

    @pl.when(step == 4)
    def _():
        receive_all(pack_far.second)
        start_all(pack_far.third)

    @pl.when(step == 5)
    def _():
        receive_all(fc_far.first)
        start_all(fc_far.second)
        g_halo.start()

    @pl.when(step == 6)
    def _():
        receive_all(pack_far.third)
        corner_pack.start()

    @pl.when(step == SLOTS)
    def _():
        corner_pack.wait_recv()
        start_all(kept)

    @pl.when(step == SLOTS + 2)
    def _():
        receive_all(fc_far.second)
        start_all(fc_far.third)

    row0, col0, kind, inside, offset, live = slot_fields(rows)
    whole_window = inside == SPAN
    tables = (wrel, bits.at[kind], lanes, sides, keys.at[kind])

    def biases(which):
        return (
            smalls[2 * which, 1:2, :half] + smalls[2 * which + 1, 2:3, :half],
            smalls[2 * which, 3:4, :half] + smalls[2 * which + 1, 4:5, :half],
        )

    @pl.when(step == SLOTS)
    def _():
        project(n1_all[...], weights.at[1], *biases(1), projected, slice(None))

    def work(count):
        place = rows_at(offset, count)

        @pl.when(far == 0)
        def _():
            target, valid = positions(0, count, col0, kind, inside)
            source = xext[pl.ds(row0, WIN)].reshape(WIN * GRID, width)
            window = gather_window(source, target)
            xs[place, :] = window.astype(narrow)
            normal, _ = norm_parts(window)
            n1 = jnp.where(valid, normal * params[8:9] + params[9:10], 0.0).astype(narrow)
            n1_all[place, :] = n1
            project(n1, weights.at[0], *biases(0), projected, place)

        _, valid = positions(0, count, col0, kind, inside)
        attend(
            count, place, valid, projected, biases(far)[1], *tables, qkv, mixed.at[far], peak.at[far]
        )

    pl.when(live & whole_window)(functools.partial(work, ROWS))
    pl.when(live & jnp.logical_not(whole_window))(functools.partial(work, SHORT))

    @pl.when(step == 2 * SLOTS - 1)
    def _():
        attn[...] = dot(mixed[0], weights[0, 3]) + dot(mixed[1], weights[1, 3])
        g_own.wait()
        g_halo.wait_from_above()
        g_halo.wait_from_below()

        @pl.loop(0, SLOTS)
        def _(slot):
            row0, col0, kind, inside, offset, live = window_fields(rows, device, slot)

            @pl.when(live)
            def _():
                target, _ = positions(0, ROWS, col0, kind, inside)
                source = gext[pl.ds(row0, WIN)].reshape(WIN * GRID, width)
                gs[rows_at(offset, ROWS), :] = gather_window(source, target).astype(narrow)

        for halo in (x_halo, g_halo):
            halo.wait_send()
        for group in (pack_far, fc_far):
            for copy in group.first + group.second:
                copy.wait_send()
        for copy in pack_far.third + [corner_pack]:
            copy.wait_send()
        for copy in kept + fc_beside + fc_far.third:
            copy.wait()


def whole(shape):
    zeros = (0,) * len(shape)
    return pl.BlockSpec(shape, lambda *_: zeros, pipeline_mode=pl.Buffered(1))


def by_slot(shape):
    rest = (0,) * len(shape)
    return pl.BlockSpec((1,) + tuple(shape), lambda s, *_: (s,) + rest)


ANY = pl.BlockSpec(memory_space=pl.ANY)


def of(shape, dtype=narrow):
    return jax.ShapeDtypeStruct(shape, dtype)


def forward(x, g, wqkv, wproj, fc1, fc2, params, wrel, tables):
    rows, _, width = x.shape
    half = 2 * wproj.shape[0]
    slab = (SLAB, width)
    outs = [
        (of(slab), whole(slab)),
        (of(slab), whole(slab)),
        (of(slab), whole(slab)),
        (of((2 * SLOTS, 4, ROWS, half)), by_slot((4, ROWS, half))),
        (of((2, SLAB, half)), whole((2, SLAB, half))),
        (of(slab, single), whole(slab)),
        (of((2, 8, ROWS), single), whole((2, 8, ROWS))),
        (of((2, 4, half, width)), ANY),
        (of(fc1.shape), ANY),
        (of(fc2.shape), ANY),
        (of(fc1.shape), ANY),
        (of(fc2.shape), ANY),
        (of((SPLIT, 8, width), single), ANY),
    ]
    operands = (x, g, wqkv, wproj, fc1, fc2, params, params, wrel, *tables)
    ext = (rows + LEFT + RIGHT, GRID, width)
    return pl.pallas_call(
        forward_kernel,
        out_shape=[o[0] for o in outs],
        grid=(2 * SLOTS,),
        in_specs=[ANY] * 7 + [whole(a.shape) for a in operands[7:]],
        out_specs=[o[1] for o in outs],
        scratch_shapes=[
            pltpu.VMEM(ext, narrow),
            pltpu.VMEM(ext, narrow),
            pltpu.VMEM((2, 4, half, width), narrow),
            pltpu.VMEM((SPLIT, 8, width), single),
            pltpu.VMEM((3, SLAB, half), narrow),
            pltpu.SemaphoreType.DMA((32,)),
            pltpu.SemaphoreType.DMA((32,)),
            pltpu.SemaphoreType.DMA((7,)),
        ],
        compiler_params=pltpu.CompilerParams(
            vmem_limit_bytes=VMEM, collective_id=0, has_side_effects=True
        ),
        cost_estimate=pl.CostEstimate(
            flops=26_000_000_000, bytes_accessed=60_000_000, transcendentals=8_000_000
        ),
        name="attention_forward",
    )(*operands)


CHUNK = SLAB // 3


def gelu_parts(z):
    size = jnp.abs(z)
    bell = jnp.exp(-0.5 * z * z)
    t = 1.0 / (1.0 + 0.2316418882663604 * size)
    poly = 0.5 * 1.061405429 * t + (0.5 * -1.453152027)
    poly = poly * t + 0.5 * 1.421413741
    poly = poly * t + 0.5 * -0.284496736
    poly = poly * t + 0.5 * 0.254829592
    tail = poly * t * bell
    phi_total = jnp.where(z >= 0, 1.0 - tail, tail)
    return z * phi_total, phi_total + z * bell * 0.3989422804014327


def mlp_kernel(
    xs, attn, gs, params, smalls, across1, across2, beside1, beside2, own1, own2,
    out, dx1, da, sums, near1, near2, far1, rest, gb,
    n2, n2t, gt, branch, dn2, w1, w2, grad1, grad2, got1, got2, near_got1, near_got2, landing,
    hs, zs, sends, recvs, locals_,
):
    step = pl.program_id(0)
    room = step % 2
    width = gs.shape[1]
    holder = jnp.where(step == 0, 2, jnp.where(step == 1, 3, jnp.where(step == 2, 1, 0)))
    beside, across, _ = partners(lax.axis_index("tensor"))
    send = Sender(sends, recvs, locals_)
    corners = [
        send.remote(0, across1, w1.at[1], {"tensor": beside}),
        send.remote(1, across2, w2.at[1], {"tensor": beside}),
    ]
    loads = [
        [send.local(2 * k, first, w1.at[at]), send.local(2 * k + 1, second, w2.at[at])]
        for k, (first, second, at) in enumerate(
            ((across1, across2, 0), (beside1, beside2, 0), (own1, own2, 1))
        )
    ]
    swaps = [
        send.remote(2, grad1.at[1], got1, {"tensor": beside}),
        send.remote(3, grad2.at[1], got2, {"tensor": beside}),
    ]
    crossing = send.remote(4, got1, far1, {"tensor": across})
    image = lax.axis_index("dp")
    mate = {"dp": mate_of(image, 0)}
    upper = got2.shape[0] // 2
    mine = (image % 2) * upper
    halving = send.remote(5, got2.at[rows_at(upper - mine, upper), :], landing, mate)
    near_swaps = [
        send.remote(6, grad1.at[2], near_got1, {"tensor": beside}),
        send.remote(7, grad2.at[2], near_got2, {"tensor": beside}),
    ]

    @pl.when(step == 0)
    def _():
        gb[...] = jnp.zeros_like(gb)
        start_all(loads[0])
        greet([{"tensor": beside}, {"tensor": across}, mate])
        start_all(corners)

        @pl.loop(0, SLAB // STRIP)
        def _(c):
            sl = rows_at(c * STRIP, STRIP)
            middle = xs[sl, :].astype(single) + (attn[sl, :] + params[10:11])
            dx1[sl, :] = middle
            normal, _ = norm_parts(middle)
            n2[sl, :] = (normal * params[11:12] + params[12:13]).astype(narrow)
            branch[sl, :] = jnp.zeros((STRIP, width), single)
            dn2[sl, :] = jnp.zeros((STRIP, width), single)

        for j in range(width // LANES):
            lanes = slice(j * LANES, (j + 1) * LANES)
            n2t[lanes, :] = n2[:, lanes].T
            gt[lanes, :] = gs[:, lanes].T
        for copy in loads[0]:
            copy.wait()

    @pl.when(step == 1)
    def _():
        start_all(loads[1])
        for copy in corners:
            copy.wait()

    @pl.when(step == 2)
    def _():
        start_all(swaps)
        start_all(loads[2])
        for copy in loads[1]:
            copy.wait()

    @pl.when(step == 3)
    def _():
        start_all(near_swaps)
        for copy in loads[2]:
            copy.wait()

    @pl.loop(0, SLAB // CHUNK)
    def _(c):
        @pl.when((step == 2) & (c == 1))
        def _():
            swaps[0].wait()
            add_rows(got1, 0, [(got1, 0), (grad1.at[0], 0)], got1.shape[0])
            crossing.start()
            swaps[1].wait()
            add_rows(got2, 0, [(got2, 0), (grad2.at[0], 0)], got2.shape[0])
            halving.start()

        sl = rows_at(c * CHUNK, CHUNK)
        z = dot(n2[sl, :], w1[room]) + smalls[holder, 0:1, :]
        dh = dot_nt(gs[sl, :], w2[room])
        act, slope = gelu_parts(z)
        h = act.astype(narrow)
        dz = (dh * slope).astype(narrow)
        hs[sl, :] = h
        zs[sl, :] = dz
        gb[holder, 0:1, :] += jnp.sum(dz.astype(single), axis=0, keepdims=True)
        branch[sl, :] += dot(h, w2[room])
        dn2[sl, :] += dot_nt(dz, w1[room])

    @pl.loop(0, 2)
    def _(r):
        sl = rows_at(r * (width // 2), width // 2)
        grad1[step, sl, :] = dot(n2t[sl, :], zs[...]).astype(narrow)
        grad2[step, sl, :] = dot(gt[sl, :], hs[...]).astype(narrow)

    @pl.when(step == 3)
    def _():
        halving.wait()
        add_rows(rest, 0, [(got2, mine), (landing, 0)], upper)
        for copy, near, grad, got in zip(
            near_swaps, (near1, near2), (grad1, grad2), (near_got1, near_got2), strict=True
        ):
            copy.wait()
            add_rows(near, 0, [(grad.at[3], 0), (got, 0)], near.shape[0])
        sums[...] = jnp.zeros_like(sums)

        @pl.loop(0, SLAB // STRIP)
        def _(c):
            sl = rows_at(c * STRIP, STRIP)
            middle = dx1[sl, :]
            normal, inverse = norm_parts(middle)
            out[sl, :] = (middle + (branch[sl, :] + params[13:14])).astype(narrow)
            grad = dn2[sl, :]
            cot = gs[sl, :].astype(single)
            total = cot + norm_back(grad, normal, inverse, params[11:12])
            dx1[sl, :] = total
            low = total.astype(narrow)
            da[sl, :] = low
            sums[0:1, :] += jnp.sum(grad * normal, axis=0, keepdims=True)
            sums[1:2, :] += jnp.sum(grad, axis=0, keepdims=True)
            sums[2:3, :] += jnp.sum(low.astype(single), axis=0, keepdims=True)
            sums[3:4, :] += jnp.sum(cot, axis=0, keepdims=True)

        crossing.wait()


def mlp(residents, across, beside, own):
    width, local = own[0].shape
    slab = (SLAB, width)
    square = (width, local)
    outs = [
        (of(slab), whole(slab)),
        (of(slab, single), whole(slab)),
        (of(slab), whole(slab)),
        (of((8, width), single), whole((8, width))),
        (of(square), whole(square)),
        (of(square), whole(square)),
        (of(square), ANY),
        (of((local // 2, width)), whole((local // 2, width))),
        (of((SPLIT, 8, local), single), whole((SPLIT, 8, local))),
    ]
    return pl.pallas_call(
        mlp_kernel,
        out_shape=[o[0] for o in outs],
        grid=(SPLIT,),
        in_specs=[whole(a.shape) for a in residents] + [ANY] * 6,
        out_specs=[o[1] for o in outs],
        scratch_shapes=[
            pltpu.VMEM(slab, narrow),
            *[pltpu.VMEM((width, SLAB), narrow)] * 2,
            *[pltpu.VMEM(slab, single)] * 2,
            *[pltpu.VMEM((2, *square), narrow)] * 2,
            *[pltpu.VMEM((SPLIT, *square), narrow)] * 2,
            *[pltpu.VMEM(square, narrow)] * 4,
            pltpu.VMEM((width // 2, local), narrow),
            *[pltpu.VMEM((SLAB, local), narrow)] * 2,
            pltpu.SemaphoreType.DMA((8,)),
            pltpu.SemaphoreType.DMA((8,)),
            pltpu.SemaphoreType.DMA((6,)),
        ],
        compiler_params=pltpu.CompilerParams(
            vmem_limit_bytes=VMEM, collective_id=1, has_side_effects=True
        ),
        cost_estimate=pl.CostEstimate(
            flops=36_000_000_000, bytes_accessed=60_000_000, transcendentals=8_000_000
        ),
        name="mlp",
    )(*residents, *across, *beside, *own)


def backward_kernel(
    rows_held, images,
    da, n1, qkv, mixed, wproj, wrel, bits, lanes, sides, keys, near1, near2, far1, rest,
    dqkv, keep, give, bias, grel, crossed, summed1, summed2,
    dmix, got_far, held1, held2, land1, land2, rest_got,
    sends, recvs, locals_,
):
    step = pl.program_id(0)
    slot, far = step % SLOTS, 1 - step // SLOTS
    image = lax.axis_index("dp")
    beside, across, _ = partners(lax.axis_index("tensor"))
    send = Sender(sends, recvs, locals_)
    half = wproj.shape[2]
    per = Halver.copies(images)
    sum1 = Halver(send, 3, image, images, 0, held1.shape[0], (1, 0, 2))
    sum2 = Halver(send, 3 + per, image, images, 0, held2.shape[0], (0, 1, 2))
    rest_cross = send.remote(0, rest, rest_got, {"tensor": across})
    far_swap = send.remote(1, give.at[0], got_far, {"tensor": beside})
    far_cross = send.remote(2, got_far, crossed, {"tensor": across})

    halvers = ((sum1, held1, land1), (sum2, held2, land2))
    summed = (summed1, summed2)

    def seed(k, halver, held, summed):
        start, length = halver.final
        copy = send.local(k, held.at[rows_at(start, length), :], summed.at[rows_at(start, length), :])
        copy.start()
        copy.wait()

    def begin():
        greet([{"tensor": beside}, {"tensor": across}] + dp_mates(image, images))
        rest_cross.start()
        sum2.start(0, near2, land2)
        add_rows(held1, 0, [(near1, 0), (far1, 0)], held1.shape[0])
        sum1.start(0, held1, land1)

    def second():
        sum1.finish(0, held1, land1)
        sum1.start(1, held1, land1)
        sum2.out(0, near2, land2).wait()
        rest_cross.wait()
        _, kept, _, length, at = sum2.stages[0]
        add_rows(held2, kept, [(near2, kept), (land2, at), (rest_got, 0)], length)
        sum2.start(1, held2, land2)

    def third():
        for halver, held, land in halvers:
            halver.finish(1, held, land)
            halver.start(2, held, land)

    def fourth():
        for n, (halver, held, land) in enumerate(halvers):
            halver.finish(2, held, land)
            halver.extras(held, land)
            seed(n, halver, held, summed[n])
            halver.back(2, summed[n]).start()

    def hand(stage):
        for (halver, _, _), total in zip(halvers, summed, strict=True):
            halver.back(stage + 1, total).wait()
            halver.back(stage, total).start()

    def swap_far():
        far_swap.start()

    def cross_far():
        far_swap.wait()
        add_rows(got_far, 0, [(got_far, 0), (keep.at[0], 0)], got_far.shape[0])
        far_cross.start()

    events = {
        (0, 0): begin,
        (3, 0): second,
        (4, 2): third,
        (7, 0): swap_far,
        (7, 1): fourth,
        (8, 0): cross_far,
        (9, 2): functools.partial(hand, 1),
        (11, 0): functools.partial(hand, 0),
    }

    def fire(section):
        for (at, place), event in events.items():
            if place == section:
                pl.when(step == at)(event)

    _, col0, kind, inside, offset, live = slot_fields(rows_held)
    whole_window = inside == SPAN

    def on_window(action):
        for count, holds in ((ROWS, whole_window), (SHORT, jnp.logical_not(whole_window))):
            pl.when(live & holds)(functools.partial(action, count))

    @pl.when(step == 0)
    def _():
        for ref in (bias, grel, dqkv):
            ref[...] = jnp.zeros_like(ref)

    fire(0)

    @pl.when(slot == 0)
    def _():
        dmix[...] = dot_nt(da[...], wproj[far, 0]).astype(narrow)

    def one_pair(pair, count):
        cut = slice(pair * LANES, (pair + 1) * LANES)
        q, k8, v, rel = (qkv[0, j, :n, cut] for j, n in enumerate((count, ROWS, ROWS, count)))
        place = rows_at(offset, count)
        do = dmix[place, cut]
        dqs, dks, dvs = [], [], []
        for head in range(2):
            mine, other = sides[head : head + 1], sides[1 - head : 2 - head]
            full_key = k8 * mine + keys[kind] * other
            scores = dot_nt(full_key, q * mine + rel * other)
            top = jnp.max(scores, axis=0, keepdims=True)
            probs = jnp.exp(scores - top)
            probs = probs * (1.0 / jnp.sum(probs, axis=0, keepdims=True))
            dprobs = dot_nt(v, do * mine)
            mean = jnp.sum(probs * dprobs, axis=0, keepdims=True)
            dscores = (probs * (dprobs - mean)).astype(narrow)
            dvs.append(dot(probs.astype(narrow), do))
            dks.append(dot(dscores, q))
            dqs.append(dot_tn(dscores, full_key))
        low_lane = lax.broadcasted_iota(jnp.int32, (ROWS, LANES), 1) < 64
        dv = jnp.where(low_lane, dvs[0], dvs[1])
        dk = jnp.where(low_lane, dks[0], dks[1]) * 0.125
        low_lane = lax.broadcasted_iota(jnp.int32, (count, LANES), 1) < 64
        dq = jnp.where(low_lane, dqs[0], dqs[1])
        drel = jnp.where(low_lane, dqs[1], dqs[0]) * lanes[0:1]
        drel = shift_right(drel, bits.at[kind]).astype(narrow)
        dq = dq + dot(drel, wrel[...])
        grel[...] += dot_tn(drel, q)
        for j, value in enumerate((dq, dk, dv)):
            value = value.astype(narrow).astype(single)
            if j != 1:
                bias[far, j : j + 1, cut] += jnp.sum(value, axis=0, keepdims=True)
            value = value[:count]
            if count < ROWS:
                _, valid = positions(0, count, 0, kind, inside)
                value = jnp.where(valid, value, 0.0)
            dqkv[far, j, place, cut] = value.astype(narrow)

    for pair in range(half // LANES):
        fire(pair + 1)
        on_window(functools.partial(one_pair, pair))

    @pl.when(slot == SLOTS - 1)
    def _():
        part = half // 2
        at = step // SLOTS
        for j in range(4):
            if j < 3:
                total = dot_tn(dqkv[far, j], n1[...])
            else:
                total = dot_tn(mixed[far], da[...])
            keep[at, j * part : (j + 1) * part, :] = total[:part].astype(narrow)
            give[at, j * part : (j + 1) * part, :] = total[part:].astype(narrow)

    @pl.when(step == 2 * SLOTS - 1)
    def _():
        for (halver, _, _), total in zip(halvers, summed, strict=True):
            halver.back(0, total).wait()
        far_cross.wait()


def backward(rows_held, images, da, n1, qkv, mixed, weights, wrel, tables, residents, rest):
    half, width = weights.shape[2:]
    operands = [da, n1, qkv, mixed, weights, wrel, *tables, *residents, rest]
    in_specs = [whole(a.shape) for a in operands]

    def halved(i):
        return (1 - i // SLOTS) * SLOTS + i % SLOTS

    in_specs[2] = pl.BlockSpec((1, 4, ROWS, half), lambda i: (halved(i), 0, 0, 0))
    in_specs[4] = pl.BlockSpec(
        (2, 1, half, width), lambda i: (0, 3, 0, 0), pipeline_mode=pl.Buffered(1)
    )
    in_specs[-1] = ANY
    packed = (2 * half, width)
    square = residents[0].shape
    outs = [
        (of((2, 3, SLAB, half)), whole((2, 3, SLAB, half))),
        (of((2, *packed)), whole((2, *packed))),
        (of((2, *packed)), whole((2, *packed))),
        (of((2, 8, half), single), whole((2, 8, half))),
        (of((LANES, LANES), single), whole((LANES, LANES))),
        (of(packed), ANY),
        (of(square), ANY),
        (of(square), ANY),
    ]
    landing = (Halver.landing_rows(images, square[0]), width)
    copies = 3 + 2 * Halver.copies(images)
    return pl.pallas_call(
        functools.partial(backward_kernel, rows_held, images),
        out_shape=[o[0] for o in outs],
        grid=(2 * SLOTS,),
        in_specs=in_specs,
        out_specs=[o[1] for o in outs],
        scratch_shapes=[
            pltpu.VMEM((SLAB, half), narrow),
            pltpu.VMEM(packed, narrow),
            *[pltpu.VMEM(square, narrow)] * 2,
            *[pltpu.VMEM(landing, narrow)] * 2,
            pltpu.VMEM(rest.shape, narrow),
            pltpu.SemaphoreType.DMA((copies,)),
            pltpu.SemaphoreType.DMA((copies,)),
            pltpu.SemaphoreType.DMA((2,)),
        ],
        compiler_params=pltpu.CompilerParams(
            vmem_limit_bytes=VMEM, collective_id=2, has_side_effects=True
        ),
        cost_estimate=pl.CostEstimate(
            flops=52_000_000_000, bytes_accessed=80_000_000, transcendentals=8_000_000
        ),
        name="attention_backward",
    )(*operands)


def clear_rows(ext):
    @pl.loop(0, ext.shape[0] // GRID)
    def _(r):
        ext[rows_at(r * GRID, GRID), :] = jnp.zeros((GRID, ext.shape[1]), narrow)


def place_windows(rows_held, device, slab, ext, first, last):
    @pl.loop(first, last)
    def _(slot):
        row0, col0, kind, inside, offset, live = window_fields(rows_held, device, slot)

        @pl.when(live)
        def _():
            target, _ = positions(1, ROWS, col0, kind, inside)
            token = lax.broadcasted_iota(jnp.int32, (WIN * GRID, ROWS), 0)
            choose = jnp.where(token == target, 1.0, 0.0).astype(narrow)
            window = slab[rows_at(offset, ROWS), :]
            where_to = pl.ds(pl.multiple_of(row0 * GRID, GRID), WIN * GRID)
            ext[where_to, :] += dot(choose, window).astype(narrow)


def tail_kernel(
    rows_held, images,
    sums2, bias, rel_sum, fc_bias, peak, params,
    out_in, keep_in, crossed_in, xs_in, dx1_in, give, dqkv, weights,
    output, input_grad, packed, totals, tops,
    ext0, ext1, below0, below1, above0, above1, got, landing, held, sum_land, top_land, back, grads,
    packs, out, keep, crossed, xs, dx1, sends, recvs, locals_,
):
    device, image = lax.axis_index("tensor"), lax.axis_index("dp")
    beside, across, corner = partners(device)
    send = Sender(sends, recvs, locals_)
    early = [send.local(0, keep_in.at[1], keep), send.local(1, crossed_in, crossed)]
    loads = [
        send.local(2, dqkv, grads),
        send.local(3, weights.at[:, 0:3], packs),
        send.local(4, xs_in, xs),
        send.local(5, dx1_in, dx1),
    ]
    late = send.local(6, out_in, out)
    start_all(early + loads + [late])
    per = Halver.copies(images)
    middle = held.shape[0] // 2
    landing_rows = Halver.landing_rows(images, middle)
    landings = [landing.at[pl.ds(k * landing_rows, landing_rows), :] for k in range(2)]
    halvers = [
        Halver(send, 1 + k * per, image, images, k * middle, middle, order)
        for k, order in enumerate(((0, 1, 2), (1, 0, 2)))
    ]
    halo_base = 1 + 2 * per
    small_base = halo_base + 4
    tokens = rows_held * GRID
    top, bottom = LEFT * GRID, RIGHT * GRID
    held_by = (device, beside, across, corner)
    mates = dp_mates(image, images)
    ring = [{"tensor": beside}, {"tensor": across}] + mates

    def reduce_start(stage):
        for halver, land in zip(halvers, landings, strict=True):
            halver.start(stage, held, land)

    def reduce_finish(stage):
        for halver, land in zip(halvers, landings, strict=True):
            halver.finish(stage, held, land)

    def hand_start(stage):
        for halver in halvers:
            halver.back(stage, packed).start()

    def hand_finish(stage):
        for halver in halvers:
            halver.back(stage, packed).wait()

    greet([{"tensor": place} for place in (beside, across, corner)] + mates)
    swap = send.remote(0, give.at[1], got, {"tensor": beside})
    swap.start()
    totals[...] = jnp.zeros_like(totals)
    tops[...] = jnp.zeros_like(tops)
    totals[2:6, :] = sums2[0:4, :]
    rel = rel_sum[...]
    rel = rel[HD:] + pltpu.roll(rel[:HD], HD, 1)
    for g in range(HD // 8):
        at = 8 * (1 + g // 6)
        totals[at : at + 8, (g % 6) * LANES : (g % 6 + 1) * LANES] = rel[8 * g : 8 * g + 8]
    half = bias.shape[2]
    for k in range(SPLIT):
        far, odd = k // 2, k % 2
        totals[pl.ds(24 + held_by[k], 1), :] = fc_bias[k, 0:1, :]
        for j, row in enumerate((0, 2)):
            value = bias[far, row : row + 1, :]
            if odd:
                value = pltpu.roll(value, half // 2, 1)
            totals[pl.ds(28 + held_by[k], 1), j * half : (j + 1) * half] = value
        best = jnp.broadcast_to(jnp.max(peak[far], axis=1, keepdims=True), (8, LANES))
        if odd:
            best = pltpu.roll(best, 8 - half // LANES, 0)
        tops[pl.ds(pl.multiple_of(held_by[k] * 8, 8), 8), :] = best

    def small_copies(k):
        return [
            send.remote(small_base + 2 * k, totals, sum_land.at[k], ring[k]),
            send.remote(small_base + 2 * k + 1, tops, top_land.at[k], ring[k]),
        ]

    def small_start(k):
        for copy in small_copies(k):
            copy.start()

    def small_finish(k):
        for copy in small_copies(k):
            copy.wait()
        totals[...] += sum_land[k]
        tops[...] = jnp.maximum(tops[...], top_land[k])

    def halo(base, ext, below, above):
        up = send.remote(
            base, ext.at[pl.ds(0, top), :], below, {"tensor": (device + SPLIT - 1) % SPLIT}
        )
        down = send.remote(
            base + 1, ext.at[pl.ds(top + tokens, bottom), :], above, {"tensor": (device + 1) % SPLIT}
        )
        return up, down

    def halo_start(copies):
        up, down = copies
        pl.when(device > 0)(up.start)
        pl.when(device < SPLIT - 1)(down.start)

    def halo_finish(copies, ext, below, above, result):
        up, down = copies
        pl.when(device > 0)(up.wait_send)
        pl.when(device < SPLIT - 1)(down.wait_send)
        add_rows(result, 0, [(ext, top)], tokens)

        @pl.when(device < SPLIT - 1)
        def _():
            up.wait_recv()
            at = tokens - top
            add_rows(result, at, [(result, at), (below, 0)], top)

        @pl.when(device > 0)
        def _():
            down.wait_recv()
            add_rows(result, 0, [(result, 0), (above, 0)], bottom)

    def norm1_back():
        @pl.loop(0, SLAB // CHUNK)
        def _(c):
            sl = rows_at(c * CHUNK, CHUNK)
            grad = None
            for far in range(2):
                for j in range(3):
                    term = dot(grads[far, j, sl, :], packs[far, j])
                    grad = term if grad is None else grad + term
            normal, inverse = norm_parts(xs[sl, :].astype(single))
            totals[0:1, :] += jnp.sum(grad * normal, axis=0, keepdims=True)
            totals[1:2, :] += jnp.sum(grad, axis=0, keepdims=True)
            result = dx1[sl, :] + norm_back(grad, normal, inverse, params[8:9])
            back[sl, :] = result.astype(narrow)

    clear_rows(ext0)
    clear_rows(ext1)
    for copy in early:
        copy.wait()
    swap.wait()
    add_rows(held, 0, [(keep, 0), (got, 0), (crossed, 0)], held.shape[0])
    reduce_start(0)
    for copy in loads:
        copy.wait()
    norm1_back()
    small_start(0)
    reduce_finish(0)
    reduce_start(1)
    place_windows(rows_held, device, back, ext1, 0, SLOTS)
    halos1 = halo(halo_base, ext1, below1, above1)
    halo_start(halos1)
    small_finish(0)
    small_start(1)
    reduce_finish(1)
    reduce_start(2)
    late.wait()
    place_windows(rows_held, device, out, ext0, 0, 4)
    small_finish(1)
    small_start(2)
    reduce_finish(2)
    for halver, land in zip(halvers, landings, strict=True):
        halver.extras(held, land)
        start, length = halver.final
        packed[rows_at(start, length), :] = held[rows_at(start, length), :]
    hand_start(2)
    place_windows(rows_held, device, out, ext0, 4, SLOTS)
    halos0 = halo(halo_base + 2, ext0, below0, above0)
    halo_start(halos0)
    small_finish(2)
    small_start(3)
    halo_finish(halos1, ext1, below1, above1, input_grad)
    hand_finish(2)
    hand_start(1)
    small_finish(3)
    small_start(4)
    hand_finish(1)
    hand_start(0)
    for k in range(4, len(ring)):
        small_finish(k)
        if k + 1 < len(ring):
            small_start(k + 1)
    halo_finish(halos0, ext0, below0, above0, output)
    hand_finish(0)


def tail(rows_held, images, *operands):
    width = operands[-1].shape[3]
    half = operands[-1].shape[2]
    packed = (2 * half, width)
    tokens = rows_held * GRID
    bits = images.bit_length() - 1
    landing = 2 * Halver.landing_rows(images, packed[0] // 2)
    copies = 1 + 2 * Halver.copies(images) + 4 + 2 * (2 + bits)
    ext = ((rows_held + LEFT + RIGHT) * GRID, width)
    outs = [
        of((tokens, width)), of((tokens, width)), of(packed),
        of((32, width), single), of((32, LANES), single),
    ]
    return pl.pallas_call(
        functools.partial(tail_kernel, rows_held, images),
        out_shape=outs,
        in_specs=[pl.BlockSpec(memory_space=pltpu.VMEM)] * (len(operands) - 8) + [ANY] * 8,
        out_specs=[pl.BlockSpec(memory_space=pltpu.VMEM)] * len(outs),
        scratch_shapes=[
            pltpu.VMEM(ext, narrow),
            pltpu.VMEM(ext, narrow),
            pltpu.VMEM((LEFT * GRID, width), narrow),
            pltpu.VMEM((LEFT * GRID, width), narrow),
            pltpu.VMEM((RIGHT * GRID, width), narrow),
            pltpu.VMEM((RIGHT * GRID, width), narrow),
            pltpu.VMEM(packed, narrow),
            pltpu.VMEM((landing, width), narrow),
            pltpu.VMEM(packed, narrow),
            pltpu.VMEM((2 + bits, 32, width), single),
            pltpu.VMEM((2 + bits, 32, LANES), single),
            pltpu.VMEM((SLAB, width), narrow),
            pltpu.VMEM((2, 3, SLAB, half), narrow),
            pltpu.VMEM((2, 3, half, width), narrow),
            pltpu.VMEM((SLAB, width), narrow),
            *[pltpu.VMEM(packed, narrow)] * 2,
            pltpu.VMEM((SLAB, width), narrow),
            pltpu.VMEM((SLAB, width), single),
            pltpu.SemaphoreType.DMA((copies,)),
            pltpu.SemaphoreType.DMA((copies,)),
            pltpu.SemaphoreType.DMA((7,)),
        ],
        compiler_params=pltpu.CompilerParams(
            vmem_limit_bytes=VMEM, collective_id=3, has_side_effects=True
        ),
        cost_estimate=pl.CostEstimate(
            flops=4_000_000_000, bytes_accessed=20_000_000, transcendentals=0
        ),
        name="tail",
    )(*operands)


def finish_kernel(
    fc1, fc2, gq, gp, totals, tops, wqkv,
    grad_fc1, grad_fc2, grad_qkv, grad_proj, clipped, qv, fc1_bias, norms, proj_bias, fc2_bias, rel,
):
    device = lax.axis_index("tensor")
    grad_fc1[...] = fc1[...].astype(single)
    grad_fc2[...] = fc2[...].astype(single).T
    grad_qkv[...] = gq[...].astype(single)
    grad_proj[...] = gp[...].astype(single)

    @pl.when(pl.program_id(0) == 0)
    def _():
        local = wqkv.shape[1]
        limit = jnp.maximum(tops[pl.ds(pl.multiple_of(8 * device, 8), 8), :], CLIP)
        factor = jnp.sqrt(CLIP / limit)
        factor = jnp.concatenate([factor] * (wqkv.shape[2] // LANES), axis=1)
        for j in range(2):
            for head in range(local // HD):
                cut = slice(head * HD, (head + 1) * HD)
                scaled = wqkv[j, cut, :].astype(single) * factor[head : head + 1]
                clipped[j, cut, :] = scaled.astype(narrow)
            qv[j : j + 1, :] = totals[pl.ds(28 + device, 1), 2 * j * local : (2 * j + 1) * local]
        fc1_bias[...] = totals[24 + device, :]
        norms[...] = totals[0:4, :]
        proj_bias[...] = totals[4, :]
        fc2_bias[...] = totals[5, :]
        span = 2 * WIN - 1
        for j in range(2):
            for first in range(0, span, 8):
                group = (32 * j + first) // 8
                count = min(8, span - first)
                at, lane = 8 * (1 + group // 6), (group % 6) * LANES
                rel[first : first + count, j, :] = totals[at : at + count, lane : lane + HD]


def finish(summed1, summed2, gpack, totals, tops, wqkv):
    _, local, width = wqkv.shape
    hidden = summed1.shape[1]
    parts = 3
    rows, cols, lines = width // parts, hidden // parts, 3 * local // parts
    few = local // parts

    def by_rows(count, columns, first=0):
        return pl.BlockSpec((count, columns), lambda i: (first + i, 0))

    span = 2 * WIN - 1
    outs = [
        (of((width, hidden), single), by_rows(rows, hidden)),
        (of((hidden, width), single), by_rows(cols, width)),
        (of((3 * local, width), single), by_rows(lines, width)),
        (of((local, width), single), by_rows(few, width)),
        (of((2, local, width)), whole((2, local, width))),
        (of((2, local), single), whole((2, local))),
        (of((hidden,), single), whole((hidden,))),
        (of((4, width), single), whole((4, width))),
        (of((width,), single), whole((width,))),
        (of((width,), single), whole((width,))),
        (of((span, 2, HD), single), whole((span, 2, HD))),
    ]
    return pl.pallas_call(
        finish_kernel,
        out_shape=[o[0] for o in outs],
        grid=(parts,),
        in_specs=[
            by_rows(rows, hidden),
            pl.BlockSpec((width, cols), lambda i: (0, i)),
            by_rows(lines, width),
            by_rows(few, width, 3 * local // few),
            whole(totals.shape),
            whole(tops.shape),
            whole(wqkv.shape),
        ],
        out_specs=[o[1] for o in outs],
        compiler_params=pltpu.CompilerParams(vmem_limit_bytes=VMEM),
        cost_estimate=pl.CostEstimate(flops=0, bytes_accessed=14_000_000, transcendentals=0),
        name="finish",
    )(summed1, summed2, gpack, gpack, totals, tops, wqkv)


def shards(
    inputs,
    w_qkv,
    qv_bias,
    w_proj,
    proj_bias,
    w_fc1,
    fc1_bias,
    w_fc2,
    fc2_bias,
    norm1_gain,
    norm1_shift,
    norm2_gain,
    norm2_shift,
    rel_h,
    rel_w,
    cotangent,
):
    width = inputs.shape[2]
    rows = inputs.shape[1] // GRID
    local = w_qkv.shape[2]
    heads = local // HD
    device = lax.axis_index("tensor")
    tables = lane_tables()

    span = 2 * WIN - 1
    wrel = sum(
        jnp.pad(table, ((at, LANES - span - at), (side, HD - side)))
        for table, at, side in (
            (rel_h, HD, 0), (rel_w, HD + 32, 0), (rel_h, 0, HD), (rel_w, 32, HD),
        )
    )

    entries = (
        (fc1_bias, 0, 0), (qv_bias[0], 1, 0), (qv_bias[0], 2, local), (qv_bias[1], 3, 0),
        (qv_bias[1], 4, local), (norm1_gain, 8, 0), (norm1_shift, 9, 0), (proj_bias, 10, 0),
        (norm2_gain, 11, 0), (norm2_shift, 12, 0), (fc2_bias, 13, 0),
    )
    params = 0.0
    for values, row, at in entries:
        before = row * width + at
        params = params + jnp.pad(values, (before, 16 * width - before - values.shape[0]))
    params = params.reshape(16, width)
    wqkv = w_qkv.transpose(0, 2, 1)

    (
        xs, gs, n1, qkv, mixed, attn, peak,
        weights, across1, across2, beside1, beside2, smalls,
    ) = forward(
        *(a.reshape(rows, GRID, width) for a in (inputs, cotangent)), wqkv, w_proj, w_fc1, w_fc2, params,
        wrel, tables
    )
    out, dx1, da, sums2, near1, near2, far1, rest, fc_bias = mlp(
        (
            xs, attn, gs, params, smalls,
        ),
        (across1, across2),
        (beside1, beside2),
        (w_fc1, w_fc2),
    )
    images = lax.axis_size("dp")
    dqkv, keep, give, bias, rel_sum, crossed, summed1, summed2 = backward(
        rows, images, da, n1, qkv, mixed, weights, wrel, tables, [near1, near2, far1], rest
    )
    output, input_grad, gpack, totals, tops = tail(
        rows, images, sums2, bias, rel_sum, fc_bias, peak, params, out, keep, crossed, xs, dx1,
        give, dqkv, weights,
    )
    (
        grad_fc1, grad_fc2, grad_qkv, grad_proj, clipped, grad_qv, grad_fc1_bias,
        grad_norms, grad_proj_bias, grad_fc2_bias, grad_rel,
    ) = finish(summed1, summed2, gpack, totals, tops, wqkv)
    head_max = lax.dynamic_slice(tops, (8 * device, 0), (heads, 1))[:, 0]

    return (
        output[None],
        input_grad[None],
        grad_qkv.reshape(3, local, width).transpose(0, 2, 1),
        grad_qv,
        grad_proj,
        grad_proj_bias,
        grad_fc1,
        grad_fc1_bias,
        grad_fc2,
        grad_fc2_bias,
        grad_norms,
        grad_rel.transpose(1, 0, 2),
        clipped.transpose(0, 2, 1),
        head_max,
    )


def solution(mesh):
    return jax.shard_map(
        shards,
        mesh=mesh,
        in_specs=(
            P("dp", "tensor", None),
            P(None, None, "tensor"),
            P(None, "tensor"),
            P("tensor", None),
            P(),
            P(None, "tensor"),
            P("tensor"),
            P("tensor", None),
            P(),
            P(),
            P(),
            P(),
            P(),
            P(),
            P(),
            P("dp", "tensor", None),
        ),
        out_specs=(
            P("dp", "tensor", None),
            P("dp", "tensor", None),
            P(None, None, "tensor"),
            P(None, "tensor"),
            P("tensor", None),
            P(),
            P(None, "tensor"),
            P("tensor"),
            P("tensor", None),
            P(),
            P(),
            P(),
            P(None, None, "tensor"),
            P("tensor"),
        ),
        check_vma=False,
    )
```

```python
import functools

import jax
import jax.numpy as jnp
import numpy as np
from jax import lax
from jax.experimental import pallas as pl
from jax.experimental.pallas import tpu as pltpu
from jax.sharding import PartitionSpec as P

HD = 64
GRID = 64
WIN = 14
TILES = 5
SPAN = WIN * WIN
ROWS = 208
SLOTS = 7
EDGE = GRID % WIN
SHORT = EDGE * WIN
SLAB = (SLOTS - 2) * ROWS + SHORT
STRIP = SLAB // 6
SPLIT = 4
LEFT = 6
RIGHT = 12
LANES = 128
EPS = 1e-6
CLIP = 3.0
VMEM = 60 * 1024 * 1024

single = jnp.float32
narrow = jnp.bfloat16

def lane_tables():
    row = np.arange(ROWS)
    late = np.maximum(row - SHORT, 0)
    outer = WIN - EDGE
    orders = (
        (row // WIN, row % WIN),
        (
            np.where(row < SHORT, row // EDGE, late // outer),
            np.where(row < SHORT, row % EDGE, EDGE + late % outer),
        ),
    )
    lane = np.arange(LANES) % 64
    part = lane // 32
    at = lane % 32
    bits, keys = [], []
    for x, y in orders:
        amount = np.where(part[None, :] == 0, x[:, None], y[:, None])
        amount = np.where((row < SPAN)[:, None], amount, 0)
        bits.append(np.stack([(amount >> b) & 1 for b in range(4)]).astype(np.float32))
        place = WIN - 1 - np.where(part[None, :] == 0, x[:, None], y[:, None])
        hot = ((at % 16)[None, :] == place) & ((at % 16) < WIN)[None, :] & (row < SPAN)[:, None]
        hot = hot.astype(np.float32)
        hot[SPAN:, lane == 31] = -1e30
        keys.append(hot)
    lanes = np.zeros((8, LANES), np.float32)
    lanes[0] = at < WIN
    lanes[1] = (at >= 16) & (at < 16 + WIN)
    lanes[2] = lane == 31
    sides = np.zeros((16, LANES), np.float32)
    sides[0] = np.arange(LANES) < 64
    sides[1] = np.arange(LANES) >= 64
    return (
        jnp.asarray(np.stack(bits)),
        jnp.asarray(lanes),
        jnp.asarray(sides, narrow),
        jnp.asarray(np.stack(keys), narrow),
    )


def dot(a, b):
    return jnp.dot(a, b, preferred_element_type=single)


def dot_nt(a, b):
    return lax.dot_general(a, b, (((1,), (1,)), ((), ())), preferred_element_type=single)


def dot_tn(a, b):
    return lax.dot_general(a, b, (((0,), (0,)), ((), ())), preferred_element_type=single)


def norm_parts(values):
    centre = values - jnp.mean(values, axis=-1, keepdims=True)
    inverse = lax.rsqrt(jnp.mean(centre * centre, axis=-1, keepdims=True) + EPS)
    return centre * inverse, inverse


def norm_back(grad, normal, inverse, gain):
    scaled = grad * gain
    first = jnp.mean(scaled, axis=-1, keepdims=True)
    second = jnp.mean(scaled * normal, axis=-1, keepdims=True)
    return inverse * (scaled - first - normal * second)


def slot_fields(rows_held):
    return window_fields(rows_held, lax.axis_index("tensor"), pl.program_id(0) % SLOTS)


def window_fields(rows_held, device, slot):
    first = device * (SLOTS - 1)
    window = first + slot
    i, j = window // TILES, window % TILES
    last = device // (SPLIT - 1)
    live = slot < SLOTS - 1 + last
    row0 = i * WIN - device * rows_held + LEFT
    high = jnp.minimum(WIN, GRID - i * WIN)
    wide = jnp.minimum(WIN, GRID - j * WIN)

    def short_before(n):
        return jnp.minimum(n // TILES, TILES - 1) + jnp.maximum(n - TILES * (TILES - 1), 0)

    offset = ROWS * slot - (ROWS - SHORT) * (short_before(window) - short_before(first))
    return row0, j * WIN, j // (TILES - 1), high * wide, offset, live


def positions(axis, count, first_col, kind, inside):
    shape = (count, 1) if axis == 0 else (1, count)
    row = lax.broadcasted_iota(jnp.int32, shape, axis)
    x = lax.shift_right_logical(row * 4682, 16)
    plain = x * GRID + (row - x * WIN)
    x = lax.shift_right_logical(row, EDGE.bit_length() - 1)
    edge = x * GRID + (row - x * EDGE)
    token = jnp.where(kind == 1, edge, plain) + first_col
    return jnp.where(row < inside, token, -1), row < inside


def gather_window(source, target):
    token = lax.broadcasted_iota(jnp.int32, (target.shape[0], WIN * GRID), 1)
    choose = jnp.where(token == target, 1.0, 0.0).astype(narrow)
    return dot(choose, source)


def shift_left(values, bits):
    for b in range(4):
        taken = bits[b, : values.shape[0]] > 0.5
        values = jnp.where(taken, pltpu.roll(values, LANES - (1 << b), 1), values)
    return values


def shift_right(values, bits):
    for b in range(4):
        taken = bits[b, : values.shape[0]] > 0.5
        values = jnp.where(taken, pltpu.roll(values, 1 << b, 1), values)
    return values


def partners(device):
    beside = device + 1 - 2 * (device % 2)
    across = (device + 2) % SPLIT
    corner = (beside + 2) % SPLIT
    return beside, across, corner


def greet(places):
    barrier = pltpu.get_barrier_semaphore()
    for place in places:
        pl.semaphore_signal(barrier, inc=1, device_id=place, device_id_type=pl.DeviceIdType.MESH)
    pl.semaphore_wait(barrier, len(places))


class Sender:
    def __init__(self, sends, recvs, locals_):
        self.sends, self.recvs, self.locals = sends, recvs, locals_

    def remote(self, at, source, target, place):
        return pltpu.make_async_remote_copy(
            src_ref=source,
            dst_ref=target,
            send_sem=self.sends.at[at],
            recv_sem=self.recvs.at[at],
            device_id=place,
            device_id_type=pl.DeviceIdType.MESH,
        )

    def local(self, at, source, target):
        return pltpu.make_async_copy(source, target, self.locals.at[at])


def mate_of(image, bit):
    unit = 1 << bit
    return image + unit * (1 - 2 * ((image // unit) % 2))


def rows_at(start, count):
    return pl.ds(pl.multiple_of(start, 16), count)


def add_rows(target, target_at, sources, count):
    chunk = next(c for c in (96, 48, 16) if count % c == 0)

    @pl.loop(0, count // chunk)
    def _(c):
        total = None
        for ref, at in sources:
            value = ref[rows_at(at + c * chunk, chunk), :]
            total = value if total is None else total + value
        target[rows_at(target_at + c * chunk, chunk), :] = total


HALVINGS = 3


class Halver:
    def __init__(self, send, base, image, images, start, rows, order):
        bits = images.bit_length() - 1
        assert images == 1 << bits and bits >= HALVINGS
        self.send, self.base, self.image = send, base, image
        self.extra_bits = range(HALVINGS, bits)
        self.stages = []
        landing, length = 0, rows
        for bit in order:
            length //= 2
            mine = (image // (1 << bit)) % 2
            keep, give = start + mine * length, start + (1 - mine) * length
            self.stages.append((mate_of(image, bit), keep, give, length, landing))
            landing += length
            start = keep
        self.final = (start, length)
        self.landing = landing

    @staticmethod
    def copies(images):
        return 2 * HALVINGS + images.bit_length() - 1 - HALVINGS

    @staticmethod
    def landing_rows(images, rows):
        last = rows >> HALVINGS
        return rows - last + last * (images.bit_length() - 1 - HALVINGS)

    def out(self, stage, held, landing):
        mate, _, give, length, at = self.stages[stage]
        return self.send.remote(
            self.base + stage,
            held.at[rows_at(give, length), :],
            landing.at[pl.ds(at, length), :],
            {"dp": mate},
        )

    def start(self, stage, held, landing):
        self.out(stage, held, landing).start()

    def finish(self, stage, held, landing):
        self.out(stage, held, landing).wait()
        _, keep, _, length, at = self.stages[stage]
        add_rows(held, keep, [(held, keep), (landing, at)], length)

    def extras(self, held, landing):
        start, length = self.final
        for k, bit in enumerate(self.extra_bits):
            at = self.landing + k * length
            copy = self.send.remote(
                self.base + HALVINGS + k,
                held.at[rows_at(start, length), :],
                landing.at[pl.ds(at, length), :],
                {"dp": mate_of(self.image, bit)},
            )
            copy.start()
            copy.wait()
            add_rows(held, start, [(held, start), (landing, at)], length)

    def back(self, stage, held):
        mate, keep, _, length, _ = self.stages[stage]
        cut = rows_at(keep, length)
        at = self.base + HALVINGS + len(self.extra_bits) + stage
        return self.send.remote(at, held.at[cut, :], held.at[cut, :], {"dp": mate})


def dp_mates(image, images):
    return [{"dp": mate_of(image, bit)} for bit in range(images.bit_length() - 1)]


def project(n1, weights, qbias, vbias, projected, place):
    projected[0, place, :] = (dot_nt(n1, weights[0]) + qbias).astype(narrow)
    projected[1, place, :] = dot_nt(n1, weights[1]).astype(narrow) * jnp.asarray(0.125, narrow)
    projected[2, place, :] = (dot_nt(n1, weights[2]) + vbias).astype(narrow)


def attend(count, place, valid, projected, vbias, wrel, bits, lanes, sides, keys, qkv, mixed, peak):
    half = projected.shape[2]
    qkv[0, 0, :count] = jnp.where(valid, projected[0, place, :].astype(single), 0.0).astype(narrow)
    qkv[0, 1, :count] = projected[1, place, :]
    qkv[0, 2, :count] = projected[2, place, :]
    if count < ROWS:
        left = ROWS - count
        qkv[0, 1, count:] = jnp.zeros((left, half), narrow)
        qkv[0, 2, count:] = jnp.broadcast_to(vbias, (left, half)).astype(narrow)
    low_lane = lax.broadcasted_iota(jnp.int32, (count, LANES), 1) < 64
    for pair in range(half // LANES):
        cut = slice(pair * LANES, (pair + 1) * LANES)
        q, k8, v = qkv[0, 0, :count, cut], qkv[0, 1, :, cut], qkv[0, 2, :, cut]
        rel = shift_left(dot_nt(q, wrel[...]), bits)
        rest = rel - rel.astype(narrow).astype(single)
        rel = rel * lanes[0:1] + pltpu.roll(rest, 16, 1) * lanes[1:2] + lanes[2:3]
        rel = rel.astype(narrow)
        qkv[0, 3, :count, cut] = rel
        pieces = []
        for head in range(2):
            mine, other = sides[head : head + 1], sides[1 - head : 2 - head]
            only = q * mine
            logits = dot_nt(only, k8)
            at = 2 * pair + head
            peak[at : at + 1, :] = jnp.maximum(
                peak[at : at + 1, :], jnp.max(logits, axis=0, keepdims=True)
            )
            scores = dot_nt(only + rel * other, k8 * mine + keys[...] * other)
            top = jnp.max(scores, axis=1, keepdims=True)
            probs = jnp.exp(scores - top)
            total = jnp.sum(probs, axis=1, keepdims=True)
            pieces.append(dot(probs.astype(narrow), v) * (1.0 / total))
        mixed[place, cut] = jnp.where(low_lane, pieces[0], pieces[1]).astype(narrow)


class Halo:
    def __init__(self, send, base, grid, ext, device, rows):
        below, above = {"tensor": (device + 1) % SPLIT}, {"tensor": (device + SPLIT - 1) % SPLIT}
        self.has_below, self.has_above = device < SPLIT - 1, device > 0
        self.cross_below, self.cross_above = device == 1, device == 2

        def copy(at, first, count, first_col, cols, target_row, place):
            window = (pl.ds(first, count), pl.ds(first_col, cols), slice(None))
            return send.remote(
                at, grid.at[window], ext.at[(pl.ds(target_row, count), *window[1:])], place
            )

        few, many = 4, 10
        self.down = copy(base, rows - LEFT, LEFT, 0, GRID, 0, below)
        self.down_cross = copy(base, rows - few, few, 16, GRID - 16, LEFT - few, below)
        self.up = copy(base + 1, 0, RIGHT, 0, GRID, LEFT + rows, above)
        self.up_cross = copy(base + 1, 0, many, 0, 32, LEFT + rows, above)

    def _each(self, down_here, up_here, act):
        for here, crossing, plain, crossed in (
            (*down_here, self.down, self.down_cross),
            (*up_here, self.up, self.up_cross),
        ):

            @pl.when(here & jnp.logical_not(crossing))
            def _():
                act(plain)

            @pl.when(crossing)
            def _():
                act(crossed)

    def _senders(self, act):
        self._each((self.has_below, self.cross_below), (self.has_above, self.cross_above), act)

    def start(self):
        self._senders(lambda copy: copy.start())

    def wait_send(self):
        self._senders(lambda copy: copy.wait_send())

    def wait_from_above(self):
        pl.when(self.has_above & jnp.logical_not(self.cross_above))(self.down.wait_recv)
        pl.when(self.cross_above)(self.down_cross.wait_recv)

    def wait_from_below(self):
        pl.when(self.has_below & jnp.logical_not(self.cross_below))(self.up.wait_recv)
        pl.when(self.cross_below)(self.up_cross.wait_recv)


class Quartet:
    def __init__(self, send, base, image, pieces, across):
        side, deep = image % 2, (image // 2) % 2
        beside, behind = {"dp": mate_of(image, 0)}, {"dp": mate_of(image, 1)}
        mine = 2 * deep + side
        from_beside, from_behind = 2 * deep + 1 - side, 2 * (1 - deep) + side
        self.first, self.second, self.third = [], [], []
        for k, (source, target, view) in enumerate(pieces):
            at = base + 5 * k

            def copy(number, origin, quarter, part, place):
                return send.remote(at + number, view(origin, quarter, part), view(target, quarter, part), place)

            self.first.append(copy(0, source, mine, None, across))
            self.second.append(copy(1, target, mine, None, beside))
            self.second.append(copy(2, target, mine, None, behind))
            if view(target, from_behind, 0) is not None:
                self.third.append(copy(3, target, from_behind, 0, beside))
            self.third.append(copy(4, target, from_beside, 1, behind))


def quarter_rows(array, quarter, part):
    size = array.shape[0] // 4
    start = quarter * size
    if part is not None:
        size //= 2
        start += part * size
    return array.at[rows_at(start, size), :]


def start_all(copies):
    for copy in copies:
        copy.start()


def receive_all(copies):
    for copy in copies:
        copy.wait_recv()


def forward_kernel(
    x, g, wqkv, wproj, fc1, fc2, vectors, qv_bias, rel_tables, bits, lanes, sides, keys,
    xs, gs, n1_all, qkv, mixed, attn, peak, params, wrel, weights_out, across1, across2, beside1,
    beside2, small_out,
    xext, gext, weights, smalls, projected, sends, recvs, locals_,
):
    step = pl.program_id(0)
    far, slot = step // SLOTS, step % SLOTS
    device, image = lax.axis_index("tensor"), lax.axis_index("dp")
    rows, _, width = x.shape
    part = wproj.shape[0]
    half = 2 * part
    beside, across, corner = partners(device)
    send = Sender(sends, recvs, locals_)
    x_halo = Halo(send, 0, x, xext, device, rows)
    g_halo = Halo(send, 2, g, gext, device, rows)
    small = params.at[pl.ds(0, 8), :]

    own_pack = [
        send.remote(4, wqkv, weights.at[0, 0:3, pl.ds(part, part), :], {"tensor": beside}),
        send.remote(5, wproj, weights.at[0, 3, pl.ds(part, part), :], {"tensor": beside}),
    ]
    notes = [
        send.remote(6 + k, small, smalls.at[k + 1], {"tensor": place})
        for k, place in enumerate((beside, across, corner))
    ]
    fc_beside = [
        send.remote(9, fc1, beside1, {"tensor": beside}),
        send.remote(10, fc2, beside2, {"tensor": beside}),
    ]
    corner_pack = send.remote(
        11, weights.at[1, :, pl.ds(0, part), :], weights.at[1, :, pl.ds(part, part), :], {"tensor": beside}
    )

    def of_qkv(array, quarter, half_of):
        size = part // 4
        cut = rows_at(quarter * size, size)
        if array is wqkv:
            return array.at[:, cut, :]
        if half_of is None:
            return array.at[1, 0:3, cut, :]
        return array.at[1, 0:2, cut, :] if half_of == 0 else array.at[1, 2:3, cut, :]

    def of_proj(array, quarter, half_of):
        size = part // 4
        cut = rows_at(quarter * size, size)
        if array is wproj:
            return array.at[cut, :]
        return None if half_of == 0 else array.at[1, 3, cut, :]

    pack_far = Quartet(
        send, 12, image, ((wqkv, weights, of_qkv), (wproj, weights, of_proj)), {"tensor": across}
    )
    fc_far = Quartet(
        send, 22, image, ((fc1, across1, quarter_rows), (fc2, across2, quarter_rows)), {"tensor": across}
    )
    own = [
        send.local(0, wqkv, weights.at[0, 0:3, pl.ds(0, part), :]),
        send.local(1, wproj, weights.at[0, 3, pl.ds(0, part), :]),
        send.local(2, x, xext.at[pl.ds(LEFT, rows)]),
        send.local(3, small, smalls.at[0]),
    ]
    g_own = send.local(4, g, gext.at[pl.ds(LEFT, rows)])
    kept = [send.local(5, weights, weights_out), send.local(6, smalls, small_out)]

    @pl.when(step == 0)
    def _():
        params[...] = jnp.zeros_like(params)
        for ref, row in zip(vectors, (0, 8, 9, 10, 11, 12, 13), strict=True):
            params[row, :] = ref[...]
        for j in range(2):
            params[1 + 2 * j, 0:part] = qv_bias[j, :]
            params[2 + 2 * j, part:half] = qv_bias[j, :]
        wrel[...] = jnp.zeros_like(wrel)
        span = 2 * WIN - 1
        for ref, at in zip(rel_tables, (0, 32), strict=True):
            wrel[HD + at : HD + at + span, :HD] = ref[...]
            wrel[at : at + span, HD:] = ref[...]
        for ref in (xext, gext):
            ref[pl.ds(0, LEFT)] = jnp.zeros((LEFT, GRID, width), narrow)
            ref[pl.ds(LEFT + rows, RIGHT)] = jnp.zeros((RIGHT, GRID, width), narrow)
        greet(
            [{"tensor": place} for place in (beside, across, corner)]
            + [{"dp": mate_of(image, bit)} for bit in range(2)]
        )
        start_all(own_pack + notes + own)
        x_halo.start()
        start_all(pack_far.first)
        for ref in (xs, gs, n1_all, mixed, peak):
            ref[...] = jnp.zeros_like(ref)
        for copy in own + notes + own_pack:
            copy.wait()
        x_halo.wait_from_above()

    @pl.when(step == 1)
    def _():
        start_all(fc_beside + [g_own])

    @pl.when(step == 2)
    def _():
        receive_all(pack_far.first)
        start_all(pack_far.second)
        start_all(fc_far.first)

    @pl.when(step == 3)
    def _():
        x_halo.wait_from_below()

    @pl.when(step == 4)
    def _():
        receive_all(pack_far.second)
        start_all(pack_far.third)

    @pl.when(step == 5)
    def _():
        receive_all(fc_far.first)
        start_all(fc_far.second)
        g_halo.start()

    @pl.when(step == 6)
    def _():
        receive_all(pack_far.third)
        corner_pack.start()

    @pl.when(step == SLOTS)
    def _():
        corner_pack.wait_recv()
        start_all(kept)

    @pl.when(step == SLOTS + 2)
    def _():
        receive_all(fc_far.second)
        start_all(fc_far.third)

    row0, col0, kind, inside, offset, live = slot_fields(rows)
    whole_window = inside == SPAN
    tables = (wrel, bits.at[kind], lanes, sides, keys.at[kind])

    def biases(which):
        return (
            smalls[2 * which, 1:2, :half] + smalls[2 * which + 1, 2:3, :half],
            smalls[2 * which, 3:4, :half] + smalls[2 * which + 1, 4:5, :half],
        )

    @pl.when(step == SLOTS)
    def _():
        project(n1_all[...], weights.at[1], *biases(1), projected, slice(None))

    def work(count):
        place = rows_at(offset, count)

        @pl.when(far == 0)
        def _():
            target, valid = positions(0, count, col0, kind, inside)
            source = xext[pl.ds(row0, WIN)].reshape(WIN * GRID, width)
            window = gather_window(source, target)
            xs[place, :] = window.astype(narrow)
            normal, _ = norm_parts(window)
            n1 = jnp.where(valid, normal * params[8:9] + params[9:10], 0.0).astype(narrow)
            n1_all[place, :] = n1
            project(n1, weights.at[0], *biases(0), projected, place)

        _, valid = positions(0, count, col0, kind, inside)
        attend(
            count, place, valid, projected, biases(far)[1], *tables, qkv, mixed.at[far], peak.at[far]
        )

    pl.when(live & whole_window)(functools.partial(work, ROWS))
    pl.when(live & jnp.logical_not(whole_window))(functools.partial(work, SHORT))

    @pl.when(step == 2 * SLOTS - 1)
    def _():
        attn[...] = dot(mixed[0], weights[0, 3]) + dot(mixed[1], weights[1, 3])
        g_own.wait()
        g_halo.wait_from_above()
        g_halo.wait_from_below()

        @pl.loop(0, SLOTS)
        def _(slot):
            row0, col0, kind, inside, offset, live = window_fields(rows, device, slot)

            @pl.when(live)
            def _():
                target, _ = positions(0, ROWS, col0, kind, inside)
                source = gext[pl.ds(row0, WIN)].reshape(WIN * GRID, width)
                gs[rows_at(offset, ROWS), :] = gather_window(source, target).astype(narrow)

        for halo in (x_halo, g_halo):
            halo.wait_send()
        for group in (pack_far, fc_far):
            for copy in group.first + group.second:
                copy.wait_send()
        for copy in pack_far.third + [corner_pack]:
            copy.wait_send()
        for copy in kept + fc_beside + fc_far.third:
            copy.wait()


def whole(shape):
    zeros = (0,) * len(shape)
    return pl.BlockSpec(shape, lambda *_: zeros, pipeline_mode=pl.Buffered(1))


def by_slot(shape):
    rest = (0,) * len(shape)
    return pl.BlockSpec((1,) + tuple(shape), lambda s, *_: (s,) + rest)


ANY = pl.BlockSpec(memory_space=pl.ANY)


def of(shape, dtype=narrow):
    return jax.ShapeDtypeStruct(shape, dtype)


def forward(x, g, wqkv, wproj, fc1, fc2, vectors, qv_bias, rel_tables, tables):
    rows, _, width = x.shape
    half = 2 * wproj.shape[0]
    slab = (SLAB, width)
    outs = [
        (of(slab), whole(slab)),
        (of(slab), whole(slab)),
        (of(slab), whole(slab)),
        (of((2 * SLOTS, 4, ROWS, half)), by_slot((4, ROWS, half))),
        (of((2, SLAB, half)), whole((2, SLAB, half))),
        (of(slab, single), whole(slab)),
        (of((2, 8, ROWS), single), whole((2, 8, ROWS))),
        (of((16, width), single), whole((16, width))),
        (of((LANES, LANES)), whole((LANES, LANES))),
        (of((2, 4, half, width)), ANY),
        (of(fc1.shape), ANY),
        (of(fc2.shape), ANY),
        (of(fc1.shape), ANY),
        (of(fc2.shape), ANY),
        (of((SPLIT, 8, width), single), ANY),
    ]
    operands = (x, g, wqkv, wproj, fc1, fc2)
    known = (tuple(vectors), qv_bias, tuple(rel_tables), *tables)
    ext = (rows + LEFT + RIGHT, GRID, width)
    return pl.pallas_call(
        forward_kernel,
        out_shape=[o[0] for o in outs],
        grid=(2 * SLOTS,),
        in_specs=[ANY] * 6 + list(jax.tree.map(lambda a: whole(a.shape), known)),
        out_specs=[o[1] for o in outs],
        scratch_shapes=[
            pltpu.VMEM(ext, narrow),
            pltpu.VMEM(ext, narrow),
            pltpu.VMEM((2, 4, half, width), narrow),
            pltpu.VMEM((SPLIT, 8, width), single),
            pltpu.VMEM((3, SLAB, half), narrow),
            pltpu.SemaphoreType.DMA((32,)),
            pltpu.SemaphoreType.DMA((32,)),
            pltpu.SemaphoreType.DMA((7,)),
        ],
        compiler_params=pltpu.CompilerParams(
            vmem_limit_bytes=VMEM, collective_id=0, has_side_effects=True
        ),
        cost_estimate=pl.CostEstimate(
            flops=26_000_000_000, bytes_accessed=60_000_000, transcendentals=8_000_000
        ),
        name="attention_forward",
    )(*operands, *known)


CHUNK = SLAB // 3


def gelu_parts(z):
    size = jnp.abs(z)
    bell = jnp.exp(-0.5 * z * z)
    t = 1.0 / (1.0 + 0.2316418882663604 * size)
    poly = 0.5 * 1.061405429 * t + (0.5 * -1.453152027)
    poly = poly * t + 0.5 * 1.421413741
    poly = poly * t + 0.5 * -0.284496736
    poly = poly * t + 0.5 * 0.254829592
    tail = poly * t * bell
    phi_total = jnp.where(z >= 0, 1.0 - tail, tail)
    return z * phi_total, phi_total + z * bell * 0.3989422804014327


def mlp_kernel(
    xs, attn, gs, params, smalls, across1, across2, beside1, beside2, own1, own2,
    out_away, dx1_away, da_away, sums, near1, near2, far1, rest, gb,
    n2, n2t, gt, branch, dn2, w1, w2, grad1, grad2, got1, got2, near_got1, near_got2, landing,
    hs, zs, out, dx1, da, sends, recvs, locals_,
):
    step = pl.program_id(0)
    room = step % 2
    width = gs.shape[1]
    holder = jnp.where(step == 0, 2, jnp.where(step == 1, 3, jnp.where(step == 2, 1, 0)))
    beside, across, _ = partners(lax.axis_index("tensor"))
    send = Sender(sends, recvs, locals_)
    corners = [
        send.remote(0, across1, w1.at[1], {"tensor": beside}),
        send.remote(1, across2, w2.at[1], {"tensor": beside}),
    ]
    loads = [
        [send.local(2 * k, first, w1.at[at]), send.local(2 * k + 1, second, w2.at[at])]
        for k, (first, second, at) in enumerate(
            ((across1, across2, 0), (beside1, beside2, 0), (own1, own2, 1))
        )
    ]
    swaps = [
        send.remote(2, grad1.at[1], got1, {"tensor": beside}),
        send.remote(3, grad2.at[1], got2, {"tensor": beside}),
    ]
    crossing = send.remote(4, got1, far1, {"tensor": across})
    image = lax.axis_index("dp")
    mate = {"dp": mate_of(image, 0)}
    upper = got2.shape[0] // 2
    mine = (image % 2) * upper
    halving = send.remote(5, got2.at[rows_at(upper - mine, upper), :], landing, mate)

    def leaving(c):
        sl = rows_at(c * STRIP, STRIP)
        return [
            send.local(6 + 3 * c + k, here.at[sl, :], away.at[sl, :])
            for k, (here, away) in enumerate(((out, out_away), (dx1, dx1_away), (da, da_away)))
        ]

    near_swaps = [
        send.remote(6, grad1.at[2], near_got1, {"tensor": beside}),
        send.remote(7, grad2.at[2], near_got2, {"tensor": beside}),
    ]

    @pl.when(step == 0)
    def _():
        gb[...] = jnp.zeros_like(gb)
        start_all(loads[0])
        greet([{"tensor": beside}, {"tensor": across}, mate])
        start_all(corners)

        @pl.loop(0, SLAB // STRIP)
        def _(c):
            sl = rows_at(c * STRIP, STRIP)
            middle = xs[sl, :].astype(single) + (attn[sl, :] + params[10:11])
            dx1[sl, :] = middle
            normal, _ = norm_parts(middle)
            n2[sl, :] = (normal * params[11:12] + params[12:13]).astype(narrow)
            branch[sl, :] = jnp.zeros((STRIP, width), single)
            dn2[sl, :] = jnp.zeros((STRIP, width), single)

        for j in range(width // LANES):
            lanes = slice(j * LANES, (j + 1) * LANES)
            n2t[lanes, :] = n2[:, lanes].T
            gt[lanes, :] = gs[:, lanes].T
        for copy in loads[0]:
            copy.wait()

    @pl.when(step == 1)
    def _():
        start_all(loads[1])
        for copy in corners:
            copy.wait()

    @pl.when(step == 2)
    def _():
        start_all(swaps)
        start_all(loads[2])
        for copy in loads[1]:
            copy.wait()

    @pl.when(step == 3)
    def _():
        start_all(near_swaps)
        for copy in loads[2]:
            copy.wait()

    @pl.loop(0, SLAB // CHUNK)
    def _(c):
        @pl.when((step == 2) & (c == 1))
        def _():
            swaps[0].wait()
            add_rows(got1, 0, [(got1, 0), (grad1.at[0], 0)], got1.shape[0])
            crossing.start()
            swaps[1].wait()
            add_rows(got2, 0, [(got2, 0), (grad2.at[0], 0)], got2.shape[0])
            halving.start()

        sl = rows_at(c * CHUNK, CHUNK)
        z = dot(n2[sl, :], w1[room]) + smalls[holder, 0:1, :]
        dh = dot_nt(gs[sl, :], w2[room])
        act, slope = gelu_parts(z)
        h = act.astype(narrow)
        dz = (dh * slope).astype(narrow)
        hs[sl, :] = h
        zs[sl, :] = dz
        gb[holder, 0:1, :] += jnp.sum(dz.astype(single), axis=0, keepdims=True)
        branch[sl, :] += dot(h, w2[room])
        dn2[sl, :] += dot_nt(dz, w1[room])

    @pl.loop(0, 2)
    def _(r):
        sl = rows_at(r * (width // 2), width // 2)
        grad1[step, sl, :] = dot(n2t[sl, :], zs[...]).astype(narrow)
        grad2[step, sl, :] = dot(gt[sl, :], hs[...]).astype(narrow)

    @pl.when(step == 3)
    def _():
        halving.wait()
        add_rows(rest, 0, [(got2, mine), (landing, 0)], upper)
        for copy, near, grad, got in zip(
            near_swaps, (near1, near2), (grad1, grad2), (near_got1, near_got2), strict=True
        ):
            copy.wait()
            add_rows(near, 0, [(grad.at[3], 0), (got, 0)], near.shape[0])
        sums[...] = jnp.zeros_like(sums)

        @pl.loop(0, SLAB // STRIP)
        def _(c):
            sl = rows_at(c * STRIP, STRIP)
            middle = dx1[sl, :]
            normal, inverse = norm_parts(middle)
            out[sl, :] = (middle + (branch[sl, :] + params[13:14])).astype(narrow)
            grad = dn2[sl, :]
            cot = gs[sl, :].astype(single)
            total = cot + norm_back(grad, normal, inverse, params[11:12])
            dx1[sl, :] = total
            low = total.astype(narrow)
            da[sl, :] = low
            for copy in leaving(c):
                copy.start()
            sums[0:1, :] += jnp.sum(grad * normal, axis=0, keepdims=True)
            sums[1:2, :] += jnp.sum(grad, axis=0, keepdims=True)
            sums[2:3, :] += jnp.sum(low.astype(single), axis=0, keepdims=True)
            sums[3:4, :] += jnp.sum(cot, axis=0, keepdims=True)

        crossing.wait()
        for c in range(SLAB // STRIP):
            for copy in leaving(c):
                copy.wait()


def mlp(residents, across, beside, own):
    width, local = own[0].shape
    slab = (SLAB, width)
    square = (width, local)
    outs = [
        (of(slab), ANY),
        (of(slab, single), ANY),
        (of(slab), ANY),
        (of((8, width), single), whole((8, width))),
        (of(square), whole(square)),
        (of(square), whole(square)),
        (of(square), ANY),
        (of((local // 2, width)), whole((local // 2, width))),
        (of((SPLIT, 8, local), single), whole((SPLIT, 8, local))),
    ]
    return pl.pallas_call(
        mlp_kernel,
        out_shape=[o[0] for o in outs],
        grid=(SPLIT,),
        in_specs=[whole(a.shape) for a in residents] + [ANY] * 6,
        out_specs=[o[1] for o in outs],
        scratch_shapes=[
            pltpu.VMEM(slab, narrow),
            *[pltpu.VMEM((width, SLAB), narrow)] * 2,
            *[pltpu.VMEM(slab, single)] * 2,
            *[pltpu.VMEM((2, *square), narrow)] * 2,
            *[pltpu.VMEM((SPLIT, *square), narrow)] * 2,
            *[pltpu.VMEM(square, narrow)] * 4,
            pltpu.VMEM((width // 2, local), narrow),
            *[pltpu.VMEM((SLAB, local), narrow)] * 2,
            pltpu.VMEM(slab, narrow),
            pltpu.VMEM(slab, single),
            pltpu.VMEM(slab, narrow),
            pltpu.SemaphoreType.DMA((8,)),
            pltpu.SemaphoreType.DMA((8,)),
            pltpu.SemaphoreType.DMA((6 + 3 * (SLAB // STRIP),)),
        ],
        compiler_params=pltpu.CompilerParams(
            vmem_limit_bytes=VMEM, collective_id=1, has_side_effects=True
        ),
        cost_estimate=pl.CostEstimate(
            flops=36_000_000_000, bytes_accessed=60_000_000, transcendentals=8_000_000
        ),
        name="mlp",
    )(*residents, *across, *beside, *own)


def backward_kernel(
    rows_held, images,
    da, n1, qkv, mixed, wproj, wrel, bits, lanes, sides, keys, near1, near2, far1, rest,
    dqkv, keep, give, bias, grel, crossed, summed1, summed2,
    dmix, got_far, held1, held2, land1, land2, rest_got,
    sends, recvs, locals_,
):
    step = pl.program_id(0)
    slot, far = step % SLOTS, 1 - step // SLOTS
    image = lax.axis_index("dp")
    beside, across, _ = partners(lax.axis_index("tensor"))
    send = Sender(sends, recvs, locals_)
    half = wproj.shape[2]
    per = Halver.copies(images)
    sum1 = Halver(send, 3, image, images, 0, held1.shape[0], (1, 0, 2))
    sum2 = Halver(send, 3 + per, image, images, 0, held2.shape[0], (0, 1, 2))
    rest_cross = send.remote(0, rest, rest_got, {"tensor": across})
    far_swap = send.remote(1, give.at[0], got_far, {"tensor": beside})
    far_cross = send.remote(2, got_far, crossed, {"tensor": across})

    halvers = ((sum1, held1, land1), (sum2, held2, land2))
    summed = (summed1, summed2)

    def seed(k, halver, held, summed):
        start, length = halver.final
        copy = send.local(k, held.at[rows_at(start, length), :], summed.at[rows_at(start, length), :])
        copy.start()
        copy.wait()

    def begin():
        greet([{"tensor": beside}, {"tensor": across}] + dp_mates(image, images))
        rest_cross.start()
        sum2.start(0, near2, land2)
        add_rows(held1, 0, [(near1, 0), (far1, 0)], held1.shape[0])
        sum1.start(0, held1, land1)

    def second():
        sum1.finish(0, held1, land1)
        sum1.start(1, held1, land1)
        sum2.out(0, near2, land2).wait()
        rest_cross.wait()
        _, kept, _, length, at = sum2.stages[0]
        add_rows(held2, kept, [(near2, kept), (land2, at), (rest_got, 0)], length)
        sum2.start(1, held2, land2)

    def third():
        for halver, held, land in halvers:
            halver.finish(1, held, land)
            halver.start(2, held, land)

    def fourth():
        for n, (halver, held, land) in enumerate(halvers):
            halver.finish(2, held, land)
            halver.extras(held, land)
            seed(n, halver, held, summed[n])
            halver.back(2, summed[n]).start()

    def hand(stage):
        for (halver, _, _), total in zip(halvers, summed, strict=True):
            halver.back(stage + 1, total).wait()
            halver.back(stage, total).start()

    def swap_far():
        far_swap.start()

    def cross_far():
        far_swap.wait()
        add_rows(got_far, 0, [(got_far, 0), (keep.at[0], 0)], got_far.shape[0])
        far_cross.start()

    events = {
        (0, 0): begin,
        (3, 0): second,
        (4, 2): third,
        (7, 0): swap_far,
        (7, 1): fourth,
        (8, 0): cross_far,
        (10, 2): functools.partial(hand, 1),
    }

    def fire(section):
        for (at, place), event in events.items():
            if place == section:
                pl.when(step == at)(event)

    _, col0, kind, inside, offset, live = slot_fields(rows_held)
    whole_window = inside == SPAN

    def on_window(action):
        for count, holds in ((ROWS, whole_window), (SHORT, jnp.logical_not(whole_window))):
            pl.when(live & holds)(functools.partial(action, count))

    @pl.when(step == 0)
    def _():
        for ref in (bias, grel, dqkv):
            ref[...] = jnp.zeros_like(ref)

    fire(0)

    @pl.when(slot == 0)
    def _():
        dmix[...] = dot_nt(da[...], wproj[far, 0]).astype(narrow)

    def one_pair(pair, count):
        cut = slice(pair * LANES, (pair + 1) * LANES)
        q, k8, v, rel = (qkv[0, j, :n, cut] for j, n in enumerate((count, ROWS, ROWS, count)))
        place = rows_at(offset, count)
        do = dmix[place, cut]
        dqs, dks, dvs = [], [], []
        for head in range(2):
            mine, other = sides[head : head + 1], sides[1 - head : 2 - head]
            full_key = k8 * mine + keys[kind] * other
            scores = dot_nt(full_key, q * mine + rel * other)
            top = jnp.max(scores, axis=0, keepdims=True)
            probs = jnp.exp(scores - top)
            probs = probs * (1.0 / jnp.sum(probs, axis=0, keepdims=True))
            dprobs = dot_nt(v, do * mine)
            mean = jnp.sum(probs * dprobs, axis=0, keepdims=True)
            dscores = (probs * (dprobs - mean)).astype(narrow)
            dvs.append(dot(probs.astype(narrow), do))
            dks.append(dot(dscores, q))
            dqs.append(dot_tn(dscores, full_key))
        low_lane = lax.broadcasted_iota(jnp.int32, (ROWS, LANES), 1) < 64
        dv = jnp.where(low_lane, dvs[0], dvs[1])
        dk = jnp.where(low_lane, dks[0], dks[1]) * 0.125
        low_lane = lax.broadcasted_iota(jnp.int32, (count, LANES), 1) < 64
        dq = jnp.where(low_lane, dqs[0], dqs[1])
        drel = jnp.where(low_lane, dqs[1], dqs[0]) * lanes[0:1]
        drel = shift_right(drel, bits.at[kind]).astype(narrow)
        dq = dq + dot(drel, wrel[...])
        grel[...] += dot_tn(drel, q)
        for j, value in enumerate((dq, dk, dv)):
            value = value.astype(narrow).astype(single)
            if j != 1:
                bias[far, j : j + 1, cut] += jnp.sum(value, axis=0, keepdims=True)
            value = value[:count]
            if count < ROWS:
                _, valid = positions(0, count, 0, kind, inside)
                value = jnp.where(valid, value, 0.0)
            dqkv[far, j, place, cut] = value.astype(narrow)

    for pair in range(half // LANES):
        fire(pair + 1)
        on_window(functools.partial(one_pair, pair))

    @pl.when(slot == SLOTS - 1)
    def _():
        part = half // 2
        at = step // SLOTS
        for j in range(4):
            if j < 3:
                total = dot_tn(dqkv[far, j], n1[...])
            else:
                total = dot_tn(mixed[far], da[...])
            keep[at, j * part : (j + 1) * part, :] = total[:part].astype(narrow)
            give[at, j * part : (j + 1) * part, :] = total[part:].astype(narrow)

    @pl.when(step == 2 * SLOTS - 1)
    def _():
        for (halver, _, _), total in zip(halvers, summed, strict=True):
            halver.back(1, total).wait()
        far_cross.wait()


def backward(rows_held, images, da, n1, qkv, mixed, weights, wrel, tables, residents, rest):
    half, width = weights.shape[2:]
    operands = [da, n1, qkv, mixed, weights, wrel, *tables, *residents, rest]
    in_specs = [whole(a.shape) for a in operands]

    def halved(i):
        return (1 - i // SLOTS) * SLOTS + i % SLOTS

    in_specs[2] = pl.BlockSpec((1, 4, ROWS, half), lambda i: (halved(i), 0, 0, 0))
    in_specs[4] = pl.BlockSpec(
        (2, 1, half, width), lambda i: (0, 3, 0, 0), pipeline_mode=pl.Buffered(1)
    )
    in_specs[-1] = ANY
    packed = (2 * half, width)
    square = residents[0].shape
    outs = [
        (of((2, 3, SLAB, half)), whole((2, 3, SLAB, half))),
        (of((2, *packed)), whole((2, *packed))),
        (of((2, *packed)), whole((2, *packed))),
        (of((2, 8, half), single), whole((2, 8, half))),
        (of((LANES, LANES), single), whole((LANES, LANES))),
        (of(packed), ANY),
        (of(square), ANY),
        (of(square), ANY),
    ]
    landing = (Halver.landing_rows(images, square[0]), width)
    copies = 3 + 2 * Halver.copies(images)
    return pl.pallas_call(
        functools.partial(backward_kernel, rows_held, images),
        out_shape=[o[0] for o in outs],
        grid=(2 * SLOTS,),
        in_specs=in_specs,
        out_specs=[o[1] for o in outs],
        scratch_shapes=[
            pltpu.VMEM((SLAB, half), narrow),
            pltpu.VMEM(packed, narrow),
            *[pltpu.VMEM(square, narrow)] * 2,
            *[pltpu.VMEM(landing, narrow)] * 2,
            pltpu.VMEM(rest.shape, narrow),
            pltpu.SemaphoreType.DMA((copies,)),
            pltpu.SemaphoreType.DMA((copies,)),
            pltpu.SemaphoreType.DMA((2,)),
        ],
        compiler_params=pltpu.CompilerParams(
            vmem_limit_bytes=VMEM, collective_id=2, has_side_effects=True
        ),
        cost_estimate=pl.CostEstimate(
            flops=52_000_000_000, bytes_accessed=80_000_000, transcendentals=8_000_000
        ),
        name="attention_backward",
    )(*operands)


def clear_rows(ext):
    @pl.loop(0, ext.shape[0] // GRID)
    def _(r):
        ext[rows_at(r * GRID, GRID), :] = jnp.zeros((GRID, ext.shape[1]), narrow)


def place_windows(rows_held, device, slab, ext, first, last):
    @pl.loop(first, last)
    def _(slot):
        row0, col0, kind, inside, offset, live = window_fields(rows_held, device, slot)

        @pl.when(live)
        def _():
            target, _ = positions(1, ROWS, col0, kind, inside)
            token = lax.broadcasted_iota(jnp.int32, (WIN * GRID, ROWS), 0)
            choose = jnp.where(token == target, 1.0, 0.0).astype(narrow)
            window = slab[rows_at(offset, ROWS), :]
            where_to = pl.ds(pl.multiple_of(row0 * GRID, GRID), WIN * GRID)
            ext[where_to, :] += dot(choose, window).astype(narrow)


def tail_kernel(
    rows_held, images,
    sums2, bias, rel_sum, fc_bias, peak, params,
    out_in, keep_in, crossed_in, xs_in, dx1_in, part1, part2, give, dqkv, weights,
    output, input_grad, packed, totals, tops, summed1, summed2,
    ext0, ext1, below0, below1, above0, above1, got, landing, held, sum_land, top_land, back, grads,
    packs, out, keep, crossed, xs, dx1, sends, recvs, locals_,
):
    device, image = lax.axis_index("tensor"), lax.axis_index("dp")
    beside, across, corner = partners(device)
    send = Sender(sends, recvs, locals_)
    hand_base = 1 + 2 * Halver.copies(images) + 4 + 2 * (1 + images.bit_length())
    early = [send.local(0, keep_in.at[1], keep), send.local(1, crossed_in, crossed)]
    loads = [
        send.local(2, dqkv, grads),
        send.local(3, weights.at[:, 0:3], packs),
        send.local(4, xs_in, xs),
        send.local(5, dx1_in, dx1),
    ]
    late = send.local(6, out_in, out)
    start_all(early + loads + [late])
    hand_last, stay = [], []
    for k, (part, summed, order) in enumerate(
        ((part1, summed1, (1, 0, 2)), (part2, summed2, (0, 1, 2)))
    ):
        mate, kept, _, length, _ = Halver(
            send, 0, image, images, 0, part.shape[0], order
        ).stages[0]
        cut = rows_at(kept, length)
        stay.append(send.local(7 + k, part.at[cut, :], summed.at[cut, :]))
        hand_last.append(
            send.remote(hand_base + k, part.at[cut, :], summed.at[cut, :], {"dp": mate})
        )
    start_all(stay)
    per = Halver.copies(images)
    middle = held.shape[0] // 2
    landing_rows = Halver.landing_rows(images, middle)
    landings = [landing.at[pl.ds(k * landing_rows, landing_rows), :] for k in range(2)]
    halvers = [
        Halver(send, 1 + k * per, image, images, k * middle, middle, order)
        for k, order in enumerate(((0, 1, 2), (1, 0, 2)))
    ]
    halo_base = 1 + 2 * per
    small_base = halo_base + 4
    tokens = rows_held * GRID
    top, bottom = LEFT * GRID, RIGHT * GRID
    held_by = (device, beside, across, corner)
    mates = dp_mates(image, images)
    ring = [{"tensor": beside}, {"tensor": across}] + mates

    def reduce_start(stage):
        for halver, land in zip(halvers, landings, strict=True):
            halver.start(stage, held, land)

    def reduce_finish(stage):
        for halver, land in zip(halvers, landings, strict=True):
            halver.finish(stage, held, land)

    def hand_start(stage):
        for halver in halvers:
            halver.back(stage, packed).start()

    def hand_finish(stage):
        for halver in halvers:
            halver.back(stage, packed).wait()

    greet([{"tensor": place} for place in (beside, across, corner)] + mates)
    swap = send.remote(0, give.at[1], got, {"tensor": beside})
    swap.start()
    totals[...] = jnp.zeros_like(totals)
    tops[...] = jnp.zeros_like(tops)
    totals[2:6, :] = sums2[0:4, :]
    rel = rel_sum[...]
    rel = rel[HD:] + pltpu.roll(rel[:HD], HD, 1)
    for g in range(HD // 8):
        at = 8 * (1 + g // 6)
        totals[at : at + 8, (g % 6) * LANES : (g % 6 + 1) * LANES] = rel[8 * g : 8 * g + 8]
    half = bias.shape[2]
    for k in range(SPLIT):
        far, odd = k // 2, k % 2
        totals[pl.ds(24 + held_by[k], 1), :] = fc_bias[k, 0:1, :]
        for j, row in enumerate((0, 2)):
            value = bias[far, row : row + 1, :]
            if odd:
                value = pltpu.roll(value, half // 2, 1)
            totals[pl.ds(28 + held_by[k], 1), j * half : (j + 1) * half] = value
        best = jnp.broadcast_to(jnp.max(peak[far], axis=1, keepdims=True), (8, LANES))
        if odd:
            best = pltpu.roll(best, 8 - half // LANES, 0)
        tops[pl.ds(pl.multiple_of(held_by[k] * 8, 8), 8), :] = best

    def small_copies(k):
        return [
            send.remote(small_base + 2 * k, totals, sum_land.at[k], ring[k]),
            send.remote(small_base + 2 * k + 1, tops, top_land.at[k], ring[k]),
        ]

    def small_start(k):
        for copy in small_copies(k):
            copy.start()

    def small_finish(k):
        for copy in small_copies(k):
            copy.wait()
        totals[...] += sum_land[k]
        tops[...] = jnp.maximum(tops[...], top_land[k])

    def halo(base, ext, below, above):
        up = send.remote(
            base, ext.at[pl.ds(0, top), :], below, {"tensor": (device + SPLIT - 1) % SPLIT}
        )
        down = send.remote(
            base + 1, ext.at[pl.ds(top + tokens, bottom), :], above, {"tensor": (device + 1) % SPLIT}
        )
        return up, down

    def halo_start(copies):
        up, down = copies
        pl.when(device > 0)(up.start)
        pl.when(device < SPLIT - 1)(down.start)

    def halo_finish(copies, ext, below, above, result):
        up, down = copies
        pl.when(device > 0)(up.wait_send)
        pl.when(device < SPLIT - 1)(down.wait_send)
        add_rows(result, 0, [(ext, top)], tokens)

        @pl.when(device < SPLIT - 1)
        def _():
            up.wait_recv()
            at = tokens - top
            add_rows(result, at, [(result, at), (below, 0)], top)

        @pl.when(device > 0)
        def _():
            down.wait_recv()
            add_rows(result, 0, [(result, 0), (above, 0)], bottom)

    def norm1_back():
        @pl.loop(0, SLAB // CHUNK)
        def _(c):
            sl = rows_at(c * CHUNK, CHUNK)
            grad = None
            for far in range(2):
                for j in range(3):
                    term = dot(grads[far, j, sl, :], packs[far, j])
                    grad = term if grad is None else grad + term
            normal, inverse = norm_parts(xs[sl, :].astype(single))
            totals[0:1, :] += jnp.sum(grad * normal, axis=0, keepdims=True)
            totals[1:2, :] += jnp.sum(grad, axis=0, keepdims=True)
            result = dx1[sl, :] + norm_back(grad, normal, inverse, params[8:9])
            back[sl, :] = result.astype(narrow)

    clear_rows(ext0)
    clear_rows(ext1)
    for copy in early:
        copy.wait()
    swap.wait()
    add_rows(held, 0, [(keep, 0), (got, 0), (crossed, 0)], held.shape[0])
    reduce_start(0)
    for copy in loads:
        copy.wait()
    norm1_back()
    small_start(0)
    reduce_finish(0)
    reduce_start(1)
    place_windows(rows_held, device, back, ext1, 0, SLOTS)
    halos1 = halo(halo_base, ext1, below1, above1)
    halo_start(halos1)
    small_finish(0)
    small_start(1)
    reduce_finish(1)
    reduce_start(2)
    start_all(hand_last)
    late.wait()
    place_windows(rows_held, device, out, ext0, 0, 4)
    small_finish(1)
    small_start(2)
    reduce_finish(2)
    for halver, land in zip(halvers, landings, strict=True):
        halver.extras(held, land)
        start, length = halver.final
        packed[rows_at(start, length), :] = held[rows_at(start, length), :]
    hand_start(2)
    place_windows(rows_held, device, out, ext0, 4, SLOTS)
    halos0 = halo(halo_base + 2, ext0, below0, above0)
    halo_start(halos0)
    small_finish(2)
    small_start(3)
    halo_finish(halos1, ext1, below1, above1, input_grad)
    hand_finish(2)
    hand_start(1)
    small_finish(3)
    small_start(4)
    hand_finish(1)
    hand_start(0)
    for k in range(4, len(ring)):
        small_finish(k)
        if k + 1 < len(ring):
            small_start(k + 1)
    halo_finish(halos0, ext0, below0, above0, output)
    hand_finish(0)
    for copy in stay + hand_last:
        copy.wait()


def tail(rows_held, images, *operands):
    width = operands[-1].shape[3]
    half = operands[-1].shape[2]
    packed = (2 * half, width)
    tokens = rows_held * GRID
    bits = images.bit_length() - 1
    landing = 2 * Halver.landing_rows(images, packed[0] // 2)
    copies = 1 + 2 * Halver.copies(images) + 4 + 2 * (2 + bits) + 2
    ext = ((rows_held + LEFT + RIGHT) * GRID, width)
    outs = [
        of((tokens, width)), of((tokens, width)), of(packed),
        of((32, width), single), of((32, LANES), single),
        of(operands[-5].shape), of(operands[-4].shape),
    ]
    return pl.pallas_call(
        functools.partial(tail_kernel, rows_held, images),
        out_shape=outs,
        in_specs=[pl.BlockSpec(memory_space=pltpu.VMEM)] * (len(operands) - 10) + [ANY] * 10,
        out_specs=[pl.BlockSpec(memory_space=pltpu.VMEM)] * 5 + [ANY] * 2,
        scratch_shapes=[
            pltpu.VMEM(ext, narrow),
            pltpu.VMEM(ext, narrow),
            pltpu.VMEM((LEFT * GRID, width), narrow),
            pltpu.VMEM((LEFT * GRID, width), narrow),
            pltpu.VMEM((RIGHT * GRID, width), narrow),
            pltpu.VMEM((RIGHT * GRID, width), narrow),
            pltpu.VMEM(packed, narrow),
            pltpu.VMEM((landing, width), narrow),
            pltpu.VMEM(packed, narrow),
            pltpu.VMEM((2 + bits, 32, width), single),
            pltpu.VMEM((2 + bits, 32, LANES), single),
            pltpu.VMEM((SLAB, width), narrow),
            pltpu.VMEM((2, 3, SLAB, half), narrow),
            pltpu.VMEM((2, 3, half, width), narrow),
            pltpu.VMEM((SLAB, width), narrow),
            *[pltpu.VMEM(packed, narrow)] * 2,
            pltpu.VMEM((SLAB, width), narrow),
            pltpu.VMEM((SLAB, width), single),
            pltpu.SemaphoreType.DMA((copies,)),
            pltpu.SemaphoreType.DMA((copies,)),
            pltpu.SemaphoreType.DMA((9,)),
        ],
        compiler_params=pltpu.CompilerParams(
            vmem_limit_bytes=VMEM, collective_id=3, has_side_effects=True
        ),
        cost_estimate=pl.CostEstimate(
            flops=4_000_000_000, bytes_accessed=20_000_000, transcendentals=0
        ),
        name="tail",
    )(*operands)


def finish_kernel(
    fc1, fc2, gq, gp, out_in, back_in, totals, tops, wqkv,
    grad_fc1, grad_fc2, grad_qkv, grad_proj, out, back, clipped, qv, fc1_bias, norms, proj_bias,
    fc2_bias, rel, head_max,
):
    device = lax.axis_index("tensor")
    out[...] = out_in[...]
    back[...] = back_in[...]
    grad_fc1[...] = fc1[...].astype(single)
    grad_fc2[...] = fc2[...].astype(single).T
    grad_qkv[...] = gq[...].astype(single)
    grad_proj[...] = gp[...].astype(single)

    @pl.when(pl.program_id(0) == 0)
    def _():
        local = wqkv.shape[1]
        largest = tops[pl.ds(pl.multiple_of(8 * device, 8), 8), :]
        head_max[...] = largest.T[0, : local // HD]
        limit = jnp.maximum(largest, CLIP)
        factor = jnp.sqrt(CLIP / limit)
        factor = jnp.concatenate([factor] * (wqkv.shape[2] // LANES), axis=1)
        for j in range(2):
            for head in range(local // HD):
                cut = slice(head * HD, (head + 1) * HD)
                scaled = wqkv[j, cut, :].astype(single) * factor[head : head + 1]
                clipped[j, cut, :] = scaled.astype(narrow)
            qv[j : j + 1, :] = totals[pl.ds(28 + device, 1), 2 * j * local : (2 * j + 1) * local]
        fc1_bias[...] = totals[24 + device, :]
        norms[...] = totals[0:4, :]
        proj_bias[...] = totals[4, :]
        fc2_bias[...] = totals[5, :]
        span = 2 * WIN - 1
        for j in range(2):
            for first in range(0, span, 8):
                group = (32 * j + first) // 8
                count = min(8, span - first)
                at, lane = 8 * (1 + group // 6), (group % 6) * LANES
                rel[first : first + count, j, :] = totals[at : at + count, lane : lane + HD]


def finish(summed1, summed2, gpack, output, input_grad, totals, tops, wqkv):
    _, local, width = wqkv.shape
    hidden = summed1.shape[1]
    parts = 3
    batch = output.shape[0] // 2
    pages = pl.BlockSpec((batch, width), lambda i: (jnp.minimum(i, 1), 0))
    heads = local // HD
    rows, cols, lines = width // parts, hidden // parts, 3 * local // parts
    few = local // parts

    def by_rows(count, columns, first=0):
        return pl.BlockSpec((count, columns), lambda i: (first + i, 0))

    span = 2 * WIN - 1
    outs = [
        (of((width, hidden), single), by_rows(rows, hidden)),
        (of((hidden, width), single), by_rows(cols, width)),
        (of((3 * local, width), single), by_rows(lines, width)),
        (of((local, width), single), by_rows(few, width)),
        (of(output.shape), pages),
        (of(output.shape), pages),
        (of((2, local, width)), whole((2, local, width))),
        (of((2, local), single), whole((2, local))),
        (of((hidden,), single), whole((hidden,))),
        (of((4, width), single), whole((4, width))),
        (of((width,), single), whole((width,))),
        (of((width,), single), whole((width,))),
        (of((span, 2, HD), single), whole((span, 2, HD))),
        (of((heads,), single), whole((heads,))),
    ]
    return pl.pallas_call(
        finish_kernel,
        out_shape=[o[0] for o in outs],
        grid=(parts,),
        in_specs=[
            by_rows(rows, hidden),
            pl.BlockSpec((width, cols), lambda i: (0, i)),
            by_rows(lines, width),
            by_rows(few, width, 3 * local // few),
            pages,
            pages,
            whole(totals.shape),
            whole(tops.shape),
            whole(wqkv.shape),
        ],
        out_specs=[o[1] for o in outs],
        compiler_params=pltpu.CompilerParams(vmem_limit_bytes=VMEM),
        cost_estimate=pl.CostEstimate(flops=0, bytes_accessed=14_000_000, transcendentals=0),
        name="finish",
    )(summed1, summed2, gpack, gpack, output, input_grad, totals, tops, wqkv)


def shards(
    inputs,
    w_qkv,
    qv_bias,
    w_proj,
    proj_bias,
    w_fc1,
    fc1_bias,
    w_fc2,
    fc2_bias,
    norm1_gain,
    norm1_shift,
    norm2_gain,
    norm2_shift,
    rel_h,
    rel_w,
    cotangent,
):
    width = inputs.shape[2]
    rows = inputs.shape[1] // GRID
    local = w_qkv.shape[2]
    tables = lane_tables()

    wqkv = w_qkv.transpose(0, 2, 1)

    (
        xs, gs, n1, qkv, mixed, attn, peak, params, wrel,
        weights, across1, across2, beside1, beside2, smalls,
    ) = forward(
        *(a.reshape(rows, GRID, width) for a in (inputs, cotangent)), wqkv, w_proj, w_fc1, w_fc2,
        (
            fc1_bias, norm1_gain, norm1_shift, proj_bias, norm2_gain, norm2_shift, fc2_bias,
        ),
        qv_bias, (rel_h, rel_w), tables
    )
    out, dx1, da, sums2, near1, near2, far1, rest, fc_bias = mlp(
        (
            xs, attn, gs, params, smalls,
        ),
        (across1, across2),
        (beside1, beside2),
        (w_fc1, w_fc2),
    )
    images = lax.axis_size("dp")
    dqkv, keep, give, bias, rel_sum, crossed, part1, part2 = backward(
        rows, images, da, n1, qkv, mixed, weights, wrel, tables, [near1, near2, far1], rest
    )
    output, input_grad, gpack, totals, tops, summed1, summed2 = tail(
        rows, images, sums2, bias, rel_sum, fc_bias, peak, params, out, keep, crossed, xs, dx1,
        part1, part2, give, dqkv, weights,
    )
    (
        grad_fc1, grad_fc2, grad_qkv, grad_proj, output, input_grad, clipped, grad_qv,
        grad_fc1_bias, grad_norms, grad_proj_bias, grad_fc2_bias, grad_rel, head_max,
    ) = finish(summed1, summed2, gpack, output, input_grad, totals, tops, wqkv)

    return (
        output[None],
        input_grad[None],
        grad_qkv.reshape(3, local, width).transpose(0, 2, 1),
        grad_qv,
        grad_proj,
        grad_proj_bias,
        grad_fc1,
        grad_fc1_bias,
        grad_fc2,
        grad_fc2_bias,
        grad_norms,
        grad_rel.transpose(1, 0, 2),
        clipped.transpose(0, 2, 1),
        head_max,
    )


def solution(mesh):
    return jax.shard_map(
        shards,
        mesh=mesh,
        in_specs=(
            P("dp", "tensor", None),
            P(None, None, "tensor"),
            P(None, "tensor"),
            P("tensor", None),
            P(),
            P(None, "tensor"),
            P("tensor"),
            P("tensor", None),
            P(),
            P(),
            P(),
            P(),
            P(),
            P(),
            P(),
            P("dp", "tensor", None),
        ),
        out_specs=(
            P("dp", "tensor", None),
            P("dp", "tensor", None),
            P(None, None, "tensor"),
            P(None, "tensor"),
            P("tensor", None),
            P(),
            P(None, "tensor"),
            P("tensor"),
            P("tensor", None),
            P(),
            P(),
            P(),
            P(None, None, "tensor"),
            P("tensor"),
        ),
        check_vma=False,
    )
```

```python
import functools

import jax
import jax.numpy as jnp
import numpy as np
from jax import lax
from jax.experimental import pallas as pl
from jax.experimental.pallas import tpu as pltpu
from jax.sharding import PartitionSpec as P

HD = 64
GRID = 64
WIN = 14
TILES = 5
SPAN = WIN * WIN
ROWS = 208
SLOTS = 7
EDGE = GRID % WIN
SHORT = EDGE * WIN
SLAB = (SLOTS - 2) * ROWS + SHORT
STRIP = SLAB // 6
SPLIT = 4
LEFT = 6
RIGHT = 12
LANES = 128
EPS = 1e-6
CLIP = 3.0
VMEM = 60 * 1024 * 1024

single = jnp.float32
narrow = jnp.bfloat16

def lane_tables():
    row = np.arange(ROWS)
    late = np.maximum(row - SHORT, 0)
    outer = WIN - EDGE
    orders = (
        (row // WIN, row % WIN),
        (
            np.where(row < SHORT, row // EDGE, late // outer),
            np.where(row < SHORT, row % EDGE, EDGE + late % outer),
        ),
    )
    lane = np.arange(LANES) % 64
    part = lane // 32
    at = lane % 32
    bits, keys = [], []
    for x, y in orders:
        amount = np.where(part[None, :] == 0, x[:, None], y[:, None])
        amount = np.where((row < SPAN)[:, None], amount, 0)
        bits.append(np.stack([(amount >> b) & 1 for b in range(4)]).astype(np.float32))
        place = WIN - 1 - np.where(part[None, :] == 0, x[:, None], y[:, None])
        hot = ((at % 16)[None, :] == place) & ((at % 16) < WIN)[None, :] & (row < SPAN)[:, None]
        hot = hot.astype(np.float32)
        hot[SPAN:, lane == 31] = -1e30
        keys.append(hot)
    lanes = np.zeros((8, LANES), np.float32)
    lanes[0] = at < WIN
    lanes[1] = (at >= 16) & (at < 16 + WIN)
    lanes[2] = lane == 31
    sides = np.zeros((16, LANES), np.float32)
    sides[0] = np.arange(LANES) < 64
    sides[1] = np.arange(LANES) >= 64
    return (
        jnp.asarray(np.stack(bits)),
        jnp.asarray(lanes),
        jnp.asarray(sides, narrow),
        jnp.asarray(np.stack(keys), narrow),
    )


def dot(a, b):
    return jnp.dot(a, b, preferred_element_type=single)


def dot_nt(a, b):
    return lax.dot_general(a, b, (((1,), (1,)), ((), ())), preferred_element_type=single)


def dot_tn(a, b):
    return lax.dot_general(a, b, (((0,), (0,)), ((), ())), preferred_element_type=single)


def norm_parts(values):
    centre = values - jnp.mean(values, axis=-1, keepdims=True)
    inverse = lax.rsqrt(jnp.mean(centre * centre, axis=-1, keepdims=True) + EPS)
    return centre * inverse, inverse


def norm_back(grad, normal, inverse, gain):
    scaled = grad * gain
    first = jnp.mean(scaled, axis=-1, keepdims=True)
    second = jnp.mean(scaled * normal, axis=-1, keepdims=True)
    return inverse * (scaled - first - normal * second)


def slot_fields(rows_held):
    return window_fields(rows_held, lax.axis_index("tensor"), pl.program_id(0) % SLOTS)


def window_fields(rows_held, device, slot):
    first = device * (SLOTS - 1)
    window = first + slot
    i, j = window // TILES, window % TILES
    last = device // (SPLIT - 1)
    live = slot < SLOTS - 1 + last
    row0 = i * WIN - device * rows_held + LEFT
    high = jnp.minimum(WIN, GRID - i * WIN)
    wide = jnp.minimum(WIN, GRID - j * WIN)

    def short_before(n):
        return jnp.minimum(n // TILES, TILES - 1) + jnp.maximum(n - TILES * (TILES - 1), 0)

    offset = ROWS * slot - (ROWS - SHORT) * (short_before(window) - short_before(first))
    return row0, j * WIN, j // (TILES - 1), high * wide, offset, live


def positions(axis, count, first_col, kind, inside):
    shape = (count, 1) if axis == 0 else (1, count)
    row = lax.broadcasted_iota(jnp.int32, shape, axis)
    x = lax.shift_right_logical(row * 4682, 16)
    plain = x * GRID + (row - x * WIN)
    x = lax.shift_right_logical(row, EDGE.bit_length() - 1)
    edge = x * GRID + (row - x * EDGE)
    token = jnp.where(kind == 1, edge, plain) + first_col
    return jnp.where(row < inside, token, -1), row < inside


def gather_window(source, target):
    token = lax.broadcasted_iota(jnp.int32, (target.shape[0], WIN * GRID), 1)
    choose = jnp.where(token == target, 1.0, 0.0).astype(narrow)
    return dot(choose, source)


def shift_left(values, bits):
    for b in range(4):
        taken = bits[b, : values.shape[0]] > 0.5
        values = jnp.where(taken, pltpu.roll(values, LANES - (1 << b), 1), values)
    return values


def shift_right(values, bits):
    for b in range(4):
        taken = bits[b, : values.shape[0]] > 0.5
        values = jnp.where(taken, pltpu.roll(values, 1 << b, 1), values)
    return values


def partners(device):
    beside = device + 1 - 2 * (device % 2)
    across = (device + 2) % SPLIT
    corner = (beside + 2) % SPLIT
    return beside, across, corner


def greet(places):
    barrier = pltpu.get_barrier_semaphore()
    for place in places:
        pl.semaphore_signal(barrier, inc=1, device_id=place, device_id_type=pl.DeviceIdType.MESH)
    pl.semaphore_wait(barrier, len(places))


class Sender:
    def __init__(self, sends, recvs, locals_):
        self.sends, self.recvs, self.locals = sends, recvs, locals_

    def remote(self, at, source, target, place):
        return pltpu.make_async_remote_copy(
            src_ref=source,
            dst_ref=target,
            send_sem=self.sends.at[at],
            recv_sem=self.recvs.at[at],
            device_id=place,
            device_id_type=pl.DeviceIdType.MESH,
        )

    def local(self, at, source, target):
        return pltpu.make_async_copy(source, target, self.locals.at[at])


def mate_of(image, bit):
    unit = 1 << bit
    return image + unit * (1 - 2 * ((image // unit) % 2))


def rows_at(start, count):
    return pl.ds(pl.multiple_of(start, 16), count)


def add_rows(target, target_at, sources, count):
    chunk = next(c for c in (96, 48, 16) if count % c == 0)

    @pl.loop(0, count // chunk)
    def _(c):
        total = None
        for ref, at in sources:
            value = ref[rows_at(at + c * chunk, chunk), :]
            total = value if total is None else total + value
        target[rows_at(target_at + c * chunk, chunk), :] = total


HALVINGS = 3


class Halver:
    def __init__(self, send, base, image, images, start, rows, order):
        bits = images.bit_length() - 1
        assert images == 1 << bits and bits >= HALVINGS
        self.send, self.base, self.image = send, base, image
        self.extra_bits = range(HALVINGS, bits)
        self.stages = []
        landing, length = 0, rows
        for bit in order:
            length //= 2
            mine = (image // (1 << bit)) % 2
            keep, give = start + mine * length, start + (1 - mine) * length
            self.stages.append((mate_of(image, bit), keep, give, length, landing))
            landing += length
            start = keep
        self.final = (start, length)
        self.landing = landing

    @staticmethod
    def copies(images):
        return 2 * HALVINGS + images.bit_length() - 1 - HALVINGS

    @staticmethod
    def landing_rows(images, rows):
        last = rows >> HALVINGS
        return rows - last + last * (images.bit_length() - 1 - HALVINGS)

    def out(self, stage, held, landing):
        mate, _, give, length, at = self.stages[stage]
        return self.send.remote(
            self.base + stage,
            held.at[rows_at(give, length), :],
            landing.at[pl.ds(at, length), :],
            {"dp": mate},
        )

    def start(self, stage, held, landing):
        self.out(stage, held, landing).start()

    def finish(self, stage, held, landing):
        self.out(stage, held, landing).wait()
        _, keep, _, length, at = self.stages[stage]
        add_rows(held, keep, [(held, keep), (landing, at)], length)

    def extras(self, held, landing):
        start, length = self.final
        for k, bit in enumerate(self.extra_bits):
            at = self.landing + k * length
            copy = self.send.remote(
                self.base + HALVINGS + k,
                held.at[rows_at(start, length), :],
                landing.at[pl.ds(at, length), :],
                {"dp": mate_of(self.image, bit)},
            )
            copy.start()
            copy.wait()
            add_rows(held, start, [(held, start), (landing, at)], length)

    def back(self, stage, held):
        mate, keep, _, length, _ = self.stages[stage]
        cut = rows_at(keep, length)
        at = self.base + HALVINGS + len(self.extra_bits) + stage
        return self.send.remote(at, held.at[cut, :], held.at[cut, :], {"dp": mate})


def dp_mates(image, images):
    return [{"dp": mate_of(image, bit)} for bit in range(images.bit_length() - 1)]


def project(n1, weights, qbias, vbias, projected, place):
    projected[0, place, :] = (dot_nt(n1, weights[0]) + qbias).astype(narrow)
    projected[1, place, :] = dot_nt(n1, weights[1]).astype(narrow) * jnp.asarray(0.125, narrow)
    projected[2, place, :] = (dot_nt(n1, weights[2]) + vbias).astype(narrow)


def attend(count, place, valid, projected, vbias, wrel, bits, lanes, sides, keys, qkv, mixed, peak):
    half = projected.shape[2]
    qkv[0, 0, :count] = jnp.where(valid, projected[0, place, :].astype(single), 0.0).astype(narrow)
    qkv[0, 1, :count] = projected[1, place, :]
    qkv[0, 2, :count] = projected[2, place, :]
    if count < ROWS:
        left = ROWS - count
        qkv[0, 1, count:] = jnp.zeros((left, half), narrow)
        qkv[0, 2, count:] = jnp.broadcast_to(vbias, (left, half)).astype(narrow)
    low_lane = lax.broadcasted_iota(jnp.int32, (count, LANES), 1) < 64
    for pair in range(half // LANES):
        cut = slice(pair * LANES, (pair + 1) * LANES)
        q, k8, v = qkv[0, 0, :count, cut], qkv[0, 1, :, cut], qkv[0, 2, :, cut]
        rel = shift_left(dot_nt(q, wrel[...]), bits)
        rest = rel - rel.astype(narrow).astype(single)
        rel = rel * lanes[0:1] + pltpu.roll(rest, 16, 1) * lanes[1:2] + lanes[2:3]
        rel = rel.astype(narrow)
        qkv[0, 3, :count, cut] = rel
        pieces = []
        for head in range(2):
            mine, other = sides[head : head + 1], sides[1 - head : 2 - head]
            only = q * mine
            logits = dot_nt(only, k8)
            at = 2 * pair + head
            peak[at : at + 1, :] = jnp.maximum(
                peak[at : at + 1, :], jnp.max(logits, axis=0, keepdims=True)
            )
            scores = dot_nt(only + rel * other, k8 * mine + keys[...] * other)
            top = jnp.max(scores, axis=1, keepdims=True)
            probs = jnp.exp(scores - top)
            total = jnp.sum(probs, axis=1, keepdims=True)
            pieces.append(dot(probs.astype(narrow), v) * (1.0 / total))
        mixed[place, cut] = jnp.where(low_lane, pieces[0], pieces[1]).astype(narrow)


class Halo:
    def __init__(self, send, base, grid, ext, device, rows):
        below, above = {"tensor": (device + 1) % SPLIT}, {"tensor": (device + SPLIT - 1) % SPLIT}
        self.has_below, self.has_above = device < SPLIT - 1, device > 0
        self.cross_below, self.cross_above = device == 1, device == 2

        def copy(at, first, count, first_col, cols, target_row, place):
            window = (pl.ds(first, count), pl.ds(first_col, cols), slice(None))
            return send.remote(
                at, grid.at[window], ext.at[(pl.ds(target_row, count), *window[1:])], place
            )

        few, many = 4, 10
        self.down = copy(base, rows - LEFT, LEFT, 0, GRID, 0, below)
        self.down_cross = copy(base, rows - few, few, 16, GRID - 16, LEFT - few, below)
        self.up = copy(base + 1, 0, RIGHT, 0, GRID, LEFT + rows, above)
        self.up_cross = copy(base + 1, 0, many, 0, 32, LEFT + rows, above)

    def _each(self, down_here, up_here, act):
        for here, crossing, plain, crossed in (
            (*down_here, self.down, self.down_cross),
            (*up_here, self.up, self.up_cross),
        ):

            @pl.when(here & jnp.logical_not(crossing))
            def _():
                act(plain)

            @pl.when(crossing)
            def _():
                act(crossed)

    def _senders(self, act):
        self._each((self.has_below, self.cross_below), (self.has_above, self.cross_above), act)

    def start(self):
        self._senders(lambda copy: copy.start())

    def wait_send(self):
        self._senders(lambda copy: copy.wait_send())

    def wait_from_above(self):
        pl.when(self.has_above & jnp.logical_not(self.cross_above))(self.down.wait_recv)
        pl.when(self.cross_above)(self.down_cross.wait_recv)

    def wait_from_below(self):
        pl.when(self.has_below & jnp.logical_not(self.cross_below))(self.up.wait_recv)
        pl.when(self.cross_below)(self.up_cross.wait_recv)


class Quartet:
    def __init__(self, send, base, image, pieces, across):
        side, deep = image % 2, (image // 2) % 2
        beside, behind = {"dp": mate_of(image, 0)}, {"dp": mate_of(image, 1)}
        mine = 2 * deep + side
        from_beside, from_behind = 2 * deep + 1 - side, 2 * (1 - deep) + side
        self.first, self.second, self.third = [], [], []
        for k, (source, target, view) in enumerate(pieces):
            at = base + 5 * k

            def copy(number, origin, quarter, part, place):
                return send.remote(at + number, view(origin, quarter, part), view(target, quarter, part), place)

            self.first.append(copy(0, source, mine, None, across))
            self.second.append(copy(1, target, mine, None, beside))
            self.second.append(copy(2, target, mine, None, behind))
            if view(target, from_behind, 0) is not None:
                self.third.append(copy(3, target, from_behind, 0, beside))
            self.third.append(copy(4, target, from_beside, 1, behind))


def quarter_rows(array, quarter, part):
    size = array.shape[0] // 4
    start = quarter * size
    if part is not None:
        size //= 2
        start += part * size
    return array.at[rows_at(start, size), :]


def start_all(copies):
    for copy in copies:
        copy.start()


def receive_all(copies):
    for copy in copies:
        copy.wait_recv()


def forward_kernel(
    x, g, wqkv, wproj, fc1, fc2, vectors, qv_bias, rel_tables, bits, lanes, sides, keys,
    xs_out, gs, n1_out, qkv, mixed, attn, peak, params, wrel, weights_out, across1, across2, beside1,
    beside2, small_out,
    xext, gext, weights, smalls, projected, xs, n1_all, sends, recvs, locals_,
):
    step = pl.program_id(0)
    far, slot = step // SLOTS, step % SLOTS
    device, image = lax.axis_index("tensor"), lax.axis_index("dp")
    rows, _, width = x.shape
    part = wproj.shape[0]
    half = 2 * part
    beside, across, corner = partners(device)
    send = Sender(sends, recvs, locals_)
    x_halo = Halo(send, 0, x, xext, device, rows)
    g_halo = Halo(send, 2, g, gext, device, rows)
    small = params.at[pl.ds(0, 8), :]

    own_pack = [
        send.remote(4, wqkv, weights.at[0, 0:3, pl.ds(part, part), :], {"tensor": beside}),
        send.remote(5, wproj, weights.at[0, 3, pl.ds(part, part), :], {"tensor": beside}),
    ]
    notes = [
        send.remote(6 + k, small, smalls.at[k + 1], {"tensor": place})
        for k, place in enumerate((beside, across, corner))
    ]
    fc_beside = [
        send.remote(9, fc1, beside1, {"tensor": beside}),
        send.remote(10, fc2, beside2, {"tensor": beside}),
    ]
    corner_pack = send.remote(
        11, weights.at[1, :, pl.ds(0, part), :], weights.at[1, :, pl.ds(part, part), :], {"tensor": beside}
    )

    def of_qkv(array, quarter, half_of):
        size = part // 4
        cut = rows_at(quarter * size, size)
        if array is wqkv:
            return array.at[:, cut, :]
        if half_of is None:
            return array.at[1, 0:3, cut, :]
        return array.at[1, 0:2, cut, :] if half_of == 0 else array.at[1, 2:3, cut, :]

    def of_proj(array, quarter, half_of):
        size = part // 4
        cut = rows_at(quarter * size, size)
        if array is wproj:
            return array.at[cut, :]
        return None if half_of == 0 else array.at[1, 3, cut, :]

    pack_far = Quartet(
        send, 12, image, ((wqkv, weights, of_qkv), (wproj, weights, of_proj)), {"tensor": across}
    )
    fc_far = Quartet(
        send, 22, image, ((fc1, across1, quarter_rows), (fc2, across2, quarter_rows)), {"tensor": across}
    )
    own = [
        send.local(0, wqkv, weights.at[0, 0:3, pl.ds(0, part), :]),
        send.local(1, wproj, weights.at[0, 3, pl.ds(0, part), :]),
        send.local(2, x, xext.at[pl.ds(LEFT, rows)]),
        send.local(3, small, smalls.at[0]),
    ]
    g_own = send.local(4, g, gext.at[pl.ds(LEFT, rows)])
    kept = [
        send.local(5, weights, weights_out),
        send.local(6, smalls, small_out),
        send.local(7, xs, xs_out),
        send.local(8, n1_all, n1_out),
    ]

    @pl.when(step == 0)
    def _():
        params[...] = jnp.zeros_like(params)
        for ref, row in zip(vectors, (0, 8, 9, 10, 11, 12, 13), strict=True):
            params[row, :] = ref[...]
        for j in range(2):
            params[1 + 2 * j, 0:part] = qv_bias[j, :]
            params[2 + 2 * j, part:half] = qv_bias[j, :]
        wrel[...] = jnp.zeros_like(wrel)
        span = 2 * WIN - 1
        for ref, at in zip(rel_tables, (0, 32), strict=True):
            wrel[HD + at : HD + at + span, :HD] = ref[...]
            wrel[at : at + span, HD:] = ref[...]
        for ref in (xext, gext):
            ref[pl.ds(0, LEFT)] = jnp.zeros((LEFT, GRID, width), narrow)
            ref[pl.ds(LEFT + rows, RIGHT)] = jnp.zeros((RIGHT, GRID, width), narrow)
        greet(
            [{"tensor": place} for place in (beside, across, corner)]
            + [{"dp": mate_of(image, bit)} for bit in range(2)]
        )
        start_all(own_pack + notes + own)
        x_halo.start()
        start_all(pack_far.first)
        for ref in (xs, gs, n1_all, mixed, peak):
            ref[...] = jnp.zeros_like(ref)
        for copy in own + notes + own_pack:
            copy.wait()
        x_halo.wait_from_above()

    @pl.when(step == 1)
    def _():
        start_all(fc_beside + [g_own])

    @pl.when(step == 2)
    def _():
        receive_all(pack_far.first)
        start_all(pack_far.second)
        start_all(fc_far.first)

    @pl.when(step == 3)
    def _():
        x_halo.wait_from_below()

    @pl.when(step == 4)
    def _():
        receive_all(pack_far.second)
        start_all(pack_far.third)

    @pl.when(step == 5)
    def _():
        receive_all(fc_far.first)
        start_all(fc_far.second)
        g_halo.start()

    @pl.when(step == 6)
    def _():
        receive_all(pack_far.third)
        corner_pack.start()

    @pl.when(step == SLOTS)
    def _():
        corner_pack.wait_recv()
        start_all(kept)

    @pl.when(step == SLOTS + 2)
    def _():
        receive_all(fc_far.second)
        start_all(fc_far.third)

    row0, col0, kind, inside, offset, live = slot_fields(rows)
    whole_window = inside == SPAN
    tables = (wrel, bits.at[kind], lanes, sides, keys.at[kind])

    def biases(which):
        return (
            smalls[2 * which, 1:2, :half] + smalls[2 * which + 1, 2:3, :half],
            smalls[2 * which, 3:4, :half] + smalls[2 * which + 1, 4:5, :half],
        )

    @pl.when(step == SLOTS)
    def _():
        project(n1_all[...], weights.at[1], *biases(1), projected, slice(None))

    def work(count):
        place = rows_at(offset, count)

        @pl.when(far == 0)
        def _():
            target, valid = positions(0, count, col0, kind, inside)
            source = xext[pl.ds(row0, WIN)].reshape(WIN * GRID, width)
            window = gather_window(source, target)
            xs[place, :] = window.astype(narrow)
            normal, _ = norm_parts(window)
            n1 = jnp.where(valid, normal * params[8:9] + params[9:10], 0.0).astype(narrow)
            n1_all[place, :] = n1
            project(n1, weights.at[0], *biases(0), projected, place)

        _, valid = positions(0, count, col0, kind, inside)
        attend(
            count, place, valid, projected, biases(far)[1], *tables, qkv, mixed.at[far], peak.at[far]
        )

    pl.when(live & whole_window)(functools.partial(work, ROWS))
    pl.when(live & jnp.logical_not(whole_window))(functools.partial(work, SHORT))

    @pl.when(step == 2 * SLOTS - 1)
    def _():
        attn[...] = dot(mixed[0], weights[0, 3]) + dot(mixed[1], weights[1, 3])
        g_own.wait()
        g_halo.wait_from_above()
        g_halo.wait_from_below()

        @pl.loop(0, SLOTS)
        def _(slot):
            row0, col0, kind, inside, offset, live = window_fields(rows, device, slot)

            @pl.when(live)
            def _():
                target, _ = positions(0, ROWS, col0, kind, inside)
                source = gext[pl.ds(row0, WIN)].reshape(WIN * GRID, width)
                gs[rows_at(offset, ROWS), :] = gather_window(source, target).astype(narrow)

        for halo in (x_halo, g_halo):
            halo.wait_send()
        for group in (pack_far, fc_far):
            for copy in group.first + group.second:
                copy.wait_send()
        for copy in pack_far.third + [corner_pack]:
            copy.wait_send()
        for copy in kept + fc_beside + fc_far.third:
            copy.wait()


def whole(shape):
    zeros = (0,) * len(shape)
    return pl.BlockSpec(shape, lambda *_: zeros, pipeline_mode=pl.Buffered(1))


def by_slot(shape):
    rest = (0,) * len(shape)
    return pl.BlockSpec((1,) + tuple(shape), lambda s, *_: (s,) + rest)


ANY = pl.BlockSpec(memory_space=pl.ANY)


def of(shape, dtype=narrow):
    return jax.ShapeDtypeStruct(shape, dtype)


def forward(x, g, wqkv, wproj, fc1, fc2, vectors, qv_bias, rel_tables, tables):
    rows, _, width = x.shape
    half = 2 * wproj.shape[0]
    slab = (SLAB, width)
    outs = [
        (of(slab), ANY),
        (of(slab), whole(slab)),
        (of(slab), ANY),
        (of((2 * SLOTS, 4, ROWS, half)), by_slot((4, ROWS, half))),
        (of((2, SLAB, half)), whole((2, SLAB, half))),
        (of(slab, single), whole(slab)),
        (of((2, 8, ROWS), single), whole((2, 8, ROWS))),
        (of((16, width), single), whole((16, width))),
        (of((LANES, LANES)), whole((LANES, LANES))),
        (of((2, 4, half, width)), ANY),
        (of(fc1.shape), ANY),
        (of(fc2.shape), ANY),
        (of(fc1.shape), ANY),
        (of(fc2.shape), ANY),
        (of((SPLIT, 8, width), single), ANY),
    ]
    operands = (x, g, wqkv, wproj, fc1, fc2)
    known = (tuple(vectors), qv_bias, tuple(rel_tables), *tables)
    ext = (rows + LEFT + RIGHT, GRID, width)
    return pl.pallas_call(
        forward_kernel,
        out_shape=[o[0] for o in outs],
        grid=(2 * SLOTS,),
        in_specs=[ANY] * 6 + list(jax.tree.map(lambda a: whole(a.shape), known)),
        out_specs=[o[1] for o in outs],
        scratch_shapes=[
            pltpu.VMEM(ext, narrow),
            pltpu.VMEM(ext, narrow),
            pltpu.VMEM((2, 4, half, width), narrow),
            pltpu.VMEM((SPLIT, 8, width), single),
            pltpu.VMEM((3, SLAB, half), narrow),
            pltpu.VMEM(slab, narrow),
            pltpu.VMEM(slab, narrow),
            pltpu.SemaphoreType.DMA((32,)),
            pltpu.SemaphoreType.DMA((32,)),
            pltpu.SemaphoreType.DMA((9,)),
        ],
        compiler_params=pltpu.CompilerParams(
            vmem_limit_bytes=VMEM, collective_id=0, has_side_effects=True
        ),
        cost_estimate=pl.CostEstimate(
            flops=26_000_000_000, bytes_accessed=60_000_000, transcendentals=8_000_000
        ),
        name="attention_forward",
    )(*operands, *known)


CHUNK = SLAB // 3


def gelu_parts(z):
    size = jnp.abs(z)
    bell = jnp.exp(-0.5 * z * z)
    t = 1.0 / (1.0 + 0.2316418882663604 * size)
    poly = 0.5 * 1.061405429 * t + (0.5 * -1.453152027)
    poly = poly * t + 0.5 * 1.421413741
    poly = poly * t + 0.5 * -0.284496736
    poly = poly * t + 0.5 * 0.254829592
    tail = poly * t * bell
    phi_total = jnp.where(z >= 0, 1.0 - tail, tail)
    return z * phi_total, phi_total + z * bell * 0.3989422804014327


def mlp_kernel(
    xs, attn, gs, params, smalls, across1, across2, beside1, beside2, own1, own2,
    out_away, dx1_away, da_away, sums, near1, near2, far1, rest, gb,
    n2, n2t, gt, branch, dn2, w1, w2, grad1, grad2, got1, got2, near_got1, near_got2, landing,
    hs, zs, out, dx1, da, sends, recvs, locals_,
):
    step = pl.program_id(0)
    room = step % 2
    width = gs.shape[1]
    holder = jnp.where(step == 0, 2, jnp.where(step == 1, 3, jnp.where(step == 2, 1, 0)))
    beside, across, _ = partners(lax.axis_index("tensor"))
    send = Sender(sends, recvs, locals_)
    corners = [
        send.remote(0, across1, w1.at[1], {"tensor": beside}),
        send.remote(1, across2, w2.at[1], {"tensor": beside}),
    ]
    loads = [
        [send.local(2 * k, first, w1.at[at]), send.local(2 * k + 1, second, w2.at[at])]
        for k, (first, second, at) in enumerate(
            ((across1, across2, 0), (beside1, beside2, 0), (own1, own2, 1))
        )
    ]
    swaps = [
        send.remote(2, grad1.at[1], got1, {"tensor": beside}),
        send.remote(3, grad2.at[1], got2, {"tensor": beside}),
    ]
    crossing = send.remote(4, got1, far1, {"tensor": across})
    image = lax.axis_index("dp")
    mate = {"dp": mate_of(image, 0)}
    upper = got2.shape[0] // 2
    mine = (image % 2) * upper
    halving = send.remote(5, got2.at[rows_at(upper - mine, upper), :], landing, mate)

    def leaving(c):
        sl = rows_at(c * STRIP, STRIP)
        return [
            send.local(6 + 3 * c + k, here.at[sl, :], away.at[sl, :])
            for k, (here, away) in enumerate(((out, out_away), (dx1, dx1_away), (da, da_away)))
        ]

    near_swaps = [
        send.remote(6, grad1.at[2], near_got1, {"tensor": beside}),
        send.remote(7, grad2.at[2], near_got2, {"tensor": beside}),
    ]

    @pl.when(step == 0)
    def _():
        gb[...] = jnp.zeros_like(gb)
        start_all(loads[0])
        greet([{"tensor": beside}, {"tensor": across}, mate])
        start_all(corners)

        @pl.loop(0, SLAB // STRIP)
        def _(c):
            sl = rows_at(c * STRIP, STRIP)
            middle = xs[sl, :].astype(single) + (attn[sl, :] + params[10:11])
            dx1[sl, :] = middle
            normal, _ = norm_parts(middle)
            n2[sl, :] = (normal * params[11:12] + params[12:13]).astype(narrow)
            branch[sl, :] = jnp.zeros((STRIP, width), single)
            dn2[sl, :] = jnp.zeros((STRIP, width), single)

        for j in range(width // LANES):
            lanes = slice(j * LANES, (j + 1) * LANES)
            n2t[lanes, :] = n2[:, lanes].T
            gt[lanes, :] = gs[:, lanes].T
        for copy in loads[0]:
            copy.wait()

    @pl.when(step == 1)
    def _():
        start_all(loads[1])
        for copy in corners:
            copy.wait()

    @pl.when(step == 2)
    def _():
        start_all(swaps)
        start_all(loads[2])
        for copy in loads[1]:
            copy.wait()

    @pl.when(step == 3)
    def _():
        start_all(near_swaps)
        for copy in loads[2]:
            copy.wait()

    @pl.loop(0, SLAB // CHUNK)
    def _(c):
        @pl.when((step == 2) & (c == 1))
        def _():
            swaps[0].wait()
            add_rows(got1, 0, [(got1, 0), (grad1.at[0], 0)], got1.shape[0])
            crossing.start()
            swaps[1].wait()
            add_rows(got2, 0, [(got2, 0), (grad2.at[0], 0)], got2.shape[0])
            halving.start()

        sl = rows_at(c * CHUNK, CHUNK)
        z = dot(n2[sl, :], w1[room]) + smalls[holder, 0:1, :]
        dh = dot_nt(gs[sl, :], w2[room])
        act, slope = gelu_parts(z)
        h = act.astype(narrow)
        dz = (dh * slope).astype(narrow)
        hs[sl, :] = h
        zs[sl, :] = dz
        gb[holder, 0:1, :] += jnp.sum(dz.astype(single), axis=0, keepdims=True)
        branch[sl, :] += dot(h, w2[room])
        dn2[sl, :] += dot_nt(dz, w1[room])

    @pl.loop(0, 2)
    def _(r):
        sl = rows_at(r * (width // 2), width // 2)
        grad1[step, sl, :] = dot(n2t[sl, :], zs[...]).astype(narrow)
        grad2[step, sl, :] = dot(gt[sl, :], hs[...]).astype(narrow)

    @pl.when(step == 3)
    def _():
        halving.wait()
        add_rows(rest, 0, [(got2, mine), (landing, 0)], upper)
        for copy, near, grad, got in zip(
            near_swaps, (near1, near2), (grad1, grad2), (near_got1, near_got2), strict=True
        ):
            copy.wait()
            add_rows(near, 0, [(grad.at[3], 0), (got, 0)], near.shape[0])
        sums[...] = jnp.zeros_like(sums)

        @pl.loop(0, SLAB // STRIP)
        def _(c):
            sl = rows_at(c * STRIP, STRIP)
            middle = dx1[sl, :]
            normal, inverse = norm_parts(middle)
            out[sl, :] = (middle + (branch[sl, :] + params[13:14])).astype(narrow)
            grad = dn2[sl, :]
            cot = gs[sl, :].astype(single)
            total = cot + norm_back(grad, normal, inverse, params[11:12])
            dx1[sl, :] = total
            low = total.astype(narrow)
            da[sl, :] = low
            for copy in leaving(c):
                copy.start()
            sums[0:1, :] += jnp.sum(grad * normal, axis=0, keepdims=True)
            sums[1:2, :] += jnp.sum(grad, axis=0, keepdims=True)
            sums[2:3, :] += jnp.sum(low.astype(single), axis=0, keepdims=True)
            sums[3:4, :] += jnp.sum(cot, axis=0, keepdims=True)

        crossing.wait()
        for c in range(SLAB // STRIP):
            for copy in leaving(c):
                copy.wait()


def mlp(residents, across, beside, own):
    width, local = own[0].shape
    slab = (SLAB, width)
    square = (width, local)
    outs = [
        (of(slab), ANY),
        (of(slab, single), ANY),
        (of(slab), ANY),
        (of((8, width), single), whole((8, width))),
        (of(square), whole(square)),
        (of(square), whole(square)),
        (of(square), ANY),
        (of((local // 2, width)), whole((local // 2, width))),
        (of((SPLIT, 8, local), single), whole((SPLIT, 8, local))),
    ]
    return pl.pallas_call(
        mlp_kernel,
        out_shape=[o[0] for o in outs],
        grid=(SPLIT,),
        in_specs=[whole(a.shape) for a in residents] + [ANY] * 6,
        out_specs=[o[1] for o in outs],
        scratch_shapes=[
            pltpu.VMEM(slab, narrow),
            *[pltpu.VMEM((width, SLAB), narrow)] * 2,
            *[pltpu.VMEM(slab, single)] * 2,
            *[pltpu.VMEM((2, *square), narrow)] * 2,
            *[pltpu.VMEM((SPLIT, *square), narrow)] * 2,
            *[pltpu.VMEM(square, narrow)] * 4,
            pltpu.VMEM((width // 2, local), narrow),
            *[pltpu.VMEM((SLAB, local), narrow)] * 2,
            pltpu.VMEM(slab, narrow),
            pltpu.VMEM(slab, single),
            pltpu.VMEM(slab, narrow),
            pltpu.SemaphoreType.DMA((8,)),
            pltpu.SemaphoreType.DMA((8,)),
            pltpu.SemaphoreType.DMA((6 + 3 * (SLAB // STRIP),)),
        ],
        compiler_params=pltpu.CompilerParams(
            vmem_limit_bytes=VMEM, collective_id=1, has_side_effects=True
        ),
        cost_estimate=pl.CostEstimate(
            flops=36_000_000_000, bytes_accessed=60_000_000, transcendentals=8_000_000
        ),
        name="mlp",
    )(*residents, *across, *beside, *own)


def backward_kernel(
    rows_held, images,
    da, n1, qkv, mixed, wproj, wrel, bits, lanes, sides, keys, near1, near2, far1, rest,
    dqkv, keep, give, bias, grel, crossed, summed1, summed2,
    dmix, got_far, held1, held2, land1, land2, rest_got,
    sends, recvs, locals_,
):
    step = pl.program_id(0)
    slot, far = step % SLOTS, 1 - step // SLOTS
    image = lax.axis_index("dp")
    beside, across, _ = partners(lax.axis_index("tensor"))
    send = Sender(sends, recvs, locals_)
    half = wproj.shape[2]
    per = Halver.copies(images)
    sum1 = Halver(send, 3, image, images, 0, held1.shape[0], (1, 0, 2))
    sum2 = Halver(send, 3 + per, image, images, 0, held2.shape[0], (0, 1, 2))
    rest_cross = send.remote(0, rest, rest_got, {"tensor": across})
    far_swap = send.remote(1, give.at[0], got_far, {"tensor": beside})
    far_cross = send.remote(2, got_far, crossed, {"tensor": across})

    halvers = ((sum1, held1, land1), (sum2, held2, land2))
    summed = (summed1, summed2)

    def seed(k, halver, held, summed):
        start, length = halver.final
        copy = send.local(k, held.at[rows_at(start, length), :], summed.at[rows_at(start, length), :])
        copy.start()
        copy.wait()

    def begin():
        greet([{"tensor": beside}, {"tensor": across}] + dp_mates(image, images))
        rest_cross.start()
        sum2.start(0, near2, land2)
        add_rows(held1, 0, [(near1, 0), (far1, 0)], held1.shape[0])
        sum1.start(0, held1, land1)

    def second():
        sum1.finish(0, held1, land1)
        sum1.start(1, held1, land1)
        sum2.out(0, near2, land2).wait()
        rest_cross.wait()
        _, kept, _, length, at = sum2.stages[0]
        add_rows(held2, kept, [(near2, kept), (land2, at), (rest_got, 0)], length)
        sum2.start(1, held2, land2)

    def third():
        for halver, held, land in halvers:
            halver.finish(1, held, land)
            halver.start(2, held, land)

    def fourth():
        for n, (halver, held, land) in enumerate(halvers):
            halver.finish(2, held, land)
            halver.extras(held, land)
            seed(n, halver, held, summed[n])
            halver.back(2, summed[n]).start()

    def hand(stage):
        for (halver, _, _), total in zip(halvers, summed, strict=True):
            halver.back(stage + 1, total).wait()
            halver.back(stage, total).start()

    def swap_far():
        far_swap.start()

    def cross_far():
        far_swap.wait()
        add_rows(got_far, 0, [(got_far, 0), (keep.at[0], 0)], got_far.shape[0])
        far_cross.start()

    events = {
        (0, 0): begin,
        (3, 0): second,
        (4, 2): third,
        (7, 0): swap_far,
        (7, 1): fourth,
        (8, 0): cross_far,
        (10, 2): functools.partial(hand, 1),
    }

    def fire(section):
        for (at, place), event in events.items():
            if place == section:
                pl.when(step == at)(event)

    _, col0, kind, inside, offset, live = slot_fields(rows_held)
    whole_window = inside == SPAN

    def on_window(action):
        for count, holds in ((ROWS, whole_window), (SHORT, jnp.logical_not(whole_window))):
            pl.when(live & holds)(functools.partial(action, count))

    @pl.when(step == 0)
    def _():
        for ref in (bias, grel, dqkv):
            ref[...] = jnp.zeros_like(ref)

    fire(0)

    @pl.when(slot == 0)
    def _():
        dmix[...] = dot_nt(da[...], wproj[far, 0]).astype(narrow)

    def one_pair(pair, count):
        cut = slice(pair * LANES, (pair + 1) * LANES)
        q, k8, v, rel = (qkv[0, j, :n, cut] for j, n in enumerate((count, ROWS, ROWS, count)))
        place = rows_at(offset, count)
        do = dmix[place, cut]
        dqs, dks, dvs = [], [], []
        for head in range(2):
            mine, other = sides[head : head + 1], sides[1 - head : 2 - head]
            full_key = k8 * mine + keys[kind] * other
            scores = dot_nt(full_key, q * mine + rel * other)
            top = jnp.max(scores, axis=0, keepdims=True)
            probs = jnp.exp(scores - top)
            probs = probs * (1.0 / jnp.sum(probs, axis=0, keepdims=True))
            dprobs = dot_nt(v, do * mine)
            mean = jnp.sum(probs * dprobs, axis=0, keepdims=True)
            dscores = (probs * (dprobs - mean)).astype(narrow)
            dvs.append(dot(probs.astype(narrow), do))
            dks.append(dot(dscores, q))
            dqs.append(dot_tn(dscores, full_key))
        low_lane = lax.broadcasted_iota(jnp.int32, (ROWS, LANES), 1) < 64
        dv = jnp.where(low_lane, dvs[0], dvs[1])
        dk = jnp.where(low_lane, dks[0], dks[1]) * 0.125
        low_lane = lax.broadcasted_iota(jnp.int32, (count, LANES), 1) < 64
        dq = jnp.where(low_lane, dqs[0], dqs[1])
        drel = jnp.where(low_lane, dqs[1], dqs[0]) * lanes[0:1]
        drel = shift_right(drel, bits.at[kind]).astype(narrow)
        dq = dq + dot(drel, wrel[...])
        grel[...] += dot_tn(drel, q)
        for j, value in enumerate((dq, dk, dv)):
            value = value.astype(narrow).astype(single)
            if j != 1:
                bias[far, j : j + 1, cut] += jnp.sum(value, axis=0, keepdims=True)
            value = value[:count]
            if count < ROWS:
                _, valid = positions(0, count, 0, kind, inside)
                value = jnp.where(valid, value, 0.0)
            dqkv[far, j, place, cut] = value.astype(narrow)

    for pair in range(half // LANES):
        fire(pair + 1)
        on_window(functools.partial(one_pair, pair))

    @pl.when(slot == SLOTS - 1)
    def _():
        part = half // 2
        at = step // SLOTS
        for j in range(4):
            if j < 3:
                total = dot_tn(dqkv[far, j], n1[...])
            else:
                total = dot_tn(mixed[far], da[...])
            keep[at, j * part : (j + 1) * part, :] = total[:part].astype(narrow)
            give[at, j * part : (j + 1) * part, :] = total[part:].astype(narrow)

    @pl.when(step == 2 * SLOTS - 1)
    def _():
        for (halver, _, _), total in zip(halvers, summed, strict=True):
            halver.back(1, total).wait()
        far_cross.wait()


def backward(rows_held, images, da, n1, qkv, mixed, weights, wrel, tables, residents, rest):
    half, width = weights.shape[2:]
    operands = [da, n1, qkv, mixed, weights, wrel, *tables, *residents, rest]
    in_specs = [whole(a.shape) for a in operands]

    def halved(i):
        return (1 - i // SLOTS) * SLOTS + i % SLOTS

    in_specs[2] = pl.BlockSpec((1, 4, ROWS, half), lambda i: (halved(i), 0, 0, 0))
    in_specs[4] = pl.BlockSpec(
        (2, 1, half, width), lambda i: (0, 3, 0, 0), pipeline_mode=pl.Buffered(1)
    )
    in_specs[-1] = ANY
    packed = (2 * half, width)
    square = residents[0].shape
    outs = [
        (of((2, 3, SLAB, half)), whole((2, 3, SLAB, half))),
        (of((2, *packed)), whole((2, *packed))),
        (of((2, *packed)), whole((2, *packed))),
        (of((2, 8, half), single), whole((2, 8, half))),
        (of((LANES, LANES), single), whole((LANES, LANES))),
        (of(packed), ANY),
        (of(square), ANY),
        (of(square), ANY),
    ]
    landing = (Halver.landing_rows(images, square[0]), width)
    copies = 3 + 2 * Halver.copies(images)
    return pl.pallas_call(
        functools.partial(backward_kernel, rows_held, images),
        out_shape=[o[0] for o in outs],
        grid=(2 * SLOTS,),
        in_specs=in_specs,
        out_specs=[o[1] for o in outs],
        scratch_shapes=[
            pltpu.VMEM((SLAB, half), narrow),
            pltpu.VMEM(packed, narrow),
            *[pltpu.VMEM(square, narrow)] * 2,
            *[pltpu.VMEM(landing, narrow)] * 2,
            pltpu.VMEM(rest.shape, narrow),
            pltpu.SemaphoreType.DMA((copies,)),
            pltpu.SemaphoreType.DMA((copies,)),
            pltpu.SemaphoreType.DMA((2,)),
        ],
        compiler_params=pltpu.CompilerParams(
            vmem_limit_bytes=VMEM, collective_id=2, has_side_effects=True
        ),
        cost_estimate=pl.CostEstimate(
            flops=52_000_000_000, bytes_accessed=80_000_000, transcendentals=8_000_000
        ),
        name="attention_backward",
    )(*operands)


def clear_rows(ext):
    @pl.loop(0, ext.shape[0] // GRID)
    def _(r):
        ext[rows_at(r * GRID, GRID), :] = jnp.zeros((GRID, ext.shape[1]), narrow)


def place_windows(rows_held, device, slab, ext, first, last):
    @pl.loop(first, last)
    def _(slot):
        row0, col0, kind, inside, offset, live = window_fields(rows_held, device, slot)

        @pl.when(live)
        def _():
            target, _ = positions(1, ROWS, col0, kind, inside)
            token = lax.broadcasted_iota(jnp.int32, (WIN * GRID, ROWS), 0)
            choose = jnp.where(token == target, 1.0, 0.0).astype(narrow)
            window = slab[rows_at(offset, ROWS), :]
            where_to = pl.ds(pl.multiple_of(row0 * GRID, GRID), WIN * GRID)
            ext[where_to, :] += dot(choose, window).astype(narrow)


def tail_kernel(
    rows_held, images,
    sums2, bias, rel_sum, fc_bias, peak, params,
    out_in, keep_in, crossed_in, xs_in, dx1_in, part1, part2, give, dqkv, weights,
    output, input_grad, packed, totals, tops, summed1, summed2,
    ext0, ext1, below0, below1, above0, above1, got, landing, held, sum_land, top_land, back, grads,
    packs, out, keep, crossed, xs, dx1, sends, recvs, locals_,
):
    device, image = lax.axis_index("tensor"), lax.axis_index("dp")
    beside, across, corner = partners(device)
    send = Sender(sends, recvs, locals_)
    hand_base = 1 + 2 * Halver.copies(images) + 4 + 2 * (1 + images.bit_length())
    early = [send.local(0, keep_in.at[1], keep), send.local(1, crossed_in, crossed)]
    loads = [
        send.local(2, dqkv, grads),
        send.local(3, weights.at[:, 0:3], packs),
        send.local(4, xs_in, xs),
        send.local(5, dx1_in, dx1),
    ]
    late = send.local(6, out_in, out)
    start_all(early + loads + [late])
    hand_last, stay = [], []
    for k, (part, summed, order) in enumerate(
        ((part1, summed1, (1, 0, 2)), (part2, summed2, (0, 1, 2)))
    ):
        mate, kept, _, length, _ = Halver(
            send, 0, image, images, 0, part.shape[0], order
        ).stages[0]
        cut = rows_at(kept, length)
        stay.append(send.local(7 + k, part.at[cut, :], summed.at[cut, :]))
        hand_last.append(
            send.remote(hand_base + k, part.at[cut, :], summed.at[cut, :], {"dp": mate})
        )
    start_all(stay)
    per = Halver.copies(images)
    middle = held.shape[0] // 2
    landing_rows = Halver.landing_rows(images, middle)
    landings = [landing.at[pl.ds(k * landing_rows, landing_rows), :] for k in range(2)]
    halvers = [
        Halver(send, 1 + k * per, image, images, k * middle, middle, order)
        for k, order in enumerate(((0, 1, 2), (1, 0, 2)))
    ]
    halo_base = 1 + 2 * per
    small_base = halo_base + 4
    tokens = rows_held * GRID
    top, bottom = LEFT * GRID, RIGHT * GRID
    held_by = (device, beside, across, corner)
    mates = dp_mates(image, images)
    ring = [{"tensor": beside}, {"tensor": across}] + mates

    def reduce_start(stage):
        for halver, land in zip(halvers, landings, strict=True):
            halver.start(stage, held, land)

    def reduce_finish(stage):
        for halver, land in zip(halvers, landings, strict=True):
            halver.finish(stage, held, land)

    def hand_start(stage):
        for halver in halvers:
            halver.back(stage, packed).start()

    def hand_finish(stage):
        for halver in halvers:
            halver.back(stage, packed).wait()

    greet([{"tensor": place} for place in (beside, across, corner)] + mates)
    swap = send.remote(0, give.at[1], got, {"tensor": beside})
    swap.start()
    totals[...] = jnp.zeros_like(totals)
    tops[...] = jnp.zeros_like(tops)
    totals[2:6, :] = sums2[0:4, :]
    rel = rel_sum[...]
    rel = rel[HD:] + pltpu.roll(rel[:HD], HD, 1)
    for g in range(HD // 8):
        at = 8 * (1 + g // 6)
        totals[at : at + 8, (g % 6) * LANES : (g % 6 + 1) * LANES] = rel[8 * g : 8 * g + 8]
    half = bias.shape[2]
    for k in range(SPLIT):
        far, odd = k // 2, k % 2
        totals[pl.ds(24 + held_by[k], 1), :] = fc_bias[k, 0:1, :]
        for j, row in enumerate((0, 2)):
            value = bias[far, row : row + 1, :]
            if odd:
                value = pltpu.roll(value, half // 2, 1)
            totals[pl.ds(28 + held_by[k], 1), j * half : (j + 1) * half] = value
        best = jnp.broadcast_to(jnp.max(peak[far], axis=1, keepdims=True), (8, LANES))
        if odd:
            best = pltpu.roll(best, 8 - half // LANES, 0)
        tops[pl.ds(pl.multiple_of(held_by[k] * 8, 8), 8), :] = best

    def small_copies(k):
        return [
            send.remote(small_base + 2 * k, totals, sum_land.at[k], ring[k]),
            send.remote(small_base + 2 * k + 1, tops, top_land.at[k], ring[k]),
        ]

    def small_start(k):
        for copy in small_copies(k):
            copy.start()

    def small_finish(k):
        for copy in small_copies(k):
            copy.wait()
        totals[...] += sum_land[k]
        tops[...] = jnp.maximum(tops[...], top_land[k])

    def halo(base, ext, below, above):
        up = send.remote(
            base, ext.at[pl.ds(0, top), :], below, {"tensor": (device + SPLIT - 1) % SPLIT}
        )
        down = send.remote(
            base + 1, ext.at[pl.ds(top + tokens, bottom), :], above, {"tensor": (device + 1) % SPLIT}
        )
        return up, down

    def halo_start(copies):
        up, down = copies
        pl.when(device > 0)(up.start)
        pl.when(device < SPLIT - 1)(down.start)

    def halo_finish(copies, ext, below, above, result):
        up, down = copies
        pl.when(device > 0)(up.wait_send)
        pl.when(device < SPLIT - 1)(down.wait_send)
        add_rows(result, 0, [(ext, top)], tokens)

        @pl.when(device < SPLIT - 1)
        def _():
            up.wait_recv()
            at = tokens - top
            add_rows(result, at, [(result, at), (below, 0)], top)

        @pl.when(device > 0)
        def _():
            down.wait_recv()
            add_rows(result, 0, [(result, 0), (above, 0)], bottom)

    def norm1_back():
        @pl.loop(0, SLAB // CHUNK)
        def _(c):
            sl = rows_at(c * CHUNK, CHUNK)
            grad = None
            for far in range(2):
                for j in range(3):
                    term = dot(grads[far, j, sl, :], packs[far, j])
                    grad = term if grad is None else grad + term
            normal, inverse = norm_parts(xs[sl, :].astype(single))
            totals[0:1, :] += jnp.sum(grad * normal, axis=0, keepdims=True)
            totals[1:2, :] += jnp.sum(grad, axis=0, keepdims=True)
            result = dx1[sl, :] + norm_back(grad, normal, inverse, params[8:9])
            back[sl, :] = result.astype(narrow)

    clear_rows(ext0)
    clear_rows(ext1)
    for copy in early:
        copy.wait()
    swap.wait()
    add_rows(held, 0, [(keep, 0), (got, 0), (crossed, 0)], held.shape[0])
    reduce_start(0)
    for copy in loads:
        copy.wait()
    norm1_back()
    small_start(0)
    reduce_finish(0)
    reduce_start(1)
    place_windows(rows_held, device, back, ext1, 0, 3)
    small_finish(0)
    small_start(1)
    reduce_finish(1)
    reduce_start(2)
    start_all(hand_last)
    place_windows(rows_held, device, back, ext1, 3, SLOTS)
    halos1 = halo(halo_base, ext1, below1, above1)
    halo_start(halos1)
    late.wait()
    place_windows(rows_held, device, out, ext0, 0, 3)
    small_finish(1)
    small_start(2)
    reduce_finish(2)
    for halver, land in zip(halvers, landings, strict=True):
        halver.extras(held, land)
        start, length = halver.final
        packed[rows_at(start, length), :] = held[rows_at(start, length), :]
    hand_start(2)
    place_windows(rows_held, device, out, ext0, 3, SLOTS)
    halos0 = halo(halo_base + 2, ext0, below0, above0)
    halo_start(halos0)
    small_finish(2)
    small_start(3)
    hand_finish(2)
    hand_start(1)
    small_finish(3)
    small_start(4)
    hand_finish(1)
    hand_start(0)
    halo_finish(halos1, ext1, below1, above1, input_grad)
    for k in range(4, len(ring)):
        small_finish(k)
        if k + 1 < len(ring):
            small_start(k + 1)
    halo_finish(halos0, ext0, below0, above0, output)
    hand_finish(0)
    for copy in stay + hand_last:
        copy.wait()


def tail(rows_held, images, *operands):
    width = operands[-1].shape[3]
    half = operands[-1].shape[2]
    packed = (2 * half, width)
    tokens = rows_held * GRID
    bits = images.bit_length() - 1
    landing = 2 * Halver.landing_rows(images, packed[0] // 2)
    copies = 1 + 2 * Halver.copies(images) + 4 + 2 * (2 + bits) + 2
    ext = ((rows_held + LEFT + RIGHT) * GRID, width)
    outs = [
        of((tokens, width)), of((tokens, width)), of(packed),
        of((32, width), single), of((32, LANES), single),
        of(operands[-5].shape), of(operands[-4].shape),
    ]
    return pl.pallas_call(
        functools.partial(tail_kernel, rows_held, images),
        out_shape=outs,
        in_specs=[pl.BlockSpec(memory_space=pltpu.VMEM)] * (len(operands) - 10) + [ANY] * 10,
        out_specs=[pl.BlockSpec(memory_space=pltpu.VMEM)] * 5 + [ANY] * 2,
        scratch_shapes=[
            pltpu.VMEM(ext, narrow),
            pltpu.VMEM(ext, narrow),
            pltpu.VMEM((LEFT * GRID, width), narrow),
            pltpu.VMEM((LEFT * GRID, width), narrow),
            pltpu.VMEM((RIGHT * GRID, width), narrow),
            pltpu.VMEM((RIGHT * GRID, width), narrow),
            pltpu.VMEM(packed, narrow),
            pltpu.VMEM((landing, width), narrow),
            pltpu.VMEM(packed, narrow),
            pltpu.VMEM((2 + bits, 32, width), single),
            pltpu.VMEM((2 + bits, 32, LANES), single),
            pltpu.VMEM((SLAB, width), narrow),
            pltpu.VMEM((2, 3, SLAB, half), narrow),
            pltpu.VMEM((2, 3, half, width), narrow),
            pltpu.VMEM((SLAB, width), narrow),
            *[pltpu.VMEM(packed, narrow)] * 2,
            pltpu.VMEM((SLAB, width), narrow),
            pltpu.VMEM((SLAB, width), single),
            pltpu.SemaphoreType.DMA((copies,)),
            pltpu.SemaphoreType.DMA((copies,)),
            pltpu.SemaphoreType.DMA((9,)),
        ],
        compiler_params=pltpu.CompilerParams(
            vmem_limit_bytes=VMEM, collective_id=3, has_side_effects=True
        ),
        cost_estimate=pl.CostEstimate(
            flops=4_000_000_000, bytes_accessed=20_000_000, transcendentals=0
        ),
        name="tail",
    )(*operands)


def finish_kernel(
    fc1, fc2, gq, gp, out_in, back_in, totals, tops, wqkv,
    grad_fc1, grad_fc2, grad_qkv, grad_proj, out, back, clipped, qv, fc1_bias, norms, proj_bias,
    fc2_bias, rel, head_max,
):
    device = lax.axis_index("tensor")
    out[...] = out_in[...]
    back[...] = back_in[...]
    grad_fc1[...] = fc1[...].astype(single)
    grad_fc2[...] = fc2[...].astype(single).T
    grad_qkv[...] = gq[...].astype(single)
    grad_proj[...] = gp[...].astype(single)

    @pl.when(pl.program_id(0) == 0)
    def _():
        local = wqkv.shape[1]
        largest = tops[pl.ds(pl.multiple_of(8 * device, 8), 8), :]
        head_max[...] = largest.T[0, : local // HD]
        limit = jnp.maximum(largest, CLIP)
        factor = jnp.sqrt(CLIP / limit)
        factor = jnp.concatenate([factor] * (wqkv.shape[2] // LANES), axis=1)
        for j in range(2):
            for head in range(local // HD):
                cut = slice(head * HD, (head + 1) * HD)
                scaled = wqkv[j, cut, :].astype(single) * factor[head : head + 1]
                clipped[j, cut, :] = scaled.astype(narrow)
            qv[j : j + 1, :] = totals[pl.ds(28 + device, 1), 2 * j * local : (2 * j + 1) * local]
        fc1_bias[...] = totals[24 + device, :]
        norms[...] = totals[0:4, :]
        proj_bias[...] = totals[4, :]
        fc2_bias[...] = totals[5, :]
        span = 2 * WIN - 1
        for j in range(2):
            for first in range(0, span, 8):
                group = (32 * j + first) // 8
                count = min(8, span - first)
                at, lane = 8 * (1 + group // 6), (group % 6) * LANES
                rel[first : first + count, j, :] = totals[at : at + count, lane : lane + HD]


def finish(summed1, summed2, gpack, output, input_grad, totals, tops, wqkv):
    _, local, width = wqkv.shape
    hidden = summed1.shape[1]
    parts = 3
    batch = output.shape[0] // 2
    pages = pl.BlockSpec((batch, width), lambda i: (jnp.minimum(i, 1), 0))
    heads = local // HD
    rows, cols, lines = width // parts, hidden // parts, 3 * local // parts
    few = local // parts

    def by_rows(count, columns, first=0):
        return pl.BlockSpec((count, columns), lambda i: (first + i, 0))

    span = 2 * WIN - 1
    outs = [
        (of((width, hidden), single), by_rows(rows, hidden)),
        (of((hidden, width), single), by_rows(cols, width)),
        (of((3 * local, width), single), by_rows(lines, width)),
        (of((local, width), single), by_rows(few, width)),
        (of(output.shape), pages),
        (of(output.shape), pages),
        (of((2, local, width)), whole((2, local, width))),
        (of((2, local), single), whole((2, local))),
        (of((hidden,), single), whole((hidden,))),
        (of((4, width), single), whole((4, width))),
        (of((width,), single), whole((width,))),
        (of((width,), single), whole((width,))),
        (of((span, 2, HD), single), whole((span, 2, HD))),
        (of((heads,), single), whole((heads,))),
    ]
    return pl.pallas_call(
        finish_kernel,
        out_shape=[o[0] for o in outs],
        grid=(parts,),
        in_specs=[
            by_rows(rows, hidden),
            pl.BlockSpec((width, cols), lambda i: (0, i)),
            by_rows(lines, width),
            by_rows(few, width, 3 * local // few),
            pages,
            pages,
            whole(totals.shape),
            whole(tops.shape),
            whole(wqkv.shape),
        ],
        out_specs=[o[1] for o in outs],
        compiler_params=pltpu.CompilerParams(vmem_limit_bytes=VMEM),
        cost_estimate=pl.CostEstimate(flops=0, bytes_accessed=14_000_000, transcendentals=0),
        name="finish",
    )(summed1, summed2, gpack, gpack, output, input_grad, totals, tops, wqkv)


def shards(
    inputs,
    w_qkv,
    qv_bias,
    w_proj,
    proj_bias,
    w_fc1,
    fc1_bias,
    w_fc2,
    fc2_bias,
    norm1_gain,
    norm1_shift,
    norm2_gain,
    norm2_shift,
    rel_h,
    rel_w,
    cotangent,
):
    width = inputs.shape[2]
    rows = inputs.shape[1] // GRID
    local = w_qkv.shape[2]
    tables = lane_tables()

    wqkv = w_qkv.transpose(0, 2, 1)

    (
        xs, gs, n1, qkv, mixed, attn, peak, params, wrel,
        weights, across1, across2, beside1, beside2, smalls,
    ) = forward(
        *(a.reshape(rows, GRID, width) for a in (inputs, cotangent)), wqkv, w_proj, w_fc1, w_fc2,
        (
            fc1_bias, norm1_gain, norm1_shift, proj_bias, norm2_gain, norm2_shift, fc2_bias,
        ),
        qv_bias, (rel_h, rel_w), tables
    )
    out, dx1, da, sums2, near1, near2, far1, rest, fc_bias = mlp(
        (
            xs, attn, gs, params, smalls,
        ),
        (across1, across2),
        (beside1, beside2),
        (w_fc1, w_fc2),
    )
    images = lax.axis_size("dp")
    dqkv, keep, give, bias, rel_sum, crossed, part1, part2 = backward(
        rows, images, da, n1, qkv, mixed, weights, wrel, tables, [near1, near2, far1], rest
    )
    output, input_grad, gpack, totals, tops, summed1, summed2 = tail(
        rows, images, sums2, bias, rel_sum, fc_bias, peak, params, out, keep, crossed, xs, dx1,
        part1, part2, give, dqkv, weights,
    )
    (
        grad_fc1, grad_fc2, grad_qkv, grad_proj, output, input_grad, clipped, grad_qv,
        grad_fc1_bias, grad_norms, grad_proj_bias, grad_fc2_bias, grad_rel, head_max,
    ) = finish(summed1, summed2, gpack, output, input_grad, totals, tops, wqkv)

    return (
        output[None],
        input_grad[None],
        grad_qkv.reshape(3, local, width).transpose(0, 2, 1),
        grad_qv,
        grad_proj,
        grad_proj_bias,
        grad_fc1,
        grad_fc1_bias,
        grad_fc2,
        grad_fc2_bias,
        grad_norms,
        grad_rel.transpose(1, 0, 2),
        clipped.transpose(0, 2, 1),
        head_max,
    )


def solution(mesh):
    return jax.shard_map(
        shards,
        mesh=mesh,
        in_specs=(
            P("dp", "tensor", None),
            P(None, None, "tensor"),
            P(None, "tensor"),
            P("tensor", None),
            P(),
            P(None, "tensor"),
            P("tensor"),
            P("tensor", None),
            P(),
            P(),
            P(),
            P(),
            P(),
            P(),
            P(),
            P("dp", "tensor", None),
        ),
        out_specs=(
            P("dp", "tensor", None),
            P("dp", "tensor", None),
            P(None, None, "tensor"),
            P(None, "tensor"),
            P("tensor", None),
            P(),
            P(None, "tensor"),
            P("tensor"),
            P("tensor", None),
            P(),
            P(),
            P(),
            P(None, None, "tensor"),
            P("tensor"),
        ),
        check_vma=False,
    )
```

```python
import functools

import jax
import jax.numpy as jnp
import numpy as np
from jax import lax
from jax.experimental import pallas as pl
from jax.experimental.pallas import tpu as pltpu
from jax.sharding import PartitionSpec as P

HD = 64
GRID = 64
WIN = 14
TILES = 5
SPAN = WIN * WIN
ROWS = 208
SLOTS = 7
EDGE = GRID % WIN
SHORT = EDGE * WIN
SLAB = (SLOTS - 2) * ROWS + SHORT
STRIP = SLAB // 6
SPLIT = 4
LEFT = 6
RIGHT = 12
LANES = 128
EPS = 1e-6
CLIP = 3.0
VMEM = 60 * 1024 * 1024

single = jnp.float32
narrow = jnp.bfloat16

def lane_tables():
    row = np.arange(ROWS)
    late = np.maximum(row - SHORT, 0)
    outer = WIN - EDGE
    orders = (
        (row // WIN, row % WIN),
        (
            np.where(row < SHORT, row // EDGE, late // outer),
            np.where(row < SHORT, row % EDGE, EDGE + late % outer),
        ),
    )
    lane = np.arange(LANES) % 64
    part = lane // 32
    at = lane % 32
    bits, keys = [], []
    for x, y in orders:
        amount = np.where(part[None, :] == 0, x[:, None], y[:, None])
        amount = np.where((row < SPAN)[:, None], amount, 0)
        bits.append(np.stack([(amount >> b) & 1 for b in range(4)]).astype(np.float32))
        place = WIN - 1 - np.where(part[None, :] == 0, x[:, None], y[:, None])
        hot = ((at % 16)[None, :] == place) & ((at % 16) < WIN)[None, :] & (row < SPAN)[:, None]
        hot = hot.astype(np.float32)
        hot[SPAN:, lane == 31] = -1e30
        keys.append(hot)
    lanes = np.zeros((8, LANES), np.float32)
    lanes[0] = at < WIN
    lanes[1] = (at >= 16) & (at < 16 + WIN)
    lanes[2] = lane == 31
    sides = np.zeros((16, LANES), np.float32)
    sides[0] = np.arange(LANES) < 64
    sides[1] = np.arange(LANES) >= 64
    return (
        jnp.asarray(np.stack(bits)),
        jnp.asarray(lanes),
        jnp.asarray(sides, narrow),
        jnp.asarray(np.stack(keys), narrow),
    )


def dot(a, b):
    return jnp.dot(a, b, preferred_element_type=single)


def dot_nt(a, b):
    return lax.dot_general(a, b, (((1,), (1,)), ((), ())), preferred_element_type=single)


def dot_tn(a, b):
    return lax.dot_general(a, b, (((0,), (0,)), ((), ())), preferred_element_type=single)


def norm_parts(values):
    centre = values - jnp.mean(values, axis=-1, keepdims=True)
    inverse = lax.rsqrt(jnp.mean(centre * centre, axis=-1, keepdims=True) + EPS)
    return centre * inverse, inverse


def norm_back(grad, normal, inverse, gain):
    scaled = grad * gain
    first = jnp.mean(scaled, axis=-1, keepdims=True)
    second = jnp.mean(scaled * normal, axis=-1, keepdims=True)
    return inverse * (scaled - first - normal * second)


def slot_fields(rows_held):
    return window_fields(rows_held, lax.axis_index("tensor"), pl.program_id(0) % SLOTS)


def window_fields(rows_held, device, slot):
    first = device * (SLOTS - 1)
    window = first + slot
    i, j = window // TILES, window % TILES
    last = device // (SPLIT - 1)
    live = slot < SLOTS - 1 + last
    row0 = i * WIN - device * rows_held + LEFT
    high = jnp.minimum(WIN, GRID - i * WIN)
    wide = jnp.minimum(WIN, GRID - j * WIN)

    def short_before(n):
        return jnp.minimum(n // TILES, TILES - 1) + jnp.maximum(n - TILES * (TILES - 1), 0)

    offset = ROWS * slot - (ROWS - SHORT) * (short_before(window) - short_before(first))
    return row0, j * WIN, j // (TILES - 1), high * wide, offset, live


def positions(axis, count, first_col, kind, inside):
    shape = (count, 1) if axis == 0 else (1, count)
    row = lax.broadcasted_iota(jnp.int32, shape, axis)
    x = lax.shift_right_logical(row * 4682, 16)
    plain = x * GRID + (row - x * WIN)
    x = lax.shift_right_logical(row, EDGE.bit_length() - 1)
    edge = x * GRID + (row - x * EDGE)
    token = jnp.where(kind == 1, edge, plain) + first_col
    return jnp.where(row < inside, token, -1), row < inside


def gather_window(source, target):
    token = lax.broadcasted_iota(jnp.int32, (target.shape[0], WIN * GRID), 1)
    choose = jnp.where(token == target, 1.0, 0.0).astype(narrow)
    return dot(choose, source)


def shift_left(values, bits):
    for b in range(4):
        taken = bits[b, : values.shape[0]] > 0.5
        values = jnp.where(taken, pltpu.roll(values, LANES - (1 << b), 1), values)
    return values


def shift_right(values, bits):
    for b in range(4):
        taken = bits[b, : values.shape[0]] > 0.5
        values = jnp.where(taken, pltpu.roll(values, 1 << b, 1), values)
    return values


def partners(device):
    beside = device + 1 - 2 * (device % 2)
    across = (device + 2) % SPLIT
    corner = (beside + 2) % SPLIT
    return beside, across, corner


def greet(places):
    barrier = pltpu.get_barrier_semaphore()
    for place in places:
        pl.semaphore_signal(barrier, inc=1, device_id=place, device_id_type=pl.DeviceIdType.MESH)
    pl.semaphore_wait(barrier, len(places))


class Sender:
    def __init__(self, sends, recvs, locals_):
        self.sends, self.recvs, self.locals = sends, recvs, locals_

    def remote(self, at, source, target, place):
        return pltpu.make_async_remote_copy(
            src_ref=source,
            dst_ref=target,
            send_sem=self.sends.at[at],
            recv_sem=self.recvs.at[at],
            device_id=place,
            device_id_type=pl.DeviceIdType.MESH,
        )

    def local(self, at, source, target):
        return pltpu.make_async_copy(source, target, self.locals.at[at])


def mate_of(image, bit):
    unit = 1 << bit
    return image + unit * (1 - 2 * ((image // unit) % 2))


def rows_at(start, count):
    return pl.ds(pl.multiple_of(start, 16), count)


def add_rows(target, target_at, sources, count):
    chunk = next(c for c in (96, 48, 16) if count % c == 0)

    @pl.loop(0, count // chunk)
    def _(c):
        total = None
        for ref, at in sources:
            value = ref[rows_at(at + c * chunk, chunk), :]
            total = value if total is None else total + value
        target[rows_at(target_at + c * chunk, chunk), :] = total


HALVINGS = 3


class Halver:
    def __init__(self, send, base, image, images, start, rows, order):
        bits = images.bit_length() - 1
        assert images == 1 << bits and bits >= HALVINGS
        self.send, self.base, self.image = send, base, image
        self.extra_bits = range(HALVINGS, bits)
        self.stages = []
        landing, length = 0, rows
        for bit in order:
            length //= 2
            mine = (image // (1 << bit)) % 2
            keep, give = start + mine * length, start + (1 - mine) * length
            self.stages.append((mate_of(image, bit), keep, give, length, landing))
            landing += length
            start = keep
        self.final = (start, length)
        self.landing = landing

    @staticmethod
    def copies(images):
        return 2 * HALVINGS + images.bit_length() - 1 - HALVINGS

    @staticmethod
    def landing_rows(images, rows):
        last = rows >> HALVINGS
        return rows - last + last * (images.bit_length() - 1 - HALVINGS)

    def out(self, stage, held, landing):
        mate, _, give, length, at = self.stages[stage]
        return self.send.remote(
            self.base + stage,
            held.at[rows_at(give, length), :],
            landing.at[pl.ds(at, length), :],
            {"dp": mate},
        )

    def start(self, stage, held, landing):
        self.out(stage, held, landing).start()

    def finish(self, stage, held, landing):
        self.out(stage, held, landing).wait()
        _, keep, _, length, at = self.stages[stage]
        add_rows(held, keep, [(held, keep), (landing, at)], length)

    def extras(self, held, landing):
        start, length = self.final
        for k, bit in enumerate(self.extra_bits):
            at = self.landing + k * length
            copy = self.send.remote(
                self.base + HALVINGS + k,
                held.at[rows_at(start, length), :],
                landing.at[pl.ds(at, length), :],
                {"dp": mate_of(self.image, bit)},
            )
            copy.start()
            copy.wait()
            add_rows(held, start, [(held, start), (landing, at)], length)

    def back(self, stage, held):
        mate, keep, _, length, _ = self.stages[stage]
        cut = rows_at(keep, length)
        at = self.base + HALVINGS + len(self.extra_bits) + stage
        return self.send.remote(at, held.at[cut, :], held.at[cut, :], {"dp": mate})


def dp_mates(image, images):
    return [{"dp": mate_of(image, bit)} for bit in range(images.bit_length() - 1)]


def project(n1, weights, qbias, vbias, projected, place):
    projected[0, place, :] = (dot_nt(n1, weights[0]) + qbias).astype(narrow)
    projected[1, place, :] = dot_nt(n1, weights[1]).astype(narrow) * jnp.asarray(0.125, narrow)
    projected[2, place, :] = (dot_nt(n1, weights[2]) + vbias).astype(narrow)


def attend(count, place, valid, projected, vbias, wrel, bits, lanes, sides, keys, qkv, mixed, peak):
    half = projected.shape[2]
    qkv[0, 0, :count] = jnp.where(valid, projected[0, place, :].astype(single), 0.0).astype(narrow)
    qkv[0, 1, :count] = projected[1, place, :]
    qkv[0, 2, :count] = projected[2, place, :]
    if count < ROWS:
        left = ROWS - count
        qkv[0, 1, count:] = jnp.zeros((left, half), narrow)
        qkv[0, 2, count:] = jnp.broadcast_to(vbias, (left, half)).astype(narrow)
    low_lane = lax.broadcasted_iota(jnp.int32, (count, LANES), 1) < 64
    for pair in range(half // LANES):
        cut = slice(pair * LANES, (pair + 1) * LANES)
        q, k8, v = qkv[0, 0, :count, cut], qkv[0, 1, :, cut], qkv[0, 2, :, cut]
        rel = shift_left(dot_nt(q, wrel[...]), bits)
        rest = rel - rel.astype(narrow).astype(single)
        rel = rel * lanes[0:1] + pltpu.roll(rest, 16, 1) * lanes[1:2] + lanes[2:3]
        rel = rel.astype(narrow)
        qkv[0, 3, :count, cut] = rel
        pieces = []
        for head in range(2):
            mine, other = sides[head : head + 1], sides[1 - head : 2 - head]
            only = q * mine
            logits = dot_nt(only, k8)
            at = 2 * pair + head
            peak[at : at + 1, :] = jnp.maximum(
                peak[at : at + 1, :], jnp.max(logits, axis=0, keepdims=True)
            )
            scores = dot_nt(only + rel * other, k8 * mine + keys[...] * other)
            top = jnp.max(scores, axis=1, keepdims=True)
            probs = jnp.exp(scores - top)
            total = jnp.sum(probs, axis=1, keepdims=True)
            pieces.append(dot(probs.astype(narrow), v) * (1.0 / total))
        mixed[place, cut] = jnp.where(low_lane, pieces[0], pieces[1]).astype(narrow)


class Halo:
    def __init__(self, send, base, grid, ext, device, rows):
        below, above = {"tensor": (device + 1) % SPLIT}, {"tensor": (device + SPLIT - 1) % SPLIT}
        self.has_below, self.has_above = device < SPLIT - 1, device > 0
        self.cross_below, self.cross_above = device == 1, device == 2

        def copy(at, first, count, first_col, cols, target_row, place):
            window = (pl.ds(first, count), pl.ds(first_col, cols), slice(None))
            return send.remote(
                at, grid.at[window], ext.at[(pl.ds(target_row, count), *window[1:])], place
            )

        few, many = 4, 10
        self.down = copy(base, rows - LEFT, LEFT, 0, GRID, 0, below)
        self.down_cross = copy(base, rows - few, few, 16, GRID - 16, LEFT - few, below)
        self.up = copy(base + 1, 0, RIGHT, 0, GRID, LEFT + rows, above)
        self.up_cross = copy(base + 1, 0, many, 0, 32, LEFT + rows, above)

    def _each(self, down_here, up_here, act):
        for here, crossing, plain, crossed in (
            (*down_here, self.down, self.down_cross),
            (*up_here, self.up, self.up_cross),
        ):

            @pl.when(here & jnp.logical_not(crossing))
            def _():
                act(plain)

            @pl.when(crossing)
            def _():
                act(crossed)

    def _senders(self, act):
        self._each((self.has_below, self.cross_below), (self.has_above, self.cross_above), act)

    def start(self):
        self._senders(lambda copy: copy.start())

    def wait_send(self):
        self._senders(lambda copy: copy.wait_send())

    def wait_from_above(self):
        pl.when(self.has_above & jnp.logical_not(self.cross_above))(self.down.wait_recv)
        pl.when(self.cross_above)(self.down_cross.wait_recv)

    def wait_from_below(self):
        pl.when(self.has_below & jnp.logical_not(self.cross_below))(self.up.wait_recv)
        pl.when(self.cross_below)(self.up_cross.wait_recv)


class Quartet:
    def __init__(self, send, base, image, pieces, across):
        side, deep = image % 2, (image // 2) % 2
        beside, behind = {"dp": mate_of(image, 0)}, {"dp": mate_of(image, 1)}
        mine = 2 * deep + side
        from_beside, from_behind = 2 * deep + 1 - side, 2 * (1 - deep) + side
        self.first, self.second, self.third = [], [], []
        for k, (source, target, view) in enumerate(pieces):
            at = base + 5 * k

            def copy(number, origin, quarter, part, place):
                return send.remote(at + number, view(origin, quarter, part), view(target, quarter, part), place)

            self.first.append(copy(0, source, mine, None, across))
            self.second.append(copy(1, target, mine, None, beside))
            self.second.append(copy(2, target, mine, None, behind))
            if view(target, from_behind, 0) is not None:
                self.third.append(copy(3, target, from_behind, 0, beside))
            self.third.append(copy(4, target, from_beside, 1, behind))


def quarter_rows(array, quarter, part):
    size = array.shape[0] // 4
    start = quarter * size
    if part is not None:
        size //= 2
        start += part * size
    return array.at[rows_at(start, size), :]


def start_all(copies):
    for copy in copies:
        copy.start()


def receive_all(copies):
    for copy in copies:
        copy.wait_recv()


def forward_kernel(
    x, g, wqkv, wproj, fc1, fc2, vectors, qv_bias, rel_tables, bits, lanes, sides, keys,
    xs_out, gs, n1_out, qkv, mixed, attn, peak, params, wrel, weights_out, across1, across2, beside1,
    beside2, small_out,
    xext, gext, weights, smalls, projected, xs, n1_all, sends, recvs, locals_,
):
    step = pl.program_id(0)
    far, slot = step // SLOTS, step % SLOTS
    device, image = lax.axis_index("tensor"), lax.axis_index("dp")
    rows, _, width = x.shape
    part = wproj.shape[0]
    half = 2 * part
    beside, across, corner = partners(device)
    send = Sender(sends, recvs, locals_)
    x_halo = Halo(send, 0, x, xext, device, rows)
    g_halo = Halo(send, 2, g, gext, device, rows)
    small = params.at[pl.ds(0, 8), :]

    own_pack = [
        send.remote(4, wqkv, weights.at[0, 0:3, pl.ds(part, part), :], {"tensor": beside}),
        send.remote(5, wproj, weights.at[0, 3, pl.ds(part, part), :], {"tensor": beside}),
    ]
    notes = [
        send.remote(6 + k, small, smalls.at[k + 1], {"tensor": place})
        for k, place in enumerate((beside, across, corner))
    ]
    fc_beside = [
        send.remote(9, fc1, beside1, {"tensor": beside}),
        send.remote(10, fc2, beside2, {"tensor": beside}),
    ]
    corner_pack = send.remote(
        11, weights.at[1, :, pl.ds(0, part), :], weights.at[1, :, pl.ds(part, part), :], {"tensor": beside}
    )

    def of_qkv(array, quarter, half_of):
        size = part // 4
        cut = rows_at(quarter * size, size)
        if array is wqkv:
            return array.at[:, cut, :]
        if half_of is None:
            return array.at[1, 0:3, cut, :]
        return array.at[1, 0:2, cut, :] if half_of == 0 else array.at[1, 2:3, cut, :]

    def of_proj(array, quarter, half_of):
        size = part // 4
        cut = rows_at(quarter * size, size)
        if array is wproj:
            return array.at[cut, :]
        return None if half_of == 0 else array.at[1, 3, cut, :]

    pack_far = Quartet(
        send, 12, image, ((wqkv, weights, of_qkv), (wproj, weights, of_proj)), {"tensor": across}
    )
    fc_far = Quartet(
        send, 22, image, ((fc1, across1, quarter_rows), (fc2, across2, quarter_rows)), {"tensor": across}
    )
    own = [
        send.local(0, wqkv, weights.at[0, 0:3, pl.ds(0, part), :]),
        send.local(1, wproj, weights.at[0, 3, pl.ds(0, part), :]),
        send.local(2, x, xext.at[pl.ds(LEFT, rows)]),
        send.local(3, small, smalls.at[0]),
    ]
    g_own = send.local(4, g, gext.at[pl.ds(LEFT, rows)])
    kept = [
        send.local(5, weights, weights_out),
        send.local(6, smalls, small_out),
        send.local(7, xs, xs_out),
        send.local(8, n1_all, n1_out),
    ]

    @pl.when(step == 0)
    def _():
        params[...] = jnp.zeros_like(params)
        for ref, row in zip(vectors, (0, 8, 9, 10, 11, 12, 13), strict=True):
            params[row, :] = ref[...]
        for j in range(2):
            params[1 + 2 * j, 0:part] = qv_bias[j, :]
            params[2 + 2 * j, part:half] = qv_bias[j, :]
        wrel[...] = jnp.zeros_like(wrel)
        span = 2 * WIN - 1
        for ref, at in zip(rel_tables, (0, 32), strict=True):
            wrel[HD + at : HD + at + span, :HD] = ref[...]
            wrel[at : at + span, HD:] = ref[...]
        for ref in (xext, gext):
            ref[pl.ds(0, LEFT)] = jnp.zeros((LEFT, GRID, width), narrow)
            ref[pl.ds(LEFT + rows, RIGHT)] = jnp.zeros((RIGHT, GRID, width), narrow)
        greet(
            [{"tensor": place} for place in (beside, across, corner)]
            + [{"dp": mate_of(image, bit)} for bit in range(2)]
        )
        start_all(own_pack + notes + own)
        x_halo.start()
        start_all(pack_far.first)
        for ref in (xs, gs, n1_all, mixed, peak):
            ref[...] = jnp.zeros_like(ref)
        for copy in own + notes + own_pack:
            copy.wait()
        x_halo.wait_from_above()

    @pl.when(step == 1)
    def _():
        start_all(fc_beside + [g_own])

    @pl.when(step == 2)
    def _():
        receive_all(pack_far.first)
        start_all(pack_far.second)
        start_all(fc_far.first)

    @pl.when(step == 3)
    def _():
        x_halo.wait_from_below()

    @pl.when(step == 4)
    def _():
        receive_all(pack_far.second)
        start_all(pack_far.third)

    @pl.when(step == 5)
    def _():
        receive_all(fc_far.first)
        start_all(fc_far.second)
        g_halo.start()

    @pl.when(step == 6)
    def _():
        receive_all(pack_far.third)
        corner_pack.start()

    @pl.when(step == SLOTS)
    def _():
        corner_pack.wait_recv()
        start_all(kept)

    @pl.when(step == SLOTS + 2)
    def _():
        receive_all(fc_far.second)
        start_all(fc_far.third)

    row0, col0, kind, inside, offset, live = slot_fields(rows)
    whole_window = inside == SPAN
    tables = (wrel, bits.at[kind], lanes, sides, keys.at[kind])

    def biases(which):
        return (
            smalls[2 * which, 1:2, :half] + smalls[2 * which + 1, 2:3, :half],
            smalls[2 * which, 3:4, :half] + smalls[2 * which + 1, 4:5, :half],
        )

    @pl.when(step == SLOTS)
    def _():
        project(n1_all[...], weights.at[1], *biases(1), projected, slice(None))

    def work(count):
        place = rows_at(offset, count)

        @pl.when(far == 0)
        def _():
            target, valid = positions(0, count, col0, kind, inside)
            source = xext[pl.ds(row0, WIN)].reshape(WIN * GRID, width)
            window = gather_window(source, target)
            xs[place, :] = window.astype(narrow)
            normal, _ = norm_parts(window)
            n1 = jnp.where(valid, normal * params[8:9] + params[9:10], 0.0).astype(narrow)
            n1_all[place, :] = n1
            project(n1, weights.at[0], *biases(0), projected, place)

        _, valid = positions(0, count, col0, kind, inside)
        attend(
            count, place, valid, projected, biases(far)[1], *tables, qkv, mixed.at[far], peak.at[far]
        )

    pl.when(live & whole_window)(functools.partial(work, ROWS))
    pl.when(live & jnp.logical_not(whole_window))(functools.partial(work, SHORT))

    @pl.when(step == 2 * SLOTS - 1)
    def _():
        attn[...] = dot(mixed[0], weights[0, 3]) + dot(mixed[1], weights[1, 3])
        g_own.wait()
        g_halo.wait_from_above()
        g_halo.wait_from_below()

        @pl.loop(0, SLOTS)
        def _(slot):
            row0, col0, kind, inside, offset, live = window_fields(rows, device, slot)

            @pl.when(live)
            def _():
                target, _ = positions(0, ROWS, col0, kind, inside)
                source = gext[pl.ds(row0, WIN)].reshape(WIN * GRID, width)
                gs[rows_at(offset, ROWS), :] = gather_window(source, target).astype(narrow)

        for halo in (x_halo, g_halo):
            halo.wait_send()
        for group in (pack_far, fc_far):
            for copy in group.first + group.second:
                copy.wait_send()
        for copy in pack_far.third + [corner_pack]:
            copy.wait_send()
        for copy in kept + fc_beside + fc_far.third:
            copy.wait()


def whole(shape):
    zeros = (0,) * len(shape)
    return pl.BlockSpec(shape, lambda *_: zeros, pipeline_mode=pl.Buffered(1))


def by_slot(shape):
    rest = (0,) * len(shape)
    return pl.BlockSpec((1,) + tuple(shape), lambda s, *_: (s,) + rest)


ANY = pl.BlockSpec(memory_space=pl.ANY)


def of(shape, dtype=narrow):
    return jax.ShapeDtypeStruct(shape, dtype)


def forward(x, g, wqkv, wproj, fc1, fc2, vectors, qv_bias, rel_tables, tables):
    rows, _, width = x.shape
    half = 2 * wproj.shape[0]
    slab = (SLAB, width)
    outs = [
        (of(slab), ANY),
        (of(slab), whole(slab)),
        (of(slab), ANY),
        (of((2 * SLOTS, 4, ROWS, half)), by_slot((4, ROWS, half))),
        (of((2, SLAB, half)), whole((2, SLAB, half))),
        (of(slab, single), whole(slab)),
        (of((2, 8, ROWS), single), whole((2, 8, ROWS))),
        (of((16, width), single), whole((16, width))),
        (of((LANES, LANES)), whole((LANES, LANES))),
        (of((2, 4, half, width)), ANY),
        (of(fc1.shape), ANY),
        (of(fc2.shape), ANY),
        (of(fc1.shape), ANY),
        (of(fc2.shape), ANY),
        (of((SPLIT, 8, width), single), ANY),
    ]
    operands = (x, g, wqkv, wproj, fc1, fc2)
    known = (tuple(vectors), qv_bias, tuple(rel_tables), *tables)
    ext = (rows + LEFT + RIGHT, GRID, width)
    return pl.pallas_call(
        forward_kernel,
        out_shape=[o[0] for o in outs],
        grid=(2 * SLOTS,),
        in_specs=[ANY] * 6 + list(jax.tree.map(lambda a: whole(a.shape), known)),
        out_specs=[o[1] for o in outs],
        scratch_shapes=[
            pltpu.VMEM(ext, narrow),
            pltpu.VMEM(ext, narrow),
            pltpu.VMEM((2, 4, half, width), narrow),
            pltpu.VMEM((SPLIT, 8, width), single),
            pltpu.VMEM((3, SLAB, half), narrow),
            pltpu.VMEM(slab, narrow),
            pltpu.VMEM(slab, narrow),
            pltpu.SemaphoreType.DMA((32,)),
            pltpu.SemaphoreType.DMA((32,)),
            pltpu.SemaphoreType.DMA((9,)),
        ],
        compiler_params=pltpu.CompilerParams(
            vmem_limit_bytes=VMEM, collective_id=0, has_side_effects=True
        ),
        cost_estimate=pl.CostEstimate(
            flops=26_000_000_000, bytes_accessed=60_000_000, transcendentals=8_000_000
        ),
        name="attention_forward",
    )(*operands, *known)


CHUNK = SLAB // 3


def gelu_parts(z):
    size = jnp.abs(z)
    bell = jnp.exp(-0.5 * z * z)
    t = 1.0 / (1.0 + 0.2316418882663604 * size)
    poly = 0.5 * 1.061405429 * t + (0.5 * -1.453152027)
    poly = poly * t + 0.5 * 1.421413741
    poly = poly * t + 0.5 * -0.284496736
    poly = poly * t + 0.5 * 0.254829592
    tail = poly * t * bell
    phi_total = jnp.where(z >= 0, 1.0 - tail, tail)
    return z * phi_total, phi_total + z * bell * 0.3989422804014327


def mlp_kernel(
    xs, attn, gs, params, smalls, across1, across2, beside1, beside2, own1, own2,
    out_away, dx1_away, da_away, sums, near1, near2, far1, rest, gb,
    n2, n2t, gt, branch, dn2, w1, w2, grad1, grad2, got1, got2, near_got1, near_got2, landing,
    hs, zs, out, dx1, da, sends, recvs, locals_,
):
    step = pl.program_id(0)
    room = step % 2
    width = gs.shape[1]
    holder = jnp.where(step == 0, 2, jnp.where(step == 1, 3, jnp.where(step == 2, 1, 0)))
    beside, across, _ = partners(lax.axis_index("tensor"))
    send = Sender(sends, recvs, locals_)
    corners = [
        send.remote(0, across1, w1.at[1], {"tensor": beside}),
        send.remote(1, across2, w2.at[1], {"tensor": beside}),
    ]
    loads = [
        [send.local(2 * k, first, w1.at[at]), send.local(2 * k + 1, second, w2.at[at])]
        for k, (first, second, at) in enumerate(
            ((across1, across2, 0), (beside1, beside2, 0), (own1, own2, 1))
        )
    ]
    swaps = [
        send.remote(2, grad1.at[1], got1, {"tensor": beside}),
        send.remote(3, grad2.at[1], got2, {"tensor": beside}),
    ]
    crossing = send.remote(4, got1, far1, {"tensor": across})
    image = lax.axis_index("dp")
    mate = {"dp": mate_of(image, 0)}
    upper = got2.shape[0] // 2
    mine = (image % 2) * upper
    halving = send.remote(5, got2.at[rows_at(upper - mine, upper), :], landing, mate)

    def leaving(c):
        sl = rows_at(c * STRIP, STRIP)
        return [
            send.local(6 + 3 * c + k, here.at[sl, :], away.at[sl, :])
            for k, (here, away) in enumerate(((out, out_away), (dx1, dx1_away), (da, da_away)))
        ]

    near_swaps = [
        send.remote(6, grad1.at[2], near_got1, {"tensor": beside}),
        send.remote(7, grad2.at[2], near_got2, {"tensor": beside}),
    ]

    @pl.when(step == 0)
    def _():
        gb[...] = jnp.zeros_like(gb)
        start_all(loads[0])
        greet([{"tensor": beside}, {"tensor": across}, mate])
        start_all(corners)

        @pl.loop(0, SLAB // STRIP)
        def _(c):
            sl = rows_at(c * STRIP, STRIP)
            middle = xs[sl, :].astype(single) + (attn[sl, :] + params[10:11])
            dx1[sl, :] = middle
            normal, _ = norm_parts(middle)
            n2[sl, :] = (normal * params[11:12] + params[12:13]).astype(narrow)
            branch[sl, :] = jnp.zeros((STRIP, width), single)
            dn2[sl, :] = jnp.zeros((STRIP, width), single)

        for j in range(width // LANES):
            lanes = slice(j * LANES, (j + 1) * LANES)
            n2t[lanes, :] = n2[:, lanes].T
            gt[lanes, :] = gs[:, lanes].T
        for copy in loads[0]:
            copy.wait()

    @pl.when(step == 1)
    def _():
        start_all(loads[1])
        for copy in corners:
            copy.wait()

    @pl.when(step == 2)
    def _():
        start_all(swaps)
        start_all(loads[2])
        for copy in loads[1]:
            copy.wait()

    @pl.when(step == 3)
    def _():
        start_all(near_swaps)
        for copy in loads[2]:
            copy.wait()

    @pl.loop(0, SLAB // CHUNK)
    def _(c):
        @pl.when((step == 2) & (c == 1))
        def _():
            swaps[0].wait()
            add_rows(got1, 0, [(got1, 0), (grad1.at[0], 0)], got1.shape[0])
            crossing.start()
            swaps[1].wait()
            add_rows(got2, 0, [(got2, 0), (grad2.at[0], 0)], got2.shape[0])
            halving.start()

        sl = rows_at(c * CHUNK, CHUNK)
        z = dot(n2[sl, :], w1[room]) + smalls[holder, 0:1, :]
        dh = dot_nt(gs[sl, :], w2[room])
        act, slope = gelu_parts(z)
        h = act.astype(narrow)
        dz = (dh * slope).astype(narrow)
        hs[sl, :] = h
        zs[sl, :] = dz
        gb[holder, 0:1, :] += jnp.sum(dz.astype(single), axis=0, keepdims=True)
        branch[sl, :] += dot(h, w2[room])
        dn2[sl, :] += dot_nt(dz, w1[room])

    @pl.loop(0, 2)
    def _(r):
        sl = rows_at(r * (width // 2), width // 2)
        grad1[step, sl, :] = dot(n2t[sl, :], zs[...]).astype(narrow)
        grad2[step, sl, :] = dot(gt[sl, :], hs[...]).astype(narrow)

    @pl.when(step == 3)
    def _():
        halving.wait()
        add_rows(rest, 0, [(got2, mine), (landing, 0)], upper)
        for copy, near, grad, got in zip(
            near_swaps, (near1, near2), (grad1, grad2), (near_got1, near_got2), strict=True
        ):
            copy.wait()
            add_rows(near, 0, [(grad.at[3], 0), (got, 0)], near.shape[0])
        sums[...] = jnp.zeros_like(sums)

        @pl.loop(0, SLAB // STRIP)
        def _(c):
            sl = rows_at(c * STRIP, STRIP)
            middle = dx1[sl, :]
            normal, inverse = norm_parts(middle)
            out[sl, :] = (middle + (branch[sl, :] + params[13:14])).astype(narrow)
            grad = dn2[sl, :]
            cot = gs[sl, :].astype(single)
            total = cot + norm_back(grad, normal, inverse, params[11:12])
            dx1[sl, :] = total
            low = total.astype(narrow)
            da[sl, :] = low
            for copy in leaving(c):
                copy.start()
            sums[0:1, :] += jnp.sum(grad * normal, axis=0, keepdims=True)
            sums[1:2, :] += jnp.sum(grad, axis=0, keepdims=True)
            sums[2:3, :] += jnp.sum(low.astype(single), axis=0, keepdims=True)
            sums[3:4, :] += jnp.sum(cot, axis=0, keepdims=True)

        crossing.wait()
        for c in range(SLAB // STRIP):
            for copy in leaving(c):
                copy.wait()


def mlp(residents, across, beside, own):
    width, local = own[0].shape
    slab = (SLAB, width)
    square = (width, local)
    outs = [
        (of(slab), ANY),
        (of(slab, single), ANY),
        (of(slab), ANY),
        (of((8, width), single), whole((8, width))),
        (of(square), whole(square)),
        (of(square), whole(square)),
        (of(square), ANY),
        (of((local // 2, width)), whole((local // 2, width))),
        (of((SPLIT, 8, local), single), whole((SPLIT, 8, local))),
    ]
    return pl.pallas_call(
        mlp_kernel,
        out_shape=[o[0] for o in outs],
        grid=(SPLIT,),
        in_specs=[whole(a.shape) for a in residents] + [ANY] * 6,
        out_specs=[o[1] for o in outs],
        scratch_shapes=[
            pltpu.VMEM(slab, narrow),
            *[pltpu.VMEM((width, SLAB), narrow)] * 2,
            *[pltpu.VMEM(slab, single)] * 2,
            *[pltpu.VMEM((2, *square), narrow)] * 2,
            *[pltpu.VMEM((SPLIT, *square), narrow)] * 2,
            *[pltpu.VMEM(square, narrow)] * 4,
            pltpu.VMEM((width // 2, local), narrow),
            *[pltpu.VMEM((SLAB, local), narrow)] * 2,
            pltpu.VMEM(slab, narrow),
            pltpu.VMEM(slab, single),
            pltpu.VMEM(slab, narrow),
            pltpu.SemaphoreType.DMA((8,)),
            pltpu.SemaphoreType.DMA((8,)),
            pltpu.SemaphoreType.DMA((6 + 3 * (SLAB // STRIP),)),
        ],
        compiler_params=pltpu.CompilerParams(
            vmem_limit_bytes=VMEM, collective_id=1, has_side_effects=True
        ),
        cost_estimate=pl.CostEstimate(
            flops=36_000_000_000, bytes_accessed=60_000_000, transcendentals=8_000_000
        ),
        name="mlp",
    )(*residents, *across, *beside, *own)


def backward_kernel(
    rows_held, images,
    da, n1, qkv, mixed, wproj, wrel, bits, lanes, sides, keys, near1, near2, far1, rest,
    dqkv, keep, give, bias, grel, crossed, summed1, summed2,
    dmix, got_far, held1, held2, land1, land2, rest_got,
    sends, recvs, locals_,
):
    step = pl.program_id(0)
    slot, far = step % SLOTS, 1 - step // SLOTS
    image = lax.axis_index("dp")
    beside, across, _ = partners(lax.axis_index("tensor"))
    send = Sender(sends, recvs, locals_)
    half = wproj.shape[2]
    per = Halver.copies(images)
    sum1 = Halver(send, 3, image, images, 0, held1.shape[0], (1, 0, 2))
    sum2 = Halver(send, 3 + per, image, images, 0, held2.shape[0], (0, 1, 2))
    rest_cross = send.remote(0, rest, rest_got, {"tensor": across})
    far_swap = send.remote(1, give.at[0], got_far, {"tensor": beside})
    far_cross = send.remote(2, got_far, crossed, {"tensor": across})

    halvers = ((sum1, held1, land1), (sum2, held2, land2))
    summed = (summed1, summed2)

    def seed(k, halver, held, summed):
        start, length = halver.final
        copy = send.local(k, held.at[rows_at(start, length), :], summed.at[rows_at(start, length), :])
        copy.start()
        copy.wait()

    def begin():
        greet([{"tensor": beside}, {"tensor": across}] + dp_mates(image, images))
        rest_cross.start()
        sum2.start(0, near2, land2)
        add_rows(held1, 0, [(near1, 0), (far1, 0)], held1.shape[0])
        sum1.start(0, held1, land1)

    def second():
        sum1.finish(0, held1, land1)
        sum1.start(1, held1, land1)
        sum2.out(0, near2, land2).wait()
        rest_cross.wait()
        _, kept, _, length, at = sum2.stages[0]
        add_rows(held2, kept, [(near2, kept), (land2, at), (rest_got, 0)], length)
        sum2.start(1, held2, land2)

    def third():
        for halver, held, land in halvers:
            halver.finish(1, held, land)
            halver.start(2, held, land)

    def fourth():
        for n, (halver, held, land) in enumerate(halvers):
            halver.finish(2, held, land)
            halver.extras(held, land)
            seed(n, halver, held, summed[n])
            halver.back(2, summed[n]).start()

    def hand(stage):
        for (halver, _, _), total in zip(halvers, summed, strict=True):
            halver.back(stage + 1, total).wait()
            halver.back(stage, total).start()

    def swap_far():
        far_swap.start()

    def cross_far():
        far_swap.wait()
        add_rows(got_far, 0, [(got_far, 0), (keep.at[0], 0)], got_far.shape[0])
        far_cross.start()

    events = {
        (0, 0): begin,
        (3, 1): second,
        (5, 0): third,
        (7, 0): swap_far,
        (7, 3): fourth,
        (8, 0): cross_far,
        (10, 3): functools.partial(hand, 1),
    }

    def fire(section):
        for (at, place), event in events.items():
            if place == section:
                pl.when(step == at)(event)

    _, col0, kind, inside, offset, live = slot_fields(rows_held)
    whole_window = inside == SPAN

    def on_window(action):
        for count, holds in ((ROWS, whole_window), (SHORT, jnp.logical_not(whole_window))):
            pl.when(live & holds)(functools.partial(action, count))

    @pl.when(step == 0)
    def _():
        for ref in (bias, grel, dqkv):
            ref[...] = jnp.zeros_like(ref)

    fire(0)

    @pl.when(slot == 0)
    def _():
        dmix[...] = dot_nt(da[...], wproj[far, 0]).astype(narrow)

    def one_pair(pair, count):
        cut = slice(pair * LANES, (pair + 1) * LANES)
        q, k8, v, rel = (qkv[0, j, :n, cut] for j, n in enumerate((count, ROWS, ROWS, count)))
        place = rows_at(offset, count)
        do = dmix[place, cut]
        dqs, dks, dvs = [], [], []
        for head in range(2):
            mine, other = sides[head : head + 1], sides[1 - head : 2 - head]
            full_key = k8 * mine + keys[kind] * other
            scores = dot_nt(full_key, q * mine + rel * other)
            top = jnp.max(scores, axis=0, keepdims=True)
            probs = jnp.exp(scores - top)
            probs = probs * (1.0 / jnp.sum(probs, axis=0, keepdims=True))
            dprobs = dot_nt(v, do * mine)
            mean = jnp.sum(probs * dprobs, axis=0, keepdims=True)
            dscores = (probs * (dprobs - mean)).astype(narrow)
            dvs.append(dot(probs.astype(narrow), do))
            dks.append(dot(dscores, q))
            dqs.append(dot_tn(dscores, full_key))
        low_lane = lax.broadcasted_iota(jnp.int32, (ROWS, LANES), 1) < 64
        dv = jnp.where(low_lane, dvs[0], dvs[1])
        dk = jnp.where(low_lane, dks[0], dks[1]) * 0.125
        low_lane = lax.broadcasted_iota(jnp.int32, (count, LANES), 1) < 64
        dq = jnp.where(low_lane, dqs[0], dqs[1])
        drel = jnp.where(low_lane, dqs[1], dqs[0]) * lanes[0:1]
        drel = shift_right(drel, bits.at[kind]).astype(narrow)
        dq = dq + dot(drel, wrel[...])
        grel[...] += dot_tn(drel, q)
        for j, value in enumerate((dq, dk, dv)):
            value = value.astype(narrow).astype(single)
            if j != 1:
                bias[far, j : j + 1, cut] += jnp.sum(value, axis=0, keepdims=True)
            value = value[:count]
            if count < ROWS:
                _, valid = positions(0, count, 0, kind, inside)
                value = jnp.where(valid, value, 0.0)
            dqkv[far, j, place, cut] = value.astype(narrow)

    for pair in range(half // LANES):
        fire(pair + 1)
        on_window(functools.partial(one_pair, pair))

    @pl.when(slot == SLOTS - 1)
    def _():
        part = half // 2
        at = step // SLOTS
        for j in range(4):
            if j < 3:
                total = dot_tn(dqkv[far, j], n1[...])
            else:
                total = dot_tn(mixed[far], da[...])
            keep[at, j * part : (j + 1) * part, :] = total[:part].astype(narrow)
            give[at, j * part : (j + 1) * part, :] = total[part:].astype(narrow)

    @pl.when(step == 2 * SLOTS - 1)
    def _():
        for (halver, _, _), total in zip(halvers, summed, strict=True):
            halver.back(1, total).wait()
        far_cross.wait()


def backward(rows_held, images, da, n1, qkv, mixed, weights, wrel, tables, residents, rest):
    half, width = weights.shape[2:]
    operands = [da, n1, qkv, mixed, weights, wrel, *tables, *residents, rest]
    in_specs = [whole(a.shape) for a in operands]

    def halved(i):
        return (1 - i // SLOTS) * SLOTS + i % SLOTS

    in_specs[2] = pl.BlockSpec((1, 4, ROWS, half), lambda i: (halved(i), 0, 0, 0))
    in_specs[4] = pl.BlockSpec(
        (2, 1, half, width), lambda i: (0, 3, 0, 0), pipeline_mode=pl.Buffered(1)
    )
    in_specs[-1] = ANY
    packed = (2 * half, width)
    square = residents[0].shape
    outs = [
        (of((2, 3, SLAB, half)), whole((2, 3, SLAB, half))),
        (of((2, *packed)), whole((2, *packed))),
        (of((2, *packed)), whole((2, *packed))),
        (of((2, 8, half), single), whole((2, 8, half))),
        (of((LANES, LANES), single), whole((LANES, LANES))),
        (of(packed), ANY),
        (of(square), ANY),
        (of(square), ANY),
    ]
    landing = (Halver.landing_rows(images, square[0]), width)
    copies = 3 + 2 * Halver.copies(images)
    return pl.pallas_call(
        functools.partial(backward_kernel, rows_held, images),
        out_shape=[o[0] for o in outs],
        grid=(2 * SLOTS,),
        in_specs=in_specs,
        out_specs=[o[1] for o in outs],
        scratch_shapes=[
            pltpu.VMEM((SLAB, half), narrow),
            pltpu.VMEM(packed, narrow),
            *[pltpu.VMEM(square, narrow)] * 2,
            *[pltpu.VMEM(landing, narrow)] * 2,
            pltpu.VMEM(rest.shape, narrow),
            pltpu.SemaphoreType.DMA((copies,)),
            pltpu.SemaphoreType.DMA((copies,)),
            pltpu.SemaphoreType.DMA((2,)),
        ],
        compiler_params=pltpu.CompilerParams(
            vmem_limit_bytes=VMEM, collective_id=2, has_side_effects=True
        ),
        cost_estimate=pl.CostEstimate(
            flops=52_000_000_000, bytes_accessed=80_000_000, transcendentals=8_000_000
        ),
        name="attention_backward",
    )(*operands)


def clear_rows(ext):
    @pl.loop(0, ext.shape[0] // GRID)
    def _(r):
        ext[rows_at(r * GRID, GRID), :] = jnp.zeros((GRID, ext.shape[1]), narrow)


def place_windows(rows_held, device, slab, ext, first, last):
    @pl.loop(first, last)
    def _(slot):
        row0, col0, kind, inside, offset, live = window_fields(rows_held, device, slot)

        @pl.when(live)
        def _():
            target, _ = positions(1, ROWS, col0, kind, inside)
            token = lax.broadcasted_iota(jnp.int32, (WIN * GRID, ROWS), 0)
            choose = jnp.where(token == target, 1.0, 0.0).astype(narrow)
            window = slab[rows_at(offset, ROWS), :]
            where_to = pl.ds(pl.multiple_of(row0 * GRID, GRID), WIN * GRID)
            ext[where_to, :] += dot(choose, window).astype(narrow)


def tail_kernel(
    rows_held, images,
    sums2, bias, rel_sum, fc_bias, peak, params,
    out_in, keep_in, crossed_in, xs_in, dx1_in, part1, part2, give, dqkv, weights,
    output, input_grad, packed, totals, tops, summed1, summed2,
    ext0, ext1, below0, below1, above0, above1, got, landing, held, sum_land, top_land, back, grads,
    packs, out, keep, crossed, xs, dx1, sends, recvs, locals_,
):
    device, image = lax.axis_index("tensor"), lax.axis_index("dp")
    beside, across, corner = partners(device)
    send = Sender(sends, recvs, locals_)
    hand_base = 1 + 2 * Halver.copies(images) + 4 + 2 * (1 + images.bit_length())
    early = [send.local(0, keep_in.at[1], keep), send.local(1, crossed_in, crossed)]
    loads = [
        send.local(2, dqkv, grads),
        send.local(3, weights.at[:, 0:3], packs),
        send.local(4, xs_in, xs),
        send.local(5, dx1_in, dx1),
    ]
    late = send.local(6, out_in, out)
    start_all(early + loads + [late])
    hand_last, stay = [], []
    for k, (part, summed, order) in enumerate(
        ((part1, summed1, (1, 0, 2)), (part2, summed2, (0, 1, 2)))
    ):
        mate, kept, _, length, _ = Halver(
            send, 0, image, images, 0, part.shape[0], order
        ).stages[0]
        cut = rows_at(kept, length)
        stay.append(send.local(7 + k, part.at[cut, :], summed.at[cut, :]))
        hand_last.append(
            send.remote(hand_base + k, part.at[cut, :], summed.at[cut, :], {"dp": mate})
        )
    start_all(stay)
    per = Halver.copies(images)
    middle = held.shape[0] // 2
    landing_rows = Halver.landing_rows(images, middle)
    landings = [landing.at[pl.ds(k * landing_rows, landing_rows), :] for k in range(2)]
    halvers = [
        Halver(send, 1 + k * per, image, images, k * middle, middle, order)
        for k, order in enumerate(((0, 1, 2), (1, 0, 2)))
    ]
    halo_base = 1 + 2 * per
    small_base = halo_base + 4
    tokens = rows_held * GRID
    top, bottom = LEFT * GRID, RIGHT * GRID
    held_by = (device, beside, across, corner)
    mates = dp_mates(image, images)
    ring = [{"tensor": beside}, {"tensor": across}] + mates

    def reduce_start(stage):
        for halver, land in zip(halvers, landings, strict=True):
            halver.start(stage, held, land)

    def reduce_finish(stage):
        for halver, land in zip(halvers, landings, strict=True):
            halver.finish(stage, held, land)

    def hand_start(stage):
        for halver in halvers:
            halver.back(stage, packed).start()

    def hand_finish(stage):
        for halver in halvers:
            halver.back(stage, packed).wait()

    greet([{"tensor": place} for place in (beside, across, corner)] + mates)
    swap = send.remote(0, give.at[1], got, {"tensor": beside})
    swap.start()
    totals[...] = jnp.zeros_like(totals)
    tops[...] = jnp.zeros_like(tops)
    totals[2:6, :] = sums2[0:4, :]
    rel = rel_sum[...]
    rel = rel[HD:] + pltpu.roll(rel[:HD], HD, 1)
    for g in range(HD // 8):
        at = 8 * (1 + g // 6)
        totals[at : at + 8, (g % 6) * LANES : (g % 6 + 1) * LANES] = rel[8 * g : 8 * g + 8]
    half = bias.shape[2]
    for k in range(SPLIT):
        far, odd = k // 2, k % 2
        totals[pl.ds(24 + held_by[k], 1), :] = fc_bias[k, 0:1, :]
        for j, row in enumerate((0, 2)):
            value = bias[far, row : row + 1, :]
            if odd:
                value = pltpu.roll(value, half // 2, 1)
            totals[pl.ds(28 + held_by[k], 1), j * half : (j + 1) * half] = value
        best = jnp.broadcast_to(jnp.max(peak[far], axis=1, keepdims=True), (8, LANES))
        if odd:
            best = pltpu.roll(best, 8 - half // LANES, 0)
        tops[pl.ds(pl.multiple_of(held_by[k] * 8, 8), 8), :] = best

    def small_copies(k):
        return [
            send.remote(small_base + 2 * k, totals, sum_land.at[k], ring[k]),
            send.remote(small_base + 2 * k + 1, tops, top_land.at[k], ring[k]),
        ]

    def small_start(k):
        for copy in small_copies(k):
            copy.start()

    def small_finish(k):
        for copy in small_copies(k):
            copy.wait()
        totals[...] += sum_land[k]
        tops[...] = jnp.maximum(tops[...], top_land[k])

    def halo(base, ext, below, above):
        up = send.remote(
            base, ext.at[pl.ds(0, top), :], below, {"tensor": (device + SPLIT - 1) % SPLIT}
        )
        down = send.remote(
            base + 1, ext.at[pl.ds(top + tokens, bottom), :], above, {"tensor": (device + 1) % SPLIT}
        )
        return up, down

    def halo_start(copies):
        up, down = copies
        pl.when(device > 0)(up.start)
        pl.when(device < SPLIT - 1)(down.start)

    def halo_finish(copies, ext, below, above, result):
        up, down = copies
        pl.when(device > 0)(up.wait_send)
        pl.when(device < SPLIT - 1)(down.wait_send)
        add_rows(result, 0, [(ext, top)], tokens)

        @pl.when(device < SPLIT - 1)
        def _():
            up.wait_recv()
            at = tokens - top
            add_rows(result, at, [(result, at), (below, 0)], top)

        @pl.when(device > 0)
        def _():
            down.wait_recv()
            add_rows(result, 0, [(result, 0), (above, 0)], bottom)

    def norm1_back():
        @pl.loop(0, SLAB // CHUNK)
        def _(c):
            sl = rows_at(c * CHUNK, CHUNK)
            grad = None
            for far in range(2):
                for j in range(3):
                    term = dot(grads[far, j, sl, :], packs[far, j])
                    grad = term if grad is None else grad + term
            normal, inverse = norm_parts(xs[sl, :].astype(single))
            totals[0:1, :] += jnp.sum(grad * normal, axis=0, keepdims=True)
            totals[1:2, :] += jnp.sum(grad, axis=0, keepdims=True)
            result = dx1[sl, :] + norm_back(grad, normal, inverse, params[8:9])
            back[sl, :] = result.astype(narrow)

    clear_rows(ext0)
    clear_rows(ext1)
    for copy in early:
        copy.wait()
    swap.wait()
    add_rows(held, 0, [(keep, 0), (got, 0), (crossed, 0)], held.shape[0])
    reduce_start(0)
    for copy in loads:
        copy.wait()
    norm1_back()
    small_start(0)
    reduce_finish(0)
    reduce_start(1)
    place_windows(rows_held, device, back, ext1, 0, 3)
    small_finish(0)
    small_start(1)
    reduce_finish(1)
    reduce_start(2)
    start_all(hand_last)
    place_windows(rows_held, device, back, ext1, 3, SLOTS)
    halos1 = halo(halo_base, ext1, below1, above1)
    halo_start(halos1)
    late.wait()
    place_windows(rows_held, device, out, ext0, 0, 3)
    small_finish(1)
    small_start(2)
    reduce_finish(2)
    for halver, land in zip(halvers, landings, strict=True):
        halver.extras(held, land)
        start, length = halver.final
        packed[rows_at(start, length), :] = held[rows_at(start, length), :]
    hand_start(2)
    place_windows(rows_held, device, out, ext0, 3, SLOTS)
    halos0 = halo(halo_base + 2, ext0, below0, above0)
    halo_start(halos0)
    small_finish(2)
    small_start(3)
    hand_finish(2)
    hand_start(1)
    small_finish(3)
    small_start(4)
    hand_finish(1)
    hand_start(0)
    halo_finish(halos1, ext1, below1, above1, input_grad)
    for k in range(4, len(ring)):
        small_finish(k)
        if k + 1 < len(ring):
            small_start(k + 1)
    halo_finish(halos0, ext0, below0, above0, output)
    hand_finish(0)
    for copy in stay + hand_last:
        copy.wait()


def tail(rows_held, images, *operands):
    width = operands[-1].shape[3]
    half = operands[-1].shape[2]
    packed = (2 * half, width)
    tokens = rows_held * GRID
    bits = images.bit_length() - 1
    landing = 2 * Halver.landing_rows(images, packed[0] // 2)
    copies = 1 + 2 * Halver.copies(images) + 4 + 2 * (2 + bits) + 2
    ext = ((rows_held + LEFT + RIGHT) * GRID, width)
    outs = [
        of((tokens, width)), of((tokens, width)), of(packed),
        of((32, width), single), of((32, LANES), single),
        of(operands[-5].shape), of(operands[-4].shape),
    ]
    return pl.pallas_call(
        functools.partial(tail_kernel, rows_held, images),
        out_shape=outs,
        in_specs=[pl.BlockSpec(memory_space=pltpu.VMEM)] * (len(operands) - 10) + [ANY] * 10,
        out_specs=[pl.BlockSpec(memory_space=pltpu.VMEM)] * 5 + [ANY] * 2,
        scratch_shapes=[
            pltpu.VMEM(ext, narrow),
            pltpu.VMEM(ext, narrow),
            pltpu.VMEM((LEFT * GRID, width), narrow),
            pltpu.VMEM((LEFT * GRID, width), narrow),
            pltpu.VMEM((RIGHT * GRID, width), narrow),
            pltpu.VMEM((RIGHT * GRID, width), narrow),
            pltpu.VMEM(packed, narrow),
            pltpu.VMEM((landing, width), narrow),
            pltpu.VMEM(packed, narrow),
            pltpu.VMEM((2 + bits, 32, width), single),
            pltpu.VMEM((2 + bits, 32, LANES), single),
            pltpu.VMEM((SLAB, width), narrow),
            pltpu.VMEM((2, 3, SLAB, half), narrow),
            pltpu.VMEM((2, 3, half, width), narrow),
            pltpu.VMEM((SLAB, width), narrow),
            *[pltpu.VMEM(packed, narrow)] * 2,
            pltpu.VMEM((SLAB, width), narrow),
            pltpu.VMEM((SLAB, width), single),
            pltpu.SemaphoreType.DMA((copies,)),
            pltpu.SemaphoreType.DMA((copies,)),
            pltpu.SemaphoreType.DMA((9,)),
        ],
        compiler_params=pltpu.CompilerParams(
            vmem_limit_bytes=VMEM, collective_id=3, has_side_effects=True
        ),
        cost_estimate=pl.CostEstimate(
            flops=4_000_000_000, bytes_accessed=20_000_000, transcendentals=0
        ),
        name="tail",
    )(*operands)


def finish_kernel(
    fc1, fc2, gq, gp, out_in, back_in, totals, tops, wqkv,
    grad_fc1, grad_fc2, grad_qkv, grad_proj, out, back, clipped, qv, fc1_bias, norms, proj_bias,
    fc2_bias, rel, head_max,
):
    device = lax.axis_index("tensor")
    out[...] = out_in[...]
    back[...] = back_in[...]
    grad_fc1[...] = fc1[...].astype(single)
    grad_fc2[...] = fc2[...].astype(single).T
    grad_qkv[...] = gq[...].astype(single)
    grad_proj[...] = gp[...].astype(single)

    @pl.when(pl.program_id(0) == 0)
    def _():
        local = wqkv.shape[1]
        largest = tops[pl.ds(pl.multiple_of(8 * device, 8), 8), :]
        head_max[...] = largest.T[0, : local // HD]
        limit = jnp.maximum(largest, CLIP)
        factor = jnp.sqrt(CLIP / limit)
        factor = jnp.concatenate([factor] * (wqkv.shape[2] // LANES), axis=1)
        for j in range(2):
            for head in range(local // HD):
                cut = slice(head * HD, (head + 1) * HD)
                scaled = wqkv[j, cut, :].astype(single) * factor[head : head + 1]
                clipped[j, cut, :] = scaled.astype(narrow)
            qv[j : j + 1, :] = totals[pl.ds(28 + device, 1), 2 * j * local : (2 * j + 1) * local]
        fc1_bias[...] = totals[24 + device, :]
        norms[...] = totals[0:4, :]
        proj_bias[...] = totals[4, :]
        fc2_bias[...] = totals[5, :]
        span = 2 * WIN - 1
        for j in range(2):
            for first in range(0, span, 8):
                group = (32 * j + first) // 8
                count = min(8, span - first)
                at, lane = 8 * (1 + group // 6), (group % 6) * LANES
                rel[first : first + count, j, :] = totals[at : at + count, lane : lane + HD]


def finish(summed1, summed2, gpack, output, input_grad, totals, tops, wqkv):
    _, local, width = wqkv.shape
    hidden = summed1.shape[1]
    parts = 3
    batch = output.shape[0] // 2
    pages = pl.BlockSpec((batch, width), lambda i: (jnp.minimum(i, 1), 0))
    heads = local // HD
    rows, cols, lines = width // parts, hidden // parts, 3 * local // parts
    few = local // parts

    def by_rows(count, columns, first=0):
        return pl.BlockSpec((count, columns), lambda i: (first + i, 0))

    span = 2 * WIN - 1
    outs = [
        (of((width, hidden), single), by_rows(rows, hidden)),
        (of((hidden, width), single), by_rows(cols, width)),
        (of((3 * local, width), single), by_rows(lines, width)),
        (of((local, width), single), by_rows(few, width)),
        (of(output.shape), pages),
        (of(output.shape), pages),
        (of((2, local, width)), whole((2, local, width))),
        (of((2, local), single), whole((2, local))),
        (of((hidden,), single), whole((hidden,))),
        (of((4, width), single), whole((4, width))),
        (of((width,), single), whole((width,))),
        (of((width,), single), whole((width,))),
        (of((span, 2, HD), single), whole((span, 2, HD))),
        (of((heads,), single), whole((heads,))),
    ]
    return pl.pallas_call(
        finish_kernel,
        out_shape=[o[0] for o in outs],
        grid=(parts,),
        in_specs=[
            by_rows(rows, hidden),
            pl.BlockSpec((width, cols), lambda i: (0, i)),
            by_rows(lines, width),
            by_rows(few, width, 3 * local // few),
            pages,
            pages,
            whole(totals.shape),
            whole(tops.shape),
            whole(wqkv.shape),
        ],
        out_specs=[o[1] for o in outs],
        compiler_params=pltpu.CompilerParams(vmem_limit_bytes=VMEM),
        cost_estimate=pl.CostEstimate(flops=0, bytes_accessed=14_000_000, transcendentals=0),
        name="finish",
    )(summed1, summed2, gpack, gpack, output, input_grad, totals, tops, wqkv)


def shards(
    inputs,
    w_qkv,
    qv_bias,
    w_proj,
    proj_bias,
    w_fc1,
    fc1_bias,
    w_fc2,
    fc2_bias,
    norm1_gain,
    norm1_shift,
    norm2_gain,
    norm2_shift,
    rel_h,
    rel_w,
    cotangent,
):
    width = inputs.shape[2]
    rows = inputs.shape[1] // GRID
    local = w_qkv.shape[2]
    tables = lane_tables()

    wqkv = w_qkv.transpose(0, 2, 1)

    (
        xs, gs, n1, qkv, mixed, attn, peak, params, wrel,
        weights, across1, across2, beside1, beside2, smalls,
    ) = forward(
        *(a.reshape(rows, GRID, width) for a in (inputs, cotangent)), wqkv, w_proj, w_fc1, w_fc2,
        (
            fc1_bias, norm1_gain, norm1_shift, proj_bias, norm2_gain, norm2_shift, fc2_bias,
        ),
        qv_bias, (rel_h, rel_w), tables
    )
    out, dx1, da, sums2, near1, near2, far1, rest, fc_bias = mlp(
        (
            xs, attn, gs, params, smalls,
        ),
        (across1, across2),
        (beside1, beside2),
        (w_fc1, w_fc2),
    )
    images = lax.axis_size("dp")
    dqkv, keep, give, bias, rel_sum, crossed, part1, part2 = backward(
        rows, images, da, n1, qkv, mixed, weights, wrel, tables, [near1, near2, far1], rest
    )
    output, input_grad, gpack, totals, tops, summed1, summed2 = tail(
        rows, images, sums2, bias, rel_sum, fc_bias, peak, params, out, keep, crossed, xs, dx1,
        part1, part2, give, dqkv, weights,
    )
    (
        grad_fc1, grad_fc2, grad_qkv, grad_proj, output, input_grad, clipped, grad_qv,
        grad_fc1_bias, grad_norms, grad_proj_bias, grad_fc2_bias, grad_rel, head_max,
    ) = finish(summed1, summed2, gpack, output, input_grad, totals, tops, wqkv)

    return (
        output[None],
        input_grad[None],
        grad_qkv.reshape(3, local, width).transpose(0, 2, 1),
        grad_qv,
        grad_proj,
        grad_proj_bias,
        grad_fc1,
        grad_fc1_bias,
        grad_fc2,
        grad_fc2_bias,
        grad_norms,
        grad_rel.transpose(1, 0, 2),
        clipped.transpose(0, 2, 1),
        head_max,
    )


def solution(mesh):
    return jax.shard_map(
        shards,
        mesh=mesh,
        in_specs=(
            P("dp", "tensor", None),
            P(None, None, "tensor"),
            P(None, "tensor"),
            P("tensor", None),
            P(),
            P(None, "tensor"),
            P("tensor"),
            P("tensor", None),
            P(),
            P(),
            P(),
            P(),
            P(),
            P(),
            P(),
            P("dp", "tensor", None),
        ),
        out_specs=(
            P("dp", "tensor", None),
            P("dp", "tensor", None),
            P(None, None, "tensor"),
            P(None, "tensor"),
            P("tensor", None),
            P(),
            P(None, "tensor"),
            P("tensor"),
            P("tensor", None),
            P(),
            P(),
            P(),
            P(None, None, "tensor"),
            P("tensor"),
        ),
        check_vma=False,
    )
```
